32 devices in a mesh: dp: 4 (over y, core), fsdp: 8 (over z, x).
Axes of the slice: x: 2, y: 2, z: 4, core: 2. Of those that a mesh axis runs over, the one named last changes fastest.
Arguments:
- tokens: bfloat16 [64, 1024, 768], P(None, ('dp', 'fsdp')), may hold values from -6 to 6
- cotangent: bfloat16 [64, 1024, 768], P(None, ('dp', 'fsdp')), may hold values from -6 to 6
- lengths: int32 [64], replicated, may hold values from 64 to 1024, as said below
- permutation: int32 [64], replicated, may hold values from 0 to 63, as said below
- q_weight: bfloat16 [768, 192], P(('dp', 'fsdp')), may hold values from -0.625 to 0.625
- q_bias: bfloat16 [768], P(('dp', 'fsdp')), may hold values from -4 to 4
- k_weight: bfloat16 [768, 192], P(('dp', 'fsdp')), may hold values from -0.625 to 0.625
- v_weight: bfloat16 [768, 192], P(('dp', 'fsdp')), may hold values from -0.4375 to 0.4375
- v_bias: bfloat16 [768], P(('dp', 'fsdp')), may hold values from -4 to 4
- o_weight: bfloat16 [768, 768], P(('dp', 'fsdp')), may hold values from -0.625 to 0.625
- o_bias: bfloat16 [768], P(('dp', 'fsdp')), may hold values from -3 to 3
- norm1_gain: bfloat16 [768], P(('dp', 'fsdp')), may hold values from 0.25 to 1.75
- norm1_bias: bfloat16 [768], P(('dp', 'fsdp')), may hold values from -3 to 3
- up_weight: bfloat16 [3072, 192], P(('dp', 'fsdp')), may hold values from -0.4375 to 0.4375
- up_bias: bfloat16 [3072], P(('dp', 'fsdp')), may hold values from -3 to 3
- down_weight: bfloat16 [768, 768], P(('dp', 'fsdp')), may hold values from -0.21875 to 0.21875
- down_bias: bfloat16 [768], P(('dp', 'fsdp')), may hold values from -3 to 3
- norm2_gain: bfloat16 [768], P(('dp', 'fsdp')), may hold values from 0.25 to 1.75
- norm2_bias: bfloat16 [768], P(('dp', 'fsdp')), may hold values from -3 to 3
Outputs:
- output: bfloat16 [64, 1024, 768], P(None, ('dp', 'fsdp'))
- input_grad: bfloat16 [64, 1024, 768], P(None, ('dp', 'fsdp'))
- q_weight_grad: float32 [768, 192], P(('dp', 'fsdp'))
- q_bias_grad: float32 [768], P(('dp', 'fsdp'))
- k_weight_grad: float32 [768, 192], P(('dp', 'fsdp'))
- v_weight_grad: float32 [768, 192], P(('dp', 'fsdp'))
- v_bias_grad: float32 [768], P(('dp', 'fsdp'))
- o_weight_grad: float32 [768, 768], P(('dp', 'fsdp'))
- o_bias_grad: float32 [768], P(('dp', 'fsdp'))
- norm1_gain_grad: float32 [768], P(('dp', 'fsdp'))
- norm1_bias_grad: float32 [768], P(('dp', 'fsdp'))
- up_weight_grad: float32 [3072, 192], P(('dp', 'fsdp'))
- up_bias_grad: float32 [3072], P(('dp', 'fsdp'))
- down_weight_grad: float32 [768, 768], P(('dp', 'fsdp'))
- down_bias_grad: float32 [768], P(('dp', 'fsdp'))
- norm2_gain_grad: float32 [768], P(('dp', 'fsdp'))
- norm2_bias_grad: float32 [768], P(('dp', 'fsdp'))
- stream_rms: float32 [4, 64], P(None, ('dp', 'fsdp'))
The draws below stay inside these ranges and needn't reach their ends.
Inputs may be any that keep to these rules, and one draw needn't show every extreme that they name: `lengths`: some sequence has exactly 1024 valid tokens and some exactly 64. A permutation of the 64 sequences; the sequences at dealt positions 2 j and 2 j + 1 have 1024 + 64 valid tokens together.
All inputs are finite; a program needn't handle non-finite values.
Results may differ from the reference program's by a relative error of at most 0.014.
The reference program's roundings to bfloat16 on the way count: a program that leaves them out, or rounds other values in their place, can miss the bound.
Values may be sent and summed in bfloat16 or wider, within the bound.
A program may use at most 320 MiB of HBM per device.

```python
import math
import jax
import jax.numpy as jnp
from jax import lax

D = 768
H = 12
HEAD = 64
FF = 3072
GROUPS = 4
L = 1024
SHORT = 64
SEQS = 64


def dealt_lengths(key):
    half_count = SEQS // 2
    first_len = jax.random.randint(jax.random.fold_in(key, 7), (half_count,), SHORT, L + 1, dtype=jnp.int32)
    first_len = first_len.at[0].set(L)
    second = L + SHORT - first_len
    return jnp.stack([first_len, second], axis=1).reshape(SEQS)


def dealt_order(key):
    return jax.random.permutation(jax.random.fold_in(key, 9), SEQS).astype(jnp.int32)


def draw_lengths(key, part):
    order_all = dealt_order(key)
    return jnp.zeros((SEQS,), jnp.int32).at[order_all].set(dealt_lengths(key))


def draw_permutation(key, part):
    return dealt_order(key)


def level_of(stream_key, extent, cuts, least, high):
    def one(dim, shards_of):
        steps = jax.random.uniform(jax.random.fold_in(jax.random.fold_in(stream_key, 6), dim), (shards_of,), jnp.float32, least / len(cuts), high / len(cuts))
        return jnp.repeat(jnp.exp(steps), extent[dim] // shards_of).reshape((-1,) + (1,) * (len(extent) - dim - 1))

    level = one(*cuts[0])
    for cut in cuts[1:]:
        level = level * one(*cut)
    return level


def gaussian(own_key, extent, scale, reach, cuts=(), held_as=jnp.bfloat16):
    factor_of = level_of(own_key, extent, cuts, -0.22, 0.18) if cuts else 1.0
    drawn = jax.random.normal(own_key, extent, jnp.float32) * scale * factor_of
    return jnp.minimum(jnp.maximum(drawn, -reach), reach).astype(held_as)


def setup_inputs(seed: int = 0) -> dict:
    seeds = jax.random.split(jax.random.key(seed), 20)
    return {
        "tokens": gaussian(seeds[0], (SEQS, L, D), 1.0, 6.0, ((1, 32),)),
        "cotangent": gaussian(seeds[1], (SEQS, L, D), 1.0, 6.0, ((1, 32),)),
        "lengths": draw_lengths(jax.random.fold_in(seeds[19], 71), 0),
        "permutation": draw_permutation(jax.random.fold_in(seeds[19], 71), 0),
        "q_weight": gaussian(seeds[4], (D, D // GROUPS), (D // GROUPS // 2) ** -0.5, 0.625, ((0, 32),)),
        "q_bias": gaussian(seeds[5], (D,), 0.3, 4.0, ((0, 32),)),
        "k_weight": gaussian(seeds[6], (D, D // GROUPS), (D // GROUPS // 2) ** -0.5, 0.625, ((0, 32),)),
        "v_weight": gaussian(seeds[7], (D, D // GROUPS), (D // GROUPS) ** -0.5, 0.4375, ((0, 32),)),
        "v_bias": gaussian(seeds[8], (D,), 0.3, 4.0, ((0, 32),)),
        "o_weight": gaussian(seeds[9], (D, D), (D // 8) ** -0.5, 0.625, ((0, 32),)),
        "o_bias": gaussian(seeds[10], (D,), 0.2, 3.0, ((0, 32),)),
        "norm1_gain": jnp.clip(1.0 + 0.15 * jax.random.normal(seeds[11], (D,), jnp.float32), 0.25, 1.75).astype(jnp.bfloat16),
        "norm1_bias": gaussian(seeds[12], (D,), 0.2, 3.0, ((0, 32),)),
        "up_weight": gaussian(seeds[13], (FF, D // GROUPS), (D // GROUPS) ** -0.5, 0.4375, ((0, 32),)),
        "up_bias": gaussian(seeds[14], (FF,), 0.2, 3.0, ((0, 32),)),
        "down_weight": gaussian(seeds[15], (D, FF // GROUPS), (FF // GROUPS) ** -0.5, 0.21875, ((0, 32),)),
        "down_bias": gaussian(seeds[16], (D,), 0.2, 3.0, ((0, 32),)),
        "norm2_gain": jnp.clip(1.0 + 0.15 * jax.random.normal(seeds[17], (D,), jnp.float32), 0.25, 1.75).astype(jnp.bfloat16),
        "norm2_bias": gaussian(seeds[18], (D,), 0.2, 3.0, ((0, 32),)),
    }


@jax.custom_vjp
def low(v):
    return lax.optimization_barrier(v.astype(jnp.bfloat16)).astype(jnp.float32)

@jax.custom_vjp
def low_back(v):
    return v

def low_keep(v):
    return (low(v), None)

def low_pass(kept, grad):
    return (grad,)

def back_keep(v):
    return (v, None)

def back_low(kept, grad):
    return (low(grad),)
low.defvjp(low_keep, low_pass)
low_back.defvjp(back_keep, back_low)
norm_eps = 1e-12
rms_eps = 1e-06
neg_fill = -1e+30
highest = lax.Precision.HIGHEST

def grouped(operand, kernel, groups):
    row_count = operand.shape[0]
    in_width = kernel.shape[1]
    out_width = kernel.shape[0] // groups
    shaped = operand.reshape(row_count, groups, in_width)
    blocks = kernel.reshape(groups, out_width, in_width)
    result = jnp.einsum('rgi,goi->rgo', shaped, blocks, precision=highest)
    return result.reshape(row_count, groups * out_width)

def normalize(values, norm_gain, norm_shift):
    row_mean = lax.optimization_barrier(jnp.mean(values, axis=-1, keepdims=True))
    centered = values - row_mean
    row_var = lax.optimization_barrier(jnp.mean(centered * centered, axis=-1, keepdims=True))
    return centered * lax.rsqrt(row_var + norm_eps) * norm_gain + norm_shift

def attention(queries, key_rows, value_rows, lengths_now):
    seq_count = queries.shape[0]
    block_rows = min(512, L)
    score_scale = HEAD ** (-0.5)
    key_live = jnp.arange(L)[None, :] < lengths_now[:, None]

    def one_block(start):
        piece = lax.dynamic_slice_in_dim(queries, start, block_rows, 1)
        scores = low_back(jnp.einsum('nqhd,nkhd->nhqk', piece, key_rows, precision=highest) * score_scale)
        scores = jnp.where(key_live[:, None, None, :], scores, neg_fill)
        top_score = lax.optimization_barrier(jnp.max(scores, axis=-1, keepdims=True))
        weights = jnp.exp(scores - top_score)
        row_total = lax.optimization_barrier(jnp.sum(weights, axis=-1, keepdims=True))
        probs_low = low(weights / row_total)
        return jnp.einsum('nhqk,nkhd->nqhd', probs_low, value_rows, precision=highest)
    starts = jnp.arange(L // block_rows, dtype=jnp.int32) * block_rows
    pieces = lax.map(jax.checkpoint(one_block), starts)
    return jnp.moveaxis(pieces, 0, 1).reshape(seq_count * L, D)

def seq_rms(values, live, lengths_now):
    seq_count = lengths_now.shape[0]
    sums = lax.optimization_barrier(jnp.sum((values * values * live).reshape(seq_count, -1), axis=1))
    return jnp.sqrt(sums / (lengths_now.astype(jnp.float32) * D) + rms_eps)

def layer(rows_in, lengths_now, params):
    q_weight, q_bias, k_weight, v_weight, v_bias, o_weight, o_bias, norm1_gain, norm1_bias, up_weight, up_bias, down_weight, down_bias, norm2_gain, norm2_bias = params
    seq_count = rows_in.shape[0]
    flat_rows = rows_in.reshape(seq_count * L, D)
    queries = low_back(low(grouped(flat_rows, q_weight, GROUPS) + q_bias))
    key_rows = low_back(low(grouped(flat_rows, k_weight, GROUPS)))
    value_rows = low_back(low(grouped(flat_rows, v_weight, GROUPS) + v_bias))
    head_shape = (seq_count, L, H, HEAD)
    context = attention(queries.reshape(head_shape), key_rows.reshape(head_shape), value_rows.reshape(head_shape), lengths_now)
    context = low_back(low(context))
    branch_attn = low_back(grouped(context, o_weight, 1) + o_bias)
    first_sum = flat_rows + branch_attn
    first_norm = normalize(first_sum, norm1_gain, norm1_bias)
    up_rows = low_back(grouped(low(first_norm), up_weight, GROUPS) + up_bias)
    act_low = low(jax.nn.gelu(up_rows, approximate=False))
    branch_ffn = low_back(grouped(act_low, down_weight, GROUPS) + down_bias)
    live = (jnp.arange(L)[None, :] < lengths_now[:, None]).astype(jnp.float32).reshape(seq_count * L, 1)
    result = normalize(first_norm + branch_ffn, norm2_gain, norm2_bias) * live
    stats = jnp.stack([seq_rms(flat_rows, live, lengths_now), seq_rms(branch_attn, live, lengths_now), seq_rms(first_norm, live, lengths_now), seq_rms(branch_ffn, live, lengths_now)], axis=0)
    return (result.reshape(seq_count, L, D), stats)

def reference(tokens, cotangent, lengths, permutation, q_weight, q_bias, k_weight, v_weight, v_bias, o_weight, o_bias, norm1_gain, norm1_bias, up_weight, up_bias, down_weight, down_bias, norm2_gain, norm2_bias):
    params = tuple((item.astype(jnp.float32) for item in (q_weight, q_bias, k_weight, v_weight, v_bias, o_weight, o_bias, norm1_gain, norm1_bias, up_weight, up_bias, down_weight, down_bias, norm2_gain, norm2_bias)))
    group_size = math.gcd(SEQS, max(1, 4096 // L))
    step_count = SEQS // group_size
    token_steps = tokens.astype(jnp.float32).reshape(step_count, group_size, L, D)
    cot_steps = cotangent.astype(jnp.float32).reshape(step_count, group_size, L, D)
    length_steps = lengths.reshape(step_count, group_size)

    def one_step(carry, item):
        rows_in, cot_rows, lengths_now = item

        def run(rows, weights):
            return layer(rows, lengths_now, weights)
        result, back_fn, stats = jax.vjp(run, rows_in, params, has_aux=True)
        grad_rows, grad_params = back_fn(cot_rows)
        carry = jax.tree.map(jnp.add, carry, grad_params)
        return (carry, (result.astype(jnp.bfloat16), grad_rows.astype(jnp.bfloat16), stats))
    zeros = tuple((jnp.zeros_like(item) for item in params))
    totals, (results, grads, stats) = lax.scan(one_step, zeros, (token_steps, cot_steps, length_steps))
    output = results.reshape(SEQS, L, D)
    input_grad = grads.reshape(SEQS, L, D)
    stats_all = jnp.moveaxis(stats, 1, 0).reshape(4, SEQS)
    stream_rms = jnp.take(stats_all, permutation, axis=1)
    return (output, input_grad, totals[0], totals[1], totals[2], totals[3], totals[4], totals[5], totals[6], totals[7], totals[8], totals[9], totals[10], totals[11], totals[12], totals[13], totals[14], stream_rms)
```

```python
import functools

import jax
import jax.numpy as jnp
from jax import lax
from jax.experimental import pallas as pl
from jax.experimental.pallas import tpu as pltpu
from jax.sharding import PartitionSpec as P

AXES = ("dp", "fsdp")
D = 768
FF = 3072
HALF = D // 2
HEAD = 64
WIN = 256
SEQ = 1024
SHORT = 64
ROWS = SEQ + SHORT
TILE = 272
TILES = ROWS // TILE
BIG = 1e30

norm_eps = 1e-12
rms_eps = 1e-06
bf16 = jnp.bfloat16
f32 = jnp.float32

NN = (((1,), (0,)), ((), ()))
NT = (((1,), (1,)), ((), ()))
TN = (((0,), (0,)), ((), ()))


def mm(left, right, dims):
    return lax.dot_general(left, right, dims, preferred_element_type=f32)


def exchange():
    row = lax.broadcasted_iota(jnp.int32, (WIN, WIN), 0)
    col = lax.broadcasted_iota(jnp.int32, (WIN, WIN), 1)
    return jnp.where(row + col == WIN - 1, 1.0, 0.0).astype(bf16)


def row_ids(start, count, width):
    return start + lax.broadcasted_iota(jnp.int32, (count, width), 0)


def merge_rows(pair_ref, packed_ref, first_len):
    width = packed_ref.shape[1]
    flip = exchange()
    packed_ref[0:SHORT, :] = pair_ref[0, 0:SHORT, :]
    for step in range(SEQ // WIN):
        start = SHORT + WIN * step
        source = SEQ - WIN * (step + 1)
        flipped = mm(flip, pair_ref[1, source : source + WIN, :], NN)
        inside = min(WIN, SEQ - start)
        own = pair_ref[0, start : start + inside, :].astype(f32)
        keep = row_ids(start, inside, width) < first_len
        packed_ref[start : start + inside, :] = jnp.where(keep, own, flipped[0:inside]).astype(bf16)
        if inside < WIN:
            packed_ref[start + inside : start + WIN, :] = flipped[inside:].astype(bf16)


def unmerge_rows(packed_ref, pair_ref, first_len):
    width = packed_ref.shape[1]
    flip = exchange()
    for step in range(SEQ // WIN):
        start = WIN * step
        ids = row_ids(start, WIN, width)
        own = packed_ref[start : start + WIN, :].astype(f32)
        pair_ref[0, start : start + WIN, :] = jnp.where(ids < first_len, own, 0.0).astype(bf16)
        source = ROWS - WIN * (step + 1)
        flipped = mm(flip, packed_ref[source : source + WIN, :], NN)
        pair_ref[1, start : start + WIN, :] = jnp.where(
            ids < ROWS - first_len, flipped, 0.0
        ).astype(bf16)


def windows(values, count):
    parts = []
    for group in range(count):
        start = (group // 2) * HALF + (group % 2) * 128
        parts.append(values[:, start : start + WIN])
    return parts


def join(parts):
    pieces = []
    for first, second in zip(parts[0::2], parts[1::2]):
        pieces += [first[:, :128], first[:, 128:] + second[:, :128], second[:, 128:]]
    return jnp.concatenate(pieces, axis=1)


def split_three(value):
    high = value.astype(bf16)
    rest = value - high.astype(f32)
    mid = rest.astype(bf16)
    low = (rest - mid.astype(f32)).astype(bf16)
    return high, mid, low


def attn_fwd_kernel(
    len_ref, tok_ref, w_ref, b_ref, x_ref, qa_ref, ka_ref, va_ref, ctx_ref, q_s, k_s, v_s
):
    pair = pl.program_id(0)
    first_len = len_ref[0]

    @pl.when(pair == 0)
    def _():
        merge_rows(tok_ref, x_ref, first_len)
        cols = windows(x_ref[...], 2)
        for which, target in enumerate((q_s, k_s, v_s)):
            value = join([mm(cols[g], w_ref[which, g], NT) for g in range(2)])
            value = value + b_ref[which : which + 1, :]
            if which == 0:
                value = value.astype(bf16).astype(f32) * (HEAD**-0.5)
            target[...] = value.astype(bf16)

    lane0 = pl.multiple_of(pair * 128, 128)
    q_pair = q_s[:, pl.ds(lane0, 128)]
    k_pair = k_s[:, pl.ds(lane0, 128)]
    v_pair = v_s[:, pl.ds(lane0, 128)]
    lane = lax.broadcasted_iota(jnp.int32, (ROWS, 128), 1)
    in_first = row_ids(0, ROWS, 128) < first_len
    one = jnp.ones((ROWS, 128), f32)
    zero = jnp.zeros((ROWS, 128), f32)
    for head in range(2):
        spare = 64 * (1 - head)
        own = (lane // 64) == head
        first_one = jnp.where(in_first, one, zero)
        q_extra = jnp.where(
            lane == spare, first_one, jnp.where(lane == spare + 1, one - first_one, zero)
        )
        k_extra = jnp.where(
            lane == spare,
            (first_one - one) * BIG,
            jnp.where(
                lane == spare + 1,
                first_one * (-BIG),
                jnp.where((lane >= spare + 2) & (lane < spare + 5), one, zero),
            ),
        )
        v_extra = jnp.where((lane >= spare) & (lane < spare + 3), one, zero)
        cols = slice(128 * head, 128 * (head + 1))
        qa_ref[:, cols] = jnp.where(own, q_pair.astype(f32), q_extra).astype(bf16)
        ka_ref[:, cols] = jnp.where(own, k_pair.astype(f32), k_extra).astype(bf16)
        va_ref[:, cols] = jnp.where(own, v_pair.astype(f32), v_extra).astype(bf16)

    tile_lane = lax.broadcasted_iota(jnp.int32, (TILE, 128), 1)

    def one_tile(index, carry):
        start = pl.multiple_of(index * TILE, 16)
        rows = pl.ds(start, TILE)
        result = None
        for head in range(2):
            cols = slice(128 * head, 128 * (head + 1))
            spare = 64 * (1 - head)
            q_tile = qa_ref[rows, cols]
            scores = mm(q_tile, ka_ref[:, cols], NT)
            top = jnp.max(scores, axis=1, keepdims=True)
            weights = jnp.exp(scores - top)
            mixed = mm(weights.astype(bf16), va_ref[:, cols], NN)
            total = mixed[:, spare : spare + 1]
            mixed = mixed / total
            log_total = top + jnp.log(total)
            high, mid, low = split_three(-log_total)
            q_new = jnp.where(
                tile_lane == spare + 2,
                high.astype(f32),
                jnp.where(
                    tile_lane == spare + 3,
                    mid.astype(f32),
                    jnp.where(tile_lane == spare + 4, low.astype(f32), q_tile.astype(f32)),
                ),
            )
            qa_ref[rows, cols] = q_new.astype(bf16)
            result = mixed if head == 0 else jnp.where(tile_lane < 64, result, mixed)
        ctx_ref[rows, :] = result.astype(bf16)
        return carry

    lax.fori_loop(0, TILES, one_tile, 0)


def attn_bwd_kernel(
    len_ref, qa_ref, ka_ref, va_ref, ctx_ref, gctx_ref, x_ref, base_ref, w_ref,
    ig_ref, dw_ref, db_ref, dq_s, dk_s, dv_s, do_s, dqt_s, ig_s,
):
    pair = pl.program_id(0)
    lane0 = pl.multiple_of(pair * 128, 128)
    lane = lax.broadcasted_iota(jnp.int32, (ROWS, 128), 1)
    grad = gctx_ref[...].astype(f32)
    product = grad * ctx_ref[...].astype(f32)
    for head in range(2):
        own = (lane // 64) == head
        spare = 64 * (1 - head)
        inner = -jnp.sum(jnp.where(own, product, 0.0), axis=1, keepdims=True)
        high, mid, low = split_three(inner)
        extra = jnp.where(
            lane == spare,
            high.astype(f32),
            jnp.where(
                lane == spare + 1,
                mid.astype(f32),
                jnp.where(lane == spare + 2, low.astype(f32), 0.0),
            ),
        )
        do_s[:, 128 * head : 128 * (head + 1)] = jnp.where(own, grad, extra).astype(bf16)
    dqt_s[...] = jnp.zeros_like(dqt_s)
    tile_lane = lax.broadcasted_iota(jnp.int32, (TILE, 128), 1)

    def one_tile(index, carry):
        start = pl.multiple_of(index * TILE, 16)
        rows = pl.ds(start, TILE)
        dk_tile = None
        dv_tile = None
        for head in range(2):
            cols = slice(128 * head, 128 * (head + 1))
            k_tile = ka_ref[rows, cols]
            probs = jnp.exp(mm(k_tile, qa_ref[:, cols], NT))
            scaled = mm(va_ref[rows, cols], do_s[:, cols], NT) * probs
            grad_scores = scaled.astype(bf16)
            dv_new = mm(probs.astype(bf16), do_s[:, cols], NN)
            dk_new = mm(grad_scores, qa_ref[:, cols], NN)
            dq_new = mm(k_tile, grad_scores, TN)
            dqt_s[64 * head : 64 * (head + 1), :] += dq_new[64 * head : 64 * (head + 1), :]
            dk_tile = dk_new if head == 0 else jnp.where(tile_lane < 64, dk_tile, dk_new)
            dv_tile = dv_new if head == 0 else jnp.where(tile_lane < 64, dv_tile, dv_new)
        dk_s[rows, pl.ds(lane0, 128)] = dk_tile.astype(bf16)
        dv_s[rows, pl.ds(lane0, 128)] = dv_tile.astype(bf16)
        return carry

    lax.fori_loop(0, TILES, one_tile, 0)
    dq_s[:, pl.ds(lane0, 128)] = (jnp.transpose(dqt_s[...]) * (HEAD**-0.5)).astype(bf16)

    @pl.when(pair == pl.num_programs(0) - 1)
    def _():
        x_cols = windows(x_ref[...], 2)
        total = [None, None]
        for which, source in enumerate((dq_s, dk_s, dv_s)):
            value = source[...]
            db_ref[which : which + 1, :] = jnp.sum(value.astype(f32), axis=0, keepdims=True)
            cols = windows(value, 2)
            for g in range(2):
                dw_ref[which, g] = mm(cols[g], x_cols[g], TN)
                part = mm(cols[g], w_ref[which, g], NN)
                total[g] = part if which == 0 else total[g] + part
        ig_s[...] = (join(total) + base_ref[...]).astype(bf16)
        unmerge_rows(ig_s, ig_ref, len_ref[0])


def mid_kernel(
    len_ref, x0_ref, x1_ref, ctx0_ref, ctx1_ref, cot_ref, wo_ref, wu_ref, wd_ref, vec_ref, ub_ref,
    out_ref, gctx_ref, base_ref, dwo_ref, dwu_ref, dwd_ref, dvec_ref, dub_ref, stat_ref,
    cot_s, out_s, act_s, slope_s, stat_s,
):
    step = pl.program_id(0)
    first_len = len_ref[0]

    @pl.when(step == 0)
    def _():
        merge_rows(cot_ref, cot_s, first_len)
        for target in (dwo_ref, dwu_ref, dwd_ref, dvec_ref, dub_ref, stat_s):
            target[...] = jnp.zeros_like(target)

    o_bias, gain1, shift1, down_bias, gain2, shift2 = (vec_ref[i : i + 1, :] for i in range(6))
    start = pl.multiple_of(step * TILE, 16)
    rows = pl.ds(start, TILE)
    keep = jnp.where(row_ids(start, TILE, D) < first_len, 1.0, 0.0)

    def note(slot, values):
        square = values * values
        stat_s[slot : slot + 1, :] += jnp.sum(square, axis=0, keepdims=True)
        stat_s[slot + 4 : slot + 5, :] += jnp.sum(square * keep, axis=0, keepdims=True)

    def add_vec(slot, values):
        dvec_ref[slot : slot + 1, :] += jnp.sum(values, axis=0, keepdims=True)

    def norm(values):
        mean = jnp.mean(values, axis=1, keepdims=True)
        centered = values - mean
        var = jnp.mean(centered * centered, axis=1, keepdims=True)
        inv = lax.rsqrt(var + norm_eps)
        return centered * inv, inv

    def norm_back(grad_n, n, inv):
        mean_g = jnp.mean(grad_n, axis=1, keepdims=True)
        mean_gn = jnp.mean(grad_n * n, axis=1, keepdims=True)
        return (grad_n - mean_g - n * mean_gn) * inv

    inputs = jnp.concatenate([x0_ref[...], x1_ref[...]], axis=1).astype(f32)
    context = jnp.concatenate([ctx0_ref[...], ctx1_ref[...]], axis=1)
    note(0, inputs)
    branch_attn = mm(context, wo_ref[...], NT) + o_bias
    note(1, branch_attn)
    n1, inv1 = norm(inputs + branch_attn)
    first_norm = n1 * gain1 + shift1
    note(2, first_norm)
    first_low = first_norm.astype(bf16)
    low_cols = windows(first_low, 4)
    parts = []
    for g in range(4):
        cols = slice(D * g, D * (g + 1))
        up = mm(low_cols[g], wu_ref[g], NT) + ub_ref[0:1, cols]
        gate = 0.5 * (1.0 + lax.erf(up * (2.0**-0.5)))
        slope_s[:, cols] = gate + up * jnp.exp(up * up * -0.5) * 0.3989422804014327
        act = (up * gate).astype(bf16)
        act_s[:, cols] = act
        parts.append(mm(act, wd_ref[g], NT))
    branch_ffn = join(parts) + down_bias
    note(3, branch_ffn)
    n2, inv2 = norm(first_norm + branch_ffn)
    out_s[rows, :] = (n2 * gain2 + shift2).astype(bf16)

    grad_out = cot_s[rows, :].astype(f32)
    add_vec(4, grad_out * n2)
    add_vec(5, grad_out)
    grad_sum2 = norm_back(grad_out * gain2, n2, inv2)
    grad_ffn = grad_sum2.astype(bf16)
    add_vec(3, grad_ffn.astype(f32))
    ffn_cols = windows(grad_ffn, 4)
    parts = []
    for g in range(4):
        cols = slice(D * g, D * (g + 1))
        dwd_ref[g] += mm(ffn_cols[g], act_s[:, cols], TN)
        grad_up = (mm(ffn_cols[g], wd_ref[g], NN) * slope_s[:, cols]).astype(bf16)
        dub_ref[0:1, cols] += jnp.sum(grad_up.astype(f32), axis=0, keepdims=True)
        dwu_ref[g] += mm(low_cols[g], grad_up, TN)
        parts.append(mm(grad_up, wu_ref[g], NN))
    grad_first = join(parts) + grad_sum2
    add_vec(1, grad_first * n1)
    add_vec(2, grad_first)
    grad_sum1 = norm_back(grad_first * gain1, n1, inv1)
    base_ref[...] = grad_sum1
    grad_branch = grad_sum1.astype(bf16)
    add_vec(0, grad_branch.astype(f32))
    dwo_ref[...] += mm(grad_branch, context, TN)
    gctx_ref[...] = mm(grad_branch, wo_ref[...], NN).astype(bf16)

    @pl.when(step == pl.num_programs(0) - 1)
    def _():
        unmerge_rows(out_s, out_ref, first_len)
        stat_ref[...] = jnp.broadcast_to(
            jnp.sum(stat_s[...], axis=1, keepdims=True), stat_ref.shape
        )


def whole(shape):
    zeros = (0,) * len(shape)
    return pl.BlockSpec(shape, lambda i, *_: zeros, pipeline_mode=pl.Buffered(1))


def kept(shape):
    zeros = (0,) * len(shape)
    return pl.BlockSpec(shape, lambda i, *_: zeros)


def struct(shape, dtype):
    return jax.ShapeDtypeStruct(shape, dtype)


PARAMS = pltpu.CompilerParams(
    dimension_semantics=("arbitrary",), vmem_limit_bytes=63_000_000
)


def attn_fwd(len_arr, tok, w, bias):
    pair_cols = lambda width: pl.BlockSpec((ROWS, width), lambda i, *_: (0, i))
    return pl.pallas_call(
        attn_fwd_kernel,
        name="attn_fwd",
        grid_spec=pltpu.PrefetchScalarGridSpec(
            num_scalar_prefetch=1,
            grid=(3,),
            in_specs=[whole(tok.shape), whole(w.shape), whole(bias.shape)],
            out_specs=[
                kept((ROWS, HALF)), pair_cols(256), pair_cols(256), pair_cols(256), pair_cols(128),
            ],
            scratch_shapes=[pltpu.VMEM((ROWS, HALF), bf16)] * 3,
        ),
        out_shape=[
            struct((ROWS, HALF), bf16), struct((ROWS, D), bf16), struct((ROWS, D), bf16),
            struct((ROWS, D), bf16), struct((ROWS, HALF), bf16),
        ],
        compiler_params=PARAMS,
        cost_estimate=pl.CostEstimate(
            flops=30_000_000_000, bytes_accessed=12_000_000, transcendentals=7_000_000
        ),
    )(len_arr, tok, w, bias)


def attn_bwd(len_arr, qa, ka, va, ctx, gctx, x, base, w, half):
    pair_cols = lambda width, first: pl.BlockSpec((ROWS, width), lambda i, *_: (0, i + first))
    return pl.pallas_call(
        attn_bwd_kernel,
        name="attn_bwd",
        grid_spec=pltpu.PrefetchScalarGridSpec(
            num_scalar_prefetch=1,
            grid=(3,),
            in_specs=[
                pair_cols(256, 0), pair_cols(256, 0), pair_cols(256, 0), pair_cols(128, 0),
                pair_cols(128, 3 * half), whole(x.shape),
                pl.BlockSpec((ROWS, HALF), lambda i, *_: (0, half), pipeline_mode=pl.Buffered(1)),
                whole(w.shape),
            ],
            out_specs=[kept((2, SEQ, HALF)), kept((3, 2, WIN, WIN)), kept((8, HALF))],
            scratch_shapes=[
                pltpu.VMEM((ROWS, HALF), bf16),
                pltpu.VMEM((ROWS, HALF), bf16),
                pltpu.VMEM((ROWS, HALF), bf16),
                pltpu.VMEM((ROWS, 256), bf16),
                pltpu.VMEM((128, ROWS), f32),
                pltpu.VMEM((ROWS, HALF), bf16),
            ],
        ),
        out_shape=[
            struct((2, SEQ, HALF), bf16), struct((3, 2, WIN, WIN), f32), struct((8, HALF), f32),
        ],
        compiler_params=PARAMS,
        cost_estimate=pl.CostEstimate(
            flops=70_000_000_000, bytes_accessed=16_000_000, transcendentals=7_000_000
        ),
    )(len_arr, qa, ka, va, ctx, gctx, x, base, w)


def middle(len_arr, x0, x1, ctx0, ctx1, cot, wo, wu, wd, vecs, ub):
    row_tile = lambda width: pl.BlockSpec((TILE, width), lambda i, *_: (i, 0))
    return pl.pallas_call(
        mid_kernel,
        name="middle",
        grid_spec=pltpu.PrefetchScalarGridSpec(
            num_scalar_prefetch=1,
            grid=(TILES,),
            in_specs=[row_tile(HALF)] * 4
            + [whole(a.shape) for a in (cot, wo, wu, wd, vecs, ub)],
            out_specs=[
                kept((2, SEQ, D)), row_tile(D), row_tile(D), kept((D, D)), kept((4, WIN, D)),
                kept((4, WIN, D)), kept((8, D)), kept((8, FF)), kept((8, 128)),
            ],
            scratch_shapes=[
                pltpu.VMEM((ROWS, D), bf16),
                pltpu.VMEM((ROWS, D), bf16),
                pltpu.VMEM((TILE, FF), bf16),
                pltpu.VMEM((TILE, FF), f32),
                pltpu.VMEM((8, D), f32),
            ],
        ),
        out_shape=[
            struct((2, SEQ, D), bf16), struct((ROWS, D), bf16), struct((ROWS, D), f32),
            struct((D, D), f32), struct((4, WIN, D), f32), struct((4, WIN, D), f32),
            struct((8, D), f32), struct((8, FF), f32), struct((8, 128), f32),
        ],
        compiler_params=PARAMS,
        cost_estimate=pl.CostEstimate(
            flops=30_000_000_000, bytes_accessed=30_000_000, transcendentals=10_000_000
        ),
    )(len_arr, x0, x1, ctx0, ctx1, cot, wo, wu, wd, vecs, ub)


def spread(weight, axis):
    even = [(0, 0)] * weight.ndim
    odd = [(0, 0)] * weight.ndim
    even[axis], odd[axis] = (0, 64), (64, 0)
    return even, odd


def window_weight(weight, axes):
    even = [(0, 0)] * 3
    odd = [(0, 0)] * 3
    for axis in axes:
        even[axis], odd[axis] = (0, 64), (64, 0)
    pairs = weight.reshape((2, 2) + weight.shape[1:])
    both = jnp.stack([jnp.pad(pairs[:, 0], even), jnp.pad(pairs[:, 1], odd)], axis=1)
    return both.reshape((4,) + both.shape[2:])


def unwindow(grad, axes):
    parts = []
    for group in range(4):
        index = [slice(None)] * 2
        for axis in axes:
            index[axis] = slice(0, 192) if group % 2 == 0 else slice(64, 256)
        parts.append(grad[group][tuple(index)])
    return jnp.stack(parts, axis=0)


def on_device(
    tokens, cotangent, lengths, permutation, q_weight, q_bias, k_weight, v_weight, v_bias, o_weight,
    o_bias, norm1_gain, norm1_bias, up_weight, up_bias, down_weight, down_bias, norm2_gain,
    norm2_bias,
):
    devices = lax.axis_size(AXES)
    my_index = lax.axis_index(AXES)
    seq_total, piece_len, _ = tokens.shape
    seq_dev = seq_total // devices
    dealt_lengths = jnp.take(lengths, permutation, axis=0).reshape(devices, seq_dev)
    swap = dealt_lengths[:, 0] < dealt_lengths[:, 1]
    dealt = permutation.reshape(devices, seq_dev)
    order = jnp.where(swap[:, None], dealt[:, ::-1], dealt).reshape(seq_total)
    inverse = (
        jnp.zeros_like(permutation).at[order].set(jnp.arange(seq_total, dtype=jnp.int32))
    )
    my_swap = lax.dynamic_index_in_dim(swap, my_index, 0, False)
    len_arr = jnp.max(lax.dynamic_slice_in_dim(dealt_lengths, my_index, 1, 0)).reshape(1)

    def arrive(rows):
        width = rows.shape[-1]
        moved = lax.all_to_all(
            rows.reshape(devices, seq_dev, 1, piece_len, width), AXES, split_axis=0, concat_axis=2,
            tiled=True,
        )
        return moved.reshape(seq_dev, SEQ, width)

    def leave(rows):
        width = rows.shape[-1]
        moved = lax.all_to_all(
            rows.reshape(1, seq_dev, devices, piece_len, width), AXES, split_axis=2, concat_axis=0,
            tiled=True,
        )
        return moved.reshape(seq_total, piece_len, width)

    dealt_tokens = jnp.take(tokens, order, axis=0)
    tok0 = arrive(dealt_tokens[:, :, :HALF])
    tok1 = arrive(dealt_tokens[:, :, HALF:])
    cot = arrive(jnp.take(cotangent, order, axis=0))

    rows_dev = q_weight.shape[0]
    up_dev = up_weight.shape[0]
    small = jnp.concatenate(
        [q_bias, v_bias, o_bias, norm1_gain, norm1_bias, down_bias, norm2_gain, norm2_bias, up_bias]
    )
    packed = jnp.concatenate(
        [
            o_weight,
            down_weight,
            q_weight,
            k_weight,
            v_weight,
            up_weight.reshape(4, rows_dev, 192).transpose(1, 0, 2).reshape(rows_dev, D),
            jnp.pad(small.reshape(12, rows_dev).transpose(1, 0), ((0, 0), (0, 52))),
        ],
        axis=1,
    )
    full = lax.all_gather(packed, AXES, axis=0, tiled=True)
    wo = full[:, :D]
    wd = window_weight(full[:, D : 2 * D].reshape(4, 192, D), (1,))
    wqkv = [
        window_weight(full[:, 2 * D + 192 * i : 2 * D + 192 * (i + 1)].reshape(4, 192, 192), (1, 2))
        for i in range(3)
    ]
    wu = window_weight(
        full[:, 2112:2880].reshape(devices, rows_dev, 4, 192).transpose(0, 2, 1, 3).reshape(4, D, 192),
        (2,),
    )
    wqkv = jnp.stack(wqkv, axis=0)
    smalls = full[:, 2880:2892].astype(f32)
    qb, vb, ob, g1, b1, db, g2, b2 = (smalls[:, i] for i in range(8))
    ub = smalls[:, 8:12].reshape(devices, rows_dev, 4).transpose(0, 2, 1).reshape(1, FF)
    vecs = jnp.stack([ob, g1, b1, db, g2, b2, ob, ob], axis=0)
    qkv_bias = jnp.stack([qb, jnp.zeros_like(qb), vb, qb, qb, qb, qb, qb], axis=0)

    x0, qa0, ka0, va0, ctx0 = attn_fwd(len_arr, tok0, wqkv[:, :2], qkv_bias[:, :HALF])
    x1, qa1, ka1, va1, ctx1 = attn_fwd(len_arr, tok1, wqkv[:, 2:], qkv_bias[:, HALF:])
    out, gctx, base, dwo, dwu, dwd, dvec, dub, stat = middle(
        len_arr, x0, x1, ctx0, ctx1, cot, wo, wu, wd, vecs, ub
    )
    back_out = leave(out)
    ig0, dw0, db0 = attn_bwd(len_arr, qa0, ka0, va0, ctx0, gctx, x0, base, wqkv[:, :2], 0)
    ig1, dw1, db1 = attn_bwd(len_arr, qa1, ka1, va1, ctx1, gctx, x1, base, wqkv[:, 2:], 1)
    back_grad = jnp.concatenate([leave(ig0), leave(ig1)], axis=-1)

    dw = jnp.concatenate([dw0, dw1], axis=1)
    dqkv = [unwindow(dw[i], (0, 1)).reshape(D, 192) for i in range(3)]
    dbias = jnp.concatenate([db0, db1], axis=1)
    d_down = unwindow(dwd, (0,)).reshape(D, D)
    d_up = unwindow(dwu, (0,)).transpose(0, 2, 1).reshape(FF, 192)
    up_back = d_up.reshape(devices, 4, rows_dev, 192).transpose(0, 2, 1, 3).reshape(D, D)
    vec_back = jnp.stack(
        [dbias[0], dbias[2], dvec[0], dvec[1], dvec[2], dvec[3], dvec[4], dvec[5]], axis=1
    )
    ub_back = dub[0].reshape(devices, 4, rows_dev).transpose(0, 2, 1).reshape(D, 4)
    grads = jnp.concatenate(
        [dwo, d_down] + dqkv + [up_back, jnp.pad(jnp.concatenate([vec_back, ub_back], 1), ((0, 0), (0, 52)))],
        axis=1,
    )
    mine = lax.psum_scatter(grads, "dp", scatter_dimension=0, tiled=True)
    mine = lax.psum_scatter(mine, "fsdp", scatter_dimension=0, tiled=True)

    output = jnp.take(back_out, inverse, axis=0)
    input_grad = jnp.take(back_grad, inverse, axis=0)
    lens = jnp.stack([len_arr[0], ROWS - len_arr[0]]).astype(f32)
    sums = jnp.stack([stat[4:8, 0], stat[0:4, 0] - stat[4:8, 0]], axis=1)
    rms = jnp.sqrt(sums / (lens[None, :] * D) + rms_eps)
    stream_rms = jnp.where(my_swap, rms[:, ::-1], rms)
    vec = lambda i: mine[:, 2880 + i]
    return (
        output,
        input_grad,
        mine[:, 1536:1728],
        vec(0),
        mine[:, 1728:1920],
        mine[:, 1920:2112],
        vec(1),
        mine[:, :D],
        vec(2),
        vec(3),
        vec(4),
        mine[:, 2112:2880].reshape(rows_dev, 4, 192).transpose(1, 0, 2).reshape(up_dev, 192),
        mine[:, 2888:2892].transpose(1, 0).reshape(up_dev),
        mine[:, D : 2 * D],
        vec(5),
        vec(6),
        vec(7),
        stream_rms,
    )


def solution(mesh):
    rows = P(None, AXES, None)
    mat = P(AXES, None)
    vec = P(AXES)
    in_specs = (
        rows, rows, P(), P(), mat, vec, mat, mat, vec, mat, vec, vec, vec, mat, vec, mat, vec, vec,
        vec,
    )
    out_specs = (
        rows, rows, mat, vec, mat, mat, vec, mat, vec, vec, vec, mat, vec, mat, vec, vec, vec,
        P(None, AXES),
    )
    return jax.shard_map(
        on_device, mesh=mesh, in_specs=in_specs, out_specs=out_specs, check_vma=False
    )
```

```python
import functools

import jax
import jax.numpy as jnp
from jax import lax
from jax.experimental import pallas as pl
from jax.experimental.pallas import tpu as pltpu
from jax.sharding import PartitionSpec as P

AXES = ("dp", "fsdp")
D = 768
FF = 3072
HALF = D // 2
HEAD = 64
WIN = 256
SEQ = 1024
SHORT = 64
BLOCK = 32
ROWS = SEQ + SHORT
TILE = 272
TILES = ROWS // TILE
BIG = 1e30

norm_eps = 1e-12
rms_eps = 1e-06
bf16 = jnp.bfloat16
f32 = jnp.float32

NN = (((1,), (0,)), ((), ()))
NT = (((1,), (1,)), ((), ()))
TN = (((0,), (0,)), ((), ()))


def mm(left, right, dims):
    return lax.dot_general(left, right, dims, preferred_element_type=f32)


def exchange():
    row = lax.broadcasted_iota(jnp.int32, (WIN, WIN), 0)
    col = lax.broadcasted_iota(jnp.int32, (WIN, WIN), 1)
    return jnp.where(row + col == WIN - 1, 1.0, 0.0).astype(bf16)


def row_ids(start, count, width):
    return start + lax.broadcasted_iota(jnp.int32, (count, width), 0)


def block_rows(ref, seq, start, count):
    values = ref[start // BLOCK : (start + count) // BLOCK, seq]
    return values.reshape(count, values.shape[-1])


def merge_rows(pair_ref, packed_ref, first_len):
    width = packed_ref.shape[1]
    flip = exchange()
    packed_ref[0:SHORT, :] = block_rows(pair_ref, 0, 0, SHORT)
    for step in range(SEQ // WIN):
        start = SHORT + WIN * step
        flipped = mm(flip, block_rows(pair_ref, 1, SEQ - WIN * (step + 1), WIN), NN)
        inside = min(WIN, SEQ - start)
        own = block_rows(pair_ref, 0, start, inside).astype(f32)
        keep = row_ids(start, inside, width) < first_len
        packed_ref[start : start + inside, :] = jnp.where(keep, own, flipped[0:inside]).astype(bf16)
        if inside < WIN:
            packed_ref[start + inside : start + WIN, :] = flipped[inside:].astype(bf16)


def unmerge_rows(packed_ref, pair_ref, first_len):
    width = packed_ref.shape[1]
    flip = exchange()
    blocks = WIN // BLOCK
    for step in range(SEQ // WIN):
        start = WIN * step
        ids = row_ids(start, WIN, width)
        own = packed_ref[start : start + WIN, :].astype(f32)
        own = jnp.where(ids < first_len, own, 0.0).astype(bf16)
        pair_ref[blocks * step : blocks * (step + 1), 0] = own.reshape(blocks, BLOCK, width)
        source = ROWS - WIN * (step + 1)
        flipped = mm(flip, packed_ref[source : source + WIN, :], NN)
        flipped = jnp.where(ids < ROWS - first_len, flipped, 0.0).astype(bf16)
        pair_ref[blocks * step : blocks * (step + 1), 1] = flipped.reshape(blocks, BLOCK, width)


def spare_of(group):
    return 192 if group % 2 == 0 else 0


def with_ones(window, group):
    lane = lax.broadcasted_iota(jnp.int32, window.shape, 1)
    return jnp.where(lane == spare_of(group), 1.0, window.astype(f32)).astype(bf16)


def without_bias(window, group):
    lane = lax.broadcasted_iota(jnp.int32, window.shape, 1)
    return jnp.where(lane == spare_of(group), 0.0, window.astype(f32)).astype(bf16)


def first_row(group):
    return 0 if group % 2 == 0 else 64


def windows(values, count):
    parts = []
    for group in range(count):
        start = (group // 2) * HALF + (group % 2) * 128
        parts.append(values[:, start : start + WIN])
    return parts


def join(parts):
    pieces = []
    for first, second in zip(parts[0::2], parts[1::2]):
        pieces += [first[:, :128], first[:, 128:] + second[:, :128], second[:, 128:]]
    return jnp.concatenate(pieces, axis=1)


def split_three(value):
    high = value.astype(bf16)
    rest = value - high.astype(f32)
    mid = rest.astype(bf16)
    low = (rest - mid.astype(f32)).astype(bf16)
    return high, mid, low


def attn_fwd_kernel(
    len_ref, tok_ref, full_ref, x_ref, qa_ref, ka_ref, va_ref, ctx_ref, q_s, k_s, v_s, w_s
):
    pair = pl.program_id(0)
    first_len = len_ref[0]

    @pl.when(pair == 0)
    def _():
        merge_rows(tok_ref, x_ref, first_len)
        w_s[...] = jnp.zeros_like(w_s)
        for which in range(3):
            for g in range(2):
                w_s[which, g, first_row(g) : first_row(g) + 192, :] = full_ref[
                    192 * g : 192 * (g + 1), WIN * which : WIN * (which + 1)
                ]
        cols = [with_ones(part, g) for g, part in enumerate(windows(x_ref[...], 2))]
        for which, target in enumerate((q_s, k_s, v_s)):
            value = join([mm(cols[g], w_s[which, g], NT) for g in range(2)])
            if which == 0:
                value = value.astype(bf16).astype(f32) * (HEAD**-0.5)
            target[...] = value.astype(bf16)

    lane0 = pl.multiple_of(pair * 128, 128)
    q_pair = q_s[:, pl.ds(lane0, 128)]
    k_pair = k_s[:, pl.ds(lane0, 128)]
    v_pair = v_s[:, pl.ds(lane0, 128)]
    lane = lax.broadcasted_iota(jnp.int32, (ROWS, 128), 1)
    in_first = row_ids(0, ROWS, 128) < first_len
    one = jnp.ones((ROWS, 128), f32)
    zero = jnp.zeros((ROWS, 128), f32)
    for head in range(2):
        spare = 64 * (1 - head)
        own = (lane // 64) == head
        first_one = jnp.where(in_first, one, zero)
        q_extra = jnp.where(
            lane == spare, first_one, jnp.where(lane == spare + 1, one - first_one, zero)
        )
        k_extra = jnp.where(
            lane == spare,
            (first_one - one) * BIG,
            jnp.where(
                lane == spare + 1,
                first_one * (-BIG),
                jnp.where((lane >= spare + 2) & (lane < spare + 5), one, zero),
            ),
        )
        v_extra = jnp.where((lane >= spare) & (lane < spare + 3), one, zero)
        cols = slice(128 * head, 128 * (head + 1))
        qa_ref[:, cols] = jnp.where(own, q_pair.astype(f32), q_extra).astype(bf16)
        ka_ref[:, cols] = jnp.where(own, k_pair.astype(f32), k_extra).astype(bf16)
        va_ref[:, cols] = jnp.where(own, v_pair.astype(f32), v_extra).astype(bf16)

    tile_lane = lax.broadcasted_iota(jnp.int32, (TILE, 128), 1)

    def one_tile(index, carry):
        start = pl.multiple_of(index * TILE, 16)
        rows = pl.ds(start, TILE)
        result = None
        for head in range(2):
            cols = slice(128 * head, 128 * (head + 1))
            spare = 64 * (1 - head)
            q_tile = qa_ref[rows, cols]
            scores = mm(q_tile, ka_ref[:, cols], NT)
            top = jnp.max(scores, axis=1, keepdims=True)
            weights = jnp.exp(scores - top)
            mixed = mm(weights.astype(bf16), va_ref[:, cols], NN)
            total = mixed[:, spare : spare + 1]
            mixed = mixed / total
            log_total = top + jnp.log(total)
            high, mid, low = split_three(-log_total)
            q_new = jnp.where(
                tile_lane == spare + 2,
                high.astype(f32),
                jnp.where(
                    tile_lane == spare + 3,
                    mid.astype(f32),
                    jnp.where(tile_lane == spare + 4, low.astype(f32), q_tile.astype(f32)),
                ),
            )
            qa_ref[rows, cols] = q_new.astype(bf16)
            result = mixed if head == 0 else jnp.where(tile_lane < 64, result, mixed)
        ctx_ref[rows, :] = result.astype(bf16)
        return carry

    lax.fori_loop(0, TILES, one_tile, 0)


def attn_bwd_kernel(
    len_ref, qa_ref, ka_ref, va_ref, ctx_ref, gctx_ref, x_ref, base_ref, full_ref,
    ig_ref, dw_ref, dq_s, dk_s, dv_s, do_s, dqt_s, ig_s, w_s,
):
    pair = pl.program_id(0)
    lane0 = pl.multiple_of(pair * 128, 128)
    lane = lax.broadcasted_iota(jnp.int32, (ROWS, 128), 1)
    grad = gctx_ref[...].astype(f32)
    product = grad * ctx_ref[...].astype(f32)
    for head in range(2):
        own = (lane // 64) == head
        spare = 64 * (1 - head)
        inner = -jnp.sum(jnp.where(own, product, 0.0), axis=1, keepdims=True)
        high, mid, low = split_three(inner)
        extra = jnp.where(
            lane == spare,
            high.astype(f32),
            jnp.where(
                lane == spare + 1,
                mid.astype(f32),
                jnp.where(lane == spare + 2, low.astype(f32), 0.0),
            ),
        )
        do_s[:, 128 * head : 128 * (head + 1)] = jnp.where(own, grad, extra).astype(bf16)
    dqt_s[...] = jnp.zeros_like(dqt_s)
    tile_lane = lax.broadcasted_iota(jnp.int32, (TILE, 128), 1)

    def one_tile(index, carry):
        start = pl.multiple_of(index * TILE, 16)
        rows = pl.ds(start, TILE)
        dk_tile = None
        dv_tile = None
        for head in range(2):
            cols = slice(128 * head, 128 * (head + 1))
            k_tile = ka_ref[rows, cols]
            probs = jnp.exp(mm(k_tile, qa_ref[:, cols], NT))
            scaled = mm(va_ref[rows, cols], do_s[:, cols], NT) * probs
            grad_scores = scaled.astype(bf16)
            dv_new = mm(probs.astype(bf16), do_s[:, cols], NN)
            dk_new = mm(grad_scores, qa_ref[:, cols], NN)
            dq_new = mm(k_tile, grad_scores, TN)
            dqt_s[64 * head : 64 * (head + 1), :] += dq_new[64 * head : 64 * (head + 1), :]
            dk_tile = dk_new if head == 0 else jnp.where(tile_lane < 64, dk_tile, dk_new)
            dv_tile = dv_new if head == 0 else jnp.where(tile_lane < 64, dv_tile, dv_new)
        dk_s[rows, pl.ds(lane0, 128)] = dk_tile.astype(bf16)
        dv_s[rows, pl.ds(lane0, 128)] = dv_tile.astype(bf16)
        return carry

    lax.fori_loop(0, TILES, one_tile, 0)
    dq_s[:, pl.ds(lane0, 128)] = (jnp.transpose(dqt_s[...]) * (HEAD**-0.5)).astype(bf16)

    @pl.when(pair == pl.num_programs(0) - 1)
    def _():
        x_cols = [with_ones(part, g) for g, part in enumerate(windows(x_ref[...], 2))]
        total = [None, None]
        for which, source in enumerate((dq_s, dk_s, dv_s)):
            cols = windows(source[...], 2)
            for g in range(2):
                own = slice(first_row(g), first_row(g) + 192)
                w_s[own, :] = without_bias(
                    full_ref[192 * g : 192 * (g + 1), WIN * which : WIN * (which + 1)], g
                )
                if first_row(g) == 0:
                    w_s[192:, :] = jnp.zeros((64, WIN), bf16)
                else:
                    w_s[:64, :] = jnp.zeros((64, WIN), bf16)
                grad = mm(cols[g], x_cols[g], TN)
                dw_ref[192 * g : 192 * (g + 1), WIN * which : WIN * (which + 1)] = grad[own].astype(
                    bf16
                )
                part = mm(cols[g], w_s[...], NN)
                total[g] = part if which == 0 else total[g] + part
        ig_s[...] = (join(total) + base_ref[...]).astype(bf16)
        unmerge_rows(ig_s, ig_ref, len_ref[0])


def norm(values):
    mean = jnp.mean(values, axis=1, keepdims=True)
    centered = values - mean
    var = jnp.mean(centered * centered, axis=1, keepdims=True)
    inv = lax.rsqrt(var + norm_eps)
    return centered * inv, inv


def norm_back(grad_n, n, inv):
    mean_g = jnp.mean(grad_n, axis=1, keepdims=True)
    mean_gn = jnp.mean(grad_n * n, axis=1, keepdims=True)
    return (grad_n - mean_g - n * mean_gn) * inv


def mid_fwd_kernel(
    len_ref, x0_ref, x1_ref, ctx0_ref, ctx1_ref, full_ref, wu_ref, vec_ref,
    out_ref, n1_ref, n2_ref, inv_ref, slope_ref, act_ref, stat_ref, out_s, wd_s, stat_s,
):
    step = pl.program_id(0)
    first_len = len_ref[0]

    @pl.when(step == 0)
    def _():
        stat_s[...] = jnp.zeros_like(stat_s)
        wd_s[...] = jnp.zeros_like(wd_s)
        for g in range(4):
            wd_s[g, first_row(g) : first_row(g) + 192, :] = full_ref[192 * g : 192 * (g + 1), D:]

    o_bias, gain1, shift1, down_bias, gain2, shift2 = (vec_ref[i : i + 1, :] for i in range(6))
    start = pl.multiple_of(step * TILE, 16)
    rows = pl.ds(start, TILE)
    keep = jnp.where(row_ids(start, TILE, D) < first_len, 1.0, 0.0)

    def note(slot, values):
        square = values * values
        stat_s[slot : slot + 1, :] += jnp.sum(square, axis=0, keepdims=True)
        stat_s[slot + 4 : slot + 5, :] += jnp.sum(square * keep, axis=0, keepdims=True)

    inputs = jnp.concatenate([x0_ref[...], x1_ref[...]], axis=1).astype(f32)
    context = jnp.concatenate([ctx0_ref[...], ctx1_ref[...]], axis=1)
    note(0, inputs)
    branch_attn = mm(context, full_ref[:, :D], NT) + o_bias
    note(1, branch_attn)
    n1, inv1 = norm(inputs + branch_attn)
    n1_ref[...] = n1
    first_norm = n1 * gain1 + shift1
    note(2, first_norm)
    low_cols = windows(first_norm.astype(bf16), 4)
    parts = []
    for g in range(4):
        cols = slice(D * g, D * (g + 1))
        up = mm(with_ones(low_cols[g], g), wu_ref[D * g : D * (g + 1), :], NT)
        gate = 0.5 * (1.0 + lax.erf(up * (2.0**-0.5)))
        slope_ref[:, cols] = gate + up * jnp.exp(up * up * -0.5) * 0.3989422804014327
        act = (up * gate).astype(bf16)
        act_ref[:, cols] = act
        parts.append(mm(act, wd_s[g], NT))
    branch_ffn = join(parts) + down_bias
    note(3, branch_ffn)
    n2, inv2 = norm(first_norm + branch_ffn)
    n2_ref[...] = n2
    lane = lax.broadcasted_iota(jnp.int32, (TILE, 128), 1)
    inv_ref[...] = jnp.where(lane < 64, inv1, inv2)
    out_s[rows, :] = (n2 * gain2 + shift2).astype(bf16)

    @pl.when(step == pl.num_programs(0) - 1)
    def _():
        unmerge_rows(out_s, out_ref, first_len)
        stat_ref[...] = jnp.broadcast_to(
            jnp.sum(stat_s[...], axis=1, keepdims=True), stat_ref.shape
        )


def mid_bwd_kernel(
    len_ref, cot_ref, ctx0_ref, ctx1_ref, n1_ref, n2_ref, inv_ref, slope_ref, act_ref,
    full_ref, wu_ref, vec_ref, gctx_ref, base_ref, grad_ref,
    cot_s, wd_s, dwd_s, dwu_s, vec_s, turn_s,
):
    step = pl.program_id(0)

    @pl.when(step == 0)
    def _():
        merge_rows(cot_ref, cot_s, len_ref[0])
        for target in (dwd_s, dwu_s, vec_s, wd_s):
            target[...] = jnp.zeros_like(target)
        grad_ref[:, :D] = jnp.zeros((D, D), f32)
        for g in range(4):
            wd_s[g, first_row(g) : first_row(g) + 192, :] = full_ref[192 * g : 192 * (g + 1), D:]

    gain1, shift1, gain2 = (vec_ref[i : i + 1, :] for i in (1, 2, 4))
    start = pl.multiple_of(step * TILE, 16)
    rows = pl.ds(start, TILE)

    def add_vec(slot, values):
        vec_s[slot : slot + 1, :] += jnp.sum(values, axis=0, keepdims=True)

    context = jnp.concatenate([ctx0_ref[...], ctx1_ref[...]], axis=1)
    n1 = n1_ref[...]
    n2 = n2_ref[...]
    inv1 = inv_ref[:, 0:1]
    inv2 = inv_ref[:, 64:65]
    low_cols = windows((n1 * gain1 + shift1).astype(bf16), 4)
    grad_out = cot_s[rows, :].astype(f32)
    add_vec(4, grad_out * n2)
    add_vec(5, grad_out)
    grad_sum2 = norm_back(grad_out * gain2, n2, inv2)
    grad_ffn = grad_sum2.astype(bf16)
    add_vec(3, grad_ffn.astype(f32))
    ffn_cols = windows(grad_ffn, 4)
    parts = []
    for g in range(4):
        cols = slice(D * g, D * (g + 1))
        dwd_s[g] += mm(ffn_cols[g], act_ref[:, cols], TN)
        grad_up = (mm(ffn_cols[g], wd_s[g], NN) * slope_ref[:, cols]).astype(bf16)
        dwu_s[g] += mm(with_ones(low_cols[g], g), grad_up, TN)
        parts.append(mm(grad_up, without_bias(wu_ref[D * g : D * (g + 1), :], g), NN))
    grad_first = join(parts) + grad_sum2
    add_vec(1, grad_first * n1)
    add_vec(2, grad_first)
    grad_sum1 = norm_back(grad_first * gain1, n1, inv1)
    base_ref[...] = grad_sum1
    grad_branch = grad_sum1.astype(bf16)
    add_vec(0, grad_branch.astype(f32))
    grad_ref[:, :D] += mm(grad_branch, context, TN)
    gctx_ref[...] = mm(grad_branch, full_ref[:, :D], NN).astype(bf16)

    @pl.when(step == pl.num_programs(0) - 1)
    def _():
        for g in range(4):
            own = slice(192 * g, 192 * (g + 1))
            grad_ref[own, D : 2 * D] = dwd_s[g, first_row(g) : first_row(g) + 192, :]
            turned = jnp.transpose(dwu_s[g])
            for half in range(2):
                turn_s[...] = turned[:, 128 * half : 128 * (half + 1)]
                for j in range(4):
                    lane0 = 2 * D + WIN * j + 128 * half
                    grad_ref[own, lane0 : lane0 + 128] = turn_s[pl.ds(j, 192, stride=4), :]
        grad_ref[:, 2 * D + 4 * WIN :] = jnp.transpose(vec_s[...])


def whole(shape):
    zeros = (0,) * len(shape)
    return pl.BlockSpec(shape, lambda i, *_: zeros, pipeline_mode=pl.Buffered(1))


def kept(shape):
    zeros = (0,) * len(shape)
    return pl.BlockSpec(shape, lambda i, *_: zeros)


def struct(shape, dtype):
    return jax.ShapeDtypeStruct(shape, dtype)


PARAMS = pltpu.CompilerParams(
    dimension_semantics=("arbitrary",), vmem_limit_bytes=63_000_000
)


GRAD_COLS = 2 * D + 4 * WIN + 128


def attn_fwd(len_arr, tok, full, half):
    pair_cols = lambda width: pl.BlockSpec((ROWS, width), lambda i, *_: (0, i))
    return pl.pallas_call(
        attn_fwd_kernel,
        name="attn_fwd",
        grid_spec=pltpu.PrefetchScalarGridSpec(
            num_scalar_prefetch=1,
            grid=(3,),
            in_specs=[
                whole(tok.shape),
                pl.BlockSpec((HALF, D), lambda i, *_: (half, 0), pipeline_mode=pl.Buffered(1)),
            ],
            out_specs=[
                kept((ROWS, HALF)), pair_cols(256), pair_cols(256), pair_cols(256), pair_cols(128),
            ],
            scratch_shapes=[pltpu.VMEM((ROWS, HALF), bf16)] * 3
            + [pltpu.VMEM((3, 2, WIN, WIN), bf16)],
        ),
        out_shape=[
            struct((ROWS, HALF), bf16), struct((ROWS, D), bf16), struct((ROWS, D), bf16),
            struct((ROWS, D), bf16), struct((ROWS, HALF), bf16),
        ],
        compiler_params=PARAMS,
        cost_estimate=pl.CostEstimate(
            flops=20_000_000_000, bytes_accessed=12_000_000, transcendentals=7_000_000
        ),
    )(len_arr, tok, full)


def attn_bwd(len_arr, qa, ka, va, ctx, gctx, x, base, full, half):
    pair_cols = lambda width, first: pl.BlockSpec((ROWS, width), lambda i, *_: (0, i + first))
    return pl.pallas_call(
        attn_bwd_kernel,
        name="attn_bwd",
        grid_spec=pltpu.PrefetchScalarGridSpec(
            num_scalar_prefetch=1,
            grid=(3,),
            in_specs=[
                pair_cols(256, 0), pair_cols(256, 0), pair_cols(256, 0), pair_cols(128, 0),
                pair_cols(128, 3 * half), whole(x.shape),
                pl.BlockSpec((ROWS, HALF), lambda i, *_: (0, half), pipeline_mode=pl.Buffered(1)),
                pl.BlockSpec((HALF, D), lambda i, *_: (half, 0), pipeline_mode=pl.Buffered(1)),
            ],
            out_specs=[kept((SEQ // BLOCK, 2, BLOCK, HALF)), kept((HALF, D))],
            scratch_shapes=[
                pltpu.VMEM((ROWS, HALF), bf16),
                pltpu.VMEM((ROWS, HALF), bf16),
                pltpu.VMEM((ROWS, HALF), bf16),
                pltpu.VMEM((ROWS, 256), bf16),
                pltpu.VMEM((128, ROWS), f32),
                pltpu.VMEM((ROWS, HALF), bf16),
                pltpu.VMEM((WIN, WIN), bf16),
            ],
        ),
        out_shape=[struct((SEQ // BLOCK, 2, BLOCK, HALF), bf16), struct((HALF, D), bf16)],
        compiler_params=PARAMS,
        cost_estimate=pl.CostEstimate(
            flops=30_000_000_000, bytes_accessed=16_000_000, transcendentals=7_000_000
        ),
    )(len_arr, qa, ka, va, ctx, gctx, x, base, full)


def row_tile(width):
    return pl.BlockSpec((TILE, width), lambda i, *_: (i, 0))


def mid_fwd(len_arr, x0, x1, ctx0, ctx1, full, wu, vecs):
    outs = [
        ((SEQ // BLOCK, 2, BLOCK, D), bf16), ((ROWS, D), f32), ((ROWS, D), f32), ((ROWS, 128), f32),
        ((ROWS, FF), f32), ((ROWS, FF), bf16), ((8, 128), f32),
    ]
    return pl.pallas_call(
        mid_fwd_kernel,
        name="mid_fwd",
        grid_spec=pltpu.PrefetchScalarGridSpec(
            num_scalar_prefetch=1,
            grid=(TILES,),
            in_specs=[row_tile(HALF)] * 4
            + [whole((D, 2 * D)), whole(wu.shape), whole(vecs.shape)],
            out_specs=[
                kept(outs[0][0]), row_tile(D), row_tile(D), row_tile(128), row_tile(FF),
                row_tile(FF), kept((8, 128)),
            ],
            scratch_shapes=[
                pltpu.VMEM((ROWS, D), bf16),
                pltpu.VMEM((4, WIN, D), bf16),
                pltpu.VMEM((8, D), f32),
            ],
        ),
        out_shape=[struct(*o) for o in outs],
        compiler_params=PARAMS,
        cost_estimate=pl.CostEstimate(
            flops=15_000_000_000, bytes_accessed=36_000_000, transcendentals=7_000_000
        ),
    )(len_arr, x0, x1, ctx0, ctx1, full, wu, vecs)


def mid_bwd(len_arr, cot, ctx0, ctx1, n1, n2, inv, slope, act, full, wu, vecs):
    outs = [((ROWS, D), bf16), ((ROWS, D), f32), ((D, GRAD_COLS), f32)]
    return pl.pallas_call(
        mid_bwd_kernel,
        name="mid_bwd",
        grid_spec=pltpu.PrefetchScalarGridSpec(
            num_scalar_prefetch=1,
            grid=(TILES,),
            in_specs=[
                whole(cot.shape), row_tile(HALF), row_tile(HALF), row_tile(D), row_tile(D),
                row_tile(128), row_tile(FF), row_tile(FF), whole((D, 2 * D)), whole(wu.shape),
                whole(vecs.shape),
            ],
            out_specs=[
                row_tile(D),
                row_tile(D),
                pl.BlockSpec((D, GRAD_COLS), lambda i, *_: (0, 0), pipeline_mode=pl.Buffered(1)),
            ],
            scratch_shapes=[
                pltpu.VMEM((ROWS, D), bf16),
                pltpu.VMEM((4, WIN, D), bf16),
                pltpu.VMEM((4, WIN, D), f32),
                pltpu.VMEM((4, WIN, D), f32),
                pltpu.VMEM((128, D), f32),
                pltpu.VMEM((D, 128), f32),
            ],
        ),
        out_shape=[struct(*o) for o in outs],
        compiler_params=PARAMS,
        cost_estimate=pl.CostEstimate(
            flops=30_000_000_000, bytes_accessed=50_000_000, transcendentals=10_000
        ),
    )(len_arr, cot, ctx0, ctx1, n1, n2, inv, slope, act, full, wu, vecs)


def pick(values, index):
    return values.at[index].get(mode="promise_in_bounds")


def tie(*values):
    return lax.optimization_barrier(values)


def on_device(
    tokens, cotangent, lengths, permutation, q_weight, q_bias, k_weight, v_weight, v_bias, o_weight,
    o_bias, norm1_gain, norm1_bias, up_weight, up_bias, down_weight, down_bias, norm2_gain,
    norm2_bias,
):
    devices = lax.axis_size(AXES)
    my_index = lax.axis_index(AXES)
    seq_total, piece_len, _ = tokens.shape
    seq_dev = seq_total // devices
    rows_dev = q_weight.shape[0]
    up_dev = up_weight.shape[0]
    odd = (my_index // (devices // 4)) % 2 == 1

    def padded(weight, bias):
        column = bias[:, None]
        gap = jnp.zeros((weight.shape[0], 63), bf16)
        return jnp.where(
            odd,
            jnp.concatenate([column, gap, weight], axis=1),
            jnp.concatenate([weight, column, gap], axis=1),
        )

    small = [o_bias, norm1_gain, norm1_bias, down_bias, norm2_gain, norm2_bias]
    full_in = lax.all_gather(
        jnp.concatenate(
            [
                padded(q_weight, q_bias),
                padded(k_weight, jnp.zeros_like(q_bias)),
                padded(v_weight, v_bias),
            ],
            axis=1,
        ),
        AXES,
        axis=0,
        tiled=True,
    )
    rest, full_in = tie(
        jnp.concatenate(
            [
                o_weight,
                down_weight,
                padded(up_weight, up_bias).reshape(rows_dev, 4 * WIN),
                jnp.pad(jnp.stack(small, axis=1), ((0, 0), (0, 122))),
            ],
            axis=1,
        ),
        full_in,
    )
    full = lax.all_gather(rest, AXES, axis=0, tiled=True)

    dealt_lengths = pick(lengths, permutation).reshape(devices, seq_dev)
    swap = dealt_lengths[:, 0] < dealt_lengths[:, 1]
    dealt = permutation.reshape(devices, seq_dev)
    order = jnp.where(swap[:, None], dealt[:, ::-1], dealt).reshape(seq_total)
    places = jnp.arange(seq_total, dtype=jnp.int32)
    inverse = jnp.sum(jnp.where(order[None, :] == places[:, None], places[None, :], 0), axis=1)
    my_swap = lax.dynamic_index_in_dim(swap, my_index, 0, False)
    len_arr = jnp.max(lax.dynamic_slice_in_dim(dealt_lengths, my_index, 1, 0)).reshape(1)

    def swap_blocks(rows):
        return lax.all_to_all(rows, AXES, split_axis=0, concat_axis=0, tiled=True)

    def arrive(rows):
        width = rows.shape[-1]
        moved = swap_blocks(rows.reshape(devices, seq_dev, piece_len, width))
        if piece_len == BLOCK:
            return moved
        moved = moved.transpose(1, 0, 2, 3).reshape(seq_dev, SEQ // BLOCK, BLOCK, width)
        return moved.transpose(1, 0, 2, 3)

    def leave(rows):
        width = rows.shape[-1]
        if piece_len != BLOCK:
            rows = rows.transpose(1, 0, 2, 3).reshape(seq_dev, devices, piece_len, width)
            rows = rows.transpose(1, 0, 2, 3)
        return swap_blocks(rows).reshape(seq_total, piece_len, width)

    dealt_tokens = pick(tokens, order)
    dealt_cot = pick(cotangent, order)
    tok0 = arrive(dealt_tokens[:, :, :HALF])
    second, tok0 = tie(dealt_tokens[:, :, HALF:], tok0)
    tok1 = arrive(second)
    dealt_cot, tok1 = tie(dealt_cot, tok1)
    cot = arrive(dealt_cot)

    x0, qa0, ka0, va0, ctx0 = attn_fwd(len_arr, tok0, full_in, 0)
    x1, qa1, ka1, va1, ctx1 = attn_fwd(len_arr, tok1, full_in, 1)
    wu = full[:, 2 * D : 2 * D + 4 * WIN].reshape(FF, WIN)
    vecs = jnp.pad(full[:, 2 * D + 4 * WIN : 2 * D + 4 * WIN + 6].astype(f32).T, ((0, 2), (0, 0)))
    out, n1, n2, inv, slope, act, stat = mid_fwd(len_arr, x0, x1, ctx0, ctx1, full, wu, vecs)
    cot, out = tie(cot, out)
    back_out = leave(out)
    gctx, base, grads = mid_bwd(
        len_arr, cot, ctx0, ctx1, n1, n2, inv, slope, act, full, wu, vecs
    )
    mine = lax.psum_scatter(grads, "dp", scatter_dimension=0, tiled=True)
    mine = lax.psum_scatter(mine, "fsdp", scatter_dimension=0, tiled=True)
    ig0, dw0 = attn_bwd(len_arr, qa0, ka0, va0, ctx0, gctx, x0, base, full_in, 0)
    ig0, back_out = tie(ig0, back_out)
    back0 = leave(ig0)
    ig1, dw1 = attn_bwd(len_arr, qa1, ka1, va1, ctx1, gctx, x1, base, full_in, 1)
    ig1, back0 = tie(ig1, back0)
    back1 = leave(ig1)
    moved = swap_blocks(jnp.concatenate([dw0, dw1], axis=0).reshape(devices, rows_dev, D))
    mine_in = jnp.sum(moved.astype(f32), axis=0)

    output = pick(back_out, inverse)
    input_grad = jnp.concatenate([pick(back0, inverse), pick(back1, inverse)], axis=-1)
    lens = jnp.stack([len_arr[0], ROWS - len_arr[0]]).astype(f32)
    sums = jnp.stack([stat[4:8, 0], stat[0:4, 0] - stat[4:8, 0]], axis=1)
    rms = jnp.sqrt(sums / (lens[None, :] * D) + rms_eps)
    stream_rms = jnp.where(my_swap, rms[:, ::-1], rms)
    vec = lambda i: mine[:, 2 * D + 4 * WIN + i]

    def unpadded(block):
        return (
            jnp.where(odd, block[:, 64:], block[:, :192]),
            jnp.where(odd, block[:, 0], block[:, 192]),
        )

    dq, dqb = unpadded(mine_in[:, :WIN])
    dk, _ = unpadded(mine_in[:, WIN : 2 * WIN])
    dv, dvb = unpadded(mine_in[:, 2 * WIN :])
    dup, dub = unpadded(mine[:, 2 * D : 2 * D + 4 * WIN].reshape(up_dev, WIN))
    return (
        output, input_grad, dq, dqb, dk, dv, dvb, mine[:, :D], vec(0), vec(1), vec(2), dup, dub,
        mine[:, D : 2 * D], vec(3), vec(4), vec(5), stream_rms,
    )


def solution(mesh):
    rows = P(None, AXES, None)
    mat = P(AXES, None)
    vec = P(AXES)
    in_specs = (
        rows, rows, P(), P(), mat, vec, mat, mat, vec, mat, vec, vec, vec, mat, vec, mat, vec, vec,
        vec,
    )
    out_specs = (
        rows, rows, mat, vec, mat, mat, vec, mat, vec, vec, vec, mat, vec, mat, vec, vec, vec,
        P(None, AXES),
    )
    return jax.shard_map(
        on_device, mesh=mesh, in_specs=in_specs, out_specs=out_specs, check_vma=False
    )
```

```python
import functools

import jax
import jax.numpy as jnp
from jax import lax
from jax.experimental import pallas as pl
from jax.experimental.pallas import tpu as pltpu
from jax.sharding import PartitionSpec as P

AXES = ("dp", "fsdp")
D = 768
FF = 3072
HALF = D // 2
HEAD = 64
WIN = 256
SEQ = 1024
SHORT = 64
BLOCK = 32
ROWS = SEQ + SHORT
TILE = 272
TILES = ROWS // TILE
BIG = 1e30

norm_eps = 1e-12
rms_eps = 1e-06
bf16 = jnp.bfloat16
f32 = jnp.float32

NN = (((1,), (0,)), ((), ()))
NT = (((1,), (1,)), ((), ()))
TN = (((0,), (0,)), ((), ()))


def mm(left, right, dims):
    return lax.dot_general(left, right, dims, preferred_element_type=f32)


def exchange():
    row = lax.broadcasted_iota(jnp.int32, (WIN, WIN), 0)
    col = lax.broadcasted_iota(jnp.int32, (WIN, WIN), 1)
    return jnp.where(row + col == WIN - 1, 1.0, 0.0).astype(bf16)


def row_ids(start, count, width):
    return start + lax.broadcasted_iota(jnp.int32, (count, width), 0)


def block_rows(ref, seq, start, count):
    values = ref[start // BLOCK : (start + count) // BLOCK, seq]
    return values.reshape(count, values.shape[-1])


def merge_rows(pair_ref, packed_ref, first_len):
    width = packed_ref.shape[1]
    flip = exchange()
    packed_ref[0:SHORT, :] = block_rows(pair_ref, 0, 0, SHORT)
    for step in range(SEQ // WIN):
        start = SHORT + WIN * step
        flipped = mm(flip, block_rows(pair_ref, 1, SEQ - WIN * (step + 1), WIN), NN)
        inside = min(WIN, SEQ - start)
        own = block_rows(pair_ref, 0, start, inside).astype(f32)
        keep = row_ids(start, inside, width) < first_len
        packed_ref[start : start + inside, :] = jnp.where(keep, own, flipped[0:inside]).astype(bf16)
        if inside < WIN:
            packed_ref[start + inside : start + WIN, :] = flipped[inside:].astype(bf16)


def unmerge_rows(packed_ref, pair_ref, first_len):
    width = packed_ref.shape[1]
    flip = exchange()
    blocks = WIN // BLOCK
    for step in range(SEQ // WIN):
        start = WIN * step
        ids = row_ids(start, WIN, width)
        own = packed_ref[start : start + WIN, :].astype(f32)
        own = jnp.where(ids < first_len, own, 0.0).astype(bf16)
        pair_ref[blocks * step : blocks * (step + 1), 0] = own.reshape(blocks, BLOCK, width)
        source = ROWS - WIN * (step + 1)
        flipped = mm(flip, packed_ref[source : source + WIN, :], NN)
        flipped = jnp.where(ids < ROWS - first_len, flipped, 0.0).astype(bf16)
        pair_ref[blocks * step : blocks * (step + 1), 1] = flipped.reshape(blocks, BLOCK, width)


def spare_of(group):
    return 192 if group % 2 == 0 else 0


def with_ones(window, group):
    lane = lax.broadcasted_iota(jnp.int32, window.shape, 1)
    return jnp.where(lane == spare_of(group), 1.0, window.astype(f32)).astype(bf16)


def without_bias(window, group):
    lane = lax.broadcasted_iota(jnp.int32, window.shape, 1)
    return jnp.where(lane == spare_of(group), 0.0, window.astype(f32)).astype(bf16)


def first_row(group):
    return 0 if group % 2 == 0 else 64


def windows(values, count):
    parts = []
    for group in range(count):
        start = (group // 2) * HALF + (group % 2) * 128
        parts.append(values[:, start : start + WIN])
    return parts


def join(parts):
    pieces = []
    for first, second in zip(parts[0::2], parts[1::2]):
        pieces += [first[:, :128], first[:, 128:] + second[:, :128], second[:, 128:]]
    return jnp.concatenate(pieces, axis=1)


def split_three(value):
    high = value.astype(bf16)
    rest = value - high.astype(f32)
    mid = rest.astype(bf16)
    low = (rest - mid.astype(f32)).astype(bf16)
    return high, mid, low


def attn_fwd_kernel(
    len_ref, tok_ref, full_ref, x_ref, qa_ref, ka_ref, va_ref, ctx_ref, q_s, k_s, v_s, w_s
):
    pair = pl.program_id(0)
    first_len = len_ref[0]

    @pl.when(pair == 0)
    def _():
        merge_rows(tok_ref, x_ref, first_len)
        w_s[...] = jnp.zeros_like(w_s)
        for which in range(3):
            for g in range(2):
                w_s[which, g, first_row(g) : first_row(g) + 192, :] = full_ref[
                    192 * g : 192 * (g + 1), WIN * which : WIN * (which + 1)
                ]
        cols = [with_ones(part, g) for g, part in enumerate(windows(x_ref[...], 2))]
        for which, target in enumerate((q_s, k_s, v_s)):
            value = join([mm(cols[g], w_s[which, g], NT) for g in range(2)])
            if which == 0:
                value = value.astype(bf16).astype(f32) * (HEAD**-0.5)
            target[...] = value.astype(bf16)

    lane0 = pl.multiple_of(pair * 128, 128)
    q_pair = q_s[:, pl.ds(lane0, 128)]
    k_pair = k_s[:, pl.ds(lane0, 128)]
    v_pair = v_s[:, pl.ds(lane0, 128)]
    lane = lax.broadcasted_iota(jnp.int32, (ROWS, 128), 1)
    in_first = row_ids(0, ROWS, 128) < first_len
    one = jnp.ones((ROWS, 128), f32)
    zero = jnp.zeros((ROWS, 128), f32)
    for head in range(2):
        spare = 64 * (1 - head)
        own = (lane // 64) == head
        first_one = jnp.where(in_first, one, zero)
        q_extra = jnp.where(
            lane == spare, first_one, jnp.where(lane == spare + 1, one - first_one, zero)
        )
        k_extra = jnp.where(
            lane == spare,
            (first_one - one) * BIG,
            jnp.where(
                lane == spare + 1,
                first_one * (-BIG),
                jnp.where((lane >= spare + 2) & (lane < spare + 5), one, zero),
            ),
        )
        v_extra = jnp.where((lane >= spare) & (lane < spare + 3), one, zero)
        cols = slice(128 * head, 128 * (head + 1))
        qa_ref[:, cols] = jnp.where(own, q_pair.astype(f32), q_extra).astype(bf16)
        ka_ref[:, cols] = jnp.where(own, k_pair.astype(f32), k_extra).astype(bf16)
        va_ref[:, cols] = jnp.where(own, v_pair.astype(f32), v_extra).astype(bf16)

    tile_lane = lax.broadcasted_iota(jnp.int32, (TILE, 128), 1)

    def one_tile(index, carry):
        start = pl.multiple_of(index * TILE, 16)
        rows = pl.ds(start, TILE)
        result = None
        for head in range(2):
            cols = slice(128 * head, 128 * (head + 1))
            spare = 64 * (1 - head)
            q_tile = qa_ref[rows, cols]
            scores = mm(q_tile, ka_ref[:, cols], NT)
            top = jnp.max(scores, axis=1, keepdims=True)
            weights = jnp.exp(scores - top)
            mixed = mm(weights.astype(bf16), va_ref[:, cols], NN)
            total = mixed[:, spare : spare + 1]
            mixed = mixed / total
            log_total = top + jnp.log(total)
            high, mid, low = split_three(-log_total)
            q_new = jnp.where(
                tile_lane == spare + 2,
                high.astype(f32),
                jnp.where(
                    tile_lane == spare + 3,
                    mid.astype(f32),
                    jnp.where(tile_lane == spare + 4, low.astype(f32), q_tile.astype(f32)),
                ),
            )
            qa_ref[rows, cols] = q_new.astype(bf16)
            result = mixed if head == 0 else jnp.where(tile_lane < 64, result, mixed)
        ctx_ref[rows, :] = result.astype(bf16)
        return carry

    lax.fori_loop(0, TILES, one_tile, 0)


def attn_bwd_kernel(
    len_ref, qa_ref, ka_ref, va_ref, ctx_ref, gctx_ref, x_ref, base_ref, full_ref,
    ig_ref, dw_ref, dq_s, dk_s, dv_s, do_s, dqt_s, ig_s, w_s,
):
    pair = pl.program_id(0)
    lane0 = pl.multiple_of(pair * 128, 128)
    lane = lax.broadcasted_iota(jnp.int32, (ROWS, 128), 1)
    grad = gctx_ref[...].astype(f32)
    product = grad * ctx_ref[...].astype(f32)
    for head in range(2):
        own = (lane // 64) == head
        spare = 64 * (1 - head)
        inner = -jnp.sum(jnp.where(own, product, 0.0), axis=1, keepdims=True)
        high, mid, low = split_three(inner)
        extra = jnp.where(
            lane == spare,
            high.astype(f32),
            jnp.where(
                lane == spare + 1,
                mid.astype(f32),
                jnp.where(lane == spare + 2, low.astype(f32), 0.0),
            ),
        )
        do_s[:, 128 * head : 128 * (head + 1)] = jnp.where(own, grad, extra).astype(bf16)
    dqt_s[...] = jnp.zeros_like(dqt_s)
    tile_lane = lax.broadcasted_iota(jnp.int32, (TILE, 128), 1)

    def one_tile(index, carry):
        start = pl.multiple_of(index * TILE, 16)
        rows = pl.ds(start, TILE)
        dk_tile = None
        dv_tile = None
        for head in range(2):
            cols = slice(128 * head, 128 * (head + 1))
            k_tile = ka_ref[rows, cols]
            probs = jnp.exp(mm(k_tile, qa_ref[:, cols], NT))
            scaled = mm(va_ref[rows, cols], do_s[:, cols], NT) * probs
            grad_scores = scaled.astype(bf16)
            dv_new = mm(probs.astype(bf16), do_s[:, cols], NN)
            dk_new = mm(grad_scores, qa_ref[:, cols], NN)
            dq_new = mm(k_tile, grad_scores, TN)
            dqt_s[64 * head : 64 * (head + 1), :] += dq_new[64 * head : 64 * (head + 1), :]
            dk_tile = dk_new if head == 0 else jnp.where(tile_lane < 64, dk_tile, dk_new)
            dv_tile = dv_new if head == 0 else jnp.where(tile_lane < 64, dv_tile, dv_new)
        dk_s[rows, pl.ds(lane0, 128)] = dk_tile.astype(bf16)
        dv_s[rows, pl.ds(lane0, 128)] = dv_tile.astype(bf16)
        return carry

    lax.fori_loop(0, TILES, one_tile, 0)
    dq_s[:, pl.ds(lane0, 128)] = (jnp.transpose(dqt_s[...]) * (HEAD**-0.5)).astype(bf16)

    @pl.when(pair == pl.num_programs(0) - 1)
    def _():
        x_cols = [with_ones(part, g) for g, part in enumerate(windows(x_ref[...], 2))]
        total = [None, None]
        for which, source in enumerate((dq_s, dk_s, dv_s)):
            cols = windows(source[...], 2)
            for g in range(2):
                own = slice(first_row(g), first_row(g) + 192)
                w_s[own, :] = without_bias(
                    full_ref[192 * g : 192 * (g + 1), WIN * which : WIN * (which + 1)], g
                )
                if first_row(g) == 0:
                    w_s[192:, :] = jnp.zeros((64, WIN), bf16)
                else:
                    w_s[:64, :] = jnp.zeros((64, WIN), bf16)
                grad = mm(cols[g], x_cols[g], TN)
                dw_ref[192 * g : 192 * (g + 1), WIN * which : WIN * (which + 1)] = grad[own].astype(
                    bf16
                )
                part = mm(cols[g], w_s[...], NN)
                total[g] = part if which == 0 else total[g] + part
        ig_s[...] = (join(total) + base_ref[...]).astype(bf16)
        unmerge_rows(ig_s, ig_ref, len_ref[0])


def norm(values):
    mean = jnp.mean(values, axis=1, keepdims=True)
    centered = values - mean
    var = jnp.mean(centered * centered, axis=1, keepdims=True)
    inv = lax.rsqrt(var + norm_eps)
    return centered * inv, inv


def norm_back(grad_n, n, inv):
    mean_g = jnp.mean(grad_n, axis=1, keepdims=True)
    mean_gn = jnp.mean(grad_n * n, axis=1, keepdims=True)
    return (grad_n - mean_g - n * mean_gn) * inv


def mid_fwd_kernel(
    len_ref, x0_ref, x1_ref, ctx0_ref, ctx1_ref, full_ref, wu_ref, vec_ref,
    out0_ref, out1_ref, n1_ref, n2_ref, inv_ref, slope_ref, act_ref, stat_ref,
    out0_s, out1_s, wd_s, stat_s,
):
    step = pl.program_id(0)
    first_len = len_ref[0]

    @pl.when(step == 0)
    def _():
        stat_s[...] = jnp.zeros_like(stat_s)
        wd_s[...] = jnp.zeros_like(wd_s)
        for g in range(4):
            wd_s[g, first_row(g) : first_row(g) + 192, :] = full_ref[192 * g : 192 * (g + 1), D:]

    o_bias, gain1, shift1, down_bias, gain2, shift2 = (vec_ref[i : i + 1, :] for i in range(6))
    start = pl.multiple_of(step * TILE, 16)
    rows = pl.ds(start, TILE)
    keep = jnp.where(row_ids(start, TILE, D) < first_len, 1.0, 0.0)

    def note(slot, values):
        square = values * values
        stat_s[slot : slot + 1, :] += jnp.sum(square, axis=0, keepdims=True)
        stat_s[slot + 4 : slot + 5, :] += jnp.sum(square * keep, axis=0, keepdims=True)

    inputs = jnp.concatenate([x0_ref[...], x1_ref[...]], axis=1).astype(f32)
    context = jnp.concatenate([ctx0_ref[...], ctx1_ref[...]], axis=1)
    note(0, inputs)
    branch_attn = mm(context, full_ref[:, :D], NT) + o_bias
    note(1, branch_attn)
    n1, inv1 = norm(inputs + branch_attn)
    n1_ref[...] = n1
    first_norm = n1 * gain1 + shift1
    note(2, first_norm)
    low_cols = windows(first_norm.astype(bf16), 4)
    parts = []
    for g in range(4):
        cols = slice(D * g, D * (g + 1))
        up = mm(with_ones(low_cols[g], g), wu_ref[D * g : D * (g + 1), :], NT)
        gate = 0.5 * (1.0 + lax.erf(up * (2.0**-0.5)))
        slope_ref[:, cols] = gate + up * jnp.exp(up * up * -0.5) * 0.3989422804014327
        act = (up * gate).astype(bf16)
        act_ref[:, cols] = act
        parts.append(mm(act, wd_s[g], NT))
    branch_ffn = join(parts) + down_bias
    note(3, branch_ffn)
    n2, inv2 = norm(first_norm + branch_ffn)
    n2_ref[...] = n2
    lane = lax.broadcasted_iota(jnp.int32, (TILE, 128), 1)
    inv_ref[...] = jnp.where(lane < 64, inv1, inv2)
    result = (n2 * gain2 + shift2).astype(bf16)
    out0_s[rows, :] = result[:, :HALF]
    out1_s[rows, :] = result[:, HALF:]

    @pl.when(step == pl.num_programs(0) - 1)
    def _():
        unmerge_rows(out0_s, out0_ref, first_len)
        unmerge_rows(out1_s, out1_ref, first_len)
        stat_ref[...] = jnp.broadcast_to(
            jnp.sum(stat_s[...], axis=1, keepdims=True), stat_ref.shape
        )


def mid_bwd_kernel(
    len_ref, cot_ref, ctx0_ref, ctx1_ref, n1_ref, n2_ref, inv_ref, slope_ref, act_ref,
    full_ref, wu_ref, vec_ref, gctx_ref, base_ref, grad_ref,
    cot_s, wd_s, dwo_s, dwd_s, dwu_s, vec_s, turn_s,
):
    step = pl.program_id(0)

    @pl.when(step == 0)
    def _():
        merge_rows(cot_ref, cot_s, len_ref[0])
        for target in (dwo_s, dwd_s, dwu_s, vec_s, wd_s):
            target[...] = jnp.zeros_like(target)
        for g in range(4):
            wd_s[g, first_row(g) : first_row(g) + 192, :] = full_ref[192 * g : 192 * (g + 1), D:]

    gain1, shift1, gain2 = (vec_ref[i : i + 1, :] for i in (1, 2, 4))
    start = pl.multiple_of(step * TILE, 16)
    rows = pl.ds(start, TILE)

    def add_vec(slot, values):
        vec_s[slot : slot + 1, :] += jnp.sum(values, axis=0, keepdims=True)

    context = jnp.concatenate([ctx0_ref[...], ctx1_ref[...]], axis=1)
    n1 = n1_ref[...]
    n2 = n2_ref[...]
    inv1 = inv_ref[:, 0:1]
    inv2 = inv_ref[:, 64:65]
    low_cols = windows((n1 * gain1 + shift1).astype(bf16), 4)
    grad_out = cot_s[rows, :].astype(f32)
    add_vec(4, grad_out * n2)
    add_vec(5, grad_out)
    grad_sum2 = norm_back(grad_out * gain2, n2, inv2)
    grad_ffn = grad_sum2.astype(bf16)
    add_vec(3, grad_ffn.astype(f32))
    ffn_cols = windows(grad_ffn, 4)
    parts = []
    for g in range(4):
        cols = slice(D * g, D * (g + 1))
        dwd_s[g] += mm(ffn_cols[g], act_ref[:, cols], TN)
        grad_up = (mm(ffn_cols[g], wd_s[g], NN) * slope_ref[:, cols]).astype(bf16)
        dwu_s[g] += mm(with_ones(low_cols[g], g), grad_up, TN)
        parts.append(mm(grad_up, without_bias(wu_ref[D * g : D * (g + 1), :], g), NN))
    grad_first = join(parts) + grad_sum2
    add_vec(1, grad_first * n1)
    add_vec(2, grad_first)
    grad_sum1 = norm_back(grad_first * gain1, n1, inv1)
    base_ref[...] = grad_sum1
    grad_branch = grad_sum1.astype(bf16)
    add_vec(0, grad_branch.astype(f32))
    dwo_s[...] += mm(grad_branch, context, TN)
    gctx_ref[...] = mm(grad_branch, full_ref[:, :D], NN).astype(bf16)

    @pl.when(step == pl.num_programs(0) - 1)
    def _():
        grad_ref[:, :D] = dwo_s[...].astype(bf16)
        for g in range(4):
            own = slice(192 * g, 192 * (g + 1))
            grad_ref[own, D : 2 * D] = dwd_s[g, first_row(g) : first_row(g) + 192, :].astype(bf16)
            turned = jnp.transpose(dwu_s[g])
            for half in range(2):
                turn_s[...] = turned[:, 128 * half : 128 * (half + 1)]
                for j in range(4):
                    lane0 = 2 * D + WIN * j + 128 * half
                    grad_ref[own, lane0 : lane0 + 128] = turn_s[pl.ds(j, 192, stride=4), :].astype(
                        bf16
                    )
        grad_ref[:, 2 * D + 4 * WIN :] = jnp.transpose(vec_s[...]).astype(bf16)


def whole(shape):
    zeros = (0,) * len(shape)
    return pl.BlockSpec(shape, lambda i, *_: zeros, pipeline_mode=pl.Buffered(1))


def kept(shape):
    zeros = (0,) * len(shape)
    return pl.BlockSpec(shape, lambda i, *_: zeros)


def struct(shape, dtype):
    return jax.ShapeDtypeStruct(shape, dtype)


PARAMS = pltpu.CompilerParams(
    dimension_semantics=("arbitrary",), vmem_limit_bytes=63_000_000
)


GRAD_COLS = 2 * D + 4 * WIN + 128


def attn_fwd(len_arr, tok, full, half):
    pair_cols = lambda width: pl.BlockSpec((ROWS, width), lambda i, *_: (0, i))
    return pl.pallas_call(
        attn_fwd_kernel,
        name="attn_fwd",
        grid_spec=pltpu.PrefetchScalarGridSpec(
            num_scalar_prefetch=1,
            grid=(3,),
            in_specs=[
                whole(tok.shape),
                pl.BlockSpec((HALF, D), lambda i, *_: (half, 2), pipeline_mode=pl.Buffered(1)),
            ],
            out_specs=[
                kept((ROWS, HALF)), pair_cols(256), pair_cols(256), pair_cols(256), pair_cols(128),
            ],
            scratch_shapes=[pltpu.VMEM((ROWS, HALF), bf16)] * 3
            + [pltpu.VMEM((3, 2, WIN, WIN), bf16)],
        ),
        out_shape=[
            struct((ROWS, HALF), bf16), struct((ROWS, D), bf16), struct((ROWS, D), bf16),
            struct((ROWS, D), bf16), struct((ROWS, HALF), bf16),
        ],
        compiler_params=PARAMS,
        cost_estimate=pl.CostEstimate(
            flops=20_000_000_000, bytes_accessed=12_000_000, transcendentals=7_000_000
        ),
    )(len_arr, tok, full)


def attn_bwd(len_arr, qa, ka, va, ctx, gctx, x, base, full, half):
    pair_cols = lambda width, first: pl.BlockSpec((ROWS, width), lambda i, *_: (0, i + first))
    return pl.pallas_call(
        attn_bwd_kernel,
        name="attn_bwd",
        grid_spec=pltpu.PrefetchScalarGridSpec(
            num_scalar_prefetch=1,
            grid=(3,),
            in_specs=[
                pair_cols(256, 0), pair_cols(256, 0), pair_cols(256, 0), pair_cols(128, 0),
                pair_cols(128, 3 * half), whole(x.shape),
                pl.BlockSpec((ROWS, HALF), lambda i, *_: (0, half), pipeline_mode=pl.Buffered(1)),
                pl.BlockSpec((HALF, D), lambda i, *_: (half, 2), pipeline_mode=pl.Buffered(1)),
            ],
            out_specs=[kept((SEQ // BLOCK, 2, BLOCK, HALF)), kept((HALF, D))],
            scratch_shapes=[
                pltpu.VMEM((ROWS, HALF), bf16),
                pltpu.VMEM((ROWS, HALF), bf16),
                pltpu.VMEM((ROWS, HALF), bf16),
                pltpu.VMEM((ROWS, 256), bf16),
                pltpu.VMEM((128, ROWS), f32),
                pltpu.VMEM((ROWS, HALF), bf16),
                pltpu.VMEM((WIN, WIN), bf16),
            ],
        ),
        out_shape=[struct((SEQ // BLOCK, 2, BLOCK, HALF), bf16), struct((HALF, D), bf16)],
        compiler_params=PARAMS,
        cost_estimate=pl.CostEstimate(
            flops=30_000_000_000, bytes_accessed=16_000_000, transcendentals=7_000_000
        ),
    )(len_arr, qa, ka, va, ctx, gctx, x, base, full)


def row_tile(width):
    return pl.BlockSpec((TILE, width), lambda i, *_: (i, 0))


def mid_fwd(len_arr, x0, x1, ctx0, ctx1, full, wu, vecs):
    outs = [
        ((SEQ // BLOCK, 2, BLOCK, HALF), bf16), ((SEQ // BLOCK, 2, BLOCK, HALF), bf16),
        ((ROWS, D), f32), ((ROWS, D), f32), ((ROWS, 128), f32), ((ROWS, FF), f32),
        ((ROWS, FF), bf16), ((8, 128), f32),
    ]
    return pl.pallas_call(
        mid_fwd_kernel,
        name="mid_fwd",
        grid_spec=pltpu.PrefetchScalarGridSpec(
            num_scalar_prefetch=1,
            grid=(TILES,),
            in_specs=[row_tile(HALF)] * 4
            + [whole((D, 2 * D)), whole(wu.shape), whole(vecs.shape)],
            out_specs=[
                kept(outs[0][0]), kept(outs[0][0]), row_tile(D), row_tile(D), row_tile(128),
                row_tile(FF), row_tile(FF), kept((8, 128)),
            ],
            scratch_shapes=[
                pltpu.VMEM((ROWS, HALF), bf16),
                pltpu.VMEM((ROWS, HALF), bf16),
                pltpu.VMEM((4, WIN, D), bf16),
                pltpu.VMEM((8, D), f32),
            ],
        ),
        out_shape=[struct(*o) for o in outs],
        compiler_params=PARAMS,
        cost_estimate=pl.CostEstimate(
            flops=15_000_000_000, bytes_accessed=36_000_000, transcendentals=7_000_000
        ),
    )(len_arr, x0, x1, ctx0, ctx1, full, wu, vecs)


def mid_bwd(len_arr, cot, ctx0, ctx1, n1, n2, inv, slope, act, full, wu, vecs):
    outs = [((ROWS, D), bf16), ((ROWS, D), f32), ((D, GRAD_COLS), bf16)]
    return pl.pallas_call(
        mid_bwd_kernel,
        name="mid_bwd",
        grid_spec=pltpu.PrefetchScalarGridSpec(
            num_scalar_prefetch=1,
            grid=(TILES,),
            in_specs=[
                whole(cot.shape), row_tile(HALF), row_tile(HALF), row_tile(D), row_tile(D),
                row_tile(128), row_tile(FF), row_tile(FF), whole((D, 2 * D)), whole(wu.shape),
                whole(vecs.shape),
            ],
            out_specs=[
                row_tile(D),
                row_tile(D),
                pl.BlockSpec((D, GRAD_COLS), lambda i, *_: (0, 0), pipeline_mode=pl.Buffered(1)),
            ],
            scratch_shapes=[
                pltpu.VMEM((ROWS, D), bf16),
                pltpu.VMEM((4, WIN, D), bf16),
                pltpu.VMEM((D, D), f32),
                pltpu.VMEM((4, WIN, D), f32),
                pltpu.VMEM((4, WIN, D), f32),
                pltpu.VMEM((128, D), f32),
                pltpu.VMEM((D, 128), f32),
            ],
        ),
        out_shape=[struct(*o) for o in outs],
        compiler_params=PARAMS,
        cost_estimate=pl.CostEstimate(
            flops=30_000_000_000, bytes_accessed=50_000_000, transcendentals=10_000
        ),
    )(len_arr, cot, ctx0, ctx1, n1, n2, inv, slope, act, full, wu, vecs)


def pick(values, index):
    return values.at[index].get(mode="promise_in_bounds")


def tie(*values):
    return lax.optimization_barrier(values)


def on_device(
    tokens, cotangent, lengths, permutation, q_weight, q_bias, k_weight, v_weight, v_bias, o_weight,
    o_bias, norm1_gain, norm1_bias, up_weight, up_bias, down_weight, down_bias, norm2_gain,
    norm2_bias,
):
    devices = lax.axis_size(AXES)
    my_index = lax.axis_index(AXES)
    seq_total, piece_len, _ = tokens.shape
    seq_dev = seq_total // devices
    rows_dev = q_weight.shape[0]
    up_dev = up_weight.shape[0]
    odd = (my_index // (devices // 4)) % 2 == 1

    def padded(weight, bias):
        column = bias[:, None]
        gap = jnp.zeros((weight.shape[0], 63), bf16)
        return jnp.where(
            odd,
            jnp.concatenate([column, gap, weight], axis=1),
            jnp.concatenate([weight, column, gap], axis=1),
        )

    small = [o_bias, norm1_gain, norm1_bias, down_bias, norm2_gain, norm2_bias]
    full = lax.all_gather(
        jnp.concatenate(
            [
                o_weight,
                down_weight,
                padded(q_weight, q_bias),
                padded(k_weight, jnp.zeros_like(q_bias)),
                padded(v_weight, v_bias),
                padded(up_weight, up_bias).reshape(rows_dev, 4 * WIN),
                jnp.pad(jnp.stack(small, axis=1), ((0, 0), (0, 122))),
            ],
            axis=1,
        ),
        AXES,
        axis=0,
        tiled=True,
    )

    dealt_lengths = pick(lengths, permutation).reshape(devices, seq_dev)
    swap = dealt_lengths[:, 0] < dealt_lengths[:, 1]
    dealt = permutation.reshape(devices, seq_dev)
    order = jnp.where(swap[:, None], dealt[:, ::-1], dealt).reshape(seq_total)
    places = jnp.arange(seq_total, dtype=jnp.int32)
    inverse = jnp.sum(jnp.where(order[None, :] == places[:, None], places[None, :], 0), axis=1)
    my_swap = lax.dynamic_index_in_dim(swap, my_index, 0, False)
    len_arr = jnp.max(lax.dynamic_slice_in_dim(dealt_lengths, my_index, 1, 0)).reshape(1)

    def swap_blocks(rows):
        return lax.all_to_all(rows, AXES, split_axis=0, concat_axis=0, tiled=True)

    def arrive(rows):
        width = rows.shape[-1]
        moved = swap_blocks(rows.reshape(devices, seq_dev, piece_len, width))
        if piece_len == BLOCK:
            return moved
        moved = moved.transpose(1, 0, 2, 3).reshape(seq_dev, SEQ // BLOCK, BLOCK, width)
        return moved.transpose(1, 0, 2, 3)

    def leave(rows):
        width = rows.shape[-1]
        if piece_len != BLOCK:
            rows = rows.transpose(1, 0, 2, 3).reshape(seq_dev, devices, piece_len, width)
            rows = rows.transpose(1, 0, 2, 3)
        return swap_blocks(rows).reshape(seq_total, piece_len, width)

    def send_over(partial, axis):
        count = lax.axis_size(axis)
        me = lax.axis_index(axis)
        size = partial.shape[0] // count
        block_of = lambda index: lax.dynamic_slice_in_dim(partial, index * size, size, 0)
        parts = [block_of(me)]
        for shift in range(1, count):
            target = [(i, (i + shift) % count) for i in range(count)]
            parts.append(lax.ppermute(block_of((me + shift) % count), axis, target))
        return parts

    def total(parts):
        return sum(part.astype(f32) for part in parts)

    dealt_tokens = pick(tokens, order)
    tok0 = arrive(dealt_tokens[:, :, :HALF])
    tok1 = arrive(dealt_tokens[:, :, HALF:])
    dealt_cot, tok0, tok1 = tie(pick(cotangent, order), tok0, tok1)
    cot = arrive(dealt_cot)

    x0, qa0, ka0, va0, ctx0 = attn_fwd(len_arr, tok0, full, 0)
    x1, qa1, ka1, va1, ctx1 = attn_fwd(len_arr, tok1, full, 1)
    wu = full[:, 3 * D : 3 * D + 4 * WIN].reshape(FF, WIN)
    vecs = jnp.pad(full[:, 3 * D + 4 * WIN : 3 * D + 4 * WIN + 6].astype(f32).T, ((0, 2), (0, 0)))
    out0, out1, n1, n2, inv, slope, act, stat = mid_fwd(
        len_arr, x0, x1, ctx0, ctx1, full, wu, vecs
    )
    cot, out0, out1 = tie(cot, out0, out1)
    back_out0 = leave(out0)
    gctx, base, grads = mid_bwd(
        len_arr, cot, ctx0, ctx1, n1, n2, inv, slope, act, full, wu, vecs
    )
    gctx, out1, back_out0 = tie(gctx, out1, back_out0)
    back_out1 = leave(out1)
    parts = send_over(grads, "dp")
    ig0, dw0 = attn_bwd(len_arr, qa0, ka0, va0, ctx0, gctx, x0, base, full, 0)
    ig0, dw0, gctx, back_out1, *parts = tie(ig0, dw0, gctx, back_out1, *parts)
    back0 = leave(ig0)
    parts = send_over(total(parts).astype(bf16), "fsdp")
    ig1, dw1 = attn_bwd(len_arr, qa1, ka1, va1, ctx1, gctx, x1, base, full, 1)
    ig1, dw1, back0, *parts = tie(ig1, dw1, back0, *parts)
    mine = total(parts)
    back1 = leave(ig1)
    parts = send_over(jnp.concatenate([dw0, dw1], axis=0), "dp")
    mine_in = total(send_over(total(parts).astype(bf16), "fsdp"))

    join_halves = lambda first, second: jnp.concatenate(
        [pick(first, inverse), pick(second, inverse)], axis=-1
    )
    output = join_halves(back_out0, back_out1)
    input_grad = join_halves(back0, back1)
    lens = jnp.stack([len_arr[0], ROWS - len_arr[0]]).astype(f32)
    sums = jnp.stack([stat[4:8, 0], stat[0:4, 0] - stat[4:8, 0]], axis=1)
    rms = jnp.sqrt(sums / (lens[None, :] * D) + rms_eps)
    stream_rms = jnp.where(my_swap, rms[:, ::-1], rms)
    vec = lambda i: mine[:, 2 * D + 4 * WIN + i]

    def unpadded(block):
        return (
            jnp.where(odd, block[:, 64:], block[:, :192]),
            jnp.where(odd, block[:, 0], block[:, 192]),
        )

    dq, dqb = unpadded(mine_in[:, :WIN])
    dk, _ = unpadded(mine_in[:, WIN : 2 * WIN])
    dv, dvb = unpadded(mine_in[:, 2 * WIN :])
    dup, dub = unpadded(mine[:, 2 * D : 2 * D + 4 * WIN].reshape(up_dev, WIN))
    return (
        output, input_grad, dq, dqb, dk, dv, dvb, mine[:, :D], vec(0), vec(1), vec(2), dup, dub,
        mine[:, D : 2 * D], vec(3), vec(4), vec(5), stream_rms,
    )


def solution(mesh):
    rows = P(None, AXES, None)
    mat = P(AXES, None)
    vec = P(AXES)
    in_specs = (
        rows, rows, P(), P(), mat, vec, mat, mat, vec, mat, vec, vec, vec, mat, vec, mat, vec, vec,
        vec,
    )
    out_specs = (
        rows, rows, mat, vec, mat, mat, vec, mat, vec, vec, vec, mat, vec, mat, vec, vec, vec,
        P(None, AXES),
    )
    return jax.shard_map(
        on_device, mesh=mesh, in_specs=in_specs, out_specs=out_specs, check_vma=False
    )
```

```python
import functools

import jax
import jax.numpy as jnp
from jax import lax
from jax.experimental import pallas as pl
from jax.experimental.pallas import tpu as pltpu
from jax.sharding import PartitionSpec as P

AXES = ("dp", "fsdp")
D = 768
FF = 3072
HALF = D // 2
HEAD = 64
WIN = 256
SEQ = 1024
SHORT = 64
BLOCK = 32
ROWS = SEQ + SHORT
TILE = 272
TILES = ROWS // TILE
BIG = 1e30
STEPS = 4

norm_eps = 1e-12
rms_eps = 1e-06
bf16 = jnp.bfloat16
f32 = jnp.float32

NN = (((1,), (0,)), ((), ()))
NT = (((1,), (1,)), ((), ()))
TN = (((0,), (0,)), ((), ()))


def mm(left, right, dims):
    return lax.dot_general(left, right, dims, preferred_element_type=f32)


def exchange():
    row = lax.broadcasted_iota(jnp.int32, (WIN, WIN), 0)
    col = lax.broadcasted_iota(jnp.int32, (WIN, WIN), 1)
    return jnp.where(row + col == WIN - 1, 1.0, 0.0).astype(bf16)


def row_ids(start, count, width):
    return start + lax.broadcasted_iota(jnp.int32, (count, width), 0)


def block_rows(ref, seq, start, count):
    values = ref[start // BLOCK : (start + count) // BLOCK, seq]
    return values.reshape(count, values.shape[-1])


def merge_rows(pair_ref, packed_ref, first_len):
    width = packed_ref.shape[1]
    flip = exchange()
    packed_ref[0:SHORT, :] = block_rows(pair_ref, 0, 0, SHORT)
    for step in range(SEQ // WIN):
        start = SHORT + WIN * step
        flipped = mm(flip, block_rows(pair_ref, 1, SEQ - WIN * (step + 1), WIN), NN)
        inside = min(WIN, SEQ - start)
        own = block_rows(pair_ref, 0, start, inside).astype(f32)
        keep = row_ids(start, inside, width) < first_len
        packed_ref[start : start + inside, :] = jnp.where(keep, own, flipped[0:inside]).astype(bf16)
        if inside < WIN:
            packed_ref[start + inside : start + WIN, :] = flipped[inside:].astype(bf16)


def unmerge_rows(packed_ref, pair_ref, first_len):
    width = packed_ref.shape[1]
    flip = exchange()
    blocks = WIN // BLOCK
    for step in range(SEQ // WIN):
        start = WIN * step
        ids = row_ids(start, WIN, width)
        own = packed_ref[start : start + WIN, :].astype(f32)
        own = jnp.where(ids < first_len, own, 0.0).astype(bf16)
        pair_ref[blocks * step : blocks * (step + 1), 0] = own.reshape(blocks, BLOCK, width)
        source = ROWS - WIN * (step + 1)
        flipped = mm(flip, packed_ref[source : source + WIN, :], NN)
        flipped = jnp.where(ids < ROWS - first_len, flipped, 0.0).astype(bf16)
        pair_ref[blocks * step : blocks * (step + 1), 1] = flipped.reshape(blocks, BLOCK, width)


def spare_of(group):
    return 192 if group % 2 == 0 else 0


def with_ones(window, group):
    lane = lax.broadcasted_iota(jnp.int32, window.shape, 1)
    return jnp.where(lane == spare_of(group), 1.0, window.astype(f32)).astype(bf16)


def without_bias(window, group):
    lane = lax.broadcasted_iota(jnp.int32, window.shape, 1)
    return jnp.where(lane == spare_of(group), 0.0, window.astype(f32)).astype(bf16)


def first_row(group):
    return 0 if group % 2 == 0 else 64


def windows(values, count):
    parts = []
    for group in range(count):
        start = (group // 2) * HALF + (group % 2) * 128
        parts.append(values[:, start : start + WIN])
    return parts


def join(parts):
    pieces = []
    for first, second in zip(parts[0::2], parts[1::2]):
        pieces += [first[:, :128], first[:, 128:] + second[:, :128], second[:, 128:]]
    return jnp.concatenate(pieces, axis=1)


def split_three(value):
    high = value.astype(bf16)
    rest = value - high.astype(f32)
    mid = rest.astype(bf16)
    low = (rest - mid.astype(f32)).astype(bf16)
    return high, mid, low


def attn_fwd_kernel(
    len_ref, tok_ref, full_ref, x_ref, qa_ref, ka_ref, va_ref, ctx_ref, q_s, k_s, v_s, w_s
):
    pair = pl.program_id(0)
    first_len = len_ref[0]

    @pl.when(pair == 0)
    def _():
        merge_rows(tok_ref, x_ref, first_len)
        w_s[...] = jnp.zeros_like(w_s)
        for which in range(3):
            for g in range(2):
                w_s[which, g, first_row(g) : first_row(g) + 192, :] = full_ref[
                    192 * g : 192 * (g + 1), WIN * which : WIN * (which + 1)
                ]
        cols = [with_ones(part, g) for g, part in enumerate(windows(x_ref[...], 2))]
        for which, target in enumerate((q_s, k_s, v_s)):
            value = join([mm(cols[g], w_s[which, g], NT) for g in range(2)])
            if which == 0:
                value = value.astype(bf16).astype(f32) * (HEAD**-0.5)
            target[...] = value.astype(bf16)

    lane0 = pl.multiple_of(pair * 128, 128)
    q_pair = q_s[:, pl.ds(lane0, 128)]
    k_pair = k_s[:, pl.ds(lane0, 128)]
    v_pair = v_s[:, pl.ds(lane0, 128)]
    lane = lax.broadcasted_iota(jnp.int32, (ROWS, 128), 1)
    in_first = row_ids(0, ROWS, 128) < first_len
    one = jnp.ones((ROWS, 128), f32)
    zero = jnp.zeros((ROWS, 128), f32)
    for head in range(2):
        spare = 64 * (1 - head)
        own = (lane // 64) == head
        first_one = jnp.where(in_first, one, zero)
        q_extra = jnp.where(
            lane == spare, first_one, jnp.where(lane == spare + 1, one - first_one, zero)
        )
        k_extra = jnp.where(
            lane == spare,
            (first_one - one) * BIG,
            jnp.where(
                lane == spare + 1,
                first_one * (-BIG),
                jnp.where((lane >= spare + 2) & (lane < spare + 5), one, zero),
            ),
        )
        v_extra = jnp.where((lane >= spare) & (lane < spare + 3), one, zero)
        cols = slice(128 * head, 128 * (head + 1))
        qa_ref[:, cols] = jnp.where(own, q_pair.astype(f32), q_extra).astype(bf16)
        ka_ref[:, cols] = jnp.where(own, k_pair.astype(f32), k_extra).astype(bf16)
        va_ref[:, cols] = jnp.where(own, v_pair.astype(f32), v_extra).astype(bf16)

    tile_lane = lax.broadcasted_iota(jnp.int32, (TILE, 128), 1)

    def one_tile(index, carry):
        start = pl.multiple_of(index * TILE, 16)
        rows = pl.ds(start, TILE)
        result = None
        for head in range(2):
            cols = slice(128 * head, 128 * (head + 1))
            spare = 64 * (1 - head)
            q_tile = qa_ref[rows, cols]
            scores = mm(q_tile, ka_ref[:, cols], NT)
            top = jnp.max(scores, axis=1, keepdims=True)
            weights = jnp.exp(scores - top)
            mixed = mm(weights.astype(bf16), va_ref[:, cols], NN)
            total = mixed[:, spare : spare + 1]
            mixed = mixed / total
            log_total = top + jnp.log(total)
            high, mid, low = split_three(-log_total)
            q_new = jnp.where(
                tile_lane == spare + 2,
                high.astype(f32),
                jnp.where(
                    tile_lane == spare + 3,
                    mid.astype(f32),
                    jnp.where(tile_lane == spare + 4, low.astype(f32), q_tile.astype(f32)),
                ),
            )
            qa_ref[rows, cols] = q_new.astype(bf16)
            result = mixed if head == 0 else jnp.where(tile_lane < 64, result, mixed)
        ctx_ref[rows, :] = result.astype(bf16)
        return carry

    lax.fori_loop(0, TILES, one_tile, 0)


def attn_bwd_kernel(
    len_ref, qa_ref, ka_ref, va_ref, ctx_ref, gctx_ref, x_ref, base_ref, full_ref,
    ig_ref, dw_ref, dq_s, dk_s, dv_s, do_s, dqt_s, ig_s, w_s,
):
    pair = pl.program_id(0)
    lane0 = pl.multiple_of(pair * 128, 128)
    lane = lax.broadcasted_iota(jnp.int32, (ROWS, 128), 1)
    grad = gctx_ref[...].astype(f32)
    product = grad * ctx_ref[...].astype(f32)
    for head in range(2):
        own = (lane // 64) == head
        spare = 64 * (1 - head)
        inner = -jnp.sum(jnp.where(own, product, 0.0), axis=1, keepdims=True)
        high, mid, low = split_three(inner)
        extra = jnp.where(
            lane == spare,
            high.astype(f32),
            jnp.where(
                lane == spare + 1,
                mid.astype(f32),
                jnp.where(lane == spare + 2, low.astype(f32), 0.0),
            ),
        )
        do_s[:, 128 * head : 128 * (head + 1)] = jnp.where(own, grad, extra).astype(bf16)
    dqt_s[...] = jnp.zeros_like(dqt_s)
    tile_lane = lax.broadcasted_iota(jnp.int32, (TILE, 128), 1)

    def one_tile(index, carry):
        start = pl.multiple_of(index * TILE, 16)
        rows = pl.ds(start, TILE)
        dk_tile = None
        dv_tile = None
        for head in range(2):
            cols = slice(128 * head, 128 * (head + 1))
            k_tile = ka_ref[rows, cols]
            probs = jnp.exp(mm(k_tile, qa_ref[:, cols], NT))
            scaled = mm(va_ref[rows, cols], do_s[:, cols], NT) * probs
            grad_scores = scaled.astype(bf16)
            dv_new = mm(probs.astype(bf16), do_s[:, cols], NN)
            dk_new = mm(grad_scores, qa_ref[:, cols], NN)
            dq_new = mm(k_tile, grad_scores, TN)
            dqt_s[64 * head : 64 * (head + 1), :] += dq_new[64 * head : 64 * (head + 1), :]
            dk_tile = dk_new if head == 0 else jnp.where(tile_lane < 64, dk_tile, dk_new)
            dv_tile = dv_new if head == 0 else jnp.where(tile_lane < 64, dv_tile, dv_new)
        dk_s[rows, pl.ds(lane0, 128)] = dk_tile.astype(bf16)
        dv_s[rows, pl.ds(lane0, 128)] = dv_tile.astype(bf16)
        return carry

    lax.fori_loop(0, TILES, one_tile, 0)
    dq_s[:, pl.ds(lane0, 128)] = (jnp.transpose(dqt_s[...]) * (HEAD**-0.5)).astype(bf16)

    @pl.when(pair == pl.num_programs(0) - 1)
    def _():
        x_cols = [with_ones(part, g) for g, part in enumerate(windows(x_ref[...], 2))]
        total = [None, None]
        for which, source in enumerate((dq_s, dk_s, dv_s)):
            cols = windows(source[...], 2)
            for g in range(2):
                own = slice(first_row(g), first_row(g) + 192)
                w_s[own, :] = without_bias(
                    full_ref[192 * g : 192 * (g + 1), WIN * which : WIN * (which + 1)], g
                )
                if first_row(g) == 0:
                    w_s[192:, :] = jnp.zeros((64, WIN), bf16)
                else:
                    w_s[:64, :] = jnp.zeros((64, WIN), bf16)
                grad = mm(cols[g], x_cols[g], TN)
                dw_ref[192 * g : 192 * (g + 1), WIN * which : WIN * (which + 1)] = grad[own].astype(
                    bf16
                )
                part = mm(cols[g], w_s[...], NN)
                total[g] = part if which == 0 else total[g] + part
        ig_s[...] = (join(total) + base_ref[...]).astype(bf16)
        unmerge_rows(ig_s, ig_ref, len_ref[0])


def norm(values):
    mean = jnp.mean(values, axis=1, keepdims=True)
    centered = values - mean
    var = jnp.mean(centered * centered, axis=1, keepdims=True)
    inv = lax.rsqrt(var + norm_eps)
    return centered * inv, inv


def norm_back(grad_n, n, inv):
    mean_g = jnp.mean(grad_n, axis=1, keepdims=True)
    mean_gn = jnp.mean(grad_n * n, axis=1, keepdims=True)
    return (grad_n - mean_g - n * mean_gn) * inv


def mid_fwd_kernel(
    len_ref, x0_ref, x1_ref, ctx0_ref, ctx1_ref, full_ref, wu_ref, vec_ref,
    out0_ref, out1_ref, n1_ref, n2_ref, inv_ref, slope_ref, act_ref, stat_ref,
    out0_s, out1_s, wd_s, stat_s,
):
    step = pl.program_id(0)
    first_len = len_ref[0]

    @pl.when(step == 0)
    def _():
        stat_s[...] = jnp.zeros_like(stat_s)
        wd_s[...] = jnp.zeros_like(wd_s)
        for g in range(4):
            wd_s[g, first_row(g) : first_row(g) + 192, :] = full_ref[192 * g : 192 * (g + 1), D:]

    o_bias, gain1, shift1, down_bias, gain2, shift2 = (vec_ref[i : i + 1, :] for i in range(6))
    start = pl.multiple_of(step * TILE, 16)
    rows = pl.ds(start, TILE)
    keep = jnp.where(row_ids(start, TILE, D) < first_len, 1.0, 0.0)

    def note(slot, values):
        square = values * values
        stat_s[slot : slot + 1, :] += jnp.sum(square, axis=0, keepdims=True)
        stat_s[slot + 4 : slot + 5, :] += jnp.sum(square * keep, axis=0, keepdims=True)

    inputs = jnp.concatenate([x0_ref[...], x1_ref[...]], axis=1).astype(f32)
    context = jnp.concatenate([ctx0_ref[...], ctx1_ref[...]], axis=1)
    note(0, inputs)
    branch_attn = mm(context, full_ref[:, :D], NT) + o_bias
    note(1, branch_attn)
    n1, inv1 = norm(inputs + branch_attn)
    n1_ref[...] = n1
    first_norm = n1 * gain1 + shift1
    note(2, first_norm)
    low_cols = windows(first_norm.astype(bf16), 4)
    parts = []
    for g in range(4):
        cols = slice(D * g, D * (g + 1))
        up = mm(with_ones(low_cols[g], g), wu_ref[D * g : D * (g + 1), :], NT)
        gate = 0.5 * (1.0 + lax.erf(up * (2.0**-0.5)))
        slope_ref[:, cols] = gate + up * jnp.exp(up * up * -0.5) * 0.3989422804014327
        act = (up * gate).astype(bf16)
        act_ref[:, cols] = act
        parts.append(mm(act, wd_s[g], NT))
    branch_ffn = join(parts) + down_bias
    note(3, branch_ffn)
    n2, inv2 = norm(first_norm + branch_ffn)
    n2_ref[...] = n2
    lane = lax.broadcasted_iota(jnp.int32, (TILE, 128), 1)
    inv_ref[...] = jnp.where(lane < 64, inv1, inv2)
    result = (n2 * gain2 + shift2).astype(bf16)
    out0_s[rows, :] = result[:, :HALF]
    out1_s[rows, :] = result[:, HALF:]

    @pl.when(step == pl.num_programs(0) - 1)
    def _():
        unmerge_rows(out0_s, out0_ref, first_len)
        unmerge_rows(out1_s, out1_ref, first_len)
        stat_ref[...] = jnp.broadcast_to(
            jnp.sum(stat_s[...], axis=1, keepdims=True), stat_ref.shape
        )


def mid_bwd_kernel(
    len_ref, cot_ref, ctx0_ref, ctx1_ref, n1_ref, n2_ref, inv_ref, slope_ref, act_ref,
    full_ref, wu_ref, vec_ref, gctx_ref, base_ref, grad_ref,
    cot_s, wd_s, dwo_s, dwd_s, dwu_s, vec_s, turn_s,
):
    step = pl.program_id(0)

    @pl.when(step == 0)
    def _():
        merge_rows(cot_ref, cot_s, len_ref[0])
        for target in (dwo_s, dwd_s, dwu_s, vec_s, wd_s):
            target[...] = jnp.zeros_like(target)
        for g in range(4):
            wd_s[g, first_row(g) : first_row(g) + 192, :] = full_ref[192 * g : 192 * (g + 1), D:]

    gain1, shift1, gain2 = (vec_ref[i : i + 1, :] for i in (1, 2, 4))
    start = pl.multiple_of(step * TILE, 16)
    rows = pl.ds(start, TILE)

    def add_vec(slot, values):
        vec_s[slot : slot + 1, :] += jnp.sum(values, axis=0, keepdims=True)

    context = jnp.concatenate([ctx0_ref[...], ctx1_ref[...]], axis=1)
    n1 = n1_ref[...]
    n2 = n2_ref[...]
    inv1 = inv_ref[:, 0:1]
    inv2 = inv_ref[:, 64:65]
    low_cols = windows((n1 * gain1 + shift1).astype(bf16), 4)
    grad_out = cot_s[rows, :].astype(f32)
    add_vec(4, grad_out * n2)
    add_vec(5, grad_out)
    grad_sum2 = norm_back(grad_out * gain2, n2, inv2)
    grad_ffn = grad_sum2.astype(bf16)
    add_vec(3, grad_ffn.astype(f32))
    ffn_cols = windows(grad_ffn, 4)
    parts = []
    for g in range(4):
        cols = slice(D * g, D * (g + 1))
        dwd_s[g] += mm(ffn_cols[g], act_ref[:, cols], TN)
        grad_up = (mm(ffn_cols[g], wd_s[g], NN) * slope_ref[:, cols]).astype(bf16)
        dwu_s[g] += mm(with_ones(low_cols[g], g), grad_up, TN)
        parts.append(mm(grad_up, without_bias(wu_ref[D * g : D * (g + 1), :], g), NN))
    grad_first = join(parts) + grad_sum2
    add_vec(1, grad_first * n1)
    add_vec(2, grad_first)
    grad_sum1 = norm_back(grad_first * gain1, n1, inv1)
    base_ref[...] = grad_sum1
    grad_branch = grad_sum1.astype(bf16)
    add_vec(0, grad_branch.astype(f32))
    dwo_s[...] += mm(grad_branch, context, TN)
    gctx_ref[...] = mm(grad_branch, full_ref[:, :D], NN).astype(bf16)

    @pl.when(step == pl.num_programs(0) - 1)
    def _():
        grad_ref[:, :D] = dwo_s[...].astype(bf16)
        for g in range(4):
            own = slice(192 * g, 192 * (g + 1))
            grad_ref[own, D : 2 * D] = dwd_s[g, first_row(g) : first_row(g) + 192, :].astype(bf16)
            turned = jnp.transpose(dwu_s[g])
            for half in range(2):
                turn_s[...] = turned[:, 128 * half : 128 * (half + 1)]
                for j in range(4):
                    lane0 = 2 * D + WIN * j + 128 * half
                    grad_ref[own, lane0 : lane0 + 128] = turn_s[pl.ds(j, 192, stride=4), :].astype(
                        bf16
                    )
        grad_ref[:, 2 * D + 4 * WIN :] = jnp.transpose(vec_s[...]).astype(bf16)


def whole(shape):
    zeros = (0,) * len(shape)
    return pl.BlockSpec(shape, lambda i, *_: zeros, pipeline_mode=pl.Buffered(1))


def kept(shape):
    zeros = (0,) * len(shape)
    return pl.BlockSpec(shape, lambda i, *_: zeros)


def struct(shape, dtype):
    return jax.ShapeDtypeStruct(shape, dtype)


PARAMS = pltpu.CompilerParams(
    dimension_semantics=("arbitrary",), vmem_limit_bytes=63_000_000
)
SMALL = pltpu.CompilerParams(
    dimension_semantics=("arbitrary",), vmem_limit_bytes=24_000_000
)


GRAD_COLS = 2 * D + 4 * WIN + 128


def attn_fwd(len_arr, tok, full, half):
    pair_cols = lambda width: pl.BlockSpec((ROWS, width), lambda i, *_: (0, i))
    return pl.pallas_call(
        attn_fwd_kernel,
        name="attn_fwd",
        grid_spec=pltpu.PrefetchScalarGridSpec(
            num_scalar_prefetch=1,
            grid=(3,),
            in_specs=[
                whole(tok.shape),
                pl.BlockSpec((HALF, D), lambda i, *_: (half, 2), pipeline_mode=pl.Buffered(1)),
            ],
            out_specs=[
                kept((ROWS, HALF)), pair_cols(256), pair_cols(256), pair_cols(256), pair_cols(128),
            ],
            scratch_shapes=[pltpu.VMEM((ROWS, HALF), bf16)] * 3
            + [pltpu.VMEM((3, 2, WIN, WIN), bf16)],
        ),
        out_shape=[
            struct((ROWS, HALF), bf16), struct((ROWS, D), bf16), struct((ROWS, D), bf16),
            struct((ROWS, D), bf16), struct((ROWS, HALF), bf16),
        ],
        compiler_params=PARAMS,
        cost_estimate=pl.CostEstimate(
            flops=20_000_000_000, bytes_accessed=12_000_000, transcendentals=7_000_000
        ),
    )(len_arr, tok, full)


def attn_bwd(len_arr, qa, ka, va, ctx, gctx, x, base, full, half):
    pair_cols = lambda width, first: pl.BlockSpec((ROWS, width), lambda i, *_: (0, i + first))
    return pl.pallas_call(
        attn_bwd_kernel,
        name="attn_bwd",
        grid_spec=pltpu.PrefetchScalarGridSpec(
            num_scalar_prefetch=1,
            grid=(3,),
            in_specs=[
                pair_cols(256, 0), pair_cols(256, 0), pair_cols(256, 0), pair_cols(128, 0),
                pair_cols(128, 3 * half), whole(x.shape),
                pl.BlockSpec((ROWS, HALF), lambda i, *_: (0, half), pipeline_mode=pl.Buffered(1)),
                pl.BlockSpec((HALF, D), lambda i, *_: (half, 2), pipeline_mode=pl.Buffered(1)),
            ],
            out_specs=[kept((SEQ // BLOCK, 2, BLOCK, HALF)), kept((HALF, D))],
            scratch_shapes=[
                pltpu.VMEM((ROWS, HALF), bf16),
                pltpu.VMEM((ROWS, HALF), bf16),
                pltpu.VMEM((ROWS, HALF), bf16),
                pltpu.VMEM((ROWS, 256), bf16),
                pltpu.VMEM((128, ROWS), f32),
                pltpu.VMEM((ROWS, HALF), bf16),
                pltpu.VMEM((WIN, WIN), bf16),
            ],
        ),
        out_shape=[struct((SEQ // BLOCK, 2, BLOCK, HALF), bf16), struct((HALF, D), bf16)],
        compiler_params=PARAMS,
        cost_estimate=pl.CostEstimate(
            flops=30_000_000_000, bytes_accessed=16_000_000, transcendentals=7_000_000
        ),
    )(len_arr, qa, ka, va, ctx, gctx, x, base, full)


def row_tile(width):
    return pl.BlockSpec((TILE, width), lambda i, *_: (i, 0))


def mid_fwd(len_arr, x0, x1, ctx0, ctx1, full, wu, vecs):
    outs = [
        ((SEQ // BLOCK, 2, BLOCK, HALF), bf16), ((SEQ // BLOCK, 2, BLOCK, HALF), bf16),
        ((ROWS, D), f32), ((ROWS, D), f32), ((ROWS, 128), f32), ((ROWS, FF), f32),
        ((ROWS, FF), bf16), ((8, 128), f32),
    ]
    return pl.pallas_call(
        mid_fwd_kernel,
        name="mid_fwd",
        grid_spec=pltpu.PrefetchScalarGridSpec(
            num_scalar_prefetch=1,
            grid=(TILES,),
            in_specs=[row_tile(HALF)] * 4
            + [whole((D, 2 * D)), whole(wu.shape), whole(vecs.shape)],
            out_specs=[
                kept(outs[0][0]), kept(outs[0][0]), row_tile(D), row_tile(D), row_tile(128),
                row_tile(FF), row_tile(FF), kept((8, 128)),
            ],
            scratch_shapes=[
                pltpu.VMEM((ROWS, HALF), bf16),
                pltpu.VMEM((ROWS, HALF), bf16),
                pltpu.VMEM((4, WIN, D), bf16),
                pltpu.VMEM((8, D), f32),
            ],
        ),
        out_shape=[struct(*o) for o in outs],
        compiler_params=PARAMS,
        cost_estimate=pl.CostEstimate(
            flops=15_000_000_000, bytes_accessed=36_000_000, transcendentals=7_000_000
        ),
    )(len_arr, x0, x1, ctx0, ctx1, full, wu, vecs)


def mid_bwd(len_arr, cot, ctx0, ctx1, n1, n2, inv, slope, act, full, wu, vecs):
    outs = [((ROWS, D), bf16), ((ROWS, D), f32), ((D, GRAD_COLS), bf16)]
    return pl.pallas_call(
        mid_bwd_kernel,
        name="mid_bwd",
        grid_spec=pltpu.PrefetchScalarGridSpec(
            num_scalar_prefetch=1,
            grid=(TILES,),
            in_specs=[
                whole(cot.shape), row_tile(HALF), row_tile(HALF), row_tile(D), row_tile(D),
                row_tile(128), row_tile(FF), row_tile(FF), whole((D, 2 * D)), whole(wu.shape),
                whole(vecs.shape),
            ],
            out_specs=[
                row_tile(D),
                row_tile(D),
                pl.BlockSpec((D, GRAD_COLS), lambda i, *_: (0, 0), pipeline_mode=pl.Buffered(1)),
            ],
            scratch_shapes=[
                pltpu.VMEM((ROWS, D), bf16),
                pltpu.VMEM((4, WIN, D), bf16),
                pltpu.VMEM((D, D), f32),
                pltpu.VMEM((4, WIN, D), f32),
                pltpu.VMEM((4, WIN, D), f32),
                pltpu.VMEM((128, D), f32),
                pltpu.VMEM((D, 128), f32),
            ],
        ),
        out_shape=[struct(*o) for o in outs],
        compiler_params=PARAMS,
        cost_estimate=pl.CostEstimate(
            flops=30_000_000_000, bytes_accessed=50_000_000, transcendentals=10_000
        ),
    )(len_arr, cot, ctx0, ctx1, n1, n2, inv, slope, act, full, wu, vecs)


def pack_kernel(
    odd_ref, bias_ref, o_ref, down_ref, q_ref, k_ref, v_ref, up_ref, out_ref, low_s, high_s
):
    rows = o_ref.shape[0]
    odd = odd_ref[0]
    eye = lax.broadcasted_iota(jnp.int32, (rows, rows), 0) == lax.broadcasted_iota(
        jnp.int32, (rows, rows), 1
    )
    columns = mm(jnp.where(eye, 1.0, 0.0).astype(bf16), bias_ref[...], NT)
    shift = lax.broadcasted_iota(jnp.int32, (192, WIN), 1) - lax.broadcasted_iota(
        jnp.int32, (192, WIN), 0
    )
    move = jnp.where(shift == 64 * odd, 1.0, 0.0).astype(bf16)

    def padded(weight, column):
        lane = lax.broadcasted_iota(jnp.int32, (weight.shape[0], WIN), 1)
        moved = mm(weight, move, NN)
        return jnp.where(lane == 192 * (1 - odd), column, moved)

    out_ref[:, :D] = o_ref[...]
    out_ref[:, D : 2 * D] = down_ref[...]
    zero = jnp.zeros((rows, 1), f32)
    sources = ((q_ref, columns[:, 6:7]), (k_ref, zero), (v_ref, columns[:, 7:8]))
    for which, (ref, column) in enumerate(sources):
        start = 2 * D + WIN * which
        out_ref[:, start : start + WIN] = padded(ref[...], column).astype(bf16)
    column = jnp.concatenate([columns[:, 8 + i : 9 + i] for i in range(4)], axis=0)
    up = padded(up_ref[...], column)
    low_s[...] = up[:, :128]
    high_s[...] = up[:, 128:]
    for j in range(4):
        for half, source in enumerate((low_s, high_s)):
            start = 3 * D + WIN * j + 128 * half
            out_ref[:, start : start + 128] = source[pl.ds(j, rows, stride=4), :].astype(bf16)
    out_ref[:, 3 * D + 4 * WIN :] = columns.astype(bf16)


def pack(odd, biases, up_bias, o_weight, down_weight, in_weights, up_weight):
    rows = o_weight.shape[0]
    flat = jnp.concatenate(biases + [up_bias]).reshape(-1, rows)
    flat = jnp.pad(flat, ((0, 128 - flat.shape[0]), (0, 0)))
    cols = 3 * D + 4 * WIN + 128
    arrays = [flat, o_weight, down_weight, *in_weights, up_weight]
    return pl.pallas_call(
        pack_kernel,
        name="pack",
        grid_spec=pltpu.PrefetchScalarGridSpec(
            num_scalar_prefetch=1,
            grid=(1,),
            in_specs=[whole(array.shape) for array in arrays],
            out_specs=[kept((rows, cols))],
            scratch_shapes=[pltpu.VMEM((4 * rows, 128), f32)] * 2,
        ),
        out_shape=[struct((rows, cols), bf16)],
        compiler_params=SMALL,
        cost_estimate=pl.CostEstimate(flops=0, bytes_accessed=400_000, transcendentals=0),
    )(odd.astype(jnp.int32).reshape(1), *arrays)[0]


def source_of(len_ref, perm_ref, place):
    first = perm_ref[place - place % 2]
    second = perm_ref[place - place % 2 + 1]
    swapped = (len_ref[first] < len_ref[second]).astype(jnp.int32)
    return jnp.where(swapped == place % 2, first, second)


def deal_kernel(len_ref, perm_ref, rows_ref, *out_refs):
    count = out_refs[0].shape[0]
    start = pl.program_id(0) * count

    def one(index, carry):
        source = source_of(len_ref, perm_ref, start + index)
        lane = 0
        for out_ref in out_refs:
            width = out_ref.shape[2]
            out_ref[index] = rows_ref[source, :, lane : lane + width]
            lane += width
        return carry

    lax.fori_loop(0, count, one, 0)


def deal(rows, lengths, permutation, parts):
    total, size, width = rows.shape
    count = total // STEPS
    return pl.pallas_call(
        deal_kernel,
        name="deal",
        grid_spec=pltpu.PrefetchScalarGridSpec(
            num_scalar_prefetch=2,
            grid=(STEPS,),
            in_specs=[whole(rows.shape)],
            out_specs=[pl.BlockSpec((count, size, width // parts), lambda i, *_: (i, 0, 0))] * parts,
        ),
        out_shape=[struct((total, size, width // parts), rows.dtype)] * parts,
        compiler_params=SMALL,
        cost_estimate=pl.CostEstimate(flops=0, bytes_accessed=8_000_000, transcendentals=0),
    )(lengths, permutation, rows)


def restore_kernel(len_ref, perm_ref, first_ref, second_ref, out_ref, place_s):
    count = out_ref.shape[0]
    start = pl.program_id(0) * count
    width = first_ref.shape[2]

    @pl.when(pl.program_id(0) == 0)
    def _():
        def note(index, carry):
            place_s[source_of(len_ref, perm_ref, index)] = index
            return carry

        lax.fori_loop(0, first_ref.shape[0], note, 0)

    def one(index, carry):
        place = place_s[start + index]
        out_ref[index, :, :width] = first_ref[place]
        out_ref[index, :, width:] = second_ref[place]
        return carry

    lax.fori_loop(0, count, one, 0)


def restore(first, second, lengths, permutation):
    total, size, width = first.shape
    count = total // STEPS
    return pl.pallas_call(
        restore_kernel,
        name="restore",
        grid_spec=pltpu.PrefetchScalarGridSpec(
            num_scalar_prefetch=2,
            grid=(STEPS,),
            in_specs=[whole(first.shape), whole(second.shape)],
            out_specs=[pl.BlockSpec((count, size, 2 * width), lambda i, *_: (i, 0, 0))],
            scratch_shapes=[pltpu.SMEM((total,), jnp.int32)],
        ),
        out_shape=[struct((total, size, 2 * width), first.dtype)],
        compiler_params=SMALL,
        cost_estimate=pl.CostEstimate(flops=0, bytes_accessed=8_000_000, transcendentals=0),
    )(lengths, permutation, first, second)[0]


def pick(values, index):
    return values.at[index].get(mode="promise_in_bounds")


def tie(*values):
    return lax.optimization_barrier(values)


def on_device(
    tokens, cotangent, lengths, permutation, q_weight, q_bias, k_weight, v_weight, v_bias, o_weight,
    o_bias, norm1_gain, norm1_bias, up_weight, up_bias, down_weight, down_bias, norm2_gain,
    norm2_bias,
):
    devices = lax.axis_size(AXES)
    my_index = lax.axis_index(AXES)
    seq_total, piece_len, _ = tokens.shape
    seq_dev = seq_total // devices
    rows_dev = q_weight.shape[0]
    up_dev = up_weight.shape[0]
    odd = (my_index // (devices // 4)) % 2 == 1

    def padded(weight, bias):
        column = bias[:, None]
        gap = jnp.zeros((weight.shape[0], 63), bf16)
        return jnp.where(
            odd,
            jnp.concatenate([column, gap, weight], axis=1),
            jnp.concatenate([weight, column, gap], axis=1),
        )

    if rows_dev % 8 == 0:
        packed = pack(
            odd,
            [o_bias, norm1_gain, norm1_bias, down_bias, norm2_gain, norm2_bias, q_bias, v_bias],
            up_bias, o_weight, down_weight, [q_weight, k_weight, v_weight], up_weight,
        )
    else:
        small = [o_bias, norm1_gain, norm1_bias, down_bias, norm2_gain, norm2_bias]
        packed = jnp.concatenate(
            [
                o_weight,
                down_weight,
                padded(q_weight, q_bias),
                padded(k_weight, jnp.zeros_like(q_bias)),
                padded(v_weight, v_bias),
                padded(up_weight, up_bias).reshape(rows_dev, 4 * WIN),
                jnp.pad(jnp.stack(small, axis=1), ((0, 0), (0, 122))),
            ],
            axis=1,
        )
    full = lax.all_gather(packed, AXES, axis=0, tiled=True)

    dealt_lengths = pick(lengths, permutation).reshape(devices, seq_dev)
    swap = dealt_lengths[:, 0] < dealt_lengths[:, 1]
    my_swap = lax.dynamic_index_in_dim(swap, my_index, 0, False)
    len_arr = jnp.max(lax.dynamic_slice_in_dim(dealt_lengths, my_index, 1, 0)).reshape(1)

    def swap_blocks(rows):
        return lax.all_to_all(rows, AXES, split_axis=0, concat_axis=0, tiled=True)

    def arrive(rows):
        width = rows.shape[-1]
        moved = swap_blocks(rows.reshape(devices, seq_dev, piece_len, width))
        if piece_len == BLOCK:
            return moved
        moved = moved.transpose(1, 0, 2, 3).reshape(seq_dev, SEQ // BLOCK, BLOCK, width)
        return moved.transpose(1, 0, 2, 3)

    def leave(rows):
        width = rows.shape[-1]
        if piece_len != BLOCK:
            rows = rows.transpose(1, 0, 2, 3).reshape(seq_dev, devices, piece_len, width)
            rows = rows.transpose(1, 0, 2, 3)
        return swap_blocks(rows).reshape(seq_total, piece_len, width)

    def send_pair(partial, axis):
        count = lax.axis_size(axis)
        parity = lax.axis_index(axis) % 2
        blocks = partial.reshape(count // 2, 2, partial.shape[0] // count, partial.shape[1])
        kept_part, given = (
            lax.dynamic_slice_in_dim(blocks, which, 1, 1) for which in (parity, 1 - parity)
        )
        return [kept_part, lax.ppermute(given, axis, [(i, i ^ 1) for i in range(count)])]

    def send_rest(partial, axis):
        count = lax.axis_size(axis)
        half = count // 2
        place = lax.axis_index(axis) // 2
        size = partial.shape[0] // half
        block_of = lambda index: lax.dynamic_slice_in_dim(partial, index * size, size, 0)
        parts = [block_of(place)]
        for shift in range(1, half):
            target = [(i, (i + 2 * shift) % count) for i in range(count)]
            parts.append(lax.ppermute(block_of((place + shift) % half), axis, target))
        return parts

    def total(parts):
        result = sum(part.astype(f32) for part in parts)
        return result.reshape(-1, result.shape[-1])

    def total_low(parts):
        return total(parts).astype(bf16)

    tok0, tok1 = deal(tokens, lengths, permutation, 2)
    tok0 = arrive(tok0)
    tok1 = arrive(tok1)
    dealt_cot, tok0, tok1 = tie(deal(cotangent, lengths, permutation, 1)[0], tok0, tok1)
    cot = arrive(dealt_cot)

    x0, qa0, ka0, va0, ctx0 = attn_fwd(len_arr, tok0, full, 0)
    x1, qa1, ka1, va1, ctx1 = attn_fwd(len_arr, tok1, full, 1)
    wu = full[:, 3 * D : 3 * D + 4 * WIN].reshape(FF, WIN)
    vecs = jnp.pad(full[:, 3 * D + 4 * WIN : 3 * D + 4 * WIN + 6].astype(f32).T, ((0, 2), (0, 0)))
    out0, out1, n1, n2, inv, slope, act, stat = mid_fwd(
        len_arr, x0, x1, ctx0, ctx1, full, wu, vecs
    )
    cot, out0, out1 = tie(cot, out0, out1)
    back_out0 = leave(out0)
    gctx, base, grads = mid_bwd(
        len_arr, cot, ctx0, ctx1, n1, n2, inv, slope, act, full, wu, vecs
    )
    gctx, out1, back_out0 = tie(gctx, out1, back_out0)
    back_out1 = leave(out1)
    parts = send_pair(grads, "dp")
    ig0, dw0 = attn_bwd(len_arr, qa0, ka0, va0, ctx0, gctx, x0, base, full, 0)
    ig0, dw0, gctx, back_out1, *parts = tie(ig0, dw0, gctx, back_out1, *parts)
    back0 = leave(ig0)
    parts = send_rest(total_low(parts), "dp")
    ig1, dw1 = attn_bwd(len_arr, qa1, ka1, va1, ctx1, gctx, x1, base, full, 1)
    ig1, dw1, back0, *parts = tie(ig1, dw1, back0, *parts)
    back1 = leave(ig1)
    mine = total(send_rest(total_low(send_pair(total_low(parts), "fsdp")), "fsdp"))
    parts = send_rest(total_low(send_pair(jnp.concatenate([dw0, dw1], axis=0), "dp")), "dp")
    mine_in = total(send_rest(total_low(send_pair(total_low(parts), "fsdp")), "fsdp"))

    back_out0, back_out1, mine = tie(back_out0, back_out1, mine)
    output = restore(back_out0, back_out1, lengths, permutation)
    input_grad = restore(back0, back1, lengths, permutation)
    lens = jnp.stack([len_arr[0], ROWS - len_arr[0]]).astype(f32)
    sums = jnp.stack([stat[4:8, 0], stat[0:4, 0] - stat[4:8, 0]], axis=1)
    rms = jnp.sqrt(sums / (lens[None, :] * D) + rms_eps)
    stream_rms = jnp.where(my_swap, rms[:, ::-1], rms)
    vec = lambda i: mine[:, 2 * D + 4 * WIN + i]

    def unpadded(block):
        return (
            jnp.where(odd, block[:, 64:], block[:, :192]),
            jnp.where(odd, block[:, 0], block[:, 192]),
        )

    dq, dqb = unpadded(mine_in[:, :WIN])
    dk, _ = unpadded(mine_in[:, WIN : 2 * WIN])
    dv, dvb = unpadded(mine_in[:, 2 * WIN :])
    dup, dub = unpadded(mine[:, 2 * D : 2 * D + 4 * WIN].reshape(up_dev, WIN))
    return (
        output, input_grad, dq, dqb, dk, dv, dvb, mine[:, :D], vec(0), vec(1), vec(2), dup, dub,
        mine[:, D : 2 * D], vec(3), vec(4), vec(5), stream_rms,
    )


def solution(mesh):
    rows = P(None, AXES, None)
    mat = P(AXES, None)
    vec = P(AXES)
    in_specs = (
        rows, rows, P(), P(), mat, vec, mat, mat, vec, mat, vec, vec, vec, mat, vec, mat, vec, vec,
        vec,
    )
    out_specs = (
        rows, rows, mat, vec, mat, mat, vec, mat, vec, vec, vec, mat, vec, mat, vec, vec, vec,
        P(None, AXES),
    )
    return jax.shard_map(
        on_device, mesh=mesh, in_specs=in_specs, out_specs=out_specs, check_vma=False
    )
```

```python
import functools

import jax
import jax.numpy as jnp
from jax import lax
from jax.experimental import pallas as pl
from jax.experimental.pallas import tpu as pltpu
from jax.sharding import PartitionSpec as P

AXES = ("dp", "fsdp")
D = 768
FF = 3072
HALF = D // 2
HEAD = 64
WIN = 256
SEQ = 1024
SHORT = 64
BLOCK = 32
ROWS = SEQ + SHORT
TILE = 272
TILES = ROWS // TILE
BIG = 1e30
STEPS = 4

norm_eps = 1e-12
rms_eps = 1e-06
bf16 = jnp.bfloat16
f32 = jnp.float32

NN = (((1,), (0,)), ((), ()))
NT = (((1,), (1,)), ((), ()))
TN = (((0,), (0,)), ((), ()))


def mm(left, right, dims):
    return lax.dot_general(left, right, dims, preferred_element_type=f32)


def exchange():
    row = lax.broadcasted_iota(jnp.int32, (WIN, WIN), 0)
    col = lax.broadcasted_iota(jnp.int32, (WIN, WIN), 1)
    return jnp.where(row + col == WIN - 1, 1.0, 0.0).astype(bf16)


def row_ids(start, count, width):
    return start + lax.broadcasted_iota(jnp.int32, (count, width), 0)


def block_rows(ref, seq, start, count):
    values = ref[start // BLOCK : (start + count) // BLOCK, seq]
    return values.reshape(count, values.shape[-1])


def merge_rows(pair_ref, packed_ref, first_len):
    width = packed_ref.shape[1]
    flip = exchange()
    packed_ref[0:SHORT, :] = block_rows(pair_ref, 0, 0, SHORT)
    for step in range(SEQ // WIN):
        start = SHORT + WIN * step
        flipped = mm(flip, block_rows(pair_ref, 1, SEQ - WIN * (step + 1), WIN), NN)
        inside = min(WIN, SEQ - start)
        own = block_rows(pair_ref, 0, start, inside).astype(f32)
        keep = row_ids(start, inside, width) < first_len
        packed_ref[start : start + inside, :] = jnp.where(keep, own, flipped[0:inside]).astype(bf16)
        if inside < WIN:
            packed_ref[start + inside : start + WIN, :] = flipped[inside:].astype(bf16)


def unmerge_rows(packed_ref, pair_ref, first_len):
    width = packed_ref.shape[1]
    flip = exchange()
    blocks = WIN // BLOCK
    for step in range(SEQ // WIN):
        start = WIN * step
        ids = row_ids(start, WIN, width)
        own = packed_ref[start : start + WIN, :].astype(f32)
        own = jnp.where(ids < first_len, own, 0.0).astype(bf16)
        pair_ref[blocks * step : blocks * (step + 1), 0] = own.reshape(blocks, BLOCK, width)
        source = ROWS - WIN * (step + 1)
        flipped = mm(flip, packed_ref[source : source + WIN, :], NN)
        flipped = jnp.where(ids < ROWS - first_len, flipped, 0.0).astype(bf16)
        pair_ref[blocks * step : blocks * (step + 1), 1] = flipped.reshape(blocks, BLOCK, width)


def spare_of(group):
    return 192 if group % 2 == 0 else 0


def with_ones(window, group):
    lane = lax.broadcasted_iota(jnp.int32, window.shape, 1)
    return jnp.where(lane == spare_of(group), 1.0, window.astype(f32)).astype(bf16)


def without_bias(window, group):
    lane = lax.broadcasted_iota(jnp.int32, window.shape, 1)
    return jnp.where(lane == spare_of(group), 0.0, window.astype(f32)).astype(bf16)


def first_row(group):
    return 0 if group % 2 == 0 else 64


def windows(values, count):
    parts = []
    for group in range(count):
        start = (group // 2) * HALF + (group % 2) * 128
        parts.append(values[:, start : start + WIN])
    return parts


def join(parts):
    pieces = []
    for first, second in zip(parts[0::2], parts[1::2]):
        pieces += [first[:, :128], first[:, 128:] + second[:, :128], second[:, 128:]]
    return jnp.concatenate(pieces, axis=1)


def split_three(value):
    high = value.astype(bf16)
    rest = value - high.astype(f32)
    mid = rest.astype(bf16)
    low = (rest - mid.astype(f32)).astype(bf16)
    return high, mid, low


def attn_fwd_kernel(
    len_ref, tok_ref, full_ref, x_ref, qa_ref, ka_ref, va_ref, ctx_ref, q_s, k_s, v_s, w_s
):
    pair = pl.program_id(0)
    first_len = len_ref[0]

    @pl.when(pair == 0)
    def _():
        merge_rows(tok_ref, x_ref, first_len)
        w_s[...] = jnp.zeros_like(w_s)
        for which in range(3):
            for g in range(2):
                w_s[which, g, first_row(g) : first_row(g) + 192, :] = full_ref[
                    192 * g : 192 * (g + 1), WIN * which : WIN * (which + 1)
                ]
        cols = [with_ones(part, g) for g, part in enumerate(windows(x_ref[...], 2))]
        for which, target in enumerate((q_s, k_s, v_s)):
            value = join([mm(cols[g], w_s[which, g], NT) for g in range(2)])
            if which == 0:
                value = value.astype(bf16).astype(f32) * (HEAD**-0.5)
            target[...] = value.astype(bf16)

    lane0 = pl.multiple_of(pair * 128, 128)
    q_pair = q_s[:, pl.ds(lane0, 128)]
    k_pair = k_s[:, pl.ds(lane0, 128)]
    v_pair = v_s[:, pl.ds(lane0, 128)]
    lane = lax.broadcasted_iota(jnp.int32, (ROWS, 128), 1)
    in_first = row_ids(0, ROWS, 128) < first_len
    one = jnp.ones((ROWS, 128), f32)
    zero = jnp.zeros((ROWS, 128), f32)
    for head in range(2):
        spare = 64 * (1 - head)
        own = (lane // 64) == head
        first_one = jnp.where(in_first, one, zero)
        q_extra = jnp.where(
            lane == spare, first_one, jnp.where(lane == spare + 1, one - first_one, zero)
        )
        k_extra = jnp.where(
            lane == spare,
            (first_one - one) * BIG,
            jnp.where(
                lane == spare + 1,
                first_one * (-BIG),
                jnp.where((lane >= spare + 2) & (lane < spare + 5), one, zero),
            ),
        )
        v_extra = jnp.where((lane >= spare) & (lane < spare + 3), one, zero)
        cols = slice(128 * head, 128 * (head + 1))
        qa_ref[:, cols] = jnp.where(own, q_pair.astype(f32), q_extra).astype(bf16)
        ka_ref[:, cols] = jnp.where(own, k_pair.astype(f32), k_extra).astype(bf16)
        va_ref[:, cols] = jnp.where(own, v_pair.astype(f32), v_extra).astype(bf16)

    tile_lane = lax.broadcasted_iota(jnp.int32, (TILE, 128), 1)

    def one_tile(index, carry):
        start = pl.multiple_of(index * TILE, 16)
        rows = pl.ds(start, TILE)
        result = None
        for head in range(2):
            cols = slice(128 * head, 128 * (head + 1))
            spare = 64 * (1 - head)
            q_tile = qa_ref[rows, cols]
            scores = mm(q_tile, ka_ref[:, cols], NT)
            top = jnp.max(scores, axis=1, keepdims=True)
            weights = jnp.exp(scores - top)
            mixed = mm(weights.astype(bf16), va_ref[:, cols], NN)
            total = mixed[:, spare : spare + 1]
            mixed = mixed / total
            log_total = top + jnp.log(total)
            high, mid, low = split_three(-log_total)
            q_new = jnp.where(
                tile_lane == spare + 2,
                high.astype(f32),
                jnp.where(
                    tile_lane == spare + 3,
                    mid.astype(f32),
                    jnp.where(tile_lane == spare + 4, low.astype(f32), q_tile.astype(f32)),
                ),
            )
            qa_ref[rows, cols] = q_new.astype(bf16)
            result = mixed if head == 0 else jnp.where(tile_lane < 64, result, mixed)
        ctx_ref[rows, :] = result.astype(bf16)
        return carry

    lax.fori_loop(0, TILES, one_tile, 0)


def attn_bwd_kernel(
    len_ref, qa_ref, ka_ref, va_ref, ctx_ref, gctx_ref, x_ref, base_ref, full_ref,
    ig_ref, kept_ref, given_ref, dq_s, dk_s, dv_s, do_s, dqt_s, ig_s, w_s, dw_ref,
):
    pair = pl.program_id(0)
    lane0 = pl.multiple_of(pair * 128, 128)
    lane = lax.broadcasted_iota(jnp.int32, (ROWS, 128), 1)
    grad = gctx_ref[...].astype(f32)
    product = grad * ctx_ref[...].astype(f32)
    for head in range(2):
        own = (lane // 64) == head
        spare = 64 * (1 - head)
        inner = -jnp.sum(jnp.where(own, product, 0.0), axis=1, keepdims=True)
        high, mid, low = split_three(inner)
        extra = jnp.where(
            lane == spare,
            high.astype(f32),
            jnp.where(
                lane == spare + 1,
                mid.astype(f32),
                jnp.where(lane == spare + 2, low.astype(f32), 0.0),
            ),
        )
        do_s[:, 128 * head : 128 * (head + 1)] = jnp.where(own, grad, extra).astype(bf16)
    dqt_s[...] = jnp.zeros_like(dqt_s)
    tile_lane = lax.broadcasted_iota(jnp.int32, (TILE, 128), 1)

    def one_tile(index, carry):
        start = pl.multiple_of(index * TILE, 16)
        rows = pl.ds(start, TILE)
        dk_tile = None
        dv_tile = None
        for head in range(2):
            cols = slice(128 * head, 128 * (head + 1))
            k_tile = ka_ref[rows, cols]
            probs = jnp.exp(mm(k_tile, qa_ref[:, cols], NT))
            scaled = mm(va_ref[rows, cols], do_s[:, cols], NT) * probs
            grad_scores = scaled.astype(bf16)
            dv_new = mm(probs.astype(bf16), do_s[:, cols], NN)
            dk_new = mm(grad_scores, qa_ref[:, cols], NN)
            dq_new = mm(k_tile, grad_scores, TN)
            dqt_s[64 * head : 64 * (head + 1), :] += dq_new[64 * head : 64 * (head + 1), :]
            dk_tile = dk_new if head == 0 else jnp.where(tile_lane < 64, dk_tile, dk_new)
            dv_tile = dv_new if head == 0 else jnp.where(tile_lane < 64, dv_tile, dv_new)
        dk_s[rows, pl.ds(lane0, 128)] = dk_tile.astype(bf16)
        dv_s[rows, pl.ds(lane0, 128)] = dv_tile.astype(bf16)
        return carry

    lax.fori_loop(0, TILES, one_tile, 0)
    dq_s[:, pl.ds(lane0, 128)] = (jnp.transpose(dqt_s[...]) * (HEAD**-0.5)).astype(bf16)

    @pl.when(pair == pl.num_programs(0) - 1)
    def _():
        x_cols = [with_ones(part, g) for g, part in enumerate(windows(x_ref[...], 2))]
        total = [None, None]
        for which, source in enumerate((dq_s, dk_s, dv_s)):
            cols = windows(source[...], 2)
            for g in range(2):
                own = slice(first_row(g), first_row(g) + 192)
                w_s[own, :] = without_bias(
                    full_ref[192 * g : 192 * (g + 1), WIN * which : WIN * (which + 1)], g
                )
                if first_row(g) == 0:
                    w_s[192:, :] = jnp.zeros((64, WIN), bf16)
                else:
                    w_s[:64, :] = jnp.zeros((64, WIN), bf16)
                grad = mm(cols[g], x_cols[g], TN)
                dw_ref[192 * g : 192 * (g + 1), WIN * which : WIN * (which + 1)] = grad[own].astype(
                    bf16
                )
                part = mm(cols[g], w_s[...], NN)
                total[g] = part if which == 0 else total[g] + part
        ig_s[...] = (join(total) + base_ref[...]).astype(bf16)
        unmerge_rows(ig_s, ig_ref, len_ref[0])
        split_chunks(dw_ref, kept_ref, given_ref, len_ref[1])


def split_chunks(rows_ref, kept_ref, given_ref, parity):
    pairs, size, _ = kept_ref.shape
    for own in range(2):

        @pl.when(parity == own)
        def _():
            for pair in range(pairs):
                for which in range(2):
                    start = (2 * pair + which) * size
                    target = kept_ref if which == own else given_ref
                    target[pair] = rows_ref[start : start + size, :]


def norm(values):
    mean = jnp.mean(values, axis=1, keepdims=True)
    centered = values - mean
    var = jnp.mean(centered * centered, axis=1, keepdims=True)
    inv = lax.rsqrt(var + norm_eps)
    return centered * inv, inv


def norm_back(grad_n, n, inv):
    mean_g = jnp.mean(grad_n, axis=1, keepdims=True)
    mean_gn = jnp.mean(grad_n * n, axis=1, keepdims=True)
    return (grad_n - mean_g - n * mean_gn) * inv


def mid_fwd_kernel(
    len_ref, x0_ref, x1_ref, ctx0_ref, ctx1_ref, full_ref, wu_ref, vec_ref,
    out_ref, n1_ref, n2_ref, inv_ref, slope_ref, act_ref, stat_ref,
    out_s, wd_s, stat_s,
):
    step = pl.program_id(0)
    first_len = len_ref[0]

    @pl.when(step == 0)
    def _():
        stat_s[...] = jnp.zeros_like(stat_s)
        wd_s[...] = jnp.zeros_like(wd_s)
        for g in range(4):
            wd_s[g, first_row(g) : first_row(g) + 192, :] = full_ref[192 * g : 192 * (g + 1), D:]

    o_bias, gain1, shift1, down_bias, gain2, shift2 = (vec_ref[i : i + 1, :] for i in range(6))
    start = pl.multiple_of(step * TILE, 16)
    rows = pl.ds(start, TILE)
    keep = jnp.where(row_ids(start, TILE, D) < first_len, 1.0, 0.0)

    def note(slot, values):
        square = values * values
        stat_s[slot : slot + 1, :] += jnp.sum(square, axis=0, keepdims=True)
        stat_s[slot + 4 : slot + 5, :] += jnp.sum(square * keep, axis=0, keepdims=True)

    inputs = jnp.concatenate([x0_ref[...], x1_ref[...]], axis=1).astype(f32)
    context = jnp.concatenate([ctx0_ref[...], ctx1_ref[...]], axis=1)
    note(0, inputs)
    branch_attn = mm(context, full_ref[:, :D], NT) + o_bias
    note(1, branch_attn)
    n1, inv1 = norm(inputs + branch_attn)
    n1_ref[...] = n1
    first_norm = n1 * gain1 + shift1
    note(2, first_norm)
    low_cols = windows(first_norm.astype(bf16), 4)
    parts = []
    for g in range(4):
        cols = slice(D * g, D * (g + 1))
        up = mm(with_ones(low_cols[g], g), wu_ref[D * g : D * (g + 1), :], NT)
        gate = 0.5 * (1.0 + lax.erf(up * (2.0**-0.5)))
        slope_ref[:, cols] = gate + up * jnp.exp(up * up * -0.5) * 0.3989422804014327
        act = (up * gate).astype(bf16)
        act_ref[:, cols] = act
        parts.append(mm(act, wd_s[g], NT))
    branch_ffn = join(parts) + down_bias
    note(3, branch_ffn)
    n2, inv2 = norm(first_norm + branch_ffn)
    n2_ref[...] = n2
    lane = lax.broadcasted_iota(jnp.int32, (TILE, 128), 1)
    inv_ref[...] = jnp.where(lane < 64, inv1, inv2)
    out_s[rows, :] = (n2 * gain2 + shift2).astype(bf16)

    @pl.when(step == pl.num_programs(0) - 1)
    def _():
        unmerge_rows(out_s, out_ref, first_len)
        stat_ref[...] = jnp.broadcast_to(
            jnp.sum(stat_s[...], axis=1, keepdims=True), stat_ref.shape
        )


def mid_bwd_kernel(
    len_ref, cot_ref, ctx0_ref, ctx1_ref, n1_ref, n2_ref, inv_ref, slope_ref, act_ref,
    full_ref, wu_ref, vec_ref, gctx_ref, base_ref, kept_ref, given_ref,
    cot_s, wd_s, dwo_s, dwd_s, dwu_s, vec_s, turn_s, grad_ref,
):
    step = pl.program_id(0)

    @pl.when(step == 0)
    def _():
        merge_rows(cot_ref, cot_s, len_ref[0])
        for target in (dwo_s, dwd_s, dwu_s, vec_s, wd_s):
            target[...] = jnp.zeros_like(target)
        for g in range(4):
            wd_s[g, first_row(g) : first_row(g) + 192, :] = full_ref[192 * g : 192 * (g + 1), D:]

    gain1, shift1, gain2 = (vec_ref[i : i + 1, :] for i in (1, 2, 4))
    start = pl.multiple_of(step * TILE, 16)
    rows = pl.ds(start, TILE)

    def add_vec(slot, values):
        vec_s[slot : slot + 1, :] += jnp.sum(values, axis=0, keepdims=True)

    context = jnp.concatenate([ctx0_ref[...], ctx1_ref[...]], axis=1)
    n1 = n1_ref[...]
    n2 = n2_ref[...]
    inv1 = inv_ref[:, 0:1]
    inv2 = inv_ref[:, 64:65]
    low_cols = windows((n1 * gain1 + shift1).astype(bf16), 4)
    grad_out = cot_s[rows, :].astype(f32)
    add_vec(4, grad_out * n2)
    add_vec(5, grad_out)
    grad_sum2 = norm_back(grad_out * gain2, n2, inv2)
    grad_ffn = grad_sum2.astype(bf16)
    add_vec(3, grad_ffn.astype(f32))
    ffn_cols = windows(grad_ffn, 4)
    parts = []
    for g in range(4):
        cols = slice(D * g, D * (g + 1))
        dwd_s[g] += mm(ffn_cols[g], act_ref[:, cols], TN)
        grad_up = (mm(ffn_cols[g], wd_s[g], NN) * slope_ref[:, cols]).astype(bf16)
        dwu_s[g] += mm(with_ones(low_cols[g], g), grad_up, TN)
        parts.append(mm(grad_up, without_bias(wu_ref[D * g : D * (g + 1), :], g), NN))
    grad_first = join(parts) + grad_sum2
    add_vec(1, grad_first * n1)
    add_vec(2, grad_first)
    grad_sum1 = norm_back(grad_first * gain1, n1, inv1)
    base_ref[...] = grad_sum1
    grad_branch = grad_sum1.astype(bf16)
    add_vec(0, grad_branch.astype(f32))
    dwo_s[...] += mm(grad_branch, context, TN)
    gctx_ref[...] = mm(grad_branch, full_ref[:, :D], NN).astype(bf16)

    @pl.when(step == pl.num_programs(0) - 1)
    def _():
        grad_ref[:, :D] = dwo_s[...].astype(bf16)
        for g in range(4):
            own = slice(192 * g, 192 * (g + 1))
            grad_ref[own, D : 2 * D] = dwd_s[g, first_row(g) : first_row(g) + 192, :].astype(bf16)
            turned = jnp.transpose(dwu_s[g])
            for half in range(2):
                turn_s[...] = turned[:, 128 * half : 128 * (half + 1)]
                for j in range(4):
                    lane0 = 2 * D + WIN * j + 128 * half
                    grad_ref[own, lane0 : lane0 + 128] = turn_s[pl.ds(j, 192, stride=4), :].astype(
                        bf16
                    )
        grad_ref[:, 2 * D + 4 * WIN :] = jnp.transpose(vec_s[...]).astype(bf16)
        split_chunks(grad_ref, kept_ref, given_ref, len_ref[1])


def whole(shape):
    zeros = (0,) * len(shape)
    return pl.BlockSpec(shape, lambda i, *_: zeros, pipeline_mode=pl.Buffered(1))


def kept(shape):
    zeros = (0,) * len(shape)
    return pl.BlockSpec(shape, lambda i, *_: zeros)


def struct(shape, dtype):
    return jax.ShapeDtypeStruct(shape, dtype)


PARAMS = pltpu.CompilerParams(
    dimension_semantics=("arbitrary",), vmem_limit_bytes=63_000_000
)
GRAD_COLS = 2 * D + 4 * WIN + 128


def attn_fwd(len_arr, tok, full, half):
    pair_cols = lambda width: pl.BlockSpec((ROWS, width), lambda i, *_: (0, i))
    return pl.pallas_call(
        attn_fwd_kernel,
        name="attn_fwd",
        grid_spec=pltpu.PrefetchScalarGridSpec(
            num_scalar_prefetch=1,
            grid=(3,),
            in_specs=[
                whole(tok.shape),
                pl.BlockSpec((HALF, D), lambda i, *_: (half, 2), pipeline_mode=pl.Buffered(1)),
            ],
            out_specs=[
                kept((ROWS, HALF)), pair_cols(256), pair_cols(256), pair_cols(256), pair_cols(128),
            ],
            scratch_shapes=[pltpu.VMEM((ROWS, HALF), bf16)] * 3
            + [pltpu.VMEM((3, 2, WIN, WIN), bf16)],
        ),
        out_shape=[
            struct((ROWS, HALF), bf16), struct((ROWS, D), bf16), struct((ROWS, D), bf16),
            struct((ROWS, D), bf16), struct((ROWS, HALF), bf16),
        ],
        compiler_params=PARAMS,
        cost_estimate=pl.CostEstimate(
            flops=20_000_000_000, bytes_accessed=12_000_000, transcendentals=7_000_000
        ),
    )(len_arr, tok, full)


def attn_bwd(len_arr, qa, ka, va, ctx, gctx, x, base, full, half, chunks):
    part = (chunks // 4, D // chunks, D)
    pair_cols = lambda width, first: pl.BlockSpec((ROWS, width), lambda i, *_: (0, i + first))
    return pl.pallas_call(
        attn_bwd_kernel,
        name="attn_bwd",
        grid_spec=pltpu.PrefetchScalarGridSpec(
            num_scalar_prefetch=1,
            grid=(3,),
            in_specs=[
                pair_cols(256, 0), pair_cols(256, 0), pair_cols(256, 0), pair_cols(128, 0),
                pair_cols(128, 3 * half), whole(x.shape),
                pl.BlockSpec((ROWS, HALF), lambda i, *_: (0, half), pipeline_mode=pl.Buffered(1)),
                pl.BlockSpec((HALF, D), lambda i, *_: (half, 2), pipeline_mode=pl.Buffered(1)),
            ],
            out_specs=[kept((SEQ // BLOCK, 2, BLOCK, HALF)), kept(part), kept(part)],
            scratch_shapes=[
                pltpu.VMEM((ROWS, HALF), bf16),
                pltpu.VMEM((ROWS, HALF), bf16),
                pltpu.VMEM((ROWS, HALF), bf16),
                pltpu.VMEM((ROWS, 256), bf16),
                pltpu.VMEM((128, ROWS), f32),
                pltpu.VMEM((ROWS, HALF), bf16),
                pltpu.VMEM((WIN, WIN), bf16),
                pltpu.VMEM((HALF, D), bf16),
            ],
        ),
        out_shape=[
            struct((SEQ // BLOCK, 2, BLOCK, HALF), bf16), struct(part, bf16), struct(part, bf16),
        ],
        compiler_params=PARAMS,
        cost_estimate=pl.CostEstimate(
            flops=100_000_000, bytes_accessed=1_000_000, transcendentals=0
        ),
    )(len_arr, qa, ka, va, ctx, gctx, x, base, full)


def row_tile(width):
    return pl.BlockSpec((TILE, width), lambda i, *_: (i, 0))


def mid_fwd(len_arr, x0, x1, ctx0, ctx1, full, wu, vecs):
    outs = [
        ((SEQ // BLOCK, 2, BLOCK, D), bf16), ((ROWS, D), f32), ((ROWS, D), f32),
        ((ROWS, 128), f32), ((ROWS, FF), f32), ((ROWS, FF), bf16), ((8, 128), f32),
    ]
    return pl.pallas_call(
        mid_fwd_kernel,
        name="mid_fwd",
        grid_spec=pltpu.PrefetchScalarGridSpec(
            num_scalar_prefetch=1,
            grid=(TILES,),
            in_specs=[row_tile(HALF)] * 4
            + [whole((D, 2 * D)), whole(wu.shape), whole(vecs.shape)],
            out_specs=[
                kept(outs[0][0]), row_tile(D), row_tile(D), row_tile(128), row_tile(FF),
                row_tile(FF), kept((8, 128)),
            ],
            scratch_shapes=[
                pltpu.VMEM((ROWS, D), bf16),
                pltpu.VMEM((4, WIN, D), bf16),
                pltpu.VMEM((8, D), f32),
            ],
        ),
        out_shape=[struct(*o) for o in outs],
        compiler_params=PARAMS,
        cost_estimate=pl.CostEstimate(
            flops=15_000_000_000, bytes_accessed=36_000_000, transcendentals=7_000_000
        ),
    )(len_arr, x0, x1, ctx0, ctx1, full, wu, vecs)


def mid_bwd(len_arr, cot, ctx0, ctx1, n1, n2, inv, slope, act, full, wu, vecs, chunks):
    part = (chunks // 2, D // chunks, GRAD_COLS)
    outs = [((ROWS, D), bf16), ((ROWS, D), f32), (part, bf16), (part, bf16)]
    return pl.pallas_call(
        mid_bwd_kernel,
        name="mid_bwd",
        grid_spec=pltpu.PrefetchScalarGridSpec(
            num_scalar_prefetch=1,
            grid=(TILES,),
            in_specs=[
                whole(cot.shape), row_tile(HALF), row_tile(HALF), row_tile(D), row_tile(D),
                row_tile(128), row_tile(FF), row_tile(FF), whole((D, 2 * D)), whole(wu.shape),
                whole(vecs.shape),
            ],
            out_specs=[
                row_tile(D),
                row_tile(D),
                whole(part),
                whole(part),
            ],
            scratch_shapes=[
                pltpu.VMEM((ROWS, D), bf16),
                pltpu.VMEM((4, WIN, D), bf16),
                pltpu.VMEM((D, D), f32),
                pltpu.VMEM((4, WIN, D), f32),
                pltpu.VMEM((4, WIN, D), f32),
                pltpu.VMEM((128, D), f32),
                pltpu.VMEM((D, 128), f32),
                pltpu.VMEM((D, GRAD_COLS), bf16),
            ],
        ),
        out_shape=[struct(*o) for o in outs],
        compiler_params=PARAMS,
        cost_estimate=pl.CostEstimate(
            flops=100_000_000, bytes_accessed=1_000_000, transcendentals=0
        ),
    )(len_arr, cot, ctx0, ctx1, n1, n2, inv, slope, act, full, wu, vecs)


def column_of(row_ref):
    count = row_ref.shape[1]
    row = lax.broadcasted_iota(jnp.int32, (count, count), 0)
    col = lax.broadcasted_iota(jnp.int32, (count, count), 1)
    values = jnp.broadcast_to(row_ref[...].astype(f32), (count, count))
    return jnp.sum(jnp.where(row == col, values, 0.0), axis=1, keepdims=True)


def pack_kernel(odd_ref, *refs):
    bias_refs, (up_bias_ref, o_ref, down_ref, q_ref, k_ref, v_ref, up_ref, out_ref) = (
        refs[:8], refs[8:16],
    )
    low_s, high_s = refs[16:]
    rows = o_ref.shape[0]
    odd = odd_ref[0]
    shift = lax.broadcasted_iota(jnp.int32, (192, WIN), 1) - lax.broadcasted_iota(
        jnp.int32, (192, WIN), 0
    )
    move = jnp.where(shift == 64 * odd, 1.0, 0.0).astype(bf16)

    def padded(weight, column):
        lane = lax.broadcasted_iota(jnp.int32, (weight.shape[0], WIN), 1)
        moved = mm(weight, move, NN)
        return jnp.where(lane == 192 * (1 - odd), column, moved)

    columns = [column_of(ref) for ref in bias_refs]
    out_ref[:, :D] = o_ref[...]
    out_ref[:, D : 2 * D] = down_ref[...]
    sources = ((q_ref, columns[6]), (k_ref, jnp.zeros((rows, 1), f32)), (v_ref, columns[7]))
    for which, (ref, column) in enumerate(sources):
        start = 2 * D + WIN * which
        out_ref[:, start : start + WIN] = padded(ref[...], column).astype(bf16)
    up = padded(up_ref[...], column_of(up_bias_ref))
    low_s[...] = up[:, :128]
    high_s[...] = up[:, 128:]
    for j in range(4):
        for half, source in enumerate((low_s, high_s)):
            start = 3 * D + WIN * j + 128 * half
            out_ref[:, start : start + 128] = source[pl.ds(j, rows, stride=4), :].astype(bf16)
    lane = lax.broadcasted_iota(jnp.int32, (rows, 128), 1)
    small = jnp.zeros((rows, 128), f32)
    for index, column in enumerate(columns[:6]):
        small = jnp.where(lane == index, column, small)
    out_ref[:, 3 * D + 4 * WIN :] = small.astype(bf16)


def pack(odd, biases, up_bias, o_weight, down_weight, in_weights, up_weight):
    rows = o_weight.shape[0]
    cols = 3 * D + 4 * WIN + 128
    arrays = [bias[None, :] for bias in (*biases, up_bias)]
    arrays += [o_weight, down_weight, *in_weights, up_weight]
    return pl.pallas_call(
        pack_kernel,
        name="pack",
        grid_spec=pltpu.PrefetchScalarGridSpec(
            num_scalar_prefetch=1,
            grid=(1,),
            in_specs=[whole(array.shape) for array in arrays],
            out_specs=[kept((rows, cols))],
            scratch_shapes=[pltpu.VMEM((4 * rows, 128), f32)] * 2,
        ),
        out_shape=[struct((rows, cols), bf16)],
        compiler_params=PARAMS,
        cost_estimate=pl.CostEstimate(flops=0, bytes_accessed=400_000, transcendentals=0),
    )(odd.astype(jnp.int32).reshape(1), *arrays)[0]


def source_of(len_ref, perm_ref, place):
    first = perm_ref[place - place % 2]
    second = perm_ref[place - place % 2 + 1]
    swapped = (len_ref[first] < len_ref[second]).astype(jnp.int32)
    return jnp.where(swapped == place % 2, first, second)


def deal_kernel(len_ref, perm_ref, rows_ref, *out_refs):
    count = out_refs[0].shape[0]
    start = pl.program_id(0) * count

    def one(index, carry):
        source = source_of(len_ref, perm_ref, start + index)
        lane = 0
        for out_ref in out_refs:
            width = out_ref.shape[2]
            out_ref[index] = rows_ref[source, :, lane : lane + width]
            lane += width
        return carry

    lax.fori_loop(0, count, one, 0)


def deal(rows, lengths, permutation, parts):
    total, size, width = rows.shape
    count = total // STEPS
    return pl.pallas_call(
        deal_kernel,
        name="deal",
        grid_spec=pltpu.PrefetchScalarGridSpec(
            num_scalar_prefetch=2,
            grid=(STEPS,),
            in_specs=[whole(rows.shape)],
            out_specs=[pl.BlockSpec((count, size, width // parts), lambda i, *_: (i, 0, 0))] * parts,
        ),
        out_shape=[struct((total, size, width // parts), rows.dtype)] * parts,
        compiler_params=PARAMS,
        cost_estimate=pl.CostEstimate(flops=0, bytes_accessed=8_000_000, transcendentals=0),
    )(lengths, permutation, rows)


def restore_kernel(len_ref, perm_ref, *refs):
    part_refs, out_ref, place_s = refs[:-2], refs[-2], refs[-1]
    count = out_ref.shape[0]
    start = pl.program_id(0) * count

    @pl.when(pl.program_id(0) == 0)
    def _():
        def note(index, carry):
            place_s[source_of(len_ref, perm_ref, index)] = index
            return carry

        lax.fori_loop(0, part_refs[0].shape[0], note, 0)

    def one(index, carry):
        place = place_s[start + index]
        lane = 0
        for ref in part_refs:
            width = ref.shape[2]
            out_ref[index, :, lane : lane + width] = ref[place]
            lane += width
        return carry

    lax.fori_loop(0, count, one, 0)


def restore(parts, lengths, permutation):
    total, size, _ = parts[0].shape
    width = sum(part.shape[2] for part in parts)
    count = total // STEPS
    return pl.pallas_call(
        restore_kernel,
        name="restore",
        grid_spec=pltpu.PrefetchScalarGridSpec(
            num_scalar_prefetch=2,
            grid=(STEPS,),
            in_specs=[whole(part.shape) for part in parts],
            out_specs=[pl.BlockSpec((count, size, width), lambda i, *_: (i, 0, 0))],
            scratch_shapes=[pltpu.SMEM((total,), jnp.int32)],
        ),
        out_shape=[struct((total, size, width), bf16)],
        compiler_params=PARAMS,
        cost_estimate=pl.CostEstimate(flops=0, bytes_accessed=8_000_000, transcendentals=0),
    )(lengths, permutation, *parts)[0]


def pick(values, index):
    return values.at[index].get(mode="promise_in_bounds")


def tie(*values):
    return lax.optimization_barrier(values)


def on_device(
    tokens, cotangent, lengths, permutation, q_weight, q_bias, k_weight, v_weight, v_bias, o_weight,
    o_bias, norm1_gain, norm1_bias, up_weight, up_bias, down_weight, down_bias, norm2_gain,
    norm2_bias,
):
    devices = lax.axis_size(AXES)
    my_index = lax.axis_index(AXES)
    seq_total, piece_len, _ = tokens.shape
    seq_dev = seq_total // devices
    rows_dev = q_weight.shape[0]
    up_dev = up_weight.shape[0]
    odd = (my_index // (devices // 4)) % 2 == 1

    def padded(weight, bias):
        column = bias[:, None]
        gap = jnp.zeros((weight.shape[0], 63), bf16)
        return jnp.where(
            odd,
            jnp.concatenate([column, gap, weight], axis=1),
            jnp.concatenate([weight, column, gap], axis=1),
        )

    if rows_dev % 8 == 0:
        packed = pack(
            odd,
            [o_bias, norm1_gain, norm1_bias, down_bias, norm2_gain, norm2_bias, q_bias, v_bias],
            up_bias, o_weight, down_weight, [q_weight, k_weight, v_weight], up_weight,
        )
    else:
        small = [o_bias, norm1_gain, norm1_bias, down_bias, norm2_gain, norm2_bias]
        packed = jnp.concatenate(
            [
                o_weight,
                down_weight,
                padded(q_weight, q_bias),
                padded(k_weight, jnp.zeros_like(q_bias)),
                padded(v_weight, v_bias),
                padded(up_weight, up_bias).reshape(rows_dev, 4 * WIN),
                jnp.pad(jnp.stack(small, axis=1), ((0, 0), (0, 122))),
            ],
            axis=1,
        )
    gathered = lax.all_gather(packed, "fsdp", axis=0, tiled=True)

    dealt_lengths = pick(lengths, permutation).reshape(devices, seq_dev)
    swap = dealt_lengths[:, 0] < dealt_lengths[:, 1]
    my_swap = lax.dynamic_index_in_dim(swap, my_index, 0, False)
    chunks = lax.axis_size("dp")
    parity = lax.axis_index("dp") % 2
    pairing = [(i, i ^ 1) for i in range(chunks)]
    len_arr = jnp.stack(
        [jnp.max(lax.dynamic_slice_in_dim(dealt_lengths, my_index, 1, 0)), parity]
    ).astype(jnp.int32)

    def swap_blocks(rows):
        return lax.all_to_all(rows, AXES, split_axis=0, concat_axis=0, tiled=True)

    def arrive(rows):
        width = rows.shape[-1]
        moved = swap_blocks(rows.reshape(devices, seq_dev, piece_len, width))
        if piece_len == BLOCK:
            return moved
        moved = moved.transpose(1, 0, 2, 3).reshape(seq_dev, SEQ // BLOCK, BLOCK, width)
        return moved.transpose(1, 0, 2, 3)

    def leave(rows):
        width = rows.shape[-1]
        if piece_len != BLOCK:
            rows = rows.transpose(1, 0, 2, 3).reshape(seq_dev, devices, piece_len, width)
            rows = rows.transpose(1, 0, 2, 3)
        return swap_blocks(rows).reshape(seq_total, piece_len, width)

    def send_pair(partial, axis):
        count = lax.axis_size(axis)
        parity = lax.axis_index(axis) % 2
        blocks = partial.reshape(count // 2, 2, partial.shape[0] // count, partial.shape[1])
        kept_part, given = (
            lax.dynamic_slice_in_dim(blocks, which, 1, 1) for which in (parity, 1 - parity)
        )
        return [kept_part, lax.ppermute(given, axis, [(i, i ^ 1) for i in range(count)])]

    def send_rest(partial, axis):
        count = lax.axis_size(axis)
        half = count // 2
        place = lax.axis_index(axis) // 2
        size = partial.shape[0] // half
        block_of = lambda index: lax.dynamic_slice_in_dim(partial, index * size, size, 0)
        parts = [block_of(place)]
        for shift in range(1, half):
            target = [(i, (i + 2 * shift) % count) for i in range(count)]
            parts.append(lax.ppermute(block_of((place + shift) % half), axis, target))
        return parts

    def total(parts):
        result = sum(part.astype(f32) for part in parts)
        return result.reshape(-1, result.shape[-1])

    def total_low(parts):
        return total(parts).astype(bf16)

    tok0, tok1 = deal(tokens, lengths, permutation, 2)
    tok0 = arrive(tok0)
    gathered, tok0 = tie(gathered, tok0)
    full = lax.all_gather(gathered, "dp", axis=0, tiled=True)
    tok1 = arrive(tok1)
    dealt_cot, tok0, tok1 = tie(deal(cotangent, lengths, permutation, 1)[0], tok0, tok1)
    cot = arrive(dealt_cot)

    x0, qa0, ka0, va0, ctx0 = attn_fwd(len_arr, tok0, full, 0)
    x1, qa1, ka1, va1, ctx1 = attn_fwd(len_arr, tok1, full, 1)
    wu = full[:, 3 * D : 3 * D + 4 * WIN].reshape(FF, WIN)
    vecs = jnp.pad(full[:, 3 * D + 4 * WIN : 3 * D + 4 * WIN + 6].astype(f32).T, ((0, 2), (0, 0)))
    out, n1, n2, inv, slope, act, stat = mid_fwd(len_arr, x0, x1, ctx0, ctx1, full, wu, vecs)
    cot, out = tie(cot, out)
    back_out = leave(out)
    gctx, base, mine, given = mid_bwd(
        len_arr, cot, ctx0, ctx1, n1, n2, inv, slope, act, full, wu, vecs, chunks
    )
    mine = total_low([mine, lax.ppermute(given, "dp", pairing)])
    gctx, mine = tie(gctx, mine)
    parts = send_rest(mine, "dp")
    ig0, dw0, given0 = attn_bwd(
        len_arr, qa0, ka0, va0, ctx0, gctx, x0, base, full, 0, chunks
    )
    ig0, dw0, given0, gctx, back_out, *parts = tie(ig0, dw0, given0, gctx, back_out, *parts)
    back0 = leave(ig0)
    given0 = lax.ppermute(given0, "dp", pairing)
    parts = send_pair(total_low(parts), "fsdp")
    ig1, dw1, given1 = attn_bwd(
        len_arr, qa1, ka1, va1, ctx1, gctx, x1, base, full, 1, chunks
    )
    ig1, dw0, dw1, given0, given1, back0, *parts = tie(
        ig1, dw0, dw1, given0, given1, back0, *parts
    )
    back1 = leave(ig1)
    mine = total(send_rest(total_low(parts), "fsdp"))
    given1 = lax.ppermute(given1, "dp", pairing)
    mine_in = jnp.concatenate([total_low([dw0, given0]), total_low([dw1, given1])], axis=0)
    parts = send_pair(total_low(send_rest(mine_in, "dp")), "fsdp")
    mine_in = total(send_rest(total_low(parts), "fsdp"))

    back_out, stat, mine = tie(back_out, stat, mine)
    output = restore([back_out], lengths, permutation)
    input_grad = restore([back0, back1], lengths, permutation)
    lens = jnp.stack([len_arr[0], ROWS - len_arr[0]]).astype(f32)
    sums = jnp.stack([stat[4:8, 0], stat[0:4, 0] - stat[4:8, 0]], axis=1)
    rms = jnp.sqrt(sums / (lens[None, :] * D) + rms_eps)
    stream_rms = jnp.where(my_swap, rms[:, ::-1], rms)
    vec = lambda i: mine[:, 2 * D + 4 * WIN + i]

    def unpadded(block):
        return (
            jnp.where(odd, block[:, 64:], block[:, :192]),
            jnp.where(odd, block[:, 0], block[:, 192]),
        )

    dq, dqb = unpadded(mine_in[:, :WIN])
    dk, _ = unpadded(mine_in[:, WIN : 2 * WIN])
    dv, dvb = unpadded(mine_in[:, 2 * WIN :])
    dup, dub = unpadded(mine[:, 2 * D : 2 * D + 4 * WIN].reshape(up_dev, WIN))
    return (
        output, input_grad, dq, dqb, dk, dv, dvb, mine[:, :D], vec(0), vec(1), vec(2), dup, dub,
        mine[:, D : 2 * D], vec(3), vec(4), vec(5), stream_rms,
    )


def solution(mesh):
    rows = P(None, AXES, None)
    mat = P(AXES, None)
    vec = P(AXES)
    in_specs = (
        rows, rows, P(), P(), mat, vec, mat, mat, vec, mat, vec, vec, vec, mat, vec, mat, vec, vec,
        vec,
    )
    out_specs = (
        rows, rows, mat, vec, mat, mat, vec, mat, vec, vec, vec, mat, vec, mat, vec, vec, vec,
        P(None, AXES),
    )
    return jax.shard_map(
        on_device, mesh=mesh, in_specs=in_specs, out_specs=out_specs, check_vma=False
    )
```

```python
import functools

import jax
import jax.numpy as jnp
from jax import lax
from jax.experimental import pallas as pl
from jax.experimental.pallas import tpu as pltpu
from jax.sharding import PartitionSpec as P

AXES = ("dp", "fsdp")
D = 768
FF = 3072
HALF = D // 2
HEAD = 64
WIN = 256
SEQ = 1024
SHORT = 64
BLOCK = 32
ROWS = SEQ + SHORT
TILE = 272
TILES = ROWS // TILE
BIG = 1e30
STEPS = 4

norm_eps = 1e-12
rms_eps = 1e-06
bf16 = jnp.bfloat16
f32 = jnp.float32

NN = (((1,), (0,)), ((), ()))
NT = (((1,), (1,)), ((), ()))
TN = (((0,), (0,)), ((), ()))


def mm(left, right, dims):
    return lax.dot_general(left, right, dims, preferred_element_type=f32)


def exchange():
    row = lax.broadcasted_iota(jnp.int32, (WIN, WIN), 0)
    col = lax.broadcasted_iota(jnp.int32, (WIN, WIN), 1)
    return jnp.where(row + col == WIN - 1, 1.0, 0.0).astype(bf16)


def row_ids(start, count, width):
    return start + lax.broadcasted_iota(jnp.int32, (count, width), 0)


def block_rows(ref, seq, start, count):
    values = ref[start // BLOCK : (start + count) // BLOCK, seq]
    return values.reshape(count, values.shape[-1])


def merge_rows(pair_ref, packed_ref, first_len):
    width = packed_ref.shape[1]
    flip = exchange()
    packed_ref[0:SHORT, :] = block_rows(pair_ref, 0, 0, SHORT)
    for step in range(SEQ // WIN):
        start = SHORT + WIN * step
        flipped = mm(flip, block_rows(pair_ref, 1, SEQ - WIN * (step + 1), WIN), NN)
        inside = min(WIN, SEQ - start)
        own = block_rows(pair_ref, 0, start, inside).astype(f32)
        keep = row_ids(start, inside, width) < first_len
        packed_ref[start : start + inside, :] = jnp.where(keep, own, flipped[0:inside]).astype(bf16)
        if inside < WIN:
            packed_ref[start + inside : start + WIN, :] = flipped[inside:].astype(bf16)


def unmerge_rows(packed_ref, pair_ref, first_len):
    width = packed_ref.shape[1]
    flip = exchange()
    blocks = WIN // BLOCK
    for step in range(SEQ // WIN):
        start = WIN * step
        ids = row_ids(start, WIN, width)
        own = packed_ref[start : start + WIN, :].astype(f32)
        own = jnp.where(ids < first_len, own, 0.0).astype(bf16)
        pair_ref[blocks * step : blocks * (step + 1), 0] = own.reshape(blocks, BLOCK, width)
        source = ROWS - WIN * (step + 1)
        flipped = mm(flip, packed_ref[source : source + WIN, :], NN)
        flipped = jnp.where(ids < ROWS - first_len, flipped, 0.0).astype(bf16)
        pair_ref[blocks * step : blocks * (step + 1), 1] = flipped.reshape(blocks, BLOCK, width)


def spare_of(group):
    return 192 if group % 2 == 0 else 0


def with_ones(window, group):
    lane = lax.broadcasted_iota(jnp.int32, window.shape, 1)
    return jnp.where(lane == spare_of(group), 1.0, window.astype(f32)).astype(bf16)


def without_bias(window, group):
    lane = lax.broadcasted_iota(jnp.int32, window.shape, 1)
    return jnp.where(lane == spare_of(group), 0.0, window.astype(f32)).astype(bf16)


def first_row(group):
    return 0 if group % 2 == 0 else 64


def windows(values, count):
    parts = []
    for group in range(count):
        start = (group // 2) * HALF + (group % 2) * 128
        parts.append(values[:, start : start + WIN])
    return parts


def join(parts):
    pieces = []
    for first, second in zip(parts[0::2], parts[1::2]):
        pieces += [first[:, :128], first[:, 128:] + second[:, :128], second[:, 128:]]
    return jnp.concatenate(pieces, axis=1)


def split_three(value):
    high = value.astype(bf16)
    rest = value - high.astype(f32)
    mid = rest.astype(bf16)
    low = (rest - mid.astype(f32)).astype(bf16)
    return high, mid, low


def attn_fwd_kernel(
    len_ref, tok_ref, full_ref, x_ref, qa_ref, ka_ref, va_ref, ctx_ref, q_s, k_s, v_s, w_s
):
    pair = pl.program_id(0)
    first_len = len_ref[0]

    @pl.when(pair == 0)
    def _():
        merge_rows(tok_ref, x_ref, first_len)
        w_s[...] = jnp.zeros_like(w_s)
        for which in range(3):
            for g in range(2):
                w_s[which, g, first_row(g) : first_row(g) + 192, :] = full_ref[
                    192 * g : 192 * (g + 1), WIN * which : WIN * (which + 1)
                ]
        cols = [with_ones(part, g) for g, part in enumerate(windows(x_ref[...], 2))]
        for which, target in enumerate((q_s, k_s, v_s)):
            value = join([mm(cols[g], w_s[which, g], NT) for g in range(2)])
            if which == 0:
                value = value.astype(bf16).astype(f32) * (HEAD**-0.5)
            target[...] = value.astype(bf16)

    lane0 = pl.multiple_of(pair * 128, 128)
    q_pair = q_s[:, pl.ds(lane0, 128)]
    k_pair = k_s[:, pl.ds(lane0, 128)]
    v_pair = v_s[:, pl.ds(lane0, 128)]
    lane = lax.broadcasted_iota(jnp.int32, (ROWS, 128), 1)
    in_first = row_ids(0, ROWS, 128) < first_len
    one = jnp.ones((ROWS, 128), f32)
    zero = jnp.zeros((ROWS, 128), f32)
    for head in range(2):
        spare = 64 * (1 - head)
        own = (lane // 64) == head
        first_one = jnp.where(in_first, one, zero)
        q_extra = jnp.where(
            lane == spare, first_one, jnp.where(lane == spare + 1, one - first_one, zero)
        )
        k_extra = jnp.where(
            lane == spare,
            (first_one - one) * BIG,
            jnp.where(
                lane == spare + 1,
                first_one * (-BIG),
                jnp.where((lane >= spare + 2) & (lane < spare + 5), one, zero),
            ),
        )
        v_extra = jnp.where((lane >= spare) & (lane < spare + 3), one, zero)
        cols = slice(128 * head, 128 * (head + 1))
        qa_ref[:, cols] = jnp.where(own, q_pair.astype(f32), q_extra).astype(bf16)
        ka_ref[:, cols] = jnp.where(own, k_pair.astype(f32), k_extra).astype(bf16)
        va_ref[:, cols] = jnp.where(own, v_pair.astype(f32), v_extra).astype(bf16)

    tile_lane = lax.broadcasted_iota(jnp.int32, (TILE, 128), 1)

    def one_tile(index, carry):
        start = pl.multiple_of(index * TILE, 16)
        rows = pl.ds(start, TILE)
        result = None
        for head in range(2):
            cols = slice(128 * head, 128 * (head + 1))
            spare = 64 * (1 - head)
            q_tile = qa_ref[rows, cols]
            scores = mm(q_tile, ka_ref[:, cols], NT)
            top = jnp.max(scores, axis=1, keepdims=True)
            weights = jnp.exp(scores - top)
            mixed = mm(weights.astype(bf16), va_ref[:, cols], NN)
            total = mixed[:, spare : spare + 1]
            mixed = mixed / total
            log_total = top + jnp.log(total)
            high, mid, low = split_three(-log_total)
            q_new = jnp.where(
                tile_lane == spare + 2,
                high.astype(f32),
                jnp.where(
                    tile_lane == spare + 3,
                    mid.astype(f32),
                    jnp.where(tile_lane == spare + 4, low.astype(f32), q_tile.astype(f32)),
                ),
            )
            qa_ref[rows, cols] = q_new.astype(bf16)
            result = mixed if head == 0 else jnp.where(tile_lane < 64, result, mixed)
        ctx_ref[rows, :] = result.astype(bf16)
        return carry

    lax.fori_loop(0, TILES, one_tile, 0)


def attn_bwd_kernel(
    len_ref, qa_ref, ka_ref, va_ref, ctx_ref, gctx_ref, x_ref, base_ref, full_ref,
    ig_ref, kept_ref, given_ref, dq_s, dk_s, dv_s, do_s, dqt_s, ig_s, w_s, dw_ref,
):
    pair = pl.program_id(0)
    lane0 = pl.multiple_of(pair * 128, 128)
    lane = lax.broadcasted_iota(jnp.int32, (ROWS, 128), 1)
    grad = gctx_ref[...].astype(f32)
    product = grad * ctx_ref[...].astype(f32)
    for head in range(2):
        own = (lane // 64) == head
        spare = 64 * (1 - head)
        inner = -jnp.sum(jnp.where(own, product, 0.0), axis=1, keepdims=True)
        high, mid, low = split_three(inner)
        extra = jnp.where(
            lane == spare,
            high.astype(f32),
            jnp.where(
                lane == spare + 1,
                mid.astype(f32),
                jnp.where(lane == spare + 2, low.astype(f32), 0.0),
            ),
        )
        do_s[:, 128 * head : 128 * (head + 1)] = jnp.where(own, grad, extra).astype(bf16)
    dqt_s[...] = jnp.zeros_like(dqt_s)
    tile_lane = lax.broadcasted_iota(jnp.int32, (TILE, 128), 1)

    def one_tile(index, carry):
        start = pl.multiple_of(index * TILE, 16)
        rows = pl.ds(start, TILE)
        dk_tile = None
        dv_tile = None
        for head in range(2):
            cols = slice(128 * head, 128 * (head + 1))
            k_tile = ka_ref[rows, cols]
            probs = jnp.exp(mm(k_tile, qa_ref[:, cols], NT))
            scaled = mm(va_ref[rows, cols], do_s[:, cols], NT) * probs
            grad_scores = scaled.astype(bf16)
            dv_new = mm(probs.astype(bf16), do_s[:, cols], NN)
            dk_new = mm(grad_scores, qa_ref[:, cols], NN)
            dq_new = mm(k_tile, grad_scores, TN)
            dqt_s[64 * head : 64 * (head + 1), :] += dq_new[64 * head : 64 * (head + 1), :]
            dk_tile = dk_new if head == 0 else jnp.where(tile_lane < 64, dk_tile, dk_new)
            dv_tile = dv_new if head == 0 else jnp.where(tile_lane < 64, dv_tile, dv_new)
        dk_s[rows, pl.ds(lane0, 128)] = dk_tile.astype(bf16)
        dv_s[rows, pl.ds(lane0, 128)] = dv_tile.astype(bf16)
        return carry

    lax.fori_loop(0, TILES, one_tile, 0)
    dq_s[:, pl.ds(lane0, 128)] = (jnp.transpose(dqt_s[...]) * (HEAD**-0.5)).astype(bf16)

    @pl.when(pair == pl.num_programs(0) - 1)
    def _():
        x_cols = [with_ones(part, g) for g, part in enumerate(windows(x_ref[...], 2))]
        total = [None, None]
        for which, source in enumerate((dq_s, dk_s, dv_s)):
            cols = windows(source[...], 2)
            for g in range(2):
                own = slice(first_row(g), first_row(g) + 192)
                w_s[own, :] = without_bias(
                    full_ref[192 * g : 192 * (g + 1), WIN * which : WIN * (which + 1)], g
                )
                if first_row(g) == 0:
                    w_s[192:, :] = jnp.zeros((64, WIN), bf16)
                else:
                    w_s[:64, :] = jnp.zeros((64, WIN), bf16)
                grad = mm(cols[g], x_cols[g], TN)
                dw_ref[192 * g : 192 * (g + 1), WIN * which : WIN * (which + 1)] = grad[own].astype(
                    bf16
                )
                part = mm(cols[g], w_s[...], NN)
                total[g] = part if which == 0 else total[g] + part
        ig_s[...] = (join(total) + base_ref[...]).astype(bf16)
        unmerge_rows(ig_s, ig_ref, len_ref[0])
        split_chunks(dw_ref, kept_ref, given_ref, len_ref[1])


def split_chunks(rows_ref, kept_ref, given_ref, parity):
    pairs, size, _ = kept_ref.shape
    for own in range(2):

        @pl.when(parity == own)
        def _():
            for pair in range(pairs):
                for which in range(2):
                    start = (2 * pair + which) * size
                    target = kept_ref if which == own else given_ref
                    target[pair] = rows_ref[start : start + size, :]


def norm(values):
    mean = jnp.mean(values, axis=1, keepdims=True)
    centered = values - mean
    var = jnp.mean(centered * centered, axis=1, keepdims=True)
    inv = lax.rsqrt(var + norm_eps)
    return centered * inv, inv


def norm_back(grad_n, n, inv):
    mean_g = jnp.mean(grad_n, axis=1, keepdims=True)
    mean_gn = jnp.mean(grad_n * n, axis=1, keepdims=True)
    return (grad_n - mean_g - n * mean_gn) * inv


def mid_fwd_kernel(
    len_ref, x0_ref, x1_ref, ctx0_ref, ctx1_ref, full_ref, wu_ref, vec_ref,
    out_ref, n1_ref, n2_ref, inv_ref, slope_ref, act_ref, stat_ref,
    out_s, wd_s, stat_s,
):
    step = pl.program_id(0)
    first_len = len_ref[0]

    @pl.when(step == 0)
    def _():
        stat_s[...] = jnp.zeros_like(stat_s)
        wd_s[...] = jnp.zeros_like(wd_s)
        for g in range(4):
            wd_s[g, first_row(g) : first_row(g) + 192, :] = full_ref[192 * g : 192 * (g + 1), D:]

    o_bias, gain1, shift1, down_bias, gain2, shift2 = (vec_ref[i : i + 1, :] for i in range(6))
    start = pl.multiple_of(step * TILE, 16)
    rows = pl.ds(start, TILE)
    keep = jnp.where(row_ids(start, TILE, D) < first_len, 1.0, 0.0)

    def note(slot, values):
        square = values * values
        stat_s[slot : slot + 1, :] += jnp.sum(square, axis=0, keepdims=True)
        stat_s[slot + 4 : slot + 5, :] += jnp.sum(square * keep, axis=0, keepdims=True)

    inputs = jnp.concatenate([x0_ref[...], x1_ref[...]], axis=1).astype(f32)
    context = jnp.concatenate([ctx0_ref[...], ctx1_ref[...]], axis=1)
    note(0, inputs)
    branch_attn = mm(context, full_ref[:, :D], NT) + o_bias
    note(1, branch_attn)
    n1, inv1 = norm(inputs + branch_attn)
    n1_ref[...] = n1
    first_norm = n1 * gain1 + shift1
    note(2, first_norm)
    low_cols = windows(first_norm.astype(bf16), 4)
    parts = []
    for g in range(4):
        cols = slice(D * g, D * (g + 1))
        up = mm(with_ones(low_cols[g], g), wu_ref[D * g : D * (g + 1), :], NT)
        gate = 0.5 * (1.0 + lax.erf(up * (2.0**-0.5)))
        slope_ref[:, cols] = gate + up * jnp.exp(up * up * -0.5) * 0.3989422804014327
        act = (up * gate).astype(bf16)
        act_ref[:, cols] = act
        parts.append(mm(act, wd_s[g], NT))
    branch_ffn = join(parts) + down_bias
    note(3, branch_ffn)
    n2, inv2 = norm(first_norm + branch_ffn)
    n2_ref[...] = n2
    lane = lax.broadcasted_iota(jnp.int32, (TILE, 128), 1)
    inv_ref[...] = jnp.where(lane < 64, inv1, inv2)
    out_s[rows, :] = (n2 * gain2 + shift2).astype(bf16)

    @pl.when(step == pl.num_programs(0) - 1)
    def _():
        unmerge_rows(out_s, out_ref, first_len)
        stat_ref[...] = jnp.broadcast_to(
            jnp.sum(stat_s[...], axis=1, keepdims=True), stat_ref.shape
        )


def mid_bwd_kernel(
    len_ref, cot_ref, ctx0_ref, ctx1_ref, n1_ref, n2_ref, inv_ref, slope_ref, act_ref,
    full_ref, wu_ref, vec_ref, gctx_ref, base_ref, kept_ref, given_ref,
    cot_s, wd_s, dwo_s, dwd_s, dwu_s, vec_s, turn_s, grad_ref,
):
    step = pl.program_id(0)

    @pl.when(step == 0)
    def _():
        merge_rows(cot_ref, cot_s, len_ref[0])
        for target in (dwo_s, dwd_s, dwu_s, vec_s, wd_s):
            target[...] = jnp.zeros_like(target)
        for g in range(4):
            wd_s[g, first_row(g) : first_row(g) + 192, :] = full_ref[192 * g : 192 * (g + 1), D:]

    gain1, shift1, gain2 = (vec_ref[i : i + 1, :] for i in (1, 2, 4))
    start = pl.multiple_of(step * TILE, 16)
    rows = pl.ds(start, TILE)

    def add_vec(slot, values):
        vec_s[slot : slot + 1, :] += jnp.sum(values, axis=0, keepdims=True)

    context = jnp.concatenate([ctx0_ref[...], ctx1_ref[...]], axis=1)
    n1 = n1_ref[...]
    n2 = n2_ref[...]
    inv1 = inv_ref[:, 0:1]
    inv2 = inv_ref[:, 64:65]
    low_cols = windows((n1 * gain1 + shift1).astype(bf16), 4)
    grad_out = cot_s[rows, :].astype(f32)
    add_vec(4, grad_out * n2)
    add_vec(5, grad_out)
    grad_sum2 = norm_back(grad_out * gain2, n2, inv2)
    grad_ffn = grad_sum2.astype(bf16)
    add_vec(3, grad_ffn.astype(f32))
    ffn_cols = windows(grad_ffn, 4)
    parts = []
    for g in range(4):
        cols = slice(D * g, D * (g + 1))
        dwd_s[g] += mm(ffn_cols[g], act_ref[:, cols], TN)
        grad_up = (mm(ffn_cols[g], wd_s[g], NN) * slope_ref[:, cols]).astype(bf16)
        dwu_s[g] += mm(with_ones(low_cols[g], g), grad_up, TN)
        parts.append(mm(grad_up, without_bias(wu_ref[D * g : D * (g + 1), :], g), NN))
    grad_first = join(parts) + grad_sum2
    add_vec(1, grad_first * n1)
    add_vec(2, grad_first)
    grad_sum1 = norm_back(grad_first * gain1, n1, inv1)
    base_ref[...] = grad_sum1
    grad_branch = grad_sum1.astype(bf16)
    add_vec(0, grad_branch.astype(f32))
    dwo_s[...] += mm(grad_branch, context, TN)
    gctx_ref[...] = mm(grad_branch, full_ref[:, :D], NN).astype(bf16)

    @pl.when(step == pl.num_programs(0) - 1)
    def _():
        grad_ref[:, :D] = dwo_s[...].astype(bf16)
        for g in range(4):
            own = slice(192 * g, 192 * (g + 1))
            grad_ref[own, D : 2 * D] = dwd_s[g, first_row(g) : first_row(g) + 192, :].astype(bf16)
            turned = jnp.transpose(dwu_s[g])
            for half in range(2):
                turn_s[...] = turned[:, 128 * half : 128 * (half + 1)]
                for j in range(4):
                    lane0 = 2 * D + WIN * j + 128 * half
                    grad_ref[own, lane0 : lane0 + 128] = turn_s[pl.ds(j, 192, stride=4), :].astype(
                        bf16
                    )
        grad_ref[:, 2 * D + 4 * WIN :] = jnp.transpose(vec_s[...]).astype(bf16)
        split_chunks(grad_ref, kept_ref, given_ref, len_ref[1])


def whole(shape):
    zeros = (0,) * len(shape)
    return pl.BlockSpec(shape, lambda i, *_: zeros, pipeline_mode=pl.Buffered(1))


def kept(shape):
    zeros = (0,) * len(shape)
    return pl.BlockSpec(shape, lambda i, *_: zeros)


def struct(shape, dtype):
    return jax.ShapeDtypeStruct(shape, dtype)


PARAMS = pltpu.CompilerParams(
    dimension_semantics=("arbitrary",), vmem_limit_bytes=63_000_000
)
GRAD_COLS = 2 * D + 4 * WIN + 128


def attn_fwd(len_arr, tok, full, half):
    pair_cols = lambda width: pl.BlockSpec((ROWS, width), lambda i, *_: (0, i))
    return pl.pallas_call(
        attn_fwd_kernel,
        name="attn_fwd",
        grid_spec=pltpu.PrefetchScalarGridSpec(
            num_scalar_prefetch=1,
            grid=(3,),
            in_specs=[
                pl.BlockSpec(
                    (SEQ // BLOCK, 2, BLOCK, HALF),
                    lambda i, *_: (0, 0, 0, half),
                    pipeline_mode=pl.Buffered(1),
                ),
                pl.BlockSpec((HALF, D), lambda i, *_: (half, 0), pipeline_mode=pl.Buffered(1)),
            ],
            out_specs=[
                kept((ROWS, HALF)), pair_cols(256), pair_cols(256), pair_cols(256), pair_cols(128),
            ],
            scratch_shapes=[pltpu.VMEM((ROWS, HALF), bf16)] * 3
            + [pltpu.VMEM((3, 2, WIN, WIN), bf16)],
        ),
        out_shape=[
            struct((ROWS, HALF), bf16), struct((ROWS, D), bf16), struct((ROWS, D), bf16),
            struct((ROWS, D), bf16), struct((ROWS, HALF), bf16),
        ],
        compiler_params=PARAMS,
        cost_estimate=pl.CostEstimate(
            flops=20_000_000_000, bytes_accessed=12_000_000, transcendentals=7_000_000
        ),
    )(len_arr, tok, full)


def attn_bwd(len_arr, qa, ka, va, ctx, gctx, x, base, full, half, chunks):
    part = (chunks // 4, D // chunks, D)
    pair_cols = lambda width, first: pl.BlockSpec((ROWS, width), lambda i, *_: (0, i + first))
    return pl.pallas_call(
        attn_bwd_kernel,
        name="attn_bwd",
        grid_spec=pltpu.PrefetchScalarGridSpec(
            num_scalar_prefetch=1,
            grid=(3,),
            in_specs=[
                pair_cols(256, 0), pair_cols(256, 0), pair_cols(256, 0), pair_cols(128, 0),
                pair_cols(128, 3 * half), whole(x.shape),
                pl.BlockSpec((ROWS, HALF), lambda i, *_: (0, half), pipeline_mode=pl.Buffered(1)),
                pl.BlockSpec((HALF, D), lambda i, *_: (half, 0), pipeline_mode=pl.Buffered(1)),
            ],
            out_specs=[kept((SEQ // BLOCK, 2, BLOCK, HALF)), kept(part), kept(part)],
            scratch_shapes=[
                pltpu.VMEM((ROWS, HALF), bf16),
                pltpu.VMEM((ROWS, HALF), bf16),
                pltpu.VMEM((ROWS, HALF), bf16),
                pltpu.VMEM((ROWS, 256), bf16),
                pltpu.VMEM((128, ROWS), f32),
                pltpu.VMEM((ROWS, HALF), bf16),
                pltpu.VMEM((WIN, WIN), bf16),
                pltpu.VMEM((HALF, D), bf16),
            ],
        ),
        out_shape=[
            struct((SEQ // BLOCK, 2, BLOCK, HALF), bf16), struct(part, bf16), struct(part, bf16),
        ],
        compiler_params=PARAMS,
        cost_estimate=pl.CostEstimate(
            flops=100_000_000, bytes_accessed=1_000_000, transcendentals=0
        ),
    )(len_arr, qa, ka, va, ctx, gctx, x, base, full)


def row_tile(width):
    return pl.BlockSpec((TILE, width), lambda i, *_: (i, 0))


def mid_fwd(len_arr, x0, x1, ctx0, ctx1, full, wu, vecs):
    outs = [
        ((SEQ // BLOCK, 2, BLOCK, D), bf16), ((ROWS, D), f32), ((ROWS, D), f32),
        ((ROWS, 128), f32), ((ROWS, FF), f32), ((ROWS, FF), bf16), ((8, 128), f32),
    ]
    return pl.pallas_call(
        mid_fwd_kernel,
        name="mid_fwd",
        grid_spec=pltpu.PrefetchScalarGridSpec(
            num_scalar_prefetch=1,
            grid=(TILES,),
            in_specs=[row_tile(HALF)] * 4
            + [whole((D, 2 * D)), whole(wu.shape), whole(vecs.shape)],
            out_specs=[
                kept(outs[0][0]), row_tile(D), row_tile(D), row_tile(128), row_tile(FF),
                row_tile(FF), kept((8, 128)),
            ],
            scratch_shapes=[
                pltpu.VMEM((ROWS, D), bf16),
                pltpu.VMEM((4, WIN, D), bf16),
                pltpu.VMEM((8, D), f32),
            ],
        ),
        out_shape=[struct(*o) for o in outs],
        compiler_params=PARAMS,
        cost_estimate=pl.CostEstimate(
            flops=15_000_000_000, bytes_accessed=36_000_000, transcendentals=7_000_000
        ),
    )(len_arr, x0, x1, ctx0, ctx1, full, wu, vecs)


def mid_bwd(len_arr, cot, ctx0, ctx1, n1, n2, inv, slope, act, full, wu, vecs, chunks):
    part = (chunks // 2, D // chunks, GRAD_COLS)
    outs = [((ROWS, D), bf16), ((ROWS, D), f32), (part, bf16), (part, bf16)]
    return pl.pallas_call(
        mid_bwd_kernel,
        name="mid_bwd",
        grid_spec=pltpu.PrefetchScalarGridSpec(
            num_scalar_prefetch=1,
            grid=(TILES,),
            in_specs=[
                whole(cot.shape), row_tile(HALF), row_tile(HALF), row_tile(D), row_tile(D),
                row_tile(128), row_tile(FF), row_tile(FF), whole((D, 2 * D)), whole(wu.shape),
                whole(vecs.shape),
            ],
            out_specs=[
                row_tile(D),
                row_tile(D),
                whole(part),
                whole(part),
            ],
            scratch_shapes=[
                pltpu.VMEM((ROWS, D), bf16),
                pltpu.VMEM((4, WIN, D), bf16),
                pltpu.VMEM((D, D), f32),
                pltpu.VMEM((4, WIN, D), f32),
                pltpu.VMEM((4, WIN, D), f32),
                pltpu.VMEM((128, D), f32),
                pltpu.VMEM((D, 128), f32),
                pltpu.VMEM((D, GRAD_COLS), bf16),
            ],
        ),
        out_shape=[struct(*o) for o in outs],
        compiler_params=PARAMS,
        cost_estimate=pl.CostEstimate(
            flops=100_000_000, bytes_accessed=1_000_000, transcendentals=0
        ),
    )(len_arr, cot, ctx0, ctx1, n1, n2, inv, slope, act, full, wu, vecs)


def column_of(row_ref):
    count = row_ref.shape[1]
    row = lax.broadcasted_iota(jnp.int32, (count, count), 0)
    col = lax.broadcasted_iota(jnp.int32, (count, count), 1)
    values = jnp.broadcast_to(row_ref[...].astype(f32), (count, count))
    return jnp.sum(jnp.where(row == col, values, 0.0), axis=1, keepdims=True)


def pack_kernel(odd_ref, *refs):
    bias_refs, (up_bias_ref, o_ref, down_ref, q_ref, k_ref, v_ref, up_ref) = refs[:8], refs[8:15]
    in_ref, out_ref, low_s, high_s = refs[15:]
    rows = o_ref.shape[0]
    odd = odd_ref[0]
    shift = lax.broadcasted_iota(jnp.int32, (192, WIN), 1) - lax.broadcasted_iota(
        jnp.int32, (192, WIN), 0
    )
    move = jnp.where(shift == 64 * odd, 1.0, 0.0).astype(bf16)

    def padded(weight, column):
        lane = lax.broadcasted_iota(jnp.int32, (weight.shape[0], WIN), 1)
        moved = mm(weight, move, NN)
        return jnp.where(lane == 192 * (1 - odd), column, moved)

    columns = [column_of(ref) for ref in bias_refs]
    out_ref[:, :D] = o_ref[...]
    out_ref[:, D : 2 * D] = down_ref[...]
    sources = ((q_ref, columns[6]), (k_ref, jnp.zeros((rows, 1), f32)), (v_ref, columns[7]))
    for which, (ref, column) in enumerate(sources):
        in_ref[:, WIN * which : WIN * (which + 1)] = padded(ref[...], column).astype(bf16)
    up = padded(up_ref[...], column_of(up_bias_ref))
    low_s[...] = up[:, :128]
    high_s[...] = up[:, 128:]
    for j in range(4):
        for half, source in enumerate((low_s, high_s)):
            start = 2 * D + WIN * j + 128 * half
            out_ref[:, start : start + 128] = source[pl.ds(j, rows, stride=4), :].astype(bf16)
    lane = lax.broadcasted_iota(jnp.int32, (rows, 128), 1)
    small = jnp.zeros((rows, 128), f32)
    for index, column in enumerate(columns[:6]):
        small = jnp.where(lane == index, column, small)
    out_ref[:, 2 * D + 4 * WIN :] = small.astype(bf16)


def pack(odd, biases, up_bias, o_weight, down_weight, in_weights, up_weight):
    rows = o_weight.shape[0]
    arrays = [bias[None, :] for bias in (*biases, up_bias)]
    arrays += [o_weight, down_weight, *in_weights, up_weight]
    return pl.pallas_call(
        pack_kernel,
        name="pack",
        grid_spec=pltpu.PrefetchScalarGridSpec(
            num_scalar_prefetch=1,
            grid=(1,),
            in_specs=[whole(array.shape) for array in arrays],
            out_specs=[kept((rows, D)), kept((rows, GRAD_COLS))],
            scratch_shapes=[pltpu.VMEM((4 * rows, 128), f32)] * 2,
        ),
        out_shape=[struct((rows, D), bf16), struct((rows, GRAD_COLS), bf16)],
        compiler_params=PARAMS,
        cost_estimate=pl.CostEstimate(flops=0, bytes_accessed=400_000, transcendentals=0),
    )(odd.astype(jnp.int32).reshape(1), *arrays)


def source_of(len_ref, perm_ref, place):
    first = perm_ref[place - place % 2]
    second = perm_ref[place - place % 2 + 1]
    swapped = (len_ref[first] < len_ref[second]).astype(jnp.int32)
    return jnp.where(swapped == place % 2, first, second)


def moved_rows(source_at, rows_refs, out_ref, buffer_ref, in_sems, out_sems):
    count = out_ref.shape[0] // STEPS

    def group(step):
        return pl.ds(step * count, count)

    for step in range(STEPS):

        def one(index, carry):
            place = step * count + index
            source = source_at(place)
            lane = 0
            for which, rows_ref in enumerate(rows_refs):
                width = rows_ref.shape[2]
                pltpu.make_async_copy(
                    rows_ref.at[source],
                    buffer_ref.at[place, :, pl.ds(lane, width)],
                    in_sems.at[step, which],
                ).start()
                lane += width
            return carry

        lax.fori_loop(0, count, one, 0)
    for step in range(STEPS):
        lane = 0
        for which, rows_ref in enumerate(rows_refs):
            width = rows_ref.shape[2]
            pltpu.make_async_copy(
                rows_ref.at[group(step)],
                buffer_ref.at[group(step), :, pl.ds(lane, width)],
                in_sems.at[step, which],
            ).wait()
            lane += width
        pltpu.make_async_copy(
            buffer_ref.at[group(step)], out_ref.at[group(step)], out_sems.at[step]
        ).start()
    for step in range(STEPS):
        pltpu.make_async_copy(
            buffer_ref.at[group(step)], out_ref.at[group(step)], out_sems.at[step]
        ).wait()


def moved_call(kernel, name, parts, lengths, permutation):
    total, size, _ = parts[0].shape
    shape = (total, size, sum(part.shape[2] for part in parts))
    return pl.pallas_call(
        kernel,
        name=name,
        grid_spec=pltpu.PrefetchScalarGridSpec(
            num_scalar_prefetch=2,
            grid=(1,),
            in_specs=[pl.BlockSpec(memory_space=pltpu.HBM)] * len(parts),
            out_specs=[pl.BlockSpec(memory_space=pltpu.HBM)],
            scratch_shapes=[
                pltpu.VMEM(shape, bf16),
                pltpu.SMEM((total,), jnp.int32),
                pltpu.SemaphoreType.DMA((STEPS, len(parts))),
                pltpu.SemaphoreType.DMA((STEPS,)),
            ],
        ),
        out_shape=[struct(shape, bf16)],
        compiler_params=PARAMS,
        cost_estimate=pl.CostEstimate(flops=0, bytes_accessed=100_000, transcendentals=0),
    )(lengths, permutation, *parts)[0]


def deal_kernel(len_ref, perm_ref, rows_ref, out_ref, buffer_ref, place_s, in_sems, out_sems):
    source_at = lambda place: source_of(len_ref, perm_ref, place)
    moved_rows(source_at, [rows_ref], out_ref, buffer_ref, in_sems, out_sems)


def deal(rows, lengths, permutation):
    return moved_call(deal_kernel, "deal", [rows], lengths, permutation)


def restore_kernel(len_ref, perm_ref, *refs):
    part_refs, (out_ref, buffer_ref, place_s, in_sems, out_sems) = refs[:-5], refs[-5:]

    def note(index, carry):
        place_s[source_of(len_ref, perm_ref, index)] = index
        return carry

    lax.fori_loop(0, out_ref.shape[0], note, 0)
    moved_rows(lambda place: place_s[place], part_refs, out_ref, buffer_ref, in_sems, out_sems)


def restore(parts, lengths, permutation):
    return moved_call(restore_kernel, "restore", parts, lengths, permutation)


def pick(values, index):
    return values.at[index].get(mode="promise_in_bounds")


def tie(*values):
    return lax.optimization_barrier(values)


def on_device(
    tokens, cotangent, lengths, permutation, q_weight, q_bias, k_weight, v_weight, v_bias, o_weight,
    o_bias, norm1_gain, norm1_bias, up_weight, up_bias, down_weight, down_bias, norm2_gain,
    norm2_bias,
):
    devices = lax.axis_size(AXES)
    my_index = lax.axis_index(AXES)
    seq_total, piece_len, _ = tokens.shape
    seq_dev = seq_total // devices
    rows_dev = q_weight.shape[0]
    up_dev = up_weight.shape[0]
    odd = (my_index // (devices // 4)) % 2 == 1

    def padded(weight, bias):
        column = bias[:, None]
        gap = jnp.zeros((weight.shape[0], 63), bf16)
        return jnp.where(
            odd,
            jnp.concatenate([column, gap, weight], axis=1),
            jnp.concatenate([weight, column, gap], axis=1),
        )

    if rows_dev % 8 == 0:
        packed_in, packed = pack(
            odd,
            [o_bias, norm1_gain, norm1_bias, down_bias, norm2_gain, norm2_bias, q_bias, v_bias],
            up_bias, o_weight, down_weight, [q_weight, k_weight, v_weight], up_weight,
        )
    else:
        small = [o_bias, norm1_gain, norm1_bias, down_bias, norm2_gain, norm2_bias]
        packed_in = jnp.concatenate(
            [
                padded(q_weight, q_bias),
                padded(k_weight, jnp.zeros_like(q_bias)),
                padded(v_weight, v_bias),
            ],
            axis=1,
        )
        packed = jnp.concatenate(
            [
                o_weight,
                down_weight,
                padded(up_weight, up_bias).reshape(rows_dev, 4 * WIN),
                jnp.pad(jnp.stack(small, axis=1), ((0, 0), (0, 122))),
            ],
            axis=1,
        )
    full_in = lax.all_gather(packed_in, AXES, axis=0, tiled=True)
    packed, full_in = tie(packed, full_in)
    full = lax.all_gather(packed, AXES, axis=0, tiled=True)

    dealt_lengths = pick(lengths, permutation).reshape(devices, seq_dev)
    chunks = lax.axis_size("dp")
    parity = lax.axis_index("dp") % 2
    pairing = [(i, i ^ 1) for i in range(chunks)]
    len_arr = jnp.stack(
        [jnp.max(lax.dynamic_slice_in_dim(dealt_lengths, my_index, 1, 0)), parity]
    ).astype(jnp.int32)

    def swap_blocks(rows):
        return lax.all_to_all(rows, AXES, split_axis=0, concat_axis=0, tiled=True)

    def arrive(rows):
        width = rows.shape[-1]
        moved = swap_blocks(rows.reshape(devices, seq_dev, piece_len, width))
        if piece_len == BLOCK:
            return moved
        moved = moved.transpose(1, 0, 2, 3).reshape(seq_dev, SEQ // BLOCK, BLOCK, width)
        return moved.transpose(1, 0, 2, 3)

    def leave(rows):
        width = rows.shape[-1]
        if piece_len != BLOCK:
            rows = rows.transpose(1, 0, 2, 3).reshape(seq_dev, devices, piece_len, width)
            rows = rows.transpose(1, 0, 2, 3)
        return swap_blocks(rows).reshape(seq_total, piece_len, width)

    def send_pair(partial, axis):
        count = lax.axis_size(axis)
        parity = lax.axis_index(axis) % 2
        blocks = partial.reshape(count // 2, 2, partial.shape[0] // count, partial.shape[1])
        kept_part, given = (
            lax.dynamic_slice_in_dim(blocks, which, 1, 1) for which in (parity, 1 - parity)
        )
        return [kept_part, lax.ppermute(given, axis, [(i, i ^ 1) for i in range(count)])]

    def send_rest(partial, axis):
        count = lax.axis_size(axis)
        half = count // 2
        place = lax.axis_index(axis) // 2
        size = partial.shape[0] // half
        block_of = lambda index: lax.dynamic_slice_in_dim(partial, index * size, size, 0)
        parts = [block_of(place)]
        for shift in range(1, half):
            target = [(i, (i + 2 * shift) % count) for i in range(count)]
            parts.append(lax.ppermute(block_of((place + shift) % half), axis, target))
        return parts

    def total(parts):
        result = sum(part.astype(f32) for part in parts)
        return result.reshape(-1, result.shape[-1])

    def total_low(parts):
        return total(parts).astype(bf16)

    tok = arrive(deal(tokens, lengths, permutation))
    dealt_cot, tok = tie(deal(cotangent, lengths, permutation), tok)
    cot = arrive(dealt_cot)

    x0, qa0, ka0, va0, ctx0 = attn_fwd(len_arr, tok, full_in, 0)
    x1, qa1, ka1, va1, ctx1 = attn_fwd(len_arr, tok, full_in, 1)
    wu = full[:, 2 * D : 2 * D + 4 * WIN].reshape(FF, WIN)
    vecs = jnp.pad(full[:, 2 * D + 4 * WIN : 2 * D + 4 * WIN + 6].astype(f32).T, ((0, 2), (0, 0)))
    out, n1, n2, inv, slope, act, stat = mid_fwd(len_arr, x0, x1, ctx0, ctx1, full, wu, vecs)
    cot, out = tie(cot, out)
    back_out = leave(out)
    gctx, base, mine, given = mid_bwd(
        len_arr, cot, ctx0, ctx1, n1, n2, inv, slope, act, full, wu, vecs, chunks
    )
    mine = total_low([mine, lax.ppermute(given, "dp", pairing)])
    gctx, mine = tie(gctx, mine)
    parts = send_rest(mine, "dp")
    ig0, dw0, given0 = attn_bwd(
        len_arr, qa0, ka0, va0, ctx0, gctx, x0, base, full_in, 0, chunks
    )
    ig0, dw0, given0, gctx, back_out, *parts = tie(ig0, dw0, given0, gctx, back_out, *parts)
    back0 = leave(ig0)
    given0 = lax.ppermute(given0, "dp", pairing)
    parts = send_pair(total_low(parts), "fsdp")
    ig1, dw1, given1 = attn_bwd(
        len_arr, qa1, ka1, va1, ctx1, gctx, x1, base, full_in, 1, chunks
    )
    ig1, dw0, dw1, given0, given1, back0, *parts = tie(
        ig1, dw0, dw1, given0, given1, back0, *parts
    )
    back1 = leave(ig1)
    given1 = lax.ppermute(given1, "dp", pairing)
    mine_in = jnp.concatenate([total_low([dw0, given0]), total_low([dw1, given1])], axis=0)
    mine_in = total_low(send_pair(total_low(send_rest(mine_in, "dp")), "fsdp"))
    mine = total(send_rest(jnp.concatenate([total_low(parts), mine_in], axis=1), "fsdp"))
    mine_in = mine[:, GRAD_COLS:]

    back_out, stat, dealt_lengths, mine = tie(back_out, stat, dealt_lengths, mine)
    swap = dealt_lengths[:, 0] < dealt_lengths[:, 1]
    my_swap = lax.dynamic_index_in_dim(swap, my_index, 0, False)
    output = restore([back_out], lengths, permutation)
    input_grad = restore([back0, back1], lengths, permutation)
    lens = jnp.stack([len_arr[0], ROWS - len_arr[0]]).astype(f32)
    sums = jnp.stack([stat[4:8, 0], stat[0:4, 0] - stat[4:8, 0]], axis=1)
    rms = jnp.sqrt(sums / (lens[None, :] * D) + rms_eps)
    stream_rms = jnp.where(my_swap, rms[:, ::-1], rms)
    vec = lambda i: mine[:, 2 * D + 4 * WIN + i]

    def unpadded(block):
        return (
            jnp.where(odd, block[:, 64:], block[:, :192]),
            jnp.where(odd, block[:, 0], block[:, 192]),
        )

    dq, dqb = unpadded(mine_in[:, :WIN])
    dk, _ = unpadded(mine_in[:, WIN : 2 * WIN])
    dv, dvb = unpadded(mine_in[:, 2 * WIN :])
    dup, dub = unpadded(mine[:, 2 * D : 2 * D + 4 * WIN].reshape(up_dev, WIN))
    return (
        output, input_grad, dq, dqb, dk, dv, dvb, mine[:, :D], vec(0), vec(1), vec(2), dup, dub,
        mine[:, D : 2 * D], vec(3), vec(4), vec(5), stream_rms,
    )


def solution(mesh):
    rows = P(None, AXES, None)
    mat = P(AXES, None)
    vec = P(AXES)
    in_specs = (
        rows, rows, P(), P(), mat, vec, mat, mat, vec, mat, vec, vec, vec, mat, vec, mat, vec, vec,
        vec,
    )
    out_specs = (
        rows, rows, mat, vec, mat, mat, vec, mat, vec, vec, vec, mat, vec, mat, vec, vec, vec,
        P(None, AXES),
    )
    return jax.shard_map(
        on_device, mesh=mesh, in_specs=in_specs, out_specs=out_specs, check_vma=False
    )
```

```python
import functools

import jax
import jax.numpy as jnp
from jax import lax
from jax.experimental import pallas as pl
from jax.experimental.pallas import tpu as pltpu
from jax.sharding import PartitionSpec as P

AXES = ("dp", "fsdp")
D = 768
FF = 3072
HALF = D // 2
HEAD = 64
WIN = 256
SEQ = 1024
SHORT = 64
BLOCK = 32
ROWS = SEQ + SHORT
TILE = 272
TILES = ROWS // TILE
BIG = 1e30
STEPS = 4
SPLIT = 1664

norm_eps = 1e-12
rms_eps = 1e-06
bf16 = jnp.bfloat16
f32 = jnp.float32

NN = (((1,), (0,)), ((), ()))
NT = (((1,), (1,)), ((), ()))
TN = (((0,), (0,)), ((), ()))


def mm(left, right, dims):
    return lax.dot_general(left, right, dims, preferred_element_type=f32)


def exchange():
    row = lax.broadcasted_iota(jnp.int32, (WIN, WIN), 0)
    col = lax.broadcasted_iota(jnp.int32, (WIN, WIN), 1)
    return jnp.where(row + col == WIN - 1, 1.0, 0.0).astype(bf16)


def row_ids(start, count, width):
    return start + lax.broadcasted_iota(jnp.int32, (count, width), 0)


def block_rows(ref, seq, start, count):
    values = ref[start // BLOCK : (start + count) // BLOCK, seq]
    return values.reshape(count, values.shape[-1])


def merge_rows(pair_ref, packed_ref, first_len):
    width = packed_ref.shape[1]
    flip = exchange()
    packed_ref[0:SHORT, :] = block_rows(pair_ref, 0, 0, SHORT)
    for step in range(SEQ // WIN):
        start = SHORT + WIN * step
        flipped = mm(flip, block_rows(pair_ref, 1, SEQ - WIN * (step + 1), WIN), NN)
        inside = min(WIN, SEQ - start)
        own = block_rows(pair_ref, 0, start, inside).astype(f32)
        keep = row_ids(start, inside, width) < first_len
        packed_ref[start : start + inside, :] = jnp.where(keep, own, flipped[0:inside]).astype(bf16)
        if inside < WIN:
            packed_ref[start + inside : start + WIN, :] = flipped[inside:].astype(bf16)


def unmerge_rows(packed_ref, pair_ref, first_len):
    width = packed_ref.shape[1]
    flip = exchange()
    blocks = WIN // BLOCK
    for step in range(SEQ // WIN):
        start = WIN * step
        ids = row_ids(start, WIN, width)
        own = packed_ref[start : start + WIN, :].astype(f32)
        own = jnp.where(ids < first_len, own, 0.0).astype(bf16)
        pair_ref[blocks * step : blocks * (step + 1), 0] = own.reshape(blocks, BLOCK, width)
        source = ROWS - WIN * (step + 1)
        flipped = mm(flip, packed_ref[source : source + WIN, :], NN)
        flipped = jnp.where(ids < ROWS - first_len, flipped, 0.0).astype(bf16)
        pair_ref[blocks * step : blocks * (step + 1), 1] = flipped.reshape(blocks, BLOCK, width)


def spare_of(group):
    return 192 if group % 2 == 0 else 0


def with_ones(window, group):
    lane = lax.broadcasted_iota(jnp.int32, window.shape, 1)
    return jnp.where(lane == spare_of(group), 1.0, window.astype(f32)).astype(bf16)


def without_bias(window, group):
    lane = lax.broadcasted_iota(jnp.int32, window.shape, 1)
    return jnp.where(lane == spare_of(group), 0.0, window.astype(f32)).astype(bf16)


def first_row(group):
    return 0 if group % 2 == 0 else 64


def windows(values, count):
    parts = []
    for group in range(count):
        start = (group // 2) * HALF + (group % 2) * 128
        parts.append(values[:, start : start + WIN])
    return parts


def join(parts):
    pieces = []
    for first, second in zip(parts[0::2], parts[1::2]):
        pieces += [first[:, :128], first[:, 128:] + second[:, :128], second[:, 128:]]
    return jnp.concatenate(pieces, axis=1)


def split_three(value):
    high = value.astype(bf16)
    rest = value - high.astype(f32)
    mid = rest.astype(bf16)
    low = (rest - mid.astype(f32)).astype(bf16)
    return high, mid, low


def attn_fwd_kernel(
    len_ref, tok_ref, full_ref, x_ref, qa_ref, ka_ref, va_ref, ctx_ref, q_s, k_s, v_s, w_s
):
    pair = pl.program_id(0)
    first_len = len_ref[0]

    @pl.when(pair == 0)
    def _():
        merge_rows(tok_ref, x_ref, first_len)
        w_s[...] = jnp.zeros_like(w_s)
        for which in range(3):
            for g in range(2):
                w_s[which, g, first_row(g) : first_row(g) + 192, :] = full_ref[
                    192 * g : 192 * (g + 1), WIN * which : WIN * (which + 1)
                ]
        cols = [with_ones(part, g) for g, part in enumerate(windows(x_ref[...], 2))]
        for which, target in enumerate((q_s, k_s, v_s)):
            value = join([mm(cols[g], w_s[which, g], NT) for g in range(2)])
            if which == 0:
                value = value.astype(bf16).astype(f32) * (HEAD**-0.5)
            target[...] = value.astype(bf16)

    lane0 = pl.multiple_of(pair * 128, 128)
    q_pair = q_s[:, pl.ds(lane0, 128)]
    k_pair = k_s[:, pl.ds(lane0, 128)]
    v_pair = v_s[:, pl.ds(lane0, 128)]
    lane = lax.broadcasted_iota(jnp.int32, (ROWS, 128), 1)
    in_first = row_ids(0, ROWS, 128) < first_len
    one = jnp.ones((ROWS, 128), f32)
    zero = jnp.zeros((ROWS, 128), f32)
    for head in range(2):
        spare = 64 * (1 - head)
        own = (lane // 64) == head
        first_one = jnp.where(in_first, one, zero)
        q_extra = jnp.where(
            lane == spare, first_one, jnp.where(lane == spare + 1, one - first_one, zero)
        )
        k_extra = jnp.where(
            lane == spare,
            (first_one - one) * BIG,
            jnp.where(
                lane == spare + 1,
                first_one * (-BIG),
                jnp.where((lane >= spare + 2) & (lane < spare + 5), one, zero),
            ),
        )
        v_extra = jnp.where((lane >= spare) & (lane < spare + 3), one, zero)
        cols = slice(128 * head, 128 * (head + 1))
        qa_ref[:, cols] = jnp.where(own, q_pair.astype(f32), q_extra).astype(bf16)
        ka_ref[:, cols] = jnp.where(own, k_pair.astype(f32), k_extra).astype(bf16)
        va_ref[:, cols] = jnp.where(own, v_pair.astype(f32), v_extra).astype(bf16)

    tile_lane = lax.broadcasted_iota(jnp.int32, (TILE, 128), 1)

    def one_tile(index, carry):
        start = pl.multiple_of(index * TILE, 16)
        rows = pl.ds(start, TILE)
        result = None
        for head in range(2):
            cols = slice(128 * head, 128 * (head + 1))
            spare = 64 * (1 - head)
            q_tile = qa_ref[rows, cols]
            scores = mm(q_tile, ka_ref[:, cols], NT)
            top = jnp.max(scores, axis=1, keepdims=True)
            weights = jnp.exp(scores - top)
            mixed = mm(weights.astype(bf16), va_ref[:, cols], NN)
            total = mixed[:, spare : spare + 1]
            mixed = mixed / total
            log_total = top + jnp.log(total)
            high, mid, low = split_three(-log_total)
            q_new = jnp.where(
                tile_lane == spare + 2,
                high.astype(f32),
                jnp.where(
                    tile_lane == spare + 3,
                    mid.astype(f32),
                    jnp.where(tile_lane == spare + 4, low.astype(f32), q_tile.astype(f32)),
                ),
            )
            qa_ref[rows, cols] = q_new.astype(bf16)
            result = mixed if head == 0 else jnp.where(tile_lane < 64, result, mixed)
        ctx_ref[rows, :] = result.astype(bf16)
        return carry

    lax.fori_loop(0, TILES, one_tile, 0)


def attn_bwd_kernel(
    len_ref, qa_ref, ka_ref, va_ref, ctx_ref, gctx_ref, x_ref, base_ref, full_ref,
    ig_ref, kept_ref, given_ref, dq_s, dk_s, dv_s, do_s, dqt_s, ig_s, w_s, dw_ref,
):
    pair = pl.program_id(0)
    lane0 = pl.multiple_of(pair * 128, 128)
    lane = lax.broadcasted_iota(jnp.int32, (ROWS, 128), 1)
    grad = gctx_ref[...].astype(f32)
    product = grad * ctx_ref[...].astype(f32)
    for head in range(2):
        own = (lane // 64) == head
        spare = 64 * (1 - head)
        inner = -jnp.sum(jnp.where(own, product, 0.0), axis=1, keepdims=True)
        high, mid, low = split_three(inner)
        extra = jnp.where(
            lane == spare,
            high.astype(f32),
            jnp.where(
                lane == spare + 1,
                mid.astype(f32),
                jnp.where(lane == spare + 2, low.astype(f32), 0.0),
            ),
        )
        do_s[:, 128 * head : 128 * (head + 1)] = jnp.where(own, grad, extra).astype(bf16)
    dqt_s[...] = jnp.zeros_like(dqt_s)
    tile_lane = lax.broadcasted_iota(jnp.int32, (TILE, 128), 1)

    def one_tile(index, carry):
        start = pl.multiple_of(index * TILE, 16)
        rows = pl.ds(start, TILE)
        dk_tile = None
        dv_tile = None
        for head in range(2):
            cols = slice(128 * head, 128 * (head + 1))
            k_tile = ka_ref[rows, cols]
            probs = jnp.exp(mm(k_tile, qa_ref[:, cols], NT))
            scaled = mm(va_ref[rows, cols], do_s[:, cols], NT) * probs
            grad_scores = scaled.astype(bf16)
            dv_new = mm(probs.astype(bf16), do_s[:, cols], NN)
            dk_new = mm(grad_scores, qa_ref[:, cols], NN)
            dq_new = mm(k_tile, grad_scores, TN)
            dqt_s[64 * head : 64 * (head + 1), :] += dq_new[64 * head : 64 * (head + 1), :]
            dk_tile = dk_new if head == 0 else jnp.where(tile_lane < 64, dk_tile, dk_new)
            dv_tile = dv_new if head == 0 else jnp.where(tile_lane < 64, dv_tile, dv_new)
        dk_s[rows, pl.ds(lane0, 128)] = dk_tile.astype(bf16)
        dv_s[rows, pl.ds(lane0, 128)] = dv_tile.astype(bf16)
        return carry

    lax.fori_loop(0, TILES, one_tile, 0)
    dq_s[:, pl.ds(lane0, 128)] = (jnp.transpose(dqt_s[...]) * (HEAD**-0.5)).astype(bf16)

    @pl.when(pair == pl.num_programs(0) - 1)
    def _():
        x_cols = [with_ones(part, g) for g, part in enumerate(windows(x_ref[...], 2))]
        total = [None, None]
        for which, source in enumerate((dq_s, dk_s, dv_s)):
            cols = windows(source[...], 2)
            for g in range(2):
                own = slice(first_row(g), first_row(g) + 192)
                w_s[own, :] = without_bias(
                    full_ref[192 * g : 192 * (g + 1), WIN * which : WIN * (which + 1)], g
                )
                if first_row(g) == 0:
                    w_s[192:, :] = jnp.zeros((64, WIN), bf16)
                else:
                    w_s[:64, :] = jnp.zeros((64, WIN), bf16)
                grad = mm(cols[g], x_cols[g], TN)
                dw_ref[192 * g : 192 * (g + 1), WIN * which : WIN * (which + 1)] = grad[own].astype(
                    bf16
                )
                part = mm(cols[g], w_s[...], NN)
                total[g] = part if which == 0 else total[g] + part
        ig_s[...] = (join(total) + base_ref[...]).astype(bf16)
        unmerge_rows(ig_s, ig_ref, len_ref[0])
        split_chunks(dw_ref, kept_ref, given_ref, len_ref[1])


def split_chunks(rows_ref, kept_ref, given_ref, parity):
    pairs, size, _ = kept_ref.shape
    for own in range(2):

        @pl.when(parity == own)
        def _():
            for pair in range(pairs):
                for which in range(2):
                    start = (2 * pair + which) * size
                    target = kept_ref if which == own else given_ref
                    target[pair] = rows_ref[start : start + size, :]


def norm(values):
    mean = jnp.mean(values, axis=1, keepdims=True)
    centered = values - mean
    var = jnp.mean(centered * centered, axis=1, keepdims=True)
    inv = lax.rsqrt(var + norm_eps)
    return centered * inv, inv


def norm_back(grad_n, n, inv):
    mean_g = jnp.mean(grad_n, axis=1, keepdims=True)
    mean_gn = jnp.mean(grad_n * n, axis=1, keepdims=True)
    return (grad_n - mean_g - n * mean_gn) * inv


def mid_fwd_kernel(
    len_ref, x0_ref, x1_ref, ctx0_ref, ctx1_ref, full_ref, wu_ref, vec_ref,
    out_ref, n1_ref, n2_ref, inv_ref, slope_ref, act_ref, stat_ref,
    out_s, wd_s, stat_s,
):
    step = pl.program_id(0)
    first_len = len_ref[0]

    @pl.when(step == 0)
    def _():
        stat_s[...] = jnp.zeros_like(stat_s)
        wd_s[...] = jnp.zeros_like(wd_s)
        for g in range(4):
            wd_s[g, first_row(g) : first_row(g) + 192, :] = full_ref[192 * g : 192 * (g + 1), D:]

    o_bias, gain1, shift1, down_bias, gain2, shift2 = (vec_ref[i : i + 1, :] for i in range(6))
    start = pl.multiple_of(step * TILE, 16)
    rows = pl.ds(start, TILE)
    keep = jnp.where(row_ids(start, TILE, D) < first_len, 1.0, 0.0)

    def note(slot, values):
        square = values * values
        stat_s[slot : slot + 1, :] += jnp.sum(square, axis=0, keepdims=True)
        stat_s[slot + 4 : slot + 5, :] += jnp.sum(square * keep, axis=0, keepdims=True)

    inputs = jnp.concatenate([x0_ref[...], x1_ref[...]], axis=1).astype(f32)
    context = jnp.concatenate([ctx0_ref[...], ctx1_ref[...]], axis=1)
    note(0, inputs)
    branch_attn = mm(context, full_ref[:, :D], NT) + o_bias
    note(1, branch_attn)
    n1, inv1 = norm(inputs + branch_attn)
    n1_ref[...] = n1
    first_norm = n1 * gain1 + shift1
    note(2, first_norm)
    low_cols = windows(first_norm.astype(bf16), 4)
    parts = []
    for g in range(4):
        cols = slice(D * g, D * (g + 1))
        up = mm(with_ones(low_cols[g], g), wu_ref[D * g : D * (g + 1), :], NT)
        gate = 0.5 * (1.0 + lax.erf(up * (2.0**-0.5)))
        slope_ref[:, cols] = gate + up * jnp.exp(up * up * -0.5) * 0.3989422804014327
        act = (up * gate).astype(bf16)
        act_ref[:, cols] = act
        parts.append(mm(act, wd_s[g], NT))
    branch_ffn = join(parts) + down_bias
    note(3, branch_ffn)
    n2, inv2 = norm(first_norm + branch_ffn)
    n2_ref[...] = n2
    lane = lax.broadcasted_iota(jnp.int32, (TILE, 128), 1)
    inv_ref[...] = jnp.where(lane < 64, inv1, inv2)
    out_s[rows, :] = (n2 * gain2 + shift2).astype(bf16)

    @pl.when(step == pl.num_programs(0) - 1)
    def _():
        unmerge_rows(out_s, out_ref, first_len)
        stat_ref[...] = jnp.broadcast_to(
            jnp.sum(stat_s[...], axis=1, keepdims=True), stat_ref.shape
        )


def mid_bwd_kernel(
    len_ref, cot_ref, ctx0_ref, ctx1_ref, n1_ref, n2_ref, inv_ref, slope_ref, act_ref,
    full_ref, wu_ref, vec_ref, gctx_ref, base_ref, kept_ref, given_ref,
    cot_s, wd_s, dwo_s, dwd_s, dwu_s, vec_s, turn_s, grad_ref,
):
    step = pl.program_id(0)

    @pl.when(step == 0)
    def _():
        merge_rows(cot_ref, cot_s, len_ref[0])
        for target in (dwo_s, dwd_s, dwu_s, vec_s, wd_s):
            target[...] = jnp.zeros_like(target)
        for g in range(4):
            wd_s[g, first_row(g) : first_row(g) + 192, :] = full_ref[192 * g : 192 * (g + 1), D:]

    gain1, shift1, gain2 = (vec_ref[i : i + 1, :] for i in (1, 2, 4))
    start = pl.multiple_of(step * TILE, 16)
    rows = pl.ds(start, TILE)

    def add_vec(slot, values):
        vec_s[slot : slot + 1, :] += jnp.sum(values, axis=0, keepdims=True)

    context = jnp.concatenate([ctx0_ref[...], ctx1_ref[...]], axis=1)
    n1 = n1_ref[...]
    n2 = n2_ref[...]
    inv1 = inv_ref[:, 0:1]
    inv2 = inv_ref[:, 64:65]
    low_cols = windows((n1 * gain1 + shift1).astype(bf16), 4)
    grad_out = cot_s[rows, :].astype(f32)
    add_vec(4, grad_out * n2)
    add_vec(5, grad_out)
    grad_sum2 = norm_back(grad_out * gain2, n2, inv2)
    grad_ffn = grad_sum2.astype(bf16)
    add_vec(3, grad_ffn.astype(f32))
    ffn_cols = windows(grad_ffn, 4)
    parts = []
    for g in range(4):
        cols = slice(D * g, D * (g + 1))
        dwd_s[g] += mm(ffn_cols[g], act_ref[:, cols], TN)
        grad_up = (mm(ffn_cols[g], wd_s[g], NN) * slope_ref[:, cols]).astype(bf16)
        dwu_s[g] += mm(with_ones(low_cols[g], g), grad_up, TN)
        parts.append(mm(grad_up, without_bias(wu_ref[D * g : D * (g + 1), :], g), NN))
    grad_first = join(parts) + grad_sum2
    add_vec(1, grad_first * n1)
    add_vec(2, grad_first)
    grad_sum1 = norm_back(grad_first * gain1, n1, inv1)
    base_ref[...] = grad_sum1
    grad_branch = grad_sum1.astype(bf16)
    add_vec(0, grad_branch.astype(f32))
    dwo_s[...] += mm(grad_branch, context, TN)
    gctx_ref[...] = mm(grad_branch, full_ref[:, :D], NN).astype(bf16)

    @pl.when(step == pl.num_programs(0) - 1)
    def _():
        grad_ref[:, :D] = dwo_s[...].astype(bf16)
        for g in range(4):
            own = slice(192 * g, 192 * (g + 1))
            grad_ref[own, D : 2 * D] = dwd_s[g, first_row(g) : first_row(g) + 192, :].astype(bf16)
            turned = jnp.transpose(dwu_s[g])
            for half in range(2):
                turn_s[...] = turned[:, 128 * half : 128 * (half + 1)]
                for j in range(4):
                    lane0 = 2 * D + WIN * j + 128 * half
                    grad_ref[own, lane0 : lane0 + 128] = turn_s[pl.ds(j, 192, stride=4), :].astype(
                        bf16
                    )
        grad_ref[:, 2 * D + 4 * WIN :] = jnp.transpose(vec_s[...]).astype(bf16)
        split_chunks(grad_ref, kept_ref, given_ref, len_ref[1])


def whole(shape):
    zeros = (0,) * len(shape)
    return pl.BlockSpec(shape, lambda i, *_: zeros, pipeline_mode=pl.Buffered(1))


def kept(shape):
    zeros = (0,) * len(shape)
    return pl.BlockSpec(shape, lambda i, *_: zeros)


def struct(shape, dtype):
    return jax.ShapeDtypeStruct(shape, dtype)


PARAMS = pltpu.CompilerParams(
    dimension_semantics=("arbitrary",), vmem_limit_bytes=63_000_000
)
GRAD_COLS = 2 * D + 4 * WIN + 128
ALL_COLS = GRAD_COLS + D


def attn_fwd(len_arr, tok, full, half):
    pair_cols = lambda width: pl.BlockSpec((ROWS, width), lambda i, *_: (0, i))
    return pl.pallas_call(
        attn_fwd_kernel,
        name="attn_fwd",
        grid_spec=pltpu.PrefetchScalarGridSpec(
            num_scalar_prefetch=1,
            grid=(3,),
            in_specs=[
                pl.BlockSpec(
                    (SEQ // BLOCK, 2, BLOCK, HALF),
                    lambda i, *_: (0, 0, 0, half),
                    pipeline_mode=pl.Buffered(1),
                ),
                pl.BlockSpec((HALF, D), lambda i, *_: (half, 2), pipeline_mode=pl.Buffered(1)),
            ],
            out_specs=[
                kept((ROWS, HALF)), pair_cols(256), pair_cols(256), pair_cols(256), pair_cols(128),
            ],
            scratch_shapes=[pltpu.VMEM((ROWS, HALF), bf16)] * 3
            + [pltpu.VMEM((3, 2, WIN, WIN), bf16)],
        ),
        out_shape=[
            struct((ROWS, HALF), bf16), struct((ROWS, D), bf16), struct((ROWS, D), bf16),
            struct((ROWS, D), bf16), struct((ROWS, HALF), bf16),
        ],
        compiler_params=PARAMS,
        cost_estimate=pl.CostEstimate(
            flops=20_000_000_000, bytes_accessed=12_000_000, transcendentals=7_000_000
        ),
    )(len_arr, tok, full)


def attn_bwd(len_arr, qa, ka, va, ctx, gctx, x, base, full, half, chunks):
    part = (chunks // 4, D // chunks, D)
    pair_cols = lambda width, first: pl.BlockSpec((ROWS, width), lambda i, *_: (0, i + first))
    return pl.pallas_call(
        attn_bwd_kernel,
        name="attn_bwd",
        grid_spec=pltpu.PrefetchScalarGridSpec(
            num_scalar_prefetch=1,
            grid=(3,),
            in_specs=[
                pair_cols(256, 0), pair_cols(256, 0), pair_cols(256, 0), pair_cols(128, 0),
                pair_cols(128, 3 * half), whole(x.shape),
                pl.BlockSpec((ROWS, HALF), lambda i, *_: (0, half), pipeline_mode=pl.Buffered(1)),
                pl.BlockSpec((HALF, D), lambda i, *_: (half, 2), pipeline_mode=pl.Buffered(1)),
            ],
            out_specs=[kept((SEQ // BLOCK, 2, BLOCK, HALF)), kept(part), kept(part)],
            scratch_shapes=[
                pltpu.VMEM((ROWS, HALF), bf16),
                pltpu.VMEM((ROWS, HALF), bf16),
                pltpu.VMEM((ROWS, HALF), bf16),
                pltpu.VMEM((ROWS, 256), bf16),
                pltpu.VMEM((128, ROWS), f32),
                pltpu.VMEM((ROWS, HALF), bf16),
                pltpu.VMEM((WIN, WIN), bf16),
                pltpu.VMEM((HALF, D), bf16),
            ],
        ),
        out_shape=[
            struct((SEQ // BLOCK, 2, BLOCK, HALF), bf16), struct(part, bf16), struct(part, bf16),
        ],
        compiler_params=PARAMS,
        cost_estimate=pl.CostEstimate(
            flops=100_000_000, bytes_accessed=1_000_000, transcendentals=0
        ),
    )(len_arr, qa, ka, va, ctx, gctx, x, base, full)


def row_tile(width):
    return pl.BlockSpec((TILE, width), lambda i, *_: (i, 0))


def mid_fwd(len_arr, x0, x1, ctx0, ctx1, full, wu, vecs):
    outs = [
        ((SEQ // BLOCK, 2, BLOCK, D), bf16), ((ROWS, D), f32), ((ROWS, D), f32),
        ((ROWS, 128), f32), ((ROWS, FF), f32), ((ROWS, FF), bf16), ((8, 128), f32),
    ]
    return pl.pallas_call(
        mid_fwd_kernel,
        name="mid_fwd",
        grid_spec=pltpu.PrefetchScalarGridSpec(
            num_scalar_prefetch=1,
            grid=(TILES,),
            in_specs=[row_tile(HALF)] * 4
            + [whole((D, 2 * D)), whole(wu.shape), whole(vecs.shape)],
            out_specs=[
                kept(outs[0][0]), row_tile(D), row_tile(D), row_tile(128), row_tile(FF),
                row_tile(FF), kept((8, 128)),
            ],
            scratch_shapes=[
                pltpu.VMEM((ROWS, D), bf16),
                pltpu.VMEM((4, WIN, D), bf16),
                pltpu.VMEM((8, D), f32),
            ],
        ),
        out_shape=[struct(*o) for o in outs],
        compiler_params=PARAMS,
        cost_estimate=pl.CostEstimate(
            flops=15_000_000_000, bytes_accessed=36_000_000, transcendentals=7_000_000
        ),
    )(len_arr, x0, x1, ctx0, ctx1, full, wu, vecs)


def mid_bwd(len_arr, cot, ctx0, ctx1, n1, n2, inv, slope, act, full, wu, vecs, chunks):
    part = (chunks // 2, D // chunks, GRAD_COLS)
    outs = [((ROWS, D), bf16), ((ROWS, D), f32), (part, bf16), (part, bf16)]
    return pl.pallas_call(
        mid_bwd_kernel,
        name="mid_bwd",
        grid_spec=pltpu.PrefetchScalarGridSpec(
            num_scalar_prefetch=1,
            grid=(TILES,),
            in_specs=[
                whole(cot.shape), row_tile(HALF), row_tile(HALF), row_tile(D), row_tile(D),
                row_tile(128), row_tile(FF), row_tile(FF), whole((D, 2 * D)), whole(wu.shape),
                whole(vecs.shape),
            ],
            out_specs=[
                row_tile(D),
                row_tile(D),
                whole(part),
                whole(part),
            ],
            scratch_shapes=[
                pltpu.VMEM((ROWS, D), bf16),
                pltpu.VMEM((4, WIN, D), bf16),
                pltpu.VMEM((D, D), f32),
                pltpu.VMEM((4, WIN, D), f32),
                pltpu.VMEM((4, WIN, D), f32),
                pltpu.VMEM((128, D), f32),
                pltpu.VMEM((D, 128), f32),
                pltpu.VMEM((D, GRAD_COLS), bf16),
            ],
        ),
        out_shape=[struct(*o) for o in outs],
        compiler_params=PARAMS,
        cost_estimate=pl.CostEstimate(
            flops=100_000_000, bytes_accessed=1_000_000, transcendentals=0
        ),
    )(len_arr, cot, ctx0, ctx1, n1, n2, inv, slope, act, full, wu, vecs)


def column_of(row_ref):
    count = row_ref.shape[1]
    row = lax.broadcasted_iota(jnp.int32, (count, count), 0)
    col = lax.broadcasted_iota(jnp.int32, (count, count), 1)
    values = jnp.broadcast_to(row_ref[...].astype(f32), (count, count))
    return jnp.sum(jnp.where(row == col, values, 0.0), axis=1, keepdims=True)


def pack_kernel(odd_ref, *refs):
    bias_refs, (up_bias_ref, o_ref, down_ref, q_ref, k_ref, v_ref, up_ref) = refs[:8], refs[8:15]
    out_ref, low_s, high_s = refs[15:]
    rows = o_ref.shape[0]
    odd = odd_ref[0]
    shift = lax.broadcasted_iota(jnp.int32, (192, WIN), 1) - lax.broadcasted_iota(
        jnp.int32, (192, WIN), 0
    )
    move = jnp.where(shift == 64 * odd, 1.0, 0.0).astype(bf16)

    def padded(weight, column):
        lane = lax.broadcasted_iota(jnp.int32, (weight.shape[0], WIN), 1)
        moved = mm(weight, move, NN)
        return jnp.where(lane == 192 * (1 - odd), column, moved)

    columns = [column_of(ref) for ref in bias_refs]
    out_ref[:, :D] = o_ref[...]
    out_ref[:, D : 2 * D] = down_ref[...]
    sources = ((q_ref, columns[6]), (k_ref, jnp.zeros((rows, 1), f32)), (v_ref, columns[7]))
    for which, (ref, column) in enumerate(sources):
        start = 2 * D + WIN * which
        out_ref[:, start : start + WIN] = padded(ref[...], column).astype(bf16)
    up = padded(up_ref[...], column_of(up_bias_ref))
    low_s[...] = up[:, :128]
    high_s[...] = up[:, 128:]
    for j in range(4):
        for half, source in enumerate((low_s, high_s)):
            start = 3 * D + WIN * j + 128 * half
            out_ref[:, start : start + 128] = source[pl.ds(j, rows, stride=4), :].astype(bf16)
    lane = lax.broadcasted_iota(jnp.int32, (rows, 128), 1)
    small = jnp.zeros((rows, 128), f32)
    for index, column in enumerate(columns[:6]):
        small = jnp.where(lane == index, column, small)
    out_ref[:, 3 * D + 4 * WIN :] = small.astype(bf16)


def pack(odd, biases, up_bias, o_weight, down_weight, in_weights, up_weight):
    rows = o_weight.shape[0]
    arrays = [bias[None, :] for bias in (*biases, up_bias)]
    arrays += [o_weight, down_weight, *in_weights, up_weight]
    return pl.pallas_call(
        pack_kernel,
        name="pack",
        grid_spec=pltpu.PrefetchScalarGridSpec(
            num_scalar_prefetch=1,
            grid=(1,),
            in_specs=[whole(array.shape) for array in arrays],
            out_specs=[kept((rows, ALL_COLS))],
            scratch_shapes=[pltpu.VMEM((4 * rows, 128), f32)] * 2,
        ),
        out_shape=[struct((rows, ALL_COLS), bf16)],
        compiler_params=PARAMS,
        cost_estimate=pl.CostEstimate(flops=0, bytes_accessed=400_000, transcendentals=0),
    )(odd.astype(jnp.int32).reshape(1), *arrays)[0]


def minor_of(count):
    return max(2, count // 4)


def spread_kernel(sizes, packed_ref, full_ref, own_sem, send_sems, recv_sems):
    far, pair, major, minor = sizes
    dp, fsdp = lax.axis_index("dp"), lax.axis_index("fsdp")
    spot = (dp // 2, dp % 2, fsdp // minor, fsdp % minor)

    def device(place):
        return (place[0] * 2 + place[1], place[2] * minor + place[3])

    def moved(dim, shift):
        place = list(spot)
        place[dim] = lax.rem(place[dim] + shift, sizes[dim])
        return tuple(place)

    barrier = pltpu.get_barrier_semaphore()
    peers = [(dim, shift) for dim in range(4) for shift in range(1, sizes[dim])]
    for dim, shift in peers:
        pl.semaphore_signal(
            barrier,
            inc=1,
            device_id=device(moved(dim, shift)),
            device_id_type=pl.DeviceIdType.MESH,
        )
    pl.semaphore_wait(barrier, len(peers))

    own = pltpu.make_async_copy(packed_ref, full_ref.at[spot], own_sem)
    own.start()
    orders = ((2, 3, 0, 1), (2, 0, 3, 1))
    lanes = (pl.ds(0, SPLIT), pl.ds(SPLIT, ALL_COLS - SPLIT))
    slot_of = {}

    def copy(route, stage, shift, place, target):
        order = orders[route]
        gathered = order[:stage]
        index = tuple(slice(None) if d in gathered else place[d] for d in range(4))
        slot = slot_of.setdefault((route, stage, shift), len(slot_of))
        region = full_ref.at[index + (slice(None), lanes[route])]
        source = packed_ref.at[:, lanes[route]] if stage == 0 else region
        return pltpu.make_async_remote_copy(
            src_ref=source,
            dst_ref=region,
            send_sem=send_sems.at[slot],
            recv_sem=recv_sems.at[slot],
            device_id=device(target),
            device_id_type=pl.DeviceIdType.MESH,
        )

    def shifts(route, stage):
        return range(1, sizes[orders[route][stage]])

    sent = []
    for stage in range(4):
        for route in range(2):
            dim = orders[route][stage]
            if stage > 0:
                before = orders[route][stage - 1]
                for shift in shifts(route, stage - 1):
                    came = moved(before, sizes[before] - shift)
                    copy(route, stage - 1, shift, came, came).wait_recv()
            if stage == 1 and route == 0:
                own.wait()
            for shift in shifts(route, stage):
                one = copy(route, stage, shift, spot, moved(dim, shift))
                one.start()
                sent.append(one)
    for route in range(2):
        for shift in shifts(route, 3):
            came = moved(orders[route][3], sizes[orders[route][3]] - shift)
            copy(route, 3, shift, came, came).wait_recv()
    for one in sent:
        one.wait_send()


def spread(packed, dp, fsdp):
    rows, cols = packed.shape
    minor = minor_of(fsdp)
    sizes = (dp // 2, 2, fsdp // minor, minor)
    copies = 2 * sum(size - 1 for size in sizes)
    full = pl.pallas_call(
        functools.partial(spread_kernel, sizes),
        name="spread",
        in_specs=[pl.BlockSpec(memory_space=pltpu.VMEM)],
        out_specs=pl.BlockSpec(memory_space=pltpu.HBM),
        out_shape=struct((*sizes, rows, cols), bf16),
        scratch_shapes=[
            pltpu.SemaphoreType.DMA(()),
            pltpu.SemaphoreType.DMA((copies,)),
            pltpu.SemaphoreType.DMA((copies,)),
        ],
        compiler_params=pltpu.CompilerParams(
            collective_id=0, has_side_effects=True, vmem_limit_bytes=63_000_000
        ),
        cost_estimate=pl.CostEstimate(flops=0, bytes_accessed=100_000_000, transcendentals=0),
    )(packed)
    return full.reshape(dp * fsdp * rows, cols)


def source_of(len_ref, perm_ref, place):
    first = perm_ref[place - place % 2]
    second = perm_ref[place - place % 2 + 1]
    swapped = (len_ref[first] < len_ref[second]).astype(jnp.int32)
    return jnp.where(swapped == place % 2, first, second)


def moved_rows(source_at, rows_refs, out_ref, buffer_ref, in_sems, out_sems):
    count = out_ref.shape[0] // STEPS

    def group(step):
        return pl.ds(step * count, count)

    for step in range(STEPS):

        def one(index, carry):
            place = step * count + index
            source = source_at(place)
            lane = 0
            for which, rows_ref in enumerate(rows_refs):
                width = rows_ref.shape[2]
                pltpu.make_async_copy(
                    rows_ref.at[source],
                    buffer_ref.at[place, :, pl.ds(lane, width)],
                    in_sems.at[step, which],
                ).start()
                lane += width
            return carry

        lax.fori_loop(0, count, one, 0)
    for step in range(STEPS):
        lane = 0
        for which, rows_ref in enumerate(rows_refs):
            width = rows_ref.shape[2]
            pltpu.make_async_copy(
                rows_ref.at[group(step)],
                buffer_ref.at[group(step), :, pl.ds(lane, width)],
                in_sems.at[step, which],
            ).wait()
            lane += width
        pltpu.make_async_copy(
            buffer_ref.at[group(step)], out_ref.at[group(step)], out_sems.at[step]
        ).start()
    for step in range(STEPS):
        pltpu.make_async_copy(
            buffer_ref.at[group(step)], out_ref.at[group(step)], out_sems.at[step]
        ).wait()


def moved_call(kernel, name, parts, lengths, permutation):
    total, size, _ = parts[0].shape
    shape = (total, size, sum(part.shape[2] for part in parts))
    return pl.pallas_call(
        kernel,
        name=name,
        grid_spec=pltpu.PrefetchScalarGridSpec(
            num_scalar_prefetch=2,
            grid=(1,),
            in_specs=[pl.BlockSpec(memory_space=pltpu.HBM)] * len(parts),
            out_specs=[pl.BlockSpec(memory_space=pltpu.HBM)],
            scratch_shapes=[
                pltpu.VMEM(shape, bf16),
                pltpu.SMEM((total,), jnp.int32),
                pltpu.SemaphoreType.DMA((STEPS, len(parts))),
                pltpu.SemaphoreType.DMA((STEPS,)),
            ],
        ),
        out_shape=[struct(shape, bf16)],
        compiler_params=PARAMS,
        cost_estimate=pl.CostEstimate(flops=0, bytes_accessed=100_000, transcendentals=0),
    )(lengths, permutation, *parts)[0]


def deal_kernel(len_ref, perm_ref, rows_ref, out_ref, buffer_ref, place_s, in_sems, out_sems):
    source_at = lambda place: source_of(len_ref, perm_ref, place)
    moved_rows(source_at, [rows_ref], out_ref, buffer_ref, in_sems, out_sems)


def deal(rows, lengths, permutation):
    return moved_call(deal_kernel, "deal", [rows], lengths, permutation)


def restore_kernel(len_ref, perm_ref, *refs):
    part_refs, (out_ref, buffer_ref, place_s, in_sems, out_sems) = refs[:-5], refs[-5:]

    def note(index, carry):
        place_s[source_of(len_ref, perm_ref, index)] = index
        return carry

    lax.fori_loop(0, out_ref.shape[0], note, 0)
    moved_rows(lambda place: place_s[place], part_refs, out_ref, buffer_ref, in_sems, out_sems)


def restore(parts, lengths, permutation):
    return moved_call(restore_kernel, "restore", parts, lengths, permutation)


def pick(values, index):
    return values.at[index].get(mode="promise_in_bounds")


def tie(*values):
    return lax.optimization_barrier(values)


def on_device(
    tokens, cotangent, lengths, permutation, q_weight, q_bias, k_weight, v_weight, v_bias, o_weight,
    o_bias, norm1_gain, norm1_bias, up_weight, up_bias, down_weight, down_bias, norm2_gain,
    norm2_bias,
):
    devices = lax.axis_size(AXES)
    my_index = lax.axis_index(AXES)
    seq_total, piece_len, _ = tokens.shape
    seq_dev = seq_total // devices
    rows_dev = q_weight.shape[0]
    up_dev = up_weight.shape[0]
    odd = (my_index // (devices // 4)) % 2 == 1

    def padded(weight, bias):
        column = bias[:, None]
        gap = jnp.zeros((weight.shape[0], 63), bf16)
        return jnp.where(
            odd,
            jnp.concatenate([column, gap, weight], axis=1),
            jnp.concatenate([weight, column, gap], axis=1),
        )

    if rows_dev % 8 == 0:
        packed = pack(
            odd,
            [o_bias, norm1_gain, norm1_bias, down_bias, norm2_gain, norm2_bias, q_bias, v_bias],
            up_bias, o_weight, down_weight, [q_weight, k_weight, v_weight], up_weight,
        )
    else:
        small = [o_bias, norm1_gain, norm1_bias, down_bias, norm2_gain, norm2_bias]
        packed = jnp.concatenate(
            [
                o_weight,
                down_weight,
                padded(q_weight, q_bias),
                padded(k_weight, jnp.zeros_like(q_bias)),
                padded(v_weight, v_bias),
                padded(up_weight, up_bias).reshape(rows_dev, 4 * WIN),
                jnp.pad(jnp.stack(small, axis=1), ((0, 0), (0, 122))),
            ],
            axis=1,
        )

    dealt_lengths = pick(lengths, permutation).reshape(devices, seq_dev)
    chunks = lax.axis_size("dp")
    parity = lax.axis_index("dp") % 2
    pairing = [(i, i ^ 1) for i in range(chunks)]
    len_arr = jnp.stack(
        [jnp.max(lax.dynamic_slice_in_dim(dealt_lengths, my_index, 1, 0)), parity]
    ).astype(jnp.int32)

    def swap_blocks(rows):
        return lax.all_to_all(rows, AXES, split_axis=0, concat_axis=0, tiled=True)

    def arrive(rows):
        width = rows.shape[-1]
        moved = swap_blocks(rows.reshape(devices, seq_dev, piece_len, width))
        if piece_len == BLOCK:
            return moved
        moved = moved.transpose(1, 0, 2, 3).reshape(seq_dev, SEQ // BLOCK, BLOCK, width)
        return moved.transpose(1, 0, 2, 3)

    def leave(rows):
        width = rows.shape[-1]
        if piece_len != BLOCK:
            rows = rows.transpose(1, 0, 2, 3).reshape(seq_dev, devices, piece_len, width)
            rows = rows.transpose(1, 0, 2, 3)
        return swap_blocks(rows).reshape(seq_total, piece_len, width)

    fsdp = lax.axis_size("fsdp")
    minor = minor_of(fsdp)
    major = fsdp // minor
    place = (lax.axis_index("dp") // 2, lax.axis_index("fsdp") // minor, my_index % minor)

    def target_of(device, far, high, low):
        dp_index, rest = device // fsdp, device % fsdp
        dp_index = (dp_index + 2 * far) % chunks
        rest = (rest // minor + high) % major * minor + (rest % minor + low) % minor
        return dp_index * fsdp + rest

    def send_blocks(partial, shifts, block_of):
        parts = [block_of(0, 0, 0)]
        for shift in shifts:
            route = [(i, target_of(i, *shift)) for i in range(devices)]
            parts.append(lax.ppermute(block_of(*shift), AXES, route))
        return parts

    def send_near(partial):
        shape = (chunks // 2, major, minor, rows_dev, partial.shape[-1])
        blocks = partial.reshape(shape)

        def block_of(far, high, low):
            start = ((place[0] + far) % shape[0], 0, (place[2] + low) % minor, 0, 0)
            return lax.dynamic_slice(blocks, start, (1, major, 1, *shape[3:]))

        shifts = [(far, 0, low) for far in range(shape[0]) for low in range(minor)][1:]
        return send_blocks(blocks, shifts, block_of)

    def send_far(partial):
        blocks = partial.reshape(major, rows_dev, partial.shape[-1])

        def block_of(far, high, low):
            return lax.dynamic_index_in_dim(blocks, (place[1] + high) % major, 0, False)

        return send_blocks(blocks, [(0, high, 0) for high in range(1, major)], block_of)

    def total(parts):
        result = sum(part.astype(f32) for part in parts)
        return result.reshape(-1, result.shape[-1])

    def total_low(parts):
        return total(parts).astype(bf16)

    tok = arrive(deal(tokens, lengths, permutation))
    packed, dealt_cot = tie(packed, deal(cotangent, lengths, permutation))
    if rows_dev % 8 == 0:
        full = spread(packed, lax.axis_size("dp"), lax.axis_size("fsdp"))
    else:
        full = lax.all_gather(packed, AXES, axis=0, tiled=True)
    dealt_cot, tok, full = tie(dealt_cot, tok, full)
    cot = arrive(dealt_cot)

    x0, qa0, ka0, va0, ctx0 = attn_fwd(len_arr, tok, full, 0)
    x1, qa1, ka1, va1, ctx1 = attn_fwd(len_arr, tok, full, 1)
    wu = full[:, 3 * D : 3 * D + 4 * WIN].reshape(FF, WIN)
    vecs = jnp.pad(full[:, 3 * D + 4 * WIN : 3 * D + 4 * WIN + 6].astype(f32).T, ((0, 2), (0, 0)))
    out, n1, n2, inv, slope, act, stat = mid_fwd(len_arr, x0, x1, ctx0, ctx1, full, wu, vecs)
    cot, out = tie(cot, out)
    back_out = leave(out)
    gctx, base, mine, given = mid_bwd(
        len_arr, cot, ctx0, ctx1, n1, n2, inv, slope, act, full, wu, vecs, chunks
    )
    mine = total_low([mine, lax.ppermute(given, "dp", pairing)])
    gctx, mine = tie(gctx, mine)
    parts = send_near(mine)
    ig0, dw0, given0 = attn_bwd(
        len_arr, qa0, ka0, va0, ctx0, gctx, x0, base, full, 0, chunks
    )
    ig0, dw0, given0, gctx, back_out, *parts = tie(ig0, dw0, given0, gctx, back_out, *parts)
    back0 = leave(ig0)
    given0 = lax.ppermute(given0, "dp", pairing)
    parts = send_far(total_low(parts))
    ig1, dw1, given1 = attn_bwd(
        len_arr, qa1, ka1, va1, ctx1, gctx, x1, base, full, 1, chunks
    )
    ig1, dw0, dw1, given0, given1, back0, *parts = tie(
        ig1, dw0, dw1, given0, given1, back0, *parts
    )
    back1 = leave(ig1)
    given1 = lax.ppermute(given1, "dp", pairing)
    mine_in = jnp.concatenate([total_low([dw0, given0]), total_low([dw1, given1])], axis=0)
    parts_in = send_near(mine_in)
    back_out, stat, dealt_lengths, *parts = tie(back_out, stat, dealt_lengths, *parts)
    mine = total(parts)
    mine_in = total(send_far(total_low(parts_in)))

    swap = dealt_lengths[:, 0] < dealt_lengths[:, 1]
    my_swap = lax.dynamic_index_in_dim(swap, my_index, 0, False)
    output = restore([back_out], lengths, permutation)
    input_grad = restore([back0, back1], lengths, permutation)
    lens = jnp.stack([len_arr[0], ROWS - len_arr[0]]).astype(f32)
    sums = jnp.stack([stat[4:8, 0], stat[0:4, 0] - stat[4:8, 0]], axis=1)
    rms = jnp.sqrt(sums / (lens[None, :] * D) + rms_eps)
    stream_rms = jnp.where(my_swap, rms[:, ::-1], rms)
    vec = lambda i: mine[:, 2 * D + 4 * WIN + i]

    def unpadded(block):
        return (
            jnp.where(odd, block[:, 64:], block[:, :192]),
            jnp.where(odd, block[:, 0], block[:, 192]),
        )

    dq, dqb = unpadded(mine_in[:, :WIN])
    dk, _ = unpadded(mine_in[:, WIN : 2 * WIN])
    dv, dvb = unpadded(mine_in[:, 2 * WIN :])
    dup, dub = unpadded(mine[:, 2 * D : 2 * D + 4 * WIN].reshape(up_dev, WIN))
    return (
        output, input_grad, dq, dqb, dk, dv, dvb, mine[:, :D], vec(0), vec(1), vec(2), dup, dub,
        mine[:, D : 2 * D], vec(3), vec(4), vec(5), stream_rms,
    )


def solution(mesh):
    rows = P(None, AXES, None)
    mat = P(AXES, None)
    vec = P(AXES)
    in_specs = (
        rows, rows, P(), P(), mat, vec, mat, mat, vec, mat, vec, vec, vec, mat, vec, mat, vec, vec,
        vec,
    )
    out_specs = (
        rows, rows, mat, vec, mat, mat, vec, mat, vec, vec, vec, mat, vec, mat, vec, vec, vec,
        P(None, AXES),
    )
    return jax.shard_map(
        on_device, mesh=mesh, in_specs=in_specs, out_specs=out_specs, check_vma=False
    )
```

```python
import functools

import jax
import jax.numpy as jnp
from jax import lax
from jax.experimental import pallas as pl
from jax.experimental.pallas import tpu as pltpu
from jax.sharding import PartitionSpec as P

AXES = ("dp", "fsdp")
D = 768
FF = 3072
HALF = D // 2
HEAD = 64
WIN = 256
SEQ = 1024
SHORT = 64
BLOCK = 32
ROWS = SEQ + SHORT
TILE = 272
TILES = ROWS // TILE
BIG = 1e30
STEPS = 4
SPLIT = 1664

norm_eps = 1e-12
rms_eps = 1e-06
bf16 = jnp.bfloat16
f32 = jnp.float32

NN = (((1,), (0,)), ((), ()))
NT = (((1,), (1,)), ((), ()))
TN = (((0,), (0,)), ((), ()))


def mm(left, right, dims):
    return lax.dot_general(left, right, dims, preferred_element_type=f32)


def exchange():
    row = lax.broadcasted_iota(jnp.int32, (WIN, WIN), 0)
    col = lax.broadcasted_iota(jnp.int32, (WIN, WIN), 1)
    return jnp.where(row + col == WIN - 1, 1.0, 0.0).astype(bf16)


def row_ids(start, count, width):
    return start + lax.broadcasted_iota(jnp.int32, (count, width), 0)


def block_rows(ref, seq, start, count):
    values = ref[start // BLOCK : (start + count) // BLOCK, seq]
    return values.reshape(count, values.shape[-1])


def merge_rows(pair_ref, packed_ref, first_len):
    width = packed_ref.shape[1]
    flip = exchange()
    packed_ref[0:SHORT, :] = block_rows(pair_ref, 0, 0, SHORT)
    for step in range(SEQ // WIN):
        start = SHORT + WIN * step
        flipped = mm(flip, block_rows(pair_ref, 1, SEQ - WIN * (step + 1), WIN), NN)
        inside = min(WIN, SEQ - start)
        own = block_rows(pair_ref, 0, start, inside).astype(f32)
        keep = row_ids(start, inside, width) < first_len
        packed_ref[start : start + inside, :] = jnp.where(keep, own, flipped[0:inside]).astype(bf16)
        if inside < WIN:
            packed_ref[start + inside : start + WIN, :] = flipped[inside:].astype(bf16)


def unmerge_rows(packed_ref, pair_ref, first_len):
    width = packed_ref.shape[1]
    flip = exchange()
    blocks = WIN // BLOCK
    for step in range(SEQ // WIN):
        start = WIN * step
        ids = row_ids(start, WIN, width)
        own = packed_ref[start : start + WIN, :].astype(f32)
        own = jnp.where(ids < first_len, own, 0.0).astype(bf16)
        pair_ref[blocks * step : blocks * (step + 1), 0] = own.reshape(blocks, BLOCK, width)
        source = ROWS - WIN * (step + 1)
        flipped = mm(flip, packed_ref[source : source + WIN, :], NN)
        flipped = jnp.where(ids < ROWS - first_len, flipped, 0.0).astype(bf16)
        pair_ref[blocks * step : blocks * (step + 1), 1] = flipped.reshape(blocks, BLOCK, width)


def spare_of(group):
    return 192 if group % 2 == 0 else 0


def with_ones(window, group):
    lane = lax.broadcasted_iota(jnp.int32, window.shape, 1)
    return jnp.where(lane == spare_of(group), 1.0, window.astype(f32)).astype(bf16)


def without_bias(window, group):
    lane = lax.broadcasted_iota(jnp.int32, window.shape, 1)
    return jnp.where(lane == spare_of(group), 0.0, window.astype(f32)).astype(bf16)


def first_row(group):
    return 0 if group % 2 == 0 else 64


def windows(values, count):
    parts = []
    for group in range(count):
        start = (group // 2) * HALF + (group % 2) * 128
        parts.append(values[:, start : start + WIN])
    return parts


def join(parts):
    pieces = []
    for first, second in zip(parts[0::2], parts[1::2]):
        pieces += [first[:, :128], first[:, 128:] + second[:, :128], second[:, 128:]]
    return jnp.concatenate(pieces, axis=1)


def split_three(value):
    high = value.astype(bf16)
    rest = value - high.astype(f32)
    mid = rest.astype(bf16)
    low = (rest - mid.astype(f32)).astype(bf16)
    return high, mid, low


def attn_fwd_kernel(
    len_ref, tok_ref, full_ref, x_ref, qa_ref, ka_ref, va_ref, ctx_ref, q_s, k_s, v_s, w_s
):
    pair = pl.program_id(0)
    first_len = len_ref[0]

    @pl.when(pair == 0)
    def _():
        merge_rows(tok_ref, x_ref, first_len)
        w_s[...] = jnp.zeros_like(w_s)
        for which in range(3):
            for g in range(2):
                w_s[which, g, first_row(g) : first_row(g) + 192, :] = full_ref[
                    192 * g : 192 * (g + 1), WIN * which : WIN * (which + 1)
                ]
        cols = [with_ones(part, g) for g, part in enumerate(windows(x_ref[...], 2))]
        for which, target in enumerate((q_s, k_s, v_s)):
            value = join([mm(cols[g], w_s[which, g], NT) for g in range(2)])
            if which == 0:
                value = value.astype(bf16).astype(f32) * (HEAD**-0.5)
            target[...] = value.astype(bf16)

    lane0 = pl.multiple_of(pair * 128, 128)
    q_pair = q_s[:, pl.ds(lane0, 128)]
    k_pair = k_s[:, pl.ds(lane0, 128)]
    v_pair = v_s[:, pl.ds(lane0, 128)]
    lane = lax.broadcasted_iota(jnp.int32, (ROWS, 128), 1)
    in_first = row_ids(0, ROWS, 128) < first_len
    one = jnp.ones((ROWS, 128), f32)
    zero = jnp.zeros((ROWS, 128), f32)
    for head in range(2):
        spare = 64 * (1 - head)
        own = (lane // 64) == head
        first_one = jnp.where(in_first, one, zero)
        q_extra = jnp.where(
            lane == spare, first_one, jnp.where(lane == spare + 1, one - first_one, zero)
        )
        k_extra = jnp.where(
            lane == spare,
            (first_one - one) * BIG,
            jnp.where(
                lane == spare + 1,
                first_one * (-BIG),
                jnp.where((lane >= spare + 2) & (lane < spare + 5), one, zero),
            ),
        )
        v_extra = jnp.where((lane >= spare) & (lane < spare + 3), one, zero)
        cols = slice(128 * head, 128 * (head + 1))
        qa_ref[:, cols] = jnp.where(own, q_pair.astype(f32), q_extra).astype(bf16)
        ka_ref[:, cols] = jnp.where(own, k_pair.astype(f32), k_extra).astype(bf16)
        va_ref[:, cols] = jnp.where(own, v_pair.astype(f32), v_extra).astype(bf16)

    tile_lane = lax.broadcasted_iota(jnp.int32, (TILE, 128), 1)

    def one_tile(index, carry):
        start = pl.multiple_of(index * TILE, 16)
        rows = pl.ds(start, TILE)
        result = None
        for head in range(2):
            cols = slice(128 * head, 128 * (head + 1))
            spare = 64 * (1 - head)
            q_tile = qa_ref[rows, cols]
            scores = mm(q_tile, ka_ref[:, cols], NT)
            top = jnp.max(scores, axis=1, keepdims=True)
            weights = jnp.exp(scores - top)
            mixed = mm(weights.astype(bf16), va_ref[:, cols], NN)
            total = mixed[:, spare : spare + 1]
            mixed = mixed / total
            log_total = top + jnp.log(total)
            high, mid, low = split_three(-log_total)
            q_new = jnp.where(
                tile_lane == spare + 2,
                high.astype(f32),
                jnp.where(
                    tile_lane == spare + 3,
                    mid.astype(f32),
                    jnp.where(tile_lane == spare + 4, low.astype(f32), q_tile.astype(f32)),
                ),
            )
            qa_ref[rows, cols] = q_new.astype(bf16)
            result = mixed if head == 0 else jnp.where(tile_lane < 64, result, mixed)
        ctx_ref[rows, :] = result.astype(bf16)
        return carry

    lax.fori_loop(0, TILES, one_tile, 0)


def attn_bwd_kernel(
    len_ref, qa_ref, ka_ref, va_ref, ctx_ref, gctx_ref, x_ref, base_ref, full_ref,
    ig_ref, kept_ref, given_ref, dq_s, dk_s, dv_s, do_s, dqt_s, ig_s, w_s, dw_ref,
):
    pair = pl.program_id(0)
    lane0 = pl.multiple_of(pair * 128, 128)
    lane = lax.broadcasted_iota(jnp.int32, (ROWS, 128), 1)
    grad = gctx_ref[...].astype(f32)
    product = grad * ctx_ref[...].astype(f32)
    for head in range(2):
        own = (lane // 64) == head
        spare = 64 * (1 - head)
        inner = -jnp.sum(jnp.where(own, product, 0.0), axis=1, keepdims=True)
        high, mid, low = split_three(inner)
        extra = jnp.where(
            lane == spare,
            high.astype(f32),
            jnp.where(
                lane == spare + 1,
                mid.astype(f32),
                jnp.where(lane == spare + 2, low.astype(f32), 0.0),
            ),
        )
        do_s[:, 128 * head : 128 * (head + 1)] = jnp.where(own, grad, extra).astype(bf16)
    dqt_s[...] = jnp.zeros_like(dqt_s)
    tile_lane = lax.broadcasted_iota(jnp.int32, (TILE, 128), 1)

    def one_tile(index, carry):
        start = pl.multiple_of(index * TILE, 16)
        rows = pl.ds(start, TILE)
        dk_tile = None
        dv_tile = None
        for head in range(2):
            cols = slice(128 * head, 128 * (head + 1))
            k_tile = ka_ref[rows, cols]
            probs = jnp.exp(mm(k_tile, qa_ref[:, cols], NT))
            scaled = mm(va_ref[rows, cols], do_s[:, cols], NT) * probs
            grad_scores = scaled.astype(bf16)
            dv_new = mm(probs.astype(bf16), do_s[:, cols], NN)
            dk_new = mm(grad_scores, qa_ref[:, cols], NN)
            dq_new = mm(k_tile, grad_scores, TN)
            dqt_s[64 * head : 64 * (head + 1), :] += dq_new[64 * head : 64 * (head + 1), :]
            dk_tile = dk_new if head == 0 else jnp.where(tile_lane < 64, dk_tile, dk_new)
            dv_tile = dv_new if head == 0 else jnp.where(tile_lane < 64, dv_tile, dv_new)
        dk_s[rows, pl.ds(lane0, 128)] = dk_tile.astype(bf16)
        dv_s[rows, pl.ds(lane0, 128)] = dv_tile.astype(bf16)
        return carry

    lax.fori_loop(0, TILES, one_tile, 0)
    dq_s[:, pl.ds(lane0, 128)] = (jnp.transpose(dqt_s[...]) * (HEAD**-0.5)).astype(bf16)

    @pl.when(pair == pl.num_programs(0) - 1)
    def _():
        x_cols = [with_ones(part, g) for g, part in enumerate(windows(x_ref[...], 2))]
        total = [None, None]
        for which, source in enumerate((dq_s, dk_s, dv_s)):
            cols = windows(source[...], 2)
            for g in range(2):
                own = slice(first_row(g), first_row(g) + 192)
                w_s[own, :] = without_bias(
                    full_ref[192 * g : 192 * (g + 1), WIN * which : WIN * (which + 1)], g
                )
                if first_row(g) == 0:
                    w_s[192:, :] = jnp.zeros((64, WIN), bf16)
                else:
                    w_s[:64, :] = jnp.zeros((64, WIN), bf16)
                grad = mm(cols[g], x_cols[g], TN)
                dw_ref[192 * g : 192 * (g + 1), WIN * which : WIN * (which + 1)] = grad[own].astype(
                    bf16
                )
                part = mm(cols[g], w_s[...], NN)
                total[g] = part if which == 0 else total[g] + part
        ig_s[...] = (join(total) + base_ref[...]).astype(bf16)
        unmerge_rows(ig_s, ig_ref, len_ref[0])
        split_chunks(dw_ref, kept_ref, given_ref, len_ref[1])


def split_chunks(rows_ref, kept_ref, given_ref, parity):
    pairs, size, _ = kept_ref.shape
    for own in range(2):

        @pl.when(parity == own)
        def _():
            for pair in range(pairs):
                for which in range(2):
                    start = (2 * pair + which) * size
                    target = kept_ref if which == own else given_ref
                    target[pair] = rows_ref[start : start + size, :]


def norm(values):
    mean = jnp.mean(values, axis=1, keepdims=True)
    centered = values - mean
    var = jnp.mean(centered * centered, axis=1, keepdims=True)
    inv = lax.rsqrt(var + norm_eps)
    return centered * inv, inv


def norm_back(grad_n, n, inv):
    mean_g = jnp.mean(grad_n, axis=1, keepdims=True)
    mean_gn = jnp.mean(grad_n * n, axis=1, keepdims=True)
    return (grad_n - mean_g - n * mean_gn) * inv


def mid_fwd_kernel(
    len_ref, x0_ref, x1_ref, ctx0_ref, ctx1_ref, full_ref, wu_ref, vec_ref,
    out_ref, n1_ref, n2_ref, inv_ref, slope_ref, act_ref, stat_ref,
    out_s, wd_s, stat_s,
):
    step = pl.program_id(0)
    first_len = len_ref[0]

    @pl.when(step == 0)
    def _():
        stat_s[...] = jnp.zeros_like(stat_s)
        wd_s[...] = jnp.zeros_like(wd_s)
        for g in range(4):
            wd_s[g, first_row(g) : first_row(g) + 192, :] = full_ref[192 * g : 192 * (g + 1), D:]

    o_bias, gain1, shift1, down_bias, gain2, shift2 = (vec_ref[i : i + 1, :] for i in range(6))
    start = pl.multiple_of(step * TILE, 16)
    rows = pl.ds(start, TILE)
    keep = jnp.where(row_ids(start, TILE, D) < first_len, 1.0, 0.0)

    def note(slot, values):
        square = values * values
        stat_s[slot : slot + 1, :] += jnp.sum(square, axis=0, keepdims=True)
        stat_s[slot + 4 : slot + 5, :] += jnp.sum(square * keep, axis=0, keepdims=True)

    inputs = jnp.concatenate([x0_ref[...], x1_ref[...]], axis=1).astype(f32)
    context = jnp.concatenate([ctx0_ref[...], ctx1_ref[...]], axis=1)
    note(0, inputs)
    branch_attn = mm(context, full_ref[:, :D], NT) + o_bias
    note(1, branch_attn)
    n1, inv1 = norm(inputs + branch_attn)
    n1_ref[...] = n1
    first_norm = n1 * gain1 + shift1
    note(2, first_norm)
    low_cols = windows(first_norm.astype(bf16), 4)
    parts = []
    for g in range(4):
        cols = slice(D * g, D * (g + 1))
        up = mm(with_ones(low_cols[g], g), wu_ref[D * g : D * (g + 1), :], NT)
        gate = 0.5 * (1.0 + lax.erf(up * (2.0**-0.5)))
        slope_ref[:, cols] = gate + up * jnp.exp(up * up * -0.5) * 0.3989422804014327
        act = (up * gate).astype(bf16)
        act_ref[:, cols] = act
        parts.append(mm(act, wd_s[g], NT))
    branch_ffn = join(parts) + down_bias
    note(3, branch_ffn)
    n2, inv2 = norm(first_norm + branch_ffn)
    n2_ref[...] = n2
    lane = lax.broadcasted_iota(jnp.int32, (TILE, 128), 1)
    inv_ref[...] = jnp.where(lane < 64, inv1, inv2)
    out_s[rows, :] = (n2 * gain2 + shift2).astype(bf16)

    @pl.when(step == pl.num_programs(0) - 1)
    def _():
        unmerge_rows(out_s, out_ref, first_len)
        stat_ref[...] = jnp.broadcast_to(
            jnp.sum(stat_s[...], axis=1, keepdims=True), stat_ref.shape
        )


def mid_bwd_kernel(
    len_ref, cot_ref, ctx0_ref, ctx1_ref, n1_ref, n2_ref, inv_ref, slope_ref, act_ref,
    full_ref, wu_ref, vec_ref, gctx_ref, base_ref, kept_ref, given_ref,
    cot_s, wd_s, dwo_s, dwd_s, dwu_s, vec_s, turn_s, grad_ref,
):
    step = pl.program_id(0)

    @pl.when(step == 0)
    def _():
        merge_rows(cot_ref, cot_s, len_ref[0])
        for target in (dwo_s, dwd_s, dwu_s, vec_s, wd_s):
            target[...] = jnp.zeros_like(target)
        for g in range(4):
            wd_s[g, first_row(g) : first_row(g) + 192, :] = full_ref[192 * g : 192 * (g + 1), D:]

    gain1, shift1, gain2 = (vec_ref[i : i + 1, :] for i in (1, 2, 4))
    start = pl.multiple_of(step * TILE, 16)
    rows = pl.ds(start, TILE)

    def add_vec(slot, values):
        vec_s[slot : slot + 1, :] += jnp.sum(values, axis=0, keepdims=True)

    context = jnp.concatenate([ctx0_ref[...], ctx1_ref[...]], axis=1)
    n1 = n1_ref[...]
    n2 = n2_ref[...]
    inv1 = inv_ref[:, 0:1]
    inv2 = inv_ref[:, 64:65]
    low_cols = windows((n1 * gain1 + shift1).astype(bf16), 4)
    grad_out = cot_s[rows, :].astype(f32)
    add_vec(4, grad_out * n2)
    add_vec(5, grad_out)
    grad_sum2 = norm_back(grad_out * gain2, n2, inv2)
    grad_ffn = grad_sum2.astype(bf16)
    add_vec(3, grad_ffn.astype(f32))
    ffn_cols = windows(grad_ffn, 4)
    parts = []
    for g in range(4):
        cols = slice(D * g, D * (g + 1))
        dwd_s[g] += mm(ffn_cols[g], act_ref[:, cols], TN)
        grad_up = (mm(ffn_cols[g], wd_s[g], NN) * slope_ref[:, cols]).astype(bf16)
        dwu_s[g] += mm(with_ones(low_cols[g], g), grad_up, TN)
        parts.append(mm(grad_up, without_bias(wu_ref[D * g : D * (g + 1), :], g), NN))
    grad_first = join(parts) + grad_sum2
    add_vec(1, grad_first * n1)
    add_vec(2, grad_first)
    grad_sum1 = norm_back(grad_first * gain1, n1, inv1)
    base_ref[...] = grad_sum1
    grad_branch = grad_sum1.astype(bf16)
    add_vec(0, grad_branch.astype(f32))
    dwo_s[...] += mm(grad_branch, context, TN)
    gctx_ref[...] = mm(grad_branch, full_ref[:, :D], NN).astype(bf16)

    @pl.when(step == pl.num_programs(0) - 1)
    def _():
        grad_ref[:, :D] = dwo_s[...].astype(bf16)
        for g in range(4):
            own = slice(192 * g, 192 * (g + 1))
            grad_ref[own, D : 2 * D] = dwd_s[g, first_row(g) : first_row(g) + 192, :].astype(bf16)
            turned = jnp.transpose(dwu_s[g])
            for half in range(2):
                turn_s[...] = turned[:, 128 * half : 128 * (half + 1)]
                for j in range(4):
                    lane0 = 2 * D + WIN * j + 128 * half
                    grad_ref[own, lane0 : lane0 + 128] = turn_s[pl.ds(j, 192, stride=4), :].astype(
                        bf16
                    )
        grad_ref[:, 2 * D + 4 * WIN :] = jnp.transpose(vec_s[...]).astype(bf16)
        split_chunks(grad_ref, kept_ref, given_ref, len_ref[1])


def whole(shape):
    zeros = (0,) * len(shape)
    return pl.BlockSpec(shape, lambda i, *_: zeros, pipeline_mode=pl.Buffered(1))


def kept(shape):
    zeros = (0,) * len(shape)
    return pl.BlockSpec(shape, lambda i, *_: zeros)


def struct(shape, dtype):
    return jax.ShapeDtypeStruct(shape, dtype)


PARAMS = pltpu.CompilerParams(
    dimension_semantics=("arbitrary",), vmem_limit_bytes=63_000_000
)
GRAD_COLS = 2 * D + 4 * WIN + 128
ALL_COLS = GRAD_COLS + D


def attn_fwd(len_arr, tok, full, half):
    pair_cols = lambda width: pl.BlockSpec((ROWS, width), lambda i, *_: (0, i))
    return pl.pallas_call(
        attn_fwd_kernel,
        name="attn_fwd",
        grid_spec=pltpu.PrefetchScalarGridSpec(
            num_scalar_prefetch=1,
            grid=(3,),
            in_specs=[
                pl.BlockSpec(
                    (SEQ // BLOCK, 2, BLOCK, HALF),
                    lambda i, *_: (0, 0, 0, half),
                    pipeline_mode=pl.Buffered(1),
                ),
                pl.BlockSpec((HALF, D), lambda i, *_: (half, 2), pipeline_mode=pl.Buffered(1)),
            ],
            out_specs=[
                kept((ROWS, HALF)), pair_cols(256), pair_cols(256), pair_cols(256), pair_cols(128),
            ],
            scratch_shapes=[pltpu.VMEM((ROWS, HALF), bf16)] * 3
            + [pltpu.VMEM((3, 2, WIN, WIN), bf16)],
        ),
        out_shape=[
            struct((ROWS, HALF), bf16), struct((ROWS, D), bf16), struct((ROWS, D), bf16),
            struct((ROWS, D), bf16), struct((ROWS, HALF), bf16),
        ],
        compiler_params=PARAMS,
        cost_estimate=pl.CostEstimate(
            flops=20_000_000_000, bytes_accessed=12_000_000, transcendentals=7_000_000
        ),
    )(len_arr, tok, full)


def attn_bwd(len_arr, qa, ka, va, ctx, gctx, x, base, full, half, chunks):
    part = (chunks // 4, D // chunks, D)
    pair_cols = lambda width, first: pl.BlockSpec((ROWS, width), lambda i, *_: (0, i + first))
    return pl.pallas_call(
        attn_bwd_kernel,
        name="attn_bwd",
        grid_spec=pltpu.PrefetchScalarGridSpec(
            num_scalar_prefetch=1,
            grid=(3,),
            in_specs=[
                pair_cols(256, 0), pair_cols(256, 0), pair_cols(256, 0), pair_cols(128, 0),
                pair_cols(128, 3 * half), whole(x.shape),
                pl.BlockSpec((ROWS, HALF), lambda i, *_: (0, half), pipeline_mode=pl.Buffered(1)),
                pl.BlockSpec((HALF, D), lambda i, *_: (half, 2), pipeline_mode=pl.Buffered(1)),
            ],
            out_specs=[kept((SEQ // BLOCK, 2, BLOCK, HALF)), kept(part), kept(part)],
            scratch_shapes=[
                pltpu.VMEM((ROWS, HALF), bf16),
                pltpu.VMEM((ROWS, HALF), bf16),
                pltpu.VMEM((ROWS, HALF), bf16),
                pltpu.VMEM((ROWS, 256), bf16),
                pltpu.VMEM((128, ROWS), f32),
                pltpu.VMEM((ROWS, HALF), bf16),
                pltpu.VMEM((WIN, WIN), bf16),
                pltpu.VMEM((HALF, D), bf16),
            ],
        ),
        out_shape=[
            struct((SEQ // BLOCK, 2, BLOCK, HALF), bf16), struct(part, bf16), struct(part, bf16),
        ],
        compiler_params=PARAMS,
        cost_estimate=pl.CostEstimate(
            flops=100_000_000, bytes_accessed=1_000_000, transcendentals=0
        ),
    )(len_arr, qa, ka, va, ctx, gctx, x, base, full)


def row_tile(width):
    return pl.BlockSpec((TILE, width), lambda i, *_: (i, 0))


def mid_fwd(len_arr, x0, x1, ctx0, ctx1, full, wu, vecs):
    outs = [
        ((SEQ // BLOCK, 2, BLOCK, D), bf16), ((ROWS, D), f32), ((ROWS, D), f32),
        ((ROWS, 128), f32), ((ROWS, FF), f32), ((ROWS, FF), bf16), ((8, 128), f32),
    ]
    return pl.pallas_call(
        mid_fwd_kernel,
        name="mid_fwd",
        grid_spec=pltpu.PrefetchScalarGridSpec(
            num_scalar_prefetch=1,
            grid=(TILES,),
            in_specs=[row_tile(HALF)] * 4
            + [whole((D, 2 * D)), whole(wu.shape), whole(vecs.shape)],
            out_specs=[
                kept(outs[0][0]), row_tile(D), row_tile(D), row_tile(128), row_tile(FF),
                row_tile(FF), kept((8, 128)),
            ],
            scratch_shapes=[
                pltpu.VMEM((ROWS, D), bf16),
                pltpu.VMEM((4, WIN, D), bf16),
                pltpu.VMEM((8, D), f32),
            ],
        ),
        out_shape=[struct(*o) for o in outs],
        compiler_params=PARAMS,
        cost_estimate=pl.CostEstimate(
            flops=15_000_000_000, bytes_accessed=36_000_000, transcendentals=7_000_000
        ),
    )(len_arr, x0, x1, ctx0, ctx1, full, wu, vecs)


def mid_bwd(len_arr, cot, ctx0, ctx1, n1, n2, inv, slope, act, full, wu, vecs, chunks):
    part = (chunks // 2, D // chunks, GRAD_COLS)
    outs = [((ROWS, D), bf16), ((ROWS, D), f32), (part, bf16), (part, bf16)]
    return pl.pallas_call(
        mid_bwd_kernel,
        name="mid_bwd",
        grid_spec=pltpu.PrefetchScalarGridSpec(
            num_scalar_prefetch=1,
            grid=(TILES,),
            in_specs=[
                whole(cot.shape), row_tile(HALF), row_tile(HALF), row_tile(D), row_tile(D),
                row_tile(128), row_tile(FF), row_tile(FF), whole((D, 2 * D)), whole(wu.shape),
                whole(vecs.shape),
            ],
            out_specs=[
                row_tile(D),
                row_tile(D),
                whole(part),
                whole(part),
            ],
            scratch_shapes=[
                pltpu.VMEM((ROWS, D), bf16),
                pltpu.VMEM((4, WIN, D), bf16),
                pltpu.VMEM((D, D), f32),
                pltpu.VMEM((4, WIN, D), f32),
                pltpu.VMEM((4, WIN, D), f32),
                pltpu.VMEM((128, D), f32),
                pltpu.VMEM((D, 128), f32),
                pltpu.VMEM((D, GRAD_COLS), bf16),
            ],
        ),
        out_shape=[struct(*o) for o in outs],
        compiler_params=PARAMS,
        cost_estimate=pl.CostEstimate(
            flops=100_000_000, bytes_accessed=1_000_000, transcendentals=0
        ),
    )(len_arr, cot, ctx0, ctx1, n1, n2, inv, slope, act, full, wu, vecs)


def column_of(row_ref):
    count = row_ref.shape[1]
    row = lax.broadcasted_iota(jnp.int32, (count, count), 0)
    col = lax.broadcasted_iota(jnp.int32, (count, count), 1)
    values = jnp.broadcast_to(row_ref[...].astype(f32), (count, count))
    return jnp.sum(jnp.where(row == col, values, 0.0), axis=1, keepdims=True)


def pack_kernel(odd_ref, *refs):
    bias_refs, (up_bias_ref, o_ref, down_ref, q_ref, k_ref, v_ref, up_ref) = refs[:8], refs[8:15]
    out_ref, low_s, high_s = refs[15:]
    rows = o_ref.shape[0]
    odd = odd_ref[0]
    shift = lax.broadcasted_iota(jnp.int32, (192, WIN), 1) - lax.broadcasted_iota(
        jnp.int32, (192, WIN), 0
    )
    move = jnp.where(shift == 64 * odd, 1.0, 0.0).astype(bf16)

    def padded(weight, column):
        lane = lax.broadcasted_iota(jnp.int32, (weight.shape[0], WIN), 1)
        moved = mm(weight, move, NN)
        return jnp.where(lane == 192 * (1 - odd), column, moved)

    columns = [column_of(ref) for ref in bias_refs]
    out_ref[:, :D] = o_ref[...]
    out_ref[:, D : 2 * D] = down_ref[...]
    sources = ((q_ref, columns[6]), (k_ref, jnp.zeros((rows, 1), f32)), (v_ref, columns[7]))
    for which, (ref, column) in enumerate(sources):
        start = 2 * D + WIN * which
        out_ref[:, start : start + WIN] = padded(ref[...], column).astype(bf16)
    up = padded(up_ref[...], column_of(up_bias_ref))
    low_s[...] = up[:, :128]
    high_s[...] = up[:, 128:]
    for j in range(4):
        for half, source in enumerate((low_s, high_s)):
            start = 3 * D + WIN * j + 128 * half
            out_ref[:, start : start + 128] = source[pl.ds(j, rows, stride=4), :].astype(bf16)
    lane = lax.broadcasted_iota(jnp.int32, (rows, 128), 1)
    small = jnp.zeros((rows, 128), f32)
    for index, column in enumerate(columns[:6]):
        small = jnp.where(lane == index, column, small)
    out_ref[:, 3 * D + 4 * WIN :] = small.astype(bf16)


def pack(odd, biases, up_bias, o_weight, down_weight, in_weights, up_weight):
    rows = o_weight.shape[0]
    arrays = [bias[None, :] for bias in (*biases, up_bias)]
    arrays += [o_weight, down_weight, *in_weights, up_weight]
    return pl.pallas_call(
        pack_kernel,
        name="pack",
        grid_spec=pltpu.PrefetchScalarGridSpec(
            num_scalar_prefetch=1,
            grid=(1,),
            in_specs=[whole(array.shape) for array in arrays],
            out_specs=[kept((rows, ALL_COLS))],
            scratch_shapes=[pltpu.VMEM((4 * rows, 128), f32)] * 2,
        ),
        out_shape=[struct((rows, ALL_COLS), bf16)],
        compiler_params=PARAMS,
        cost_estimate=pl.CostEstimate(flops=0, bytes_accessed=400_000, transcendentals=0),
    )(odd.astype(jnp.int32).reshape(1), *arrays)[0]


def minor_of(count):
    return max(2, count // 4)


def spread_kernel(sizes, orders, lanes, *refs):
    held_ref, full_ref, own_sem, send_sems, recv_sems = refs
    minor = sizes[3]
    dp, fsdp = lax.axis_index("dp"), lax.axis_index("fsdp")
    spot = (dp // 2, dp % 2, fsdp // minor, fsdp % minor)
    done = (2,) if 2 not in orders[0] else ()
    lead = 4 if done else 1

    def device(place):
        return (place[0] * 2 + place[1], place[2] * minor + place[3])

    def moved(dim, shift):
        place = list(spot)
        place[dim] = lax.rem(place[dim] + shift, sizes[dim])
        return tuple(place)

    def region(place, gathered):
        index = tuple(slice(None) if d in gathered else place[d] for d in range(4))
        return index if lead == 4 else (index[2],)

    barrier = pltpu.get_barrier_semaphore()
    peers = [(dim, shift) for dim in orders[0] for shift in range(1, sizes[dim])]
    for dim, shift in peers:
        pl.semaphore_signal(
            barrier,
            inc=1,
            device_id=device(moved(dim, shift)),
            device_id_type=pl.DeviceIdType.MESH,
        )
    own = pltpu.make_async_copy(held_ref, full_ref.at[region(spot, done)], own_sem)
    own.start()
    pl.semaphore_wait(barrier, len(peers))
    slot_of = {}

    def copy(route, stage, shift, place, target):
        gathered = done + orders[route][:stage]
        slot = slot_of.setdefault((route, stage, shift), len(slot_of))
        window = full_ref.at[region(place, gathered)]
        window = window.at[(slice(None),) * (len(window.shape) - 1) + (lanes[route],)]
        source = window
        if stage == 0:
            source = held_ref.at[(slice(None),) * (len(held_ref.shape) - 1) + (lanes[route],)]
        return pltpu.make_async_remote_copy(
            src_ref=source,
            dst_ref=window,
            send_sem=send_sems.at[slot],
            recv_sem=recv_sems.at[slot],
            device_id=device(target),
            device_id_type=pl.DeviceIdType.MESH,
        )

    def shifts(route, stage):
        return range(1, sizes[orders[route][stage]])

    def arrived(route, stage):
        dim = orders[route][stage]
        for shift in shifts(route, stage):
            came = moved(dim, sizes[dim] - shift)
            copy(route, stage, shift, came, came).wait_recv()

    sent = []
    for stage in range(len(orders[0])):
        for route, order in enumerate(orders):
            if stage > 0:
                arrived(route, stage - 1)
            if stage == 1 and route == 0:
                own.wait()
            for shift in shifts(route, stage):
                one = copy(route, stage, shift, spot, moved(order[stage], shift))
                one.start()
                sent.append(one)
    if len(orders[0]) == 1:
        own.wait()
    for route in range(len(orders)):
        arrived(route, len(orders[0]) - 1)
    for one in sent:
        one.wait_send()


def spread_call(held, sizes, orders, lanes, shape, space, identity):
    copies = len(orders) * sum(sizes[dim] - 1 for dim in orders[0])
    return pl.pallas_call(
        functools.partial(spread_kernel, sizes, orders, lanes),
        name="spread",
        in_specs=[pl.BlockSpec(memory_space=pltpu.VMEM)],
        out_specs=pl.BlockSpec(memory_space=space),
        out_shape=struct(shape, bf16),
        scratch_shapes=[
            pltpu.SemaphoreType.DMA(()),
            pltpu.SemaphoreType.DMA((copies,)),
            pltpu.SemaphoreType.DMA((copies,)),
        ],
        compiler_params=pltpu.CompilerParams(
            collective_id=identity, has_side_effects=True, vmem_limit_bytes=63_000_000
        ),
        cost_estimate=pl.CostEstimate(flops=0, bytes_accessed=100_000_000, transcendentals=0),
    )(held)


def sizes_of(dp, fsdp):
    minor = minor_of(fsdp)
    return (dp // 2, 2, fsdp // minor, minor)


def spread_far(packed, sizes):
    whole_lanes = (pl.ds(0, packed.shape[1]),)
    shape = (sizes[2], *packed.shape)
    return spread_call(packed, sizes, ((2,),), whole_lanes, shape, pltpu.VMEM, 0)


def spread_near(held, sizes):
    _, rows, cols = held.shape
    lanes = (pl.ds(0, SPLIT), pl.ds(SPLIT, cols - SPLIT))
    orders = ((3, 0, 1), (0, 3, 1))
    full = spread_call(held, sizes, orders, lanes, (*sizes, rows, cols), pltpu.HBM, 1)
    return full.reshape(-1, cols)


def source_of(len_ref, perm_ref, place):
    first = perm_ref[place - place % 2]
    second = perm_ref[place - place % 2 + 1]
    swapped = (len_ref[first] < len_ref[second]).astype(jnp.int32)
    return jnp.where(swapped == place % 2, first, second)


def moved_rows(source_at, rows_refs, out_ref, buffer_ref, in_sems, out_sems):
    count = out_ref.shape[0] // STEPS

    def group(step):
        return pl.ds(step * count, count)

    for step in range(STEPS):

        def one(index, carry):
            place = step * count + index
            source = source_at(place)
            lane = 0
            for which, rows_ref in enumerate(rows_refs):
                width = rows_ref.shape[2]
                pltpu.make_async_copy(
                    rows_ref.at[source],
                    buffer_ref.at[place, :, pl.ds(lane, width)],
                    in_sems.at[step, which],
                ).start()
                lane += width
            return carry

        lax.fori_loop(0, count, one, 0)
    for step in range(STEPS):
        lane = 0
        for which, rows_ref in enumerate(rows_refs):
            width = rows_ref.shape[2]
            pltpu.make_async_copy(
                rows_ref.at[group(step)],
                buffer_ref.at[group(step), :, pl.ds(lane, width)],
                in_sems.at[step, which],
            ).wait()
            lane += width
        pltpu.make_async_copy(
            buffer_ref.at[group(step)], out_ref.at[group(step)], out_sems.at[step]
        ).start()
    for step in range(STEPS):
        pltpu.make_async_copy(
            buffer_ref.at[group(step)], out_ref.at[group(step)], out_sems.at[step]
        ).wait()


def moved_call(kernel, name, parts, lengths, permutation):
    total, size, _ = parts[0].shape
    shape = (total, size, sum(part.shape[2] for part in parts))
    return pl.pallas_call(
        kernel,
        name=name,
        grid_spec=pltpu.PrefetchScalarGridSpec(
            num_scalar_prefetch=2,
            grid=(1,),
            in_specs=[pl.BlockSpec(memory_space=pltpu.HBM)] * len(parts),
            out_specs=[pl.BlockSpec(memory_space=pltpu.HBM)],
            scratch_shapes=[
                pltpu.VMEM(shape, bf16),
                pltpu.SMEM((total,), jnp.int32),
                pltpu.SemaphoreType.DMA((STEPS, len(parts))),
                pltpu.SemaphoreType.DMA((STEPS,)),
            ],
        ),
        out_shape=[struct(shape, bf16)],
        compiler_params=PARAMS,
        cost_estimate=pl.CostEstimate(flops=0, bytes_accessed=100_000, transcendentals=0),
    )(lengths, permutation, *parts)[0]


def deal_kernel(len_ref, perm_ref, rows_ref, out_ref, buffer_ref, place_s, in_sems, out_sems):
    source_at = lambda place: source_of(len_ref, perm_ref, place)
    moved_rows(source_at, [rows_ref], out_ref, buffer_ref, in_sems, out_sems)


def deal(rows, lengths, permutation):
    return moved_call(deal_kernel, "deal", [rows], lengths, permutation)


def restore_kernel(len_ref, perm_ref, *refs):
    part_refs, (out_ref, buffer_ref, place_s, in_sems, out_sems) = refs[:-5], refs[-5:]

    def note(index, carry):
        place_s[source_of(len_ref, perm_ref, index)] = index
        return carry

    lax.fori_loop(0, out_ref.shape[0], note, 0)
    moved_rows(lambda place: place_s[place], part_refs, out_ref, buffer_ref, in_sems, out_sems)


def restore(parts, lengths, permutation):
    return moved_call(restore_kernel, "restore", parts, lengths, permutation)


def pick(values, index):
    return values.at[index].get(mode="promise_in_bounds")


def tie(*values):
    return lax.optimization_barrier(values)


def on_device(
    tokens, cotangent, lengths, permutation, q_weight, q_bias, k_weight, v_weight, v_bias, o_weight,
    o_bias, norm1_gain, norm1_bias, up_weight, up_bias, down_weight, down_bias, norm2_gain,
    norm2_bias,
):
    devices = lax.axis_size(AXES)
    my_index = lax.axis_index(AXES)
    seq_total, piece_len, _ = tokens.shape
    seq_dev = seq_total // devices
    rows_dev = q_weight.shape[0]
    up_dev = up_weight.shape[0]
    odd = (my_index // (devices // 4)) % 2 == 1

    def padded(weight, bias):
        column = bias[:, None]
        gap = jnp.zeros((weight.shape[0], 63), bf16)
        return jnp.where(
            odd,
            jnp.concatenate([column, gap, weight], axis=1),
            jnp.concatenate([weight, column, gap], axis=1),
        )

    if rows_dev % 8 == 0:
        packed = pack(
            odd,
            [o_bias, norm1_gain, norm1_bias, down_bias, norm2_gain, norm2_bias, q_bias, v_bias],
            up_bias, o_weight, down_weight, [q_weight, k_weight, v_weight], up_weight,
        )
    else:
        small = [o_bias, norm1_gain, norm1_bias, down_bias, norm2_gain, norm2_bias]
        packed = jnp.concatenate(
            [
                o_weight,
                down_weight,
                padded(q_weight, q_bias),
                padded(k_weight, jnp.zeros_like(q_bias)),
                padded(v_weight, v_bias),
                padded(up_weight, up_bias).reshape(rows_dev, 4 * WIN),
                jnp.pad(jnp.stack(small, axis=1), ((0, 0), (0, 122))),
            ],
            axis=1,
        )

    dealt_lengths = pick(lengths, permutation).reshape(devices, seq_dev)
    chunks = lax.axis_size("dp")
    parity = lax.axis_index("dp") % 2
    pairing = [(i, i ^ 1) for i in range(chunks)]
    len_arr = jnp.stack(
        [jnp.max(lax.dynamic_slice_in_dim(dealt_lengths, my_index, 1, 0)), parity]
    ).astype(jnp.int32)

    def swap_blocks(rows):
        return lax.all_to_all(rows, AXES, split_axis=0, concat_axis=0, tiled=True)

    def arrive(rows):
        width = rows.shape[-1]
        moved = swap_blocks(rows.reshape(devices, seq_dev, piece_len, width))
        if piece_len == BLOCK:
            return moved
        moved = moved.transpose(1, 0, 2, 3).reshape(seq_dev, SEQ // BLOCK, BLOCK, width)
        return moved.transpose(1, 0, 2, 3)

    def leave(rows):
        width = rows.shape[-1]
        if piece_len != BLOCK:
            rows = rows.transpose(1, 0, 2, 3).reshape(seq_dev, devices, piece_len, width)
            rows = rows.transpose(1, 0, 2, 3)
        return swap_blocks(rows).reshape(seq_total, piece_len, width)

    fsdp = lax.axis_size("fsdp")
    minor = minor_of(fsdp)
    major = fsdp // minor
    place = (lax.axis_index("dp") // 2, lax.axis_index("fsdp") // minor, my_index % minor)

    def target_of(device, far, high, low):
        dp_index, rest = device // fsdp, device % fsdp
        dp_index = (dp_index + 2 * far) % chunks
        rest = (rest // minor + high) % major * minor + (rest % minor + low) % minor
        return dp_index * fsdp + rest

    def send_blocks(partial, shifts, block_of):
        parts = [block_of(0, 0, 0)]
        for shift in shifts:
            route = [(i, target_of(i, *shift)) for i in range(devices)]
            parts.append(lax.ppermute(block_of(*shift), AXES, route))
        return parts

    def send_near(partial):
        shape = (chunks // 2, major, minor, rows_dev, partial.shape[-1])
        blocks = partial.reshape(shape)

        def block_of(far, high, low):
            start = ((place[0] + far) % shape[0], 0, (place[2] + low) % minor, 0, 0)
            return lax.dynamic_slice(blocks, start, (1, major, 1, *shape[3:]))

        shifts = [(far, 0, low) for far in range(shape[0]) for low in range(minor)][1:]
        return send_blocks(blocks, shifts, block_of)

    def send_far(partial):
        blocks = partial.reshape(major, rows_dev, partial.shape[-1])

        def block_of(far, high, low):
            return lax.dynamic_index_in_dim(blocks, (place[1] + high) % major, 0, False)

        return send_blocks(blocks, [(0, high, 0) for high in range(1, major)], block_of)

    def total(parts):
        result = sum(part.astype(f32) for part in parts)
        return result.reshape(-1, result.shape[-1])

    def total_low(parts):
        return total(parts).astype(bf16)

    dealt_tok = deal(tokens, lengths, permutation)
    dealt_cot = deal(cotangent, lengths, permutation)
    if rows_dev % 8 == 0:
        sizes = sizes_of(chunks, lax.axis_size("fsdp"))
        packed, dealt_tok = tie(packed, dealt_tok)
        held = spread_far(packed, sizes)
        dealt_tok, held = tie(dealt_tok, held)
        tok = arrive(dealt_tok)
        held, dealt_cot = tie(held, dealt_cot)
        full = spread_near(held, sizes)
    else:
        tok = arrive(dealt_tok)
        full = lax.all_gather(packed, AXES, axis=0, tiled=True)
    wu = full[:, 3 * D : 3 * D + 4 * WIN].reshape(FF, WIN)
    vecs = jnp.pad(full[:, 3 * D + 4 * WIN : 3 * D + 4 * WIN + 6].astype(f32).T, ((0, 2), (0, 0)))
    dealt_cot, tok, full, wu, vecs, len_arr = tie(dealt_cot, tok, full, wu, vecs, len_arr)
    cot = arrive(dealt_cot)

    x0, qa0, ka0, va0, ctx0 = attn_fwd(len_arr, tok, full, 0)
    x1, qa1, ka1, va1, ctx1 = attn_fwd(len_arr, tok, full, 1)
    out, n1, n2, inv, slope, act, stat = mid_fwd(len_arr, x0, x1, ctx0, ctx1, full, wu, vecs)
    cot, out = tie(cot, out)
    back_out = leave(out)
    gctx, base, mine, given = mid_bwd(
        len_arr, cot, ctx0, ctx1, n1, n2, inv, slope, act, full, wu, vecs, chunks
    )
    mine = total_low([mine, lax.ppermute(given, "dp", pairing)])
    gctx, mine = tie(gctx, mine)
    parts = send_near(mine)
    ig0, dw0, given0 = attn_bwd(
        len_arr, qa0, ka0, va0, ctx0, gctx, x0, base, full, 0, chunks
    )
    ig0, dw0, given0, gctx, back_out, *parts = tie(ig0, dw0, given0, gctx, back_out, *parts)
    back0 = leave(ig0)
    given0 = lax.ppermute(given0, "dp", pairing)
    parts = send_far(total_low(parts))
    ig1, dw1, given1 = attn_bwd(
        len_arr, qa1, ka1, va1, ctx1, gctx, x1, base, full, 1, chunks
    )
    ig1, dw0, dw1, given0, given1, back0, *parts = tie(
        ig1, dw0, dw1, given0, given1, back0, *parts
    )
    back1 = leave(ig1)
    given1 = lax.ppermute(given1, "dp", pairing)
    mine_in = jnp.concatenate([total_low([dw0, given0]), total_low([dw1, given1])], axis=0)
    parts_in = send_near(mine_in)
    back_out, stat, dealt_lengths, *parts = tie(back_out, stat, dealt_lengths, *parts)
    mine = total(parts)
    mine_in = total(send_far(total_low(parts_in)))

    swap = dealt_lengths[:, 0] < dealt_lengths[:, 1]
    my_swap = lax.dynamic_index_in_dim(swap, my_index, 0, False)
    output = restore([back_out], lengths, permutation)
    input_grad = restore([back0, back1], lengths, permutation)
    lens = jnp.stack([len_arr[0], ROWS - len_arr[0]]).astype(f32)
    sums = jnp.stack([stat[4:8, 0], stat[0:4, 0] - stat[4:8, 0]], axis=1)
    rms = jnp.sqrt(sums / (lens[None, :] * D) + rms_eps)
    stream_rms = jnp.where(my_swap, rms[:, ::-1], rms)
    vec = lambda i: mine[:, 2 * D + 4 * WIN + i]

    def unpadded(block):
        return (
            jnp.where(odd, block[:, 64:], block[:, :192]),
            jnp.where(odd, block[:, 0], block[:, 192]),
        )

    dq, dqb = unpadded(mine_in[:, :WIN])
    dk, _ = unpadded(mine_in[:, WIN : 2 * WIN])
    dv, dvb = unpadded(mine_in[:, 2 * WIN :])
    dup, dub = unpadded(mine[:, 2 * D : 2 * D + 4 * WIN].reshape(up_dev, WIN))
    return (
        output, input_grad, dq, dqb, dk, dv, dvb, mine[:, :D], vec(0), vec(1), vec(2), dup, dub,
        mine[:, D : 2 * D], vec(3), vec(4), vec(5), stream_rms,
    )


def solution(mesh):
    rows = P(None, AXES, None)
    mat = P(AXES, None)
    vec = P(AXES)
    in_specs = (
        rows, rows, P(), P(), mat, vec, mat, mat, vec, mat, vec, vec, vec, mat, vec, mat, vec, vec,
        vec,
    )
    out_specs = (
        rows, rows, mat, vec, mat, mat, vec, mat, vec, vec, vec, mat, vec, mat, vec, vec, vec,
        P(None, AXES),
    )
    return jax.shard_map(
        on_device, mesh=mesh, in_specs=in_specs, out_specs=out_specs, check_vma=False
    )
```

```python
import functools

import jax
import jax.numpy as jnp
from jax import lax
from jax.experimental import pallas as pl
from jax.experimental.pallas import tpu as pltpu
from jax.sharding import PartitionSpec as P

AXES = ("dp", "fsdp")
D = 768
FF = 3072
HALF = D // 2
HEAD = 64
WIN = 256
SEQ = 1024
SHORT = 64
BLOCK = 32
ROWS = SEQ + SHORT
TILE = 272
TILES = ROWS // TILE
ATTN_TILE = 544
ATTN_TILES = ROWS // ATTN_TILE
BIG = 1e30
STEPS = 4
SPLIT = 1664

norm_eps = 1e-12
rms_eps = 1e-06
bf16 = jnp.bfloat16
f32 = jnp.float32

NN = (((1,), (0,)), ((), ()))
NT = (((1,), (1,)), ((), ()))
TN = (((0,), (0,)), ((), ()))


def mm(left, right, dims):
    return lax.dot_general(left, right, dims, preferred_element_type=f32)


def exchange():
    row = lax.broadcasted_iota(jnp.int32, (WIN, WIN), 0)
    col = lax.broadcasted_iota(jnp.int32, (WIN, WIN), 1)
    return jnp.where(row + col == WIN - 1, 1.0, 0.0).astype(bf16)


def row_ids(start, count, width):
    return start + lax.broadcasted_iota(jnp.int32, (count, width), 0)


def block_rows(ref, seq, start, count):
    values = ref[start // BLOCK : (start + count) // BLOCK, seq]
    return values.reshape(count, values.shape[-1])


def merge_rows(pair_ref, packed_ref, first_len):
    width = packed_ref.shape[1]
    flip = exchange()
    packed_ref[0:SHORT, :] = block_rows(pair_ref, 0, 0, SHORT)
    for step in range(SEQ // WIN):
        start = SHORT + WIN * step
        flipped = mm(flip, block_rows(pair_ref, 1, SEQ - WIN * (step + 1), WIN), NN)
        inside = min(WIN, SEQ - start)
        own = block_rows(pair_ref, 0, start, inside).astype(f32)
        keep = row_ids(start, inside, width) < first_len
        packed_ref[start : start + inside, :] = jnp.where(keep, own, flipped[0:inside]).astype(bf16)
        if inside < WIN:
            packed_ref[start + inside : start + WIN, :] = flipped[inside:].astype(bf16)


def unmerge_rows(packed_ref, pair_ref, first_len):
    width = packed_ref.shape[1]
    flip = exchange()
    blocks = WIN // BLOCK
    for step in range(SEQ // WIN):
        start = WIN * step
        ids = row_ids(start, WIN, width)
        own = packed_ref[start : start + WIN, :].astype(f32)
        own = jnp.where(ids < first_len, own, 0.0).astype(bf16)
        pair_ref[blocks * step : blocks * (step + 1), 0] = own.reshape(blocks, BLOCK, width)
        source = ROWS - WIN * (step + 1)
        flipped = mm(flip, packed_ref[source : source + WIN, :], NN)
        flipped = jnp.where(ids < ROWS - first_len, flipped, 0.0).astype(bf16)
        pair_ref[blocks * step : blocks * (step + 1), 1] = flipped.reshape(blocks, BLOCK, width)


def spare_of(group):
    return 192 if group % 2 == 0 else 0


def with_ones(window, group):
    lane = lax.broadcasted_iota(jnp.int32, window.shape, 1)
    return jnp.where(lane == spare_of(group), 1.0, window.astype(f32)).astype(bf16)


def without_bias(window, group):
    lane = lax.broadcasted_iota(jnp.int32, window.shape, 1)
    return jnp.where(lane == spare_of(group), 0.0, window.astype(f32)).astype(bf16)


def first_row(group):
    return 0 if group % 2 == 0 else 64


def windows(values, count):
    parts = []
    for group in range(count):
        start = (group // 2) * HALF + (group % 2) * 128
        parts.append(values[:, start : start + WIN])
    return parts


def join(parts):
    pieces = []
    for first, second in zip(parts[0::2], parts[1::2]):
        pieces += [first[:, :128], first[:, 128:] + second[:, :128], second[:, 128:]]
    return jnp.concatenate(pieces, axis=1)


def split_three(value):
    high = value.astype(bf16)
    rest = value - high.astype(f32)
    mid = rest.astype(bf16)
    low = (rest - mid.astype(f32)).astype(bf16)
    return high, mid, low


def attn_fwd_kernel(
    len_ref, tok_ref, full_ref, x_ref, qa_ref, ka_ref, va_ref, ctx_ref, q_s, k_s, v_s, w_s
):
    pair = pl.program_id(0)
    first_len = len_ref[0]

    @pl.when(pair == 0)
    def _():
        merge_rows(tok_ref, x_ref, first_len)
        w_s[...] = jnp.zeros_like(w_s)
        for which in range(3):
            for g in range(2):
                w_s[which, g, first_row(g) : first_row(g) + 192, :] = full_ref[
                    192 * g : 192 * (g + 1), WIN * which : WIN * (which + 1)
                ]
        cols = [with_ones(part, g) for g, part in enumerate(windows(x_ref[...], 2))]
        for which, target in enumerate((q_s, k_s, v_s)):
            value = join([mm(cols[g], w_s[which, g], NT) for g in range(2)])
            if which == 0:
                value = value.astype(bf16).astype(f32) * (HEAD**-0.5)
            target[...] = value.astype(bf16)

    lane0 = pl.multiple_of(pair * 128, 128)
    q_pair = q_s[:, pl.ds(lane0, 128)]
    k_pair = k_s[:, pl.ds(lane0, 128)]
    v_pair = v_s[:, pl.ds(lane0, 128)]
    lane = lax.broadcasted_iota(jnp.int32, (ROWS, 128), 1)
    in_first = row_ids(0, ROWS, 128) < first_len
    one = jnp.ones((ROWS, 128), f32)
    zero = jnp.zeros((ROWS, 128), f32)
    for head in range(2):
        spare = 64 * (1 - head)
        own = (lane // 64) == head
        first_one = jnp.where(in_first, one, zero)
        q_extra = jnp.where(
            lane == spare, first_one, jnp.where(lane == spare + 1, one - first_one, zero)
        )
        k_extra = jnp.where(
            lane == spare,
            (first_one - one) * BIG,
            jnp.where(
                lane == spare + 1,
                first_one * (-BIG),
                jnp.where((lane >= spare + 2) & (lane < spare + 5), one, zero),
            ),
        )
        v_extra = jnp.where((lane >= spare) & (lane < spare + 3), one, zero)
        cols = slice(128 * head, 128 * (head + 1))
        qa_ref[:, cols] = jnp.where(own, q_pair.astype(f32), q_extra).astype(bf16)
        ka_ref[:, cols] = jnp.where(own, k_pair.astype(f32), k_extra).astype(bf16)
        va_ref[:, cols] = jnp.where(own, v_pair.astype(f32), v_extra).astype(bf16)

    tile_lane = lax.broadcasted_iota(jnp.int32, (ATTN_TILE, 128), 1)

    def one_tile(index, carry):
        start = pl.multiple_of(index * ATTN_TILE, 16)
        rows = pl.ds(start, ATTN_TILE)
        result = None
        for head in range(2):
            cols = slice(128 * head, 128 * (head + 1))
            spare = 64 * (1 - head)
            q_tile = qa_ref[rows, cols]
            scores = mm(q_tile, ka_ref[:, cols], NT)
            top = jnp.max(scores, axis=1, keepdims=True)
            weights = jnp.exp(scores - top)
            mixed = mm(weights.astype(bf16), va_ref[:, cols], NN)
            total = mixed[:, spare : spare + 1]
            mixed = mixed / total
            log_total = top + jnp.log(total)
            high, mid, low = split_three(-log_total)
            q_new = jnp.where(
                tile_lane == spare + 2,
                high.astype(f32),
                jnp.where(
                    tile_lane == spare + 3,
                    mid.astype(f32),
                    jnp.where(tile_lane == spare + 4, low.astype(f32), q_tile.astype(f32)),
                ),
            )
            qa_ref[rows, cols] = q_new.astype(bf16)
            result = mixed if head == 0 else jnp.where(tile_lane < 64, result, mixed)
        ctx_ref[rows, :] = result.astype(bf16)
        return carry

    lax.fori_loop(0, ATTN_TILES, one_tile, 0)


def attn_bwd_kernel(
    len_ref, qa_ref, ka_ref, va_ref, ctx_ref, gctx_ref, x_ref, base_ref, full_ref,
    ig_ref, kept_ref, given_ref, dq_s, dk_s, dv_s, do_s, dqt_s, ig_s, w_s, dw_ref,
):
    pair = pl.program_id(0)
    lane0 = pl.multiple_of(pair * 128, 128)
    lane = lax.broadcasted_iota(jnp.int32, (ROWS, 128), 1)
    grad = gctx_ref[...].astype(f32)
    product = grad * ctx_ref[...].astype(f32)
    for head in range(2):
        own = (lane // 64) == head
        spare = 64 * (1 - head)
        inner = -jnp.sum(jnp.where(own, product, 0.0), axis=1, keepdims=True)
        high, mid, low = split_three(inner)
        extra = jnp.where(
            lane == spare,
            high.astype(f32),
            jnp.where(
                lane == spare + 1,
                mid.astype(f32),
                jnp.where(lane == spare + 2, low.astype(f32), 0.0),
            ),
        )
        do_s[:, 128 * head : 128 * (head + 1)] = jnp.where(own, grad, extra).astype(bf16)
    dqt_s[...] = jnp.zeros_like(dqt_s)
    tile_lane = lax.broadcasted_iota(jnp.int32, (ATTN_TILE, 128), 1)

    def one_tile(index, carry):
        start = pl.multiple_of(index * ATTN_TILE, 16)
        rows = pl.ds(start, ATTN_TILE)
        dk_tile = None
        dv_tile = None
        for head in range(2):
            cols = slice(128 * head, 128 * (head + 1))
            k_tile = ka_ref[rows, cols]
            probs = jnp.exp(mm(k_tile, qa_ref[:, cols], NT))
            scaled = mm(va_ref[rows, cols], do_s[:, cols], NT) * probs
            grad_scores = scaled.astype(bf16)
            dv_new = mm(probs.astype(bf16), do_s[:, cols], NN)
            dk_new = mm(grad_scores, qa_ref[:, cols], NN)
            dq_new = mm(k_tile, grad_scores, TN)
            dqt_s[64 * head : 64 * (head + 1), :] += dq_new[64 * head : 64 * (head + 1), :]
            dk_tile = dk_new if head == 0 else jnp.where(tile_lane < 64, dk_tile, dk_new)
            dv_tile = dv_new if head == 0 else jnp.where(tile_lane < 64, dv_tile, dv_new)
        dk_s[rows, pl.ds(lane0, 128)] = dk_tile.astype(bf16)
        dv_s[rows, pl.ds(lane0, 128)] = dv_tile.astype(bf16)
        return carry

    lax.fori_loop(0, ATTN_TILES, one_tile, 0)
    dq_s[:, pl.ds(lane0, 128)] = (jnp.transpose(dqt_s[...]) * (HEAD**-0.5)).astype(bf16)

    @pl.when(pair == pl.num_programs(0) - 1)
    def _():
        x_cols = [with_ones(part, g) for g, part in enumerate(windows(x_ref[...], 2))]
        total = [None, None]
        for which, source in enumerate((dq_s, dk_s, dv_s)):
            cols = windows(source[...], 2)
            for g in range(2):
                own = slice(first_row(g), first_row(g) + 192)
                w_s[own, :] = without_bias(
                    full_ref[192 * g : 192 * (g + 1), WIN * which : WIN * (which + 1)], g
                )
                if first_row(g) == 0:
                    w_s[192:, :] = jnp.zeros((64, WIN), bf16)
                else:
                    w_s[:64, :] = jnp.zeros((64, WIN), bf16)
                grad = mm(cols[g], x_cols[g], TN)
                dw_ref[192 * g : 192 * (g + 1), WIN * which : WIN * (which + 1)] = grad[own].astype(
                    bf16
                )
                part = mm(cols[g], w_s[...], NN)
                total[g] = part if which == 0 else total[g] + part
        ig_s[...] = (join(total) + base_ref[...]).astype(bf16)
        unmerge_rows(ig_s, ig_ref, len_ref[0])
        split_chunks(dw_ref, kept_ref, given_ref, len_ref[1])


def split_chunks(rows_ref, kept_ref, given_ref, parity):
    pairs, size, _ = kept_ref.shape
    for own in range(2):

        @pl.when(parity == own)
        def _():
            for pair in range(pairs):
                for which in range(2):
                    start = (2 * pair + which) * size
                    target = kept_ref if which == own else given_ref
                    target[pair] = rows_ref[start : start + size, :]


def norm(values):
    mean = jnp.mean(values, axis=1, keepdims=True)
    centered = values - mean
    var = jnp.mean(centered * centered, axis=1, keepdims=True)
    inv = lax.rsqrt(var + norm_eps)
    return centered * inv, inv


def norm_back(grad_n, n, inv):
    mean_g = jnp.mean(grad_n, axis=1, keepdims=True)
    mean_gn = jnp.mean(grad_n * n, axis=1, keepdims=True)
    return (grad_n - mean_g - n * mean_gn) * inv


def mid_fwd_kernel(
    len_ref, x0_ref, x1_ref, ctx0_ref, ctx1_ref, full_ref, wu_ref, vec_ref,
    out_ref, n1_ref, n2_ref, inv_ref, slope_ref, act_ref, stat_ref,
    out_s, wd_s, stat_s,
):
    step = pl.program_id(0)
    first_len = len_ref[0]

    @pl.when(step == 0)
    def _():
        stat_s[...] = jnp.zeros_like(stat_s)
        wd_s[...] = jnp.zeros_like(wd_s)
        for g in range(4):
            wd_s[g, first_row(g) : first_row(g) + 192, :] = full_ref[192 * g : 192 * (g + 1), D:]

    o_bias, gain1, shift1, down_bias, gain2, shift2 = (vec_ref[i : i + 1, :] for i in range(6))
    start = pl.multiple_of(step * TILE, 16)
    rows = pl.ds(start, TILE)
    keep = jnp.where(row_ids(start, TILE, D) < first_len, 1.0, 0.0)

    def note(slot, values):
        square = values * values
        stat_s[slot : slot + 1, :] += jnp.sum(square, axis=0, keepdims=True)
        stat_s[slot + 4 : slot + 5, :] += jnp.sum(square * keep, axis=0, keepdims=True)

    inputs = jnp.concatenate([x0_ref[...], x1_ref[...]], axis=1).astype(f32)
    context = jnp.concatenate([ctx0_ref[...], ctx1_ref[...]], axis=1)
    note(0, inputs)
    branch_attn = mm(context, full_ref[:, :D], NT) + o_bias
    note(1, branch_attn)
    n1, inv1 = norm(inputs + branch_attn)
    n1_ref[...] = n1
    first_norm = n1 * gain1 + shift1
    note(2, first_norm)
    low_cols = windows(first_norm.astype(bf16), 4)
    parts = []
    for g in range(4):
        cols = slice(D * g, D * (g + 1))
        up = mm(with_ones(low_cols[g], g), wu_ref[D * g : D * (g + 1), :], NT)
        gate = 0.5 * (1.0 + lax.erf(up * (2.0**-0.5)))
        slope_ref[:, cols] = gate + up * jnp.exp(up * up * -0.5) * 0.3989422804014327
        act = (up * gate).astype(bf16)
        act_ref[:, cols] = act
        parts.append(mm(act, wd_s[g], NT))
    branch_ffn = join(parts) + down_bias
    note(3, branch_ffn)
    n2, inv2 = norm(first_norm + branch_ffn)
    n2_ref[...] = n2
    lane = lax.broadcasted_iota(jnp.int32, (TILE, 128), 1)
    inv_ref[...] = jnp.where(lane < 64, inv1, inv2)
    out_s[rows, :] = (n2 * gain2 + shift2).astype(bf16)

    @pl.when(step == pl.num_programs(0) - 1)
    def _():
        unmerge_rows(out_s, out_ref, first_len)
        stat_ref[...] = jnp.broadcast_to(
            jnp.sum(stat_s[...], axis=1, keepdims=True), stat_ref.shape
        )


def mid_bwd_kernel(
    len_ref, cot_ref, ctx0_ref, ctx1_ref, n1_ref, n2_ref, inv_ref, slope_ref, act_ref,
    full_ref, wu_ref, vec_ref, gctx_ref, base_ref, kept_ref, given_ref,
    cot_s, wd_s, dwo_s, dwd_s, dwu_s, vec_s, turn_s, grad_ref,
):
    step = pl.program_id(0)

    @pl.when(step == 0)
    def _():
        merge_rows(cot_ref, cot_s, len_ref[0])
        for target in (dwo_s, dwd_s, dwu_s, vec_s, wd_s):
            target[...] = jnp.zeros_like(target)
        for g in range(4):
            wd_s[g, first_row(g) : first_row(g) + 192, :] = full_ref[192 * g : 192 * (g + 1), D:]

    gain1, shift1, gain2 = (vec_ref[i : i + 1, :] for i in (1, 2, 4))
    start = pl.multiple_of(step * TILE, 16)
    rows = pl.ds(start, TILE)

    def add_vec(slot, values):
        vec_s[slot : slot + 1, :] += jnp.sum(values, axis=0, keepdims=True)

    context = jnp.concatenate([ctx0_ref[...], ctx1_ref[...]], axis=1)
    n1 = n1_ref[...]
    n2 = n2_ref[...]
    inv1 = inv_ref[:, 0:1]
    inv2 = inv_ref[:, 64:65]
    low_cols = windows((n1 * gain1 + shift1).astype(bf16), 4)
    grad_out = cot_s[rows, :].astype(f32)
    add_vec(4, grad_out * n2)
    add_vec(5, grad_out)
    grad_sum2 = norm_back(grad_out * gain2, n2, inv2)
    grad_ffn = grad_sum2.astype(bf16)
    add_vec(3, grad_ffn.astype(f32))
    ffn_cols = windows(grad_ffn, 4)
    parts = []
    for g in range(4):
        cols = slice(D * g, D * (g + 1))
        dwd_s[g] += mm(ffn_cols[g], act_ref[:, cols], TN)
        grad_up = (mm(ffn_cols[g], wd_s[g], NN) * slope_ref[:, cols]).astype(bf16)
        dwu_s[g] += mm(with_ones(low_cols[g], g), grad_up, TN)
        parts.append(mm(grad_up, without_bias(wu_ref[D * g : D * (g + 1), :], g), NN))
    grad_first = join(parts) + grad_sum2
    add_vec(1, grad_first * n1)
    add_vec(2, grad_first)
    grad_sum1 = norm_back(grad_first * gain1, n1, inv1)
    base_ref[...] = grad_sum1
    grad_branch = grad_sum1.astype(bf16)
    add_vec(0, grad_branch.astype(f32))
    dwo_s[...] += mm(grad_branch, context, TN)
    gctx_ref[...] = mm(grad_branch, full_ref[:, :D], NN).astype(bf16)

    @pl.when(step == pl.num_programs(0) - 1)
    def _():
        grad_ref[:, :D] = dwo_s[...].astype(bf16)
        for g in range(4):
            own = slice(192 * g, 192 * (g + 1))
            grad_ref[own, D : 2 * D] = dwd_s[g, first_row(g) : first_row(g) + 192, :].astype(bf16)
            turned = jnp.transpose(dwu_s[g])
            for half in range(2):
                turn_s[...] = turned[:, 128 * half : 128 * (half + 1)]
                for j in range(4):
                    lane0 = 2 * D + WIN * j + 128 * half
                    grad_ref[own, lane0 : lane0 + 128] = turn_s[pl.ds(j, 192, stride=4), :].astype(
                        bf16
                    )
        grad_ref[:, 2 * D + 4 * WIN :] = jnp.transpose(vec_s[...]).astype(bf16)
        split_chunks(grad_ref, kept_ref, given_ref, len_ref[1])


def whole(shape):
    zeros = (0,) * len(shape)
    return pl.BlockSpec(shape, lambda i, *_: zeros, pipeline_mode=pl.Buffered(1))


def kept(shape):
    zeros = (0,) * len(shape)
    return pl.BlockSpec(shape, lambda i, *_: zeros)


def struct(shape, dtype):
    return jax.ShapeDtypeStruct(shape, dtype)


PARAMS = pltpu.CompilerParams(
    dimension_semantics=("arbitrary",), vmem_limit_bytes=63_000_000
)
GRAD_COLS = 2 * D + 4 * WIN + 128
ALL_COLS = GRAD_COLS + D


def attn_fwd(len_arr, tok, full, half):
    pair_cols = lambda width: pl.BlockSpec((ROWS, width), lambda i, *_: (0, i))
    return pl.pallas_call(
        attn_fwd_kernel,
        name="attn_fwd",
        grid_spec=pltpu.PrefetchScalarGridSpec(
            num_scalar_prefetch=1,
            grid=(3,),
            in_specs=[
                pl.BlockSpec(
                    (SEQ // BLOCK, 2, BLOCK, HALF),
                    lambda i, *_: (0, 0, 0, half),
                    pipeline_mode=pl.Buffered(1),
                ),
                pl.BlockSpec((HALF, D), lambda i, *_: (half, 2), pipeline_mode=pl.Buffered(1)),
            ],
            out_specs=[
                kept((ROWS, HALF)), pair_cols(256), pair_cols(256), pair_cols(256), pair_cols(128),
            ],
            scratch_shapes=[pltpu.VMEM((ROWS, HALF), bf16)] * 3
            + [pltpu.VMEM((3, 2, WIN, WIN), bf16)],
        ),
        out_shape=[
            struct((ROWS, HALF), bf16), struct((ROWS, D), bf16), struct((ROWS, D), bf16),
            struct((ROWS, D), bf16), struct((ROWS, HALF), bf16),
        ],
        compiler_params=PARAMS,
        cost_estimate=pl.CostEstimate(
            flops=20_000_000_000, bytes_accessed=12_000_000, transcendentals=7_000_000
        ),
    )(len_arr, tok, full)


def attn_bwd(len_arr, qa, ka, va, ctx, gctx, x, base, full, half, chunks):
    part = (chunks // 4, D // chunks, D)
    pair_cols = lambda width, first: pl.BlockSpec((ROWS, width), lambda i, *_: (0, i + first))
    return pl.pallas_call(
        attn_bwd_kernel,
        name="attn_bwd",
        grid_spec=pltpu.PrefetchScalarGridSpec(
            num_scalar_prefetch=1,
            grid=(3,),
            in_specs=[
                pair_cols(256, 0), pair_cols(256, 0), pair_cols(256, 0), pair_cols(128, 0),
                pair_cols(128, 3 * half), whole(x.shape),
                pl.BlockSpec((ROWS, HALF), lambda i, *_: (0, half), pipeline_mode=pl.Buffered(1)),
                pl.BlockSpec((HALF, D), lambda i, *_: (half, 2), pipeline_mode=pl.Buffered(1)),
            ],
            out_specs=[kept((SEQ // BLOCK, 2, BLOCK, HALF)), kept(part), kept(part)],
            scratch_shapes=[
                pltpu.VMEM((ROWS, HALF), bf16),
                pltpu.VMEM((ROWS, HALF), bf16),
                pltpu.VMEM((ROWS, HALF), bf16),
                pltpu.VMEM((ROWS, 256), bf16),
                pltpu.VMEM((128, ROWS), f32),
                pltpu.VMEM((ROWS, HALF), bf16),
                pltpu.VMEM((WIN, WIN), bf16),
                pltpu.VMEM((HALF, D), bf16),
            ],
        ),
        out_shape=[
            struct((SEQ // BLOCK, 2, BLOCK, HALF), bf16), struct(part, bf16), struct(part, bf16),
        ],
        compiler_params=PARAMS,
        cost_estimate=pl.CostEstimate(
            flops=100_000_000, bytes_accessed=1_000_000, transcendentals=0
        ),
    )(len_arr, qa, ka, va, ctx, gctx, x, base, full)


def row_tile(width):
    return pl.BlockSpec((TILE, width), lambda i, *_: (i, 0))


def mid_fwd(len_arr, x0, x1, ctx0, ctx1, full, wu, vecs):
    outs = [
        ((SEQ // BLOCK, 2, BLOCK, D), bf16), ((ROWS, D), f32), ((ROWS, D), f32),
        ((ROWS, 128), f32), ((ROWS, FF), f32), ((ROWS, FF), bf16), ((8, 128), f32),
    ]
    return pl.pallas_call(
        mid_fwd_kernel,
        name="mid_fwd",
        grid_spec=pltpu.PrefetchScalarGridSpec(
            num_scalar_prefetch=1,
            grid=(TILES,),
            in_specs=[row_tile(HALF)] * 4
            + [whole((D, 2 * D)), whole(wu.shape), whole(vecs.shape)],
            out_specs=[
                kept(outs[0][0]), row_tile(D), row_tile(D), row_tile(128), row_tile(FF),
                row_tile(FF), kept((8, 128)),
            ],
            scratch_shapes=[
                pltpu.VMEM((ROWS, D), bf16),
                pltpu.VMEM((4, WIN, D), bf16),
                pltpu.VMEM((8, D), f32),
            ],
        ),
        out_shape=[struct(*o) for o in outs],
        compiler_params=PARAMS,
        cost_estimate=pl.CostEstimate(
            flops=15_000_000_000, bytes_accessed=36_000_000, transcendentals=7_000_000
        ),
    )(len_arr, x0, x1, ctx0, ctx1, full, wu, vecs)


def mid_bwd(len_arr, cot, ctx0, ctx1, n1, n2, inv, slope, act, full, wu, vecs, chunks):
    part = (chunks // 2, D // chunks, GRAD_COLS)
    outs = [((ROWS, D), bf16), ((ROWS, D), f32), (part, bf16), (part, bf16)]
    return pl.pallas_call(
        mid_bwd_kernel,
        name="mid_bwd",
        grid_spec=pltpu.PrefetchScalarGridSpec(
            num_scalar_prefetch=1,
            grid=(TILES,),
            in_specs=[
                whole(cot.shape), row_tile(HALF), row_tile(HALF), row_tile(D), row_tile(D),
                row_tile(128), row_tile(FF), row_tile(FF), whole((D, 2 * D)), whole(wu.shape),
                whole(vecs.shape),
            ],
            out_specs=[
                row_tile(D),
                row_tile(D),
                whole(part),
                whole(part),
            ],
            scratch_shapes=[
                pltpu.VMEM((ROWS, D), bf16),
                pltpu.VMEM((4, WIN, D), bf16),
                pltpu.VMEM((D, D), f32),
                pltpu.VMEM((4, WIN, D), f32),
                pltpu.VMEM((4, WIN, D), f32),
                pltpu.VMEM((128, D), f32),
                pltpu.VMEM((D, 128), f32),
                pltpu.VMEM((D, GRAD_COLS), bf16),
            ],
        ),
        out_shape=[struct(*o) for o in outs],
        compiler_params=PARAMS,
        cost_estimate=pl.CostEstimate(
            flops=100_000_000, bytes_accessed=1_000_000, transcendentals=0
        ),
    )(len_arr, cot, ctx0, ctx1, n1, n2, inv, slope, act, full, wu, vecs)


def column_of(row_ref):
    count = row_ref.shape[1]
    row = lax.broadcasted_iota(jnp.int32, (count, count), 0)
    col = lax.broadcasted_iota(jnp.int32, (count, count), 1)
    values = jnp.broadcast_to(row_ref[...].astype(f32), (count, count))
    return jnp.sum(jnp.where(row == col, values, 0.0), axis=1, keepdims=True)


def pack_kernel(odd_ref, *refs):
    bias_refs, (up_bias_ref, o_ref, down_ref, q_ref, k_ref, v_ref, up_ref) = refs[:8], refs[8:15]
    out_ref, low_s, high_s = refs[15:]
    rows = o_ref.shape[0]
    odd = odd_ref[0]
    shift = lax.broadcasted_iota(jnp.int32, (192, WIN), 1) - lax.broadcasted_iota(
        jnp.int32, (192, WIN), 0
    )
    move = jnp.where(shift == 64 * odd, 1.0, 0.0).astype(bf16)

    def padded(weight, column):
        lane = lax.broadcasted_iota(jnp.int32, (weight.shape[0], WIN), 1)
        moved = mm(weight, move, NN)
        return jnp.where(lane == 192 * (1 - odd), column, moved)

    columns = [column_of(ref) for ref in bias_refs]
    out_ref[:, :D] = o_ref[...]
    out_ref[:, D : 2 * D] = down_ref[...]
    sources = ((q_ref, columns[6]), (k_ref, jnp.zeros((rows, 1), f32)), (v_ref, columns[7]))
    for which, (ref, column) in enumerate(sources):
        start = 2 * D + WIN * which
        out_ref[:, start : start + WIN] = padded(ref[...], column).astype(bf16)
    up = padded(up_ref[...], column_of(up_bias_ref))
    low_s[...] = up[:, :128]
    high_s[...] = up[:, 128:]
    for j in range(4):
        for half, source in enumerate((low_s, high_s)):
            start = 3 * D + WIN * j + 128 * half
            out_ref[:, start : start + 128] = source[pl.ds(j, rows, stride=4), :].astype(bf16)
    lane = lax.broadcasted_iota(jnp.int32, (rows, 128), 1)
    small = jnp.zeros((rows, 128), f32)
    for index, column in enumerate(columns[:6]):
        small = jnp.where(lane == index, column, small)
    out_ref[:, 3 * D + 4 * WIN :] = small.astype(bf16)


def pack(odd, biases, up_bias, o_weight, down_weight, in_weights, up_weight):
    rows = o_weight.shape[0]
    arrays = [bias[None, :] for bias in (*biases, up_bias)]
    arrays += [o_weight, down_weight, *in_weights, up_weight]
    return pl.pallas_call(
        pack_kernel,
        name="pack",
        grid_spec=pltpu.PrefetchScalarGridSpec(
            num_scalar_prefetch=1,
            grid=(1,),
            in_specs=[whole(array.shape) for array in arrays],
            out_specs=[kept((rows, ALL_COLS))],
            scratch_shapes=[pltpu.VMEM((4 * rows, 128), f32)] * 2,
        ),
        out_shape=[struct((rows, ALL_COLS), bf16)],
        compiler_params=PARAMS,
        cost_estimate=pl.CostEstimate(flops=0, bytes_accessed=400_000, transcendentals=0),
    )(odd.astype(jnp.int32).reshape(1), *arrays)[0]


def minor_of(count):
    return max(2, count // 4)


def spread_kernel(sizes, orders, lanes, *refs):
    held_ref, full_ref, own_sem, send_sems, recv_sems = refs
    minor = sizes[3]
    dp, fsdp = lax.axis_index("dp"), lax.axis_index("fsdp")
    spot = (dp // 2, dp % 2, fsdp // minor, fsdp % minor)
    done = (2,) if 2 not in orders[0] else ()
    lead = 4 if done else 1

    def device(place):
        return (place[0] * 2 + place[1], place[2] * minor + place[3])

    def moved(dim, shift):
        place = list(spot)
        place[dim] = lax.rem(place[dim] + shift, sizes[dim])
        return tuple(place)

    def region(place, gathered):
        index = tuple(slice(None) if d in gathered else place[d] for d in range(4))
        return index if lead == 4 else (index[2],)

    barrier = pltpu.get_barrier_semaphore()
    peers = [(dim, shift) for dim in orders[0] for shift in range(1, sizes[dim])]
    for dim, shift in peers:
        pl.semaphore_signal(
            barrier,
            inc=1,
            device_id=device(moved(dim, shift)),
            device_id_type=pl.DeviceIdType.MESH,
        )
    own = pltpu.make_async_copy(held_ref, full_ref.at[region(spot, done)], own_sem)
    own.start()
    pl.semaphore_wait(barrier, len(peers))
    slot_of = {}

    def copy(route, stage, shift, place, target):
        gathered = done + orders[route][:stage]
        slot = slot_of.setdefault((route, stage, shift), len(slot_of))
        window = full_ref.at[region(place, gathered)]
        window = window.at[(slice(None),) * (len(window.shape) - 1) + (lanes[route],)]
        source = window
        if stage == 0:
            source = held_ref.at[(slice(None),) * (len(held_ref.shape) - 1) + (lanes[route],)]
        return pltpu.make_async_remote_copy(
            src_ref=source,
            dst_ref=window,
            send_sem=send_sems.at[slot],
            recv_sem=recv_sems.at[slot],
            device_id=device(target),
            device_id_type=pl.DeviceIdType.MESH,
        )

    def shifts(route, stage):
        return range(1, sizes[orders[route][stage]])

    def arrived(route, stage):
        dim = orders[route][stage]
        for shift in shifts(route, stage):
            came = moved(dim, sizes[dim] - shift)
            copy(route, stage, shift, came, came).wait_recv()

    sent = []
    for stage in range(len(orders[0])):
        for route, order in enumerate(orders):
            if stage > 0:
                arrived(route, stage - 1)
            if stage == 1 and route == 0:
                own.wait()
            for shift in shifts(route, stage):
                one = copy(route, stage, shift, spot, moved(order[stage], shift))
                one.start()
                sent.append(one)
    if len(orders[0]) == 1:
        own.wait()
    for route in range(len(orders)):
        arrived(route, len(orders[0]) - 1)
    for one in sent:
        one.wait_send()


def spread_call(held, sizes, orders, lanes, shape, space, identity):
    copies = len(orders) * sum(sizes[dim] - 1 for dim in orders[0])
    return pl.pallas_call(
        functools.partial(spread_kernel, sizes, orders, lanes),
        name="spread",
        in_specs=[pl.BlockSpec(memory_space=pltpu.VMEM)],
        out_specs=pl.BlockSpec(memory_space=space),
        out_shape=struct(shape, bf16),
        scratch_shapes=[
            pltpu.SemaphoreType.DMA(()),
            pltpu.SemaphoreType.DMA((copies,)),
            pltpu.SemaphoreType.DMA((copies,)),
        ],
        compiler_params=pltpu.CompilerParams(
            collective_id=identity, has_side_effects=True, vmem_limit_bytes=63_000_000
        ),
        cost_estimate=pl.CostEstimate(flops=0, bytes_accessed=100_000_000, transcendentals=0),
    )(held)


def sizes_of(dp, fsdp):
    minor = minor_of(fsdp)
    return (dp // 2, 2, fsdp // minor, minor)


def spread_far(packed, sizes):
    whole_lanes = (pl.ds(0, packed.shape[1]),)
    shape = (sizes[2], *packed.shape)
    return spread_call(packed, sizes, ((2,),), whole_lanes, shape, pltpu.VMEM, 0)


def spread_near(held, sizes):
    _, rows, cols = held.shape
    lanes = (pl.ds(0, SPLIT), pl.ds(SPLIT, cols - SPLIT))
    orders = ((3, 0, 1), (0, 3, 1))
    full = spread_call(held, sizes, orders, lanes, (*sizes, rows, cols), pltpu.HBM, 1)
    return full.reshape(-1, cols)


def source_of(len_ref, perm_ref, place):
    first = perm_ref[place - place % 2]
    second = perm_ref[place - place % 2 + 1]
    swapped = (len_ref[first] < len_ref[second]).astype(jnp.int32)
    return jnp.where(swapped == place % 2, first, second)


def moved_rows(source_at, rows_refs, out_ref, buffer_ref, in_sems, out_sems, lane0=0):
    count = out_ref.shape[0] // STEPS

    lanes = pl.ds(lane0, buffer_ref.shape[2])

    def group(step):
        return pl.ds(step * count, count)

    for step in range(STEPS):

        def one(index, carry):
            place = step * count + index
            source = source_at(place)
            lane = 0
            for which, rows_ref in enumerate(rows_refs):
                width = rows_ref.shape[2]
                pltpu.make_async_copy(
                    rows_ref.at[source],
                    buffer_ref.at[place, :, pl.ds(lane, width)],
                    in_sems.at[step, which],
                ).start()
                lane += width
            return carry

        lax.fori_loop(0, count, one, 0)
    for step in range(STEPS):
        lane = 0
        for which, rows_ref in enumerate(rows_refs):
            width = rows_ref.shape[2]
            pltpu.make_async_copy(
                rows_ref.at[group(step)],
                buffer_ref.at[group(step), :, pl.ds(lane, width)],
                in_sems.at[step, which],
            ).wait()
            lane += width
        pltpu.make_async_copy(
            buffer_ref.at[group(step)], out_ref.at[group(step), :, lanes], out_sems.at[step]
        ).start()
    for step in range(STEPS):
        pltpu.make_async_copy(
            buffer_ref.at[group(step)], out_ref.at[group(step), :, lanes], out_sems.at[step]
        ).wait()


def moved_call(kernel, name, parts, lengths, permutation):
    total, size, _ = parts[0].shape
    shape = (total, size, sum(part.shape[2] for part in parts))
    return pl.pallas_call(
        kernel,
        name=name,
        grid_spec=pltpu.PrefetchScalarGridSpec(
            num_scalar_prefetch=2,
            grid=(1,),
            in_specs=[pl.BlockSpec(memory_space=pltpu.HBM)] * len(parts),
            out_specs=[pl.BlockSpec(memory_space=pltpu.HBM)],
            scratch_shapes=[
                pltpu.VMEM(shape, bf16),
                pltpu.SemaphoreType.DMA((STEPS, len(parts))),
                pltpu.SemaphoreType.DMA((STEPS,)),
            ],
        ),
        out_shape=[struct(shape, bf16)],
        compiler_params=PARAMS,
        cost_estimate=pl.CostEstimate(flops=0, bytes_accessed=100_000, transcendentals=0),
    )(lengths, permutation, *parts)[0]


def deal_kernel(len_ref, perm_ref, rows_ref, out_ref, buffer_ref, in_sems, out_sems):
    source_at = lambda place: source_of(len_ref, perm_ref, place)
    moved_rows(source_at, [rows_ref], out_ref, buffer_ref, in_sems, out_sems)


def deal(rows, lengths, permutation):
    return moved_call(deal_kernel, "deal", [rows], lengths, permutation)


def places_kernel(len_ref, perm_ref, place_ref):
    def note(index, carry):
        place_ref[source_of(len_ref, perm_ref, index)] = index
        return carry

    lax.fori_loop(0, place_ref.shape[0], note, 0)


def places_of(lengths, permutation):
    smem = pl.BlockSpec(memory_space=pltpu.SMEM)
    return pl.pallas_call(
        places_kernel,
        name="places",
        in_specs=[smem, smem],
        out_specs=smem,
        out_shape=struct(lengths.shape, jnp.int32),
        cost_estimate=pl.CostEstimate(flops=0, bytes_accessed=1_000, transcendentals=0),
    )(lengths, permutation)


def restore_kernel(lane0, place_ref, *refs):
    rows_ref, (out_ref, buffer_ref, in_sems, out_sems) = refs[0], refs[-4:]
    source_at = lambda place: place_ref[place]
    moved_rows(source_at, [rows_ref], out_ref, buffer_ref, in_sems, out_sems, lane0)


def restore(rows, places, base=None):
    total, size, width = rows.shape
    operands = [rows] if base is None else [rows, base]
    lane0 = 0 if base is None else base.shape[2] - width
    return pl.pallas_call(
        functools.partial(restore_kernel, lane0),
        name="restore",
        grid_spec=pltpu.PrefetchScalarGridSpec(
            num_scalar_prefetch=1,
            grid=(1,),
            in_specs=[pl.BlockSpec(memory_space=pltpu.HBM)] * len(operands),
            out_specs=[pl.BlockSpec(memory_space=pltpu.HBM)],
            scratch_shapes=[
                pltpu.VMEM(rows.shape, bf16),
                pltpu.SemaphoreType.DMA((STEPS, 1)),
                pltpu.SemaphoreType.DMA((STEPS,)),
            ],
        ),
        out_shape=[struct((total, size, D), bf16)],
        input_output_aliases={} if base is None else {2: 0},
        compiler_params=PARAMS,
        cost_estimate=pl.CostEstimate(flops=0, bytes_accessed=100_000, transcendentals=0),
    )(places, *operands)[0]


def pick(values, index):
    return values.at[index].get(mode="promise_in_bounds")


def tie(*values):
    return lax.optimization_barrier(values)


def on_device(
    tokens, cotangent, lengths, permutation, q_weight, q_bias, k_weight, v_weight, v_bias, o_weight,
    o_bias, norm1_gain, norm1_bias, up_weight, up_bias, down_weight, down_bias, norm2_gain,
    norm2_bias,
):
    devices = lax.axis_size(AXES)
    my_index = lax.axis_index(AXES)
    seq_total, piece_len, _ = tokens.shape
    seq_dev = seq_total // devices
    rows_dev = q_weight.shape[0]
    up_dev = up_weight.shape[0]
    odd = (my_index // (devices // 4)) % 2 == 1

    def padded(weight, bias):
        column = bias[:, None]
        gap = jnp.zeros((weight.shape[0], 63), bf16)
        return jnp.where(
            odd,
            jnp.concatenate([column, gap, weight], axis=1),
            jnp.concatenate([weight, column, gap], axis=1),
        )

    if rows_dev % 8 == 0:
        packed = pack(
            odd,
            [o_bias, norm1_gain, norm1_bias, down_bias, norm2_gain, norm2_bias, q_bias, v_bias],
            up_bias, o_weight, down_weight, [q_weight, k_weight, v_weight], up_weight,
        )
    else:
        small = [o_bias, norm1_gain, norm1_bias, down_bias, norm2_gain, norm2_bias]
        packed = jnp.concatenate(
            [
                o_weight,
                down_weight,
                padded(q_weight, q_bias),
                padded(k_weight, jnp.zeros_like(q_bias)),
                padded(v_weight, v_bias),
                padded(up_weight, up_bias).reshape(rows_dev, 4 * WIN),
                jnp.pad(jnp.stack(small, axis=1), ((0, 0), (0, 122))),
            ],
            axis=1,
        )

    dealt_lengths = pick(lengths, permutation).reshape(devices, seq_dev)
    chunks = lax.axis_size("dp")
    parity = lax.axis_index("dp") % 2
    pairing = [(i, i ^ 1) for i in range(chunks)]
    len_arr = jnp.stack(
        [jnp.max(lax.dynamic_slice_in_dim(dealt_lengths, my_index, 1, 0)), parity]
    ).astype(jnp.int32)

    def swap_blocks(rows):
        return lax.all_to_all(rows, AXES, split_axis=0, concat_axis=0, tiled=True)

    def arrive(rows):
        width = rows.shape[-1]
        moved = swap_blocks(rows.reshape(devices, seq_dev, piece_len, width))
        if piece_len == BLOCK:
            return moved
        moved = moved.transpose(1, 0, 2, 3).reshape(seq_dev, SEQ // BLOCK, BLOCK, width)
        return moved.transpose(1, 0, 2, 3)

    def leave(rows):
        width = rows.shape[-1]
        if piece_len != BLOCK:
            rows = rows.transpose(1, 0, 2, 3).reshape(seq_dev, devices, piece_len, width)
            rows = rows.transpose(1, 0, 2, 3)
        return swap_blocks(rows).reshape(seq_total, piece_len, width)

    fsdp = lax.axis_size("fsdp")
    minor = minor_of(fsdp)
    major = fsdp // minor
    place = (lax.axis_index("dp") // 2, lax.axis_index("fsdp") // minor, my_index % minor)

    def target_of(device, far, high, low):
        dp_index, rest = device // fsdp, device % fsdp
        dp_index = (dp_index + 2 * far) % chunks
        rest = (rest // minor + high) % major * minor + (rest % minor + low) % minor
        return dp_index * fsdp + rest

    def send_blocks(partial, shifts, block_of):
        parts = [block_of(0, 0, 0)]
        for shift in shifts:
            route = [(i, target_of(i, *shift)) for i in range(devices)]
            parts.append(lax.ppermute(block_of(*shift), AXES, route))
        return parts

    def send_near(partial):
        shape = (chunks // 2, major, minor, rows_dev, partial.shape[-1])
        blocks = partial.reshape(shape)

        def block_of(far, high, low):
            start = ((place[0] + far) % shape[0], 0, (place[2] + low) % minor, 0, 0)
            return lax.dynamic_slice(blocks, start, (1, major, 1, *shape[3:]))

        shifts = [(far, 0, low) for far in range(shape[0]) for low in range(minor)][1:]
        return send_blocks(blocks, shifts, block_of)

    def send_far(partial):
        blocks = partial.reshape(major, rows_dev, partial.shape[-1])

        def block_of(far, high, low):
            return lax.dynamic_index_in_dim(blocks, (place[1] + high) % major, 0, False)

        return send_blocks(blocks, [(0, high, 0) for high in range(1, major)], block_of)

    def total(parts):
        result = sum(part.astype(f32) for part in parts)
        return result.reshape(-1, result.shape[-1])

    def total_low(parts):
        return total(parts).astype(bf16)

    dealt_tok = deal(tokens, lengths, permutation)
    dealt_cot = deal(cotangent, lengths, permutation)
    if rows_dev % 8 == 0:
        sizes = sizes_of(chunks, lax.axis_size("fsdp"))
        packed, dealt_tok = tie(packed, dealt_tok)
        held = spread_far(packed, sizes)
        dealt_tok, held = tie(dealt_tok, held)
        tok = arrive(dealt_tok)
        held, dealt_cot = tie(held, dealt_cot)
        full = spread_near(held, sizes)
    else:
        tok = arrive(dealt_tok)
        full = lax.all_gather(packed, AXES, axis=0, tiled=True)
    wu = full[:, 3 * D : 3 * D + 4 * WIN].reshape(FF, WIN)
    vecs = jnp.pad(full[:, 3 * D + 4 * WIN : 3 * D + 4 * WIN + 6].astype(f32).T, ((0, 2), (0, 0)))
    dealt_cot, tok, full, wu, vecs, len_arr = tie(dealt_cot, tok, full, wu, vecs, len_arr)
    cot = arrive(dealt_cot)

    x0, qa0, ka0, va0, ctx0 = attn_fwd(len_arr, tok, full, 0)
    x1, qa1, ka1, va1, ctx1 = attn_fwd(len_arr, tok, full, 1)
    out, n1, n2, inv, slope, act, stat = mid_fwd(len_arr, x0, x1, ctx0, ctx1, full, wu, vecs)
    cot, out = tie(cot, out)
    back_out = leave(out)
    gctx, base, mine, given = mid_bwd(
        len_arr, cot, ctx0, ctx1, n1, n2, inv, slope, act, full, wu, vecs, chunks
    )
    mine = total_low([mine, lax.ppermute(given, "dp", pairing)])
    gctx, mine = tie(gctx, mine)
    parts = send_near(mine)
    ig0, dw0, given0 = attn_bwd(
        len_arr, qa0, ka0, va0, ctx0, gctx, x0, base, full, 0, chunks
    )
    ig0, dw0, given0, gctx, back_out, *parts = tie(ig0, dw0, given0, gctx, back_out, *parts)
    back0 = leave(ig0)
    given0 = lax.ppermute(given0, "dp", pairing)
    parts = send_far(total_low(parts))
    ig1, dw1, given1 = attn_bwd(
        len_arr, qa1, ka1, va1, ctx1, gctx, x1, base, full, 1, chunks
    )
    ig1, dw0, dw1, given0, given1, back0, *parts = tie(
        ig1, dw0, dw1, given0, given1, back0, *parts
    )
    back1 = leave(ig1)
    given1 = lax.ppermute(given1, "dp", pairing)
    mine_in = jnp.concatenate([total_low([dw0, given0]), total_low([dw1, given1])], axis=0)
    parts_in = send_near(mine_in)
    stat, dealt_lengths, lengths, *parts = tie(stat, dealt_lengths, lengths, *parts)
    places = places_of(lengths, permutation)
    output = restore(back_out, places)
    input_grad = restore(back0, places)
    output, input_grad, *parts_in = tie(output, input_grad, *parts_in)
    mine = total(parts)
    mine_in = total(send_far(total_low(parts_in)))

    swap = dealt_lengths[:, 0] < dealt_lengths[:, 1]
    my_swap = lax.dynamic_index_in_dim(swap, my_index, 0, False)
    input_grad = restore(back1, places, input_grad)
    lens = jnp.stack([len_arr[0], ROWS - len_arr[0]]).astype(f32)
    sums = jnp.stack([stat[4:8, 0], stat[0:4, 0] - stat[4:8, 0]], axis=1)
    rms = jnp.sqrt(sums / (lens[None, :] * D) + rms_eps)
    stream_rms = jnp.where(my_swap, rms[:, ::-1], rms)
    vec = lambda i: mine[:, 2 * D + 4 * WIN + i]

    def unpadded(block):
        return (
            jnp.where(odd, block[:, 64:], block[:, :192]),
            jnp.where(odd, block[:, 0], block[:, 192]),
        )

    dq, dqb = unpadded(mine_in[:, :WIN])
    dk, _ = unpadded(mine_in[:, WIN : 2 * WIN])
    dv, dvb = unpadded(mine_in[:, 2 * WIN :])
    dup, dub = unpadded(mine[:, 2 * D : 2 * D + 4 * WIN].reshape(up_dev, WIN))
    return (
        output, input_grad, dq, dqb, dk, dv, dvb, mine[:, :D], vec(0), vec(1), vec(2), dup, dub,
        mine[:, D : 2 * D], vec(3), vec(4), vec(5), stream_rms,
    )


def solution(mesh):
    rows = P(None, AXES, None)
    mat = P(AXES, None)
    vec = P(AXES)
    in_specs = (
        rows, rows, P(), P(), mat, vec, mat, mat, vec, mat, vec, vec, vec, mat, vec, mat, vec, vec,
        vec,
    )
    out_specs = (
        rows, rows, mat, vec, mat, mat, vec, mat, vec, vec, vec, mat, vec, mat, vec, vec, vec,
        P(None, AXES),
    )
    return jax.shard_map(
        on_device, mesh=mesh, in_specs=in_specs, out_specs=out_specs, check_vma=False
    )
```

```python
import functools

import jax
import jax.numpy as jnp
from jax import lax
from jax.experimental import pallas as pl
from jax.experimental.pallas import tpu as pltpu
from jax.sharding import PartitionSpec as P

AXES = ("dp", "fsdp")
D = 768
FF = 3072
HALF = D // 2
HEAD = 64
WIN = 256
SEQ = 1024
SHORT = 64
BLOCK = 32
ROWS = SEQ + SHORT
TILE = 272
TILES = ROWS // TILE
ATTN_TILE = 272
ATTN_TILES = ROWS // ATTN_TILE
BIG = 1e30
STEPS = 4
SPLIT = 1664

norm_eps = 1e-12
rms_eps = 1e-06
bf16 = jnp.bfloat16
f32 = jnp.float32

NN = (((1,), (0,)), ((), ()))
NT = (((1,), (1,)), ((), ()))
TN = (((0,), (0,)), ((), ()))


def mm(left, right, dims):
    return lax.dot_general(left, right, dims, preferred_element_type=f32)


def exchange():
    row = lax.broadcasted_iota(jnp.int32, (WIN, WIN), 0)
    col = lax.broadcasted_iota(jnp.int32, (WIN, WIN), 1)
    return jnp.where(row + col == WIN - 1, 1.0, 0.0).astype(bf16)


def row_ids(start, count, width):
    return start + lax.broadcasted_iota(jnp.int32, (count, width), 0)


def block_rows(ref, seq, start, count):
    values = ref[start // BLOCK : (start + count) // BLOCK, seq]
    return values.reshape(count, values.shape[-1])


def merge_rows(pair_ref, packed_ref, first_len):
    width = packed_ref.shape[1]
    flip = exchange()
    packed_ref[0:SHORT, :] = block_rows(pair_ref, 0, 0, SHORT)
    for step in range(SEQ // WIN):
        start = SHORT + WIN * step
        flipped = mm(flip, block_rows(pair_ref, 1, SEQ - WIN * (step + 1), WIN), NN)
        inside = min(WIN, SEQ - start)
        own = block_rows(pair_ref, 0, start, inside).astype(f32)
        keep = row_ids(start, inside, width) < first_len
        packed_ref[start : start + inside, :] = jnp.where(keep, own, flipped[0:inside]).astype(bf16)
        if inside < WIN:
            packed_ref[start + inside : start + WIN, :] = flipped[inside:].astype(bf16)


def unmerge_rows(packed_ref, pair_ref, first_len):
    width = packed_ref.shape[1]
    flip = exchange()
    blocks = WIN // BLOCK
    for step in range(SEQ // WIN):
        start = WIN * step
        ids = row_ids(start, WIN, width)
        own = packed_ref[start : start + WIN, :].astype(f32)
        own = jnp.where(ids < first_len, own, 0.0).astype(bf16)
        pair_ref[blocks * step : blocks * (step + 1), 0] = own.reshape(blocks, BLOCK, width)
        source = ROWS - WIN * (step + 1)
        flipped = mm(flip, packed_ref[source : source + WIN, :], NN)
        flipped = jnp.where(ids < ROWS - first_len, flipped, 0.0).astype(bf16)
        pair_ref[blocks * step : blocks * (step + 1), 1] = flipped.reshape(blocks, BLOCK, width)


def spare_of(group):
    return 192 if group % 2 == 0 else 0


def with_ones(window, group):
    lane = lax.broadcasted_iota(jnp.int32, window.shape, 1)
    return jnp.where(lane == spare_of(group), 1.0, window.astype(f32)).astype(bf16)


def without_bias(window, group):
    lane = lax.broadcasted_iota(jnp.int32, window.shape, 1)
    return jnp.where(lane == spare_of(group), 0.0, window.astype(f32)).astype(bf16)


def first_row(group):
    return 0 if group % 2 == 0 else 64


def windows(values, count):
    parts = []
    for group in range(count):
        start = (group // 2) * HALF + (group % 2) * 128
        parts.append(values[:, start : start + WIN])
    return parts


def join(parts):
    pieces = []
    for first, second in zip(parts[0::2], parts[1::2]):
        pieces += [first[:, :128], first[:, 128:] + second[:, :128], second[:, 128:]]
    return jnp.concatenate(pieces, axis=1)


def split_three(value):
    high = value.astype(bf16)
    rest = value - high.astype(f32)
    mid = rest.astype(bf16)
    low = (rest - mid.astype(f32)).astype(bf16)
    return high, mid, low


def attn_fwd_kernel(
    len_ref, tok_ref, full_ref, x_ref, qa_ref, ka_ref, va_ref, ctx_ref, q_s, k_s, v_s, w_s
):
    pair = pl.program_id(0)
    first_len = len_ref[0]

    @pl.when(pair == 0)
    def _():
        merge_rows(tok_ref, x_ref, first_len)
        w_s[...] = jnp.zeros_like(w_s)
        for which in range(3):
            for g in range(2):
                w_s[which, g, first_row(g) : first_row(g) + 192, :] = full_ref[
                    192 * g : 192 * (g + 1), WIN * which : WIN * (which + 1)
                ]
        cols = [with_ones(part, g) for g, part in enumerate(windows(x_ref[...], 2))]
        for which, target in enumerate((q_s, k_s, v_s)):
            value = join([mm(cols[g], w_s[which, g], NT) for g in range(2)])
            if which == 0:
                value = value.astype(bf16).astype(f32) * (HEAD**-0.5)
            target[...] = value.astype(bf16)

    lane0 = pl.multiple_of(pair * 128, 128)
    q_pair = q_s[:, pl.ds(lane0, 128)]
    k_pair = k_s[:, pl.ds(lane0, 128)]
    v_pair = v_s[:, pl.ds(lane0, 128)]
    lane = lax.broadcasted_iota(jnp.int32, (ROWS, 128), 1)
    in_first = row_ids(0, ROWS, 128) < first_len
    one = jnp.ones((ROWS, 128), f32)
    zero = jnp.zeros((ROWS, 128), f32)
    for head in range(2):
        spare = 64 * (1 - head)
        own = (lane // 64) == head
        first_one = jnp.where(in_first, one, zero)
        q_extra = jnp.where(
            lane == spare, first_one, jnp.where(lane == spare + 1, one - first_one, zero)
        )
        k_extra = jnp.where(
            lane == spare,
            (first_one - one) * BIG,
            jnp.where(
                lane == spare + 1,
                first_one * (-BIG),
                jnp.where((lane >= spare + 2) & (lane < spare + 5), one, zero),
            ),
        )
        v_extra = jnp.where((lane >= spare) & (lane < spare + 3), one, zero)
        cols = slice(128 * head, 128 * (head + 1))
        qa_ref[:, cols] = jnp.where(own, q_pair.astype(f32), q_extra).astype(bf16)
        ka_ref[:, cols] = jnp.where(own, k_pair.astype(f32), k_extra).astype(bf16)
        va_ref[:, cols] = jnp.where(own, v_pair.astype(f32), v_extra).astype(bf16)

    tile_lane = lax.broadcasted_iota(jnp.int32, (ATTN_TILE, 128), 1)

    def one_tile(index, carry):
        start = pl.multiple_of(index * ATTN_TILE, 16)
        rows = pl.ds(start, ATTN_TILE)
        result = None
        for head in range(2):
            cols = slice(128 * head, 128 * (head + 1))
            spare = 64 * (1 - head)
            q_tile = qa_ref[rows, cols]
            scores = mm(q_tile, ka_ref[:, cols], NT)
            top = jnp.max(scores, axis=1, keepdims=True)
            weights = jnp.exp(scores - top)
            mixed = mm(weights.astype(bf16), va_ref[:, cols], NN)
            total = mixed[:, spare : spare + 1]
            mixed = mixed / total
            log_total = top + jnp.log(total)
            high, mid, low = split_three(-log_total)
            q_new = jnp.where(
                tile_lane == spare + 2,
                high.astype(f32),
                jnp.where(
                    tile_lane == spare + 3,
                    mid.astype(f32),
                    jnp.where(tile_lane == spare + 4, low.astype(f32), q_tile.astype(f32)),
                ),
            )
            qa_ref[rows, cols] = q_new.astype(bf16)
            result = mixed if head == 0 else jnp.where(tile_lane < 64, result, mixed)
        ctx_ref[rows, :] = result.astype(bf16)
        return carry

    lax.fori_loop(0, ATTN_TILES, one_tile, 0)


def attn_bwd_kernel(
    len_ref, qa_ref, ka_ref, va_ref, ctx_ref, gctx_ref, x_ref, base_ref, full_ref,
    ig_ref, kept_ref, given_ref, dq_s, dk_s, dv_s, do_s, dqt_s, ig_s, w_s, dw_ref,
):
    pair = pl.program_id(0)
    lane0 = pl.multiple_of(pair * 128, 128)
    lane = lax.broadcasted_iota(jnp.int32, (ROWS, 128), 1)
    grad = gctx_ref[...].astype(f32)
    product = grad * ctx_ref[...].astype(f32)
    for head in range(2):
        own = (lane // 64) == head
        spare = 64 * (1 - head)
        inner = -jnp.sum(jnp.where(own, product, 0.0), axis=1, keepdims=True)
        high, mid, low = split_three(inner)
        extra = jnp.where(
            lane == spare,
            high.astype(f32),
            jnp.where(
                lane == spare + 1,
                mid.astype(f32),
                jnp.where(lane == spare + 2, low.astype(f32), 0.0),
            ),
        )
        do_s[:, 128 * head : 128 * (head + 1)] = jnp.where(own, grad, extra).astype(bf16)
    dqt_s[...] = jnp.zeros_like(dqt_s)
    tile_lane = lax.broadcasted_iota(jnp.int32, (ATTN_TILE, 128), 1)

    def one_tile(index, carry):
        start = pl.multiple_of(index * ATTN_TILE, 16)
        rows = pl.ds(start, ATTN_TILE)
        dk_tile = None
        dv_tile = None
        for head in range(2):
            cols = slice(128 * head, 128 * (head + 1))
            k_tile = ka_ref[rows, cols]
            probs = jnp.exp(mm(k_tile, qa_ref[:, cols], NT))
            scaled = mm(va_ref[rows, cols], do_s[:, cols], NT) * probs
            grad_scores = scaled.astype(bf16)
            dv_new = mm(probs.astype(bf16), do_s[:, cols], NN)
            dk_new = mm(grad_scores, qa_ref[:, cols], NN)
            dq_new = mm(k_tile, grad_scores, TN)
            dqt_s[64 * head : 64 * (head + 1), :] += dq_new[64 * head : 64 * (head + 1), :]
            dk_tile = dk_new if head == 0 else jnp.where(tile_lane < 64, dk_tile, dk_new)
            dv_tile = dv_new if head == 0 else jnp.where(tile_lane < 64, dv_tile, dv_new)
        dk_s[rows, pl.ds(lane0, 128)] = dk_tile.astype(bf16)
        dv_s[rows, pl.ds(lane0, 128)] = dv_tile.astype(bf16)
        return carry

    lax.fori_loop(0, ATTN_TILES, one_tile, 0)
    dq_s[:, pl.ds(lane0, 128)] = (jnp.transpose(dqt_s[...]) * (HEAD**-0.5)).astype(bf16)

    @pl.when(pair == pl.num_programs(0) - 1)
    def _():
        x_cols = [with_ones(part, g) for g, part in enumerate(windows(x_ref[...], 2))]
        total = [None, None]
        for which, source in enumerate((dq_s, dk_s, dv_s)):
            cols = windows(source[...], 2)
            for g in range(2):
                own = slice(first_row(g), first_row(g) + 192)
                w_s[own, :] = without_bias(
                    full_ref[192 * g : 192 * (g + 1), WIN * which : WIN * (which + 1)], g
                )
                if first_row(g) == 0:
                    w_s[192:, :] = jnp.zeros((64, WIN), bf16)
                else:
                    w_s[:64, :] = jnp.zeros((64, WIN), bf16)
                grad = mm(cols[g], x_cols[g], TN)
                dw_ref[192 * g : 192 * (g + 1), WIN * which : WIN * (which + 1)] = grad[own].astype(
                    bf16
                )
                part = mm(cols[g], w_s[...], NN)
                total[g] = part if which == 0 else total[g] + part
        ig_s[...] = (join(total) + base_ref[...]).astype(bf16)
        unmerge_rows(ig_s, ig_ref, len_ref[0])
        split_chunks(dw_ref, kept_ref, given_ref, len_ref[1])


def split_chunks(rows_ref, kept_ref, given_ref, parity):
    pairs, size, _ = kept_ref.shape
    for own in range(2):

        @pl.when(parity == own)
        def _():
            for pair in range(pairs):
                for which in range(2):
                    start = (2 * pair + which) * size
                    target = kept_ref if which == own else given_ref
                    target[pair] = rows_ref[start : start + size, :]


def norm(values):
    mean = jnp.mean(values, axis=1, keepdims=True)
    centered = values - mean
    var = jnp.mean(centered * centered, axis=1, keepdims=True)
    inv = lax.rsqrt(var + norm_eps)
    return centered * inv, inv


def norm_back(grad_n, n, inv):
    mean_g = jnp.mean(grad_n, axis=1, keepdims=True)
    mean_gn = jnp.mean(grad_n * n, axis=1, keepdims=True)
    return (grad_n - mean_g - n * mean_gn) * inv


def mid_fwd_kernel(
    len_ref, x0_ref, x1_ref, ctx0_ref, ctx1_ref, full_ref, wu_ref, vec_ref,
    out_ref, n1_ref, n2_ref, inv_ref, slope_ref, act_ref, stat_ref,
    out_s, wd_s, stat_s,
):
    step = pl.program_id(0)
    first_len = len_ref[0]

    @pl.when(step == 0)
    def _():
        stat_s[...] = jnp.zeros_like(stat_s)
        wd_s[...] = jnp.zeros_like(wd_s)
        for g in range(4):
            wd_s[g, first_row(g) : first_row(g) + 192, :] = full_ref[192 * g : 192 * (g + 1), D:]

    o_bias, gain1, shift1, down_bias, gain2, shift2 = (vec_ref[i : i + 1, :] for i in range(6))
    start = pl.multiple_of(step * TILE, 16)
    rows = pl.ds(start, TILE)
    keep = jnp.where(row_ids(start, TILE, D) < first_len, 1.0, 0.0)

    def note(slot, values):
        square = values * values
        stat_s[slot : slot + 1, :] += jnp.sum(square, axis=0, keepdims=True)
        stat_s[slot + 4 : slot + 5, :] += jnp.sum(square * keep, axis=0, keepdims=True)

    inputs = jnp.concatenate([x0_ref[...], x1_ref[...]], axis=1).astype(f32)
    context = jnp.concatenate([ctx0_ref[...], ctx1_ref[...]], axis=1)
    note(0, inputs)
    branch_attn = mm(context, full_ref[:, :D], NT) + o_bias
    note(1, branch_attn)
    n1, inv1 = norm(inputs + branch_attn)
    n1_ref[...] = n1
    first_norm = n1 * gain1 + shift1
    note(2, first_norm)
    low_cols = windows(first_norm.astype(bf16), 4)
    parts = []
    for g in range(4):
        cols = slice(D * g, D * (g + 1))
        up = mm(with_ones(low_cols[g], g), wu_ref[D * g : D * (g + 1), :], NT)
        gate = 0.5 * (1.0 + lax.erf(up * (2.0**-0.5)))
        slope_ref[:, cols] = gate + up * jnp.exp(up * up * -0.5) * 0.3989422804014327
        act = (up * gate).astype(bf16)
        act_ref[:, cols] = act
        parts.append(mm(act, wd_s[g], NT))
    branch_ffn = join(parts) + down_bias
    note(3, branch_ffn)
    n2, inv2 = norm(first_norm + branch_ffn)
    n2_ref[...] = n2
    lane = lax.broadcasted_iota(jnp.int32, (TILE, 128), 1)
    inv_ref[...] = jnp.where(lane < 64, inv1, inv2)
    out_s[rows, :] = (n2 * gain2 + shift2).astype(bf16)

    @pl.when(step == pl.num_programs(0) - 1)
    def _():
        unmerge_rows(out_s, out_ref, first_len)
        stat_ref[...] = jnp.broadcast_to(
            jnp.sum(stat_s[...], axis=1, keepdims=True), stat_ref.shape
        )


def mid_bwd_kernel(
    len_ref, cot_ref, ctx0_ref, ctx1_ref, n1_ref, n2_ref, inv_ref, slope_ref, act_ref,
    full_ref, wu_ref, vec_ref, gctx_ref, base_ref, kept_ref, given_ref,
    cot_s, wd_s, dwo_s, dwd_s, dwu_s, vec_s, turn_s, grad_ref,
):
    step = pl.program_id(0)

    @pl.when(step == 0)
    def _():
        merge_rows(cot_ref, cot_s, len_ref[0])
        for target in (dwo_s, dwd_s, dwu_s, vec_s, wd_s):
            target[...] = jnp.zeros_like(target)
        for g in range(4):
            wd_s[g, first_row(g) : first_row(g) + 192, :] = full_ref[192 * g : 192 * (g + 1), D:]

    gain1, shift1, gain2 = (vec_ref[i : i + 1, :] for i in (1, 2, 4))
    start = pl.multiple_of(step * TILE, 16)
    rows = pl.ds(start, TILE)

    def add_vec(slot, values):
        vec_s[slot : slot + 1, :] += jnp.sum(values, axis=0, keepdims=True)

    context = jnp.concatenate([ctx0_ref[...], ctx1_ref[...]], axis=1)
    n1 = n1_ref[...]
    n2 = n2_ref[...]
    inv1 = inv_ref[:, 0:1]
    inv2 = inv_ref[:, 64:65]
    low_cols = windows((n1 * gain1 + shift1).astype(bf16), 4)
    grad_out = cot_s[rows, :].astype(f32)
    add_vec(4, grad_out * n2)
    add_vec(5, grad_out)
    grad_sum2 = norm_back(grad_out * gain2, n2, inv2)
    grad_ffn = grad_sum2.astype(bf16)
    add_vec(3, grad_ffn.astype(f32))
    ffn_cols = windows(grad_ffn, 4)
    parts = []
    for g in range(4):
        cols = slice(D * g, D * (g + 1))
        dwd_s[g] += mm(ffn_cols[g], act_ref[:, cols], TN)
        grad_up = (mm(ffn_cols[g], wd_s[g], NN) * slope_ref[:, cols]).astype(bf16)
        dwu_s[g] += mm(with_ones(low_cols[g], g), grad_up, TN)
        parts.append(mm(grad_up, without_bias(wu_ref[D * g : D * (g + 1), :], g), NN))
    grad_first = join(parts) + grad_sum2
    add_vec(1, grad_first * n1)
    add_vec(2, grad_first)
    grad_sum1 = norm_back(grad_first * gain1, n1, inv1)
    base_ref[...] = grad_sum1
    grad_branch = grad_sum1.astype(bf16)
    add_vec(0, grad_branch.astype(f32))
    dwo_s[...] += mm(grad_branch, context, TN)
    gctx_ref[...] = mm(grad_branch, full_ref[:, :D], NN).astype(bf16)

    @pl.when(step == pl.num_programs(0) - 1)
    def _():
        grad_ref[:, :D] = dwo_s[...].astype(bf16)
        for g in range(4):
            own = slice(192 * g, 192 * (g + 1))
            grad_ref[own, D : 2 * D] = dwd_s[g, first_row(g) : first_row(g) + 192, :].astype(bf16)
            turned = jnp.transpose(dwu_s[g])
            for half in range(2):
                turn_s[...] = turned[:, 128 * half : 128 * (half + 1)]
                for j in range(4):
                    lane0 = 2 * D + WIN * j + 128 * half
                    grad_ref[own, lane0 : lane0 + 128] = turn_s[pl.ds(j, 192, stride=4), :].astype(
                        bf16
                    )
        grad_ref[:, 2 * D + 4 * WIN :] = jnp.transpose(vec_s[...]).astype(bf16)
        split_chunks(grad_ref, kept_ref, given_ref, len_ref[1])


def whole(shape):
    zeros = (0,) * len(shape)
    return pl.BlockSpec(shape, lambda i, *_: zeros, pipeline_mode=pl.Buffered(1))


def kept(shape):
    zeros = (0,) * len(shape)
    return pl.BlockSpec(shape, lambda i, *_: zeros)


def struct(shape, dtype):
    return jax.ShapeDtypeStruct(shape, dtype)


PARAMS = pltpu.CompilerParams(
    dimension_semantics=("arbitrary",), vmem_limit_bytes=63_000_000
)
GRAD_COLS = 2 * D + 4 * WIN + 128
ALL_COLS = GRAD_COLS + D


def attn_fwd(len_arr, tok, full, half):
    pair_cols = lambda width: pl.BlockSpec((ROWS, width), lambda i, *_: (0, i))
    return pl.pallas_call(
        attn_fwd_kernel,
        name="attn_fwd",
        grid_spec=pltpu.PrefetchScalarGridSpec(
            num_scalar_prefetch=1,
            grid=(3,),
            in_specs=[
                pl.BlockSpec(
                    (SEQ // BLOCK, 2, BLOCK, HALF),
                    lambda i, *_: (0, 0, 0, half),
                    pipeline_mode=pl.Buffered(1),
                ),
                pl.BlockSpec((HALF, D), lambda i, *_: (half, 2), pipeline_mode=pl.Buffered(1)),
            ],
            out_specs=[
                kept((ROWS, HALF)), pair_cols(256), pair_cols(256), pair_cols(256), pair_cols(128),
            ],
            scratch_shapes=[pltpu.VMEM((ROWS, HALF), bf16)] * 3
            + [pltpu.VMEM((3, 2, WIN, WIN), bf16)],
        ),
        out_shape=[
            struct((ROWS, HALF), bf16), struct((ROWS, D), bf16), struct((ROWS, D), bf16),
            struct((ROWS, D), bf16), struct((ROWS, HALF), bf16),
        ],
        compiler_params=PARAMS,
        cost_estimate=pl.CostEstimate(
            flops=20_000_000_000, bytes_accessed=12_000_000, transcendentals=7_000_000
        ),
    )(len_arr, tok, full)


def attn_bwd(len_arr, qa, ka, va, ctx, gctx, x, base, full, half, chunks):
    part = (chunks // 4, D // chunks, D)
    pair_cols = lambda width, first: pl.BlockSpec((ROWS, width), lambda i, *_: (0, i + first))
    return pl.pallas_call(
        attn_bwd_kernel,
        name="attn_bwd",
        grid_spec=pltpu.PrefetchScalarGridSpec(
            num_scalar_prefetch=1,
            grid=(3,),
            in_specs=[
                pair_cols(256, 0), pair_cols(256, 0), pair_cols(256, 0), pair_cols(128, 0),
                pair_cols(128, 3 * half), whole(x.shape),
                pl.BlockSpec((ROWS, HALF), lambda i, *_: (0, half), pipeline_mode=pl.Buffered(1)),
                pl.BlockSpec((HALF, D), lambda i, *_: (half, 2), pipeline_mode=pl.Buffered(1)),
            ],
            out_specs=[kept((SEQ // BLOCK, 2, BLOCK, HALF)), kept(part), kept(part)],
            scratch_shapes=[
                pltpu.VMEM((ROWS, HALF), bf16),
                pltpu.VMEM((ROWS, HALF), bf16),
                pltpu.VMEM((ROWS, HALF), bf16),
                pltpu.VMEM((ROWS, 256), bf16),
                pltpu.VMEM((128, ROWS), f32),
                pltpu.VMEM((ROWS, HALF), bf16),
                pltpu.VMEM((WIN, WIN), bf16),
                pltpu.VMEM((HALF, D), bf16),
            ],
        ),
        out_shape=[
            struct((SEQ // BLOCK, 2, BLOCK, HALF), bf16), struct(part, bf16), struct(part, bf16),
        ],
        compiler_params=PARAMS,
        cost_estimate=pl.CostEstimate(
            flops=100_000_000, bytes_accessed=1_000_000, transcendentals=0
        ),
    )(len_arr, qa, ka, va, ctx, gctx, x, base, full)


def row_tile(width):
    return pl.BlockSpec((TILE, width), lambda i, *_: (i, 0))


def mid_fwd(len_arr, x0, x1, ctx0, ctx1, full, wu, vecs):
    outs = [
        ((SEQ // BLOCK, 2, BLOCK, D), bf16), ((ROWS, D), f32), ((ROWS, D), f32),
        ((ROWS, 128), f32), ((ROWS, FF), f32), ((ROWS, FF), bf16), ((8, 128), f32),
    ]
    return pl.pallas_call(
        mid_fwd_kernel,
        name="mid_fwd",
        grid_spec=pltpu.PrefetchScalarGridSpec(
            num_scalar_prefetch=1,
            grid=(TILES,),
            in_specs=[row_tile(HALF)] * 4
            + [whole((D, 2 * D)), whole(wu.shape), whole(vecs.shape)],
            out_specs=[
                kept(outs[0][0]), row_tile(D), row_tile(D), row_tile(128), row_tile(FF),
                row_tile(FF), kept((8, 128)),
            ],
            scratch_shapes=[
                pltpu.VMEM((ROWS, D), bf16),
                pltpu.VMEM((4, WIN, D), bf16),
                pltpu.VMEM((8, D), f32),
            ],
        ),
        out_shape=[struct(*o) for o in outs],
        compiler_params=PARAMS,
        cost_estimate=pl.CostEstimate(
            flops=15_000_000_000, bytes_accessed=36_000_000, transcendentals=7_000_000
        ),
    )(len_arr, x0, x1, ctx0, ctx1, full, wu, vecs)


def mid_bwd(len_arr, cot, ctx0, ctx1, n1, n2, inv, slope, act, full, wu, vecs, chunks):
    part = (chunks // 2, D // chunks, GRAD_COLS)
    outs = [((ROWS, D), bf16), ((ROWS, D), f32), (part, bf16), (part, bf16)]
    return pl.pallas_call(
        mid_bwd_kernel,
        name="mid_bwd",
        grid_spec=pltpu.PrefetchScalarGridSpec(
            num_scalar_prefetch=1,
            grid=(TILES,),
            in_specs=[
                whole(cot.shape), row_tile(HALF), row_tile(HALF), row_tile(D), row_tile(D),
                row_tile(128), row_tile(FF), row_tile(FF), whole((D, 2 * D)), whole(wu.shape),
                whole(vecs.shape),
            ],
            out_specs=[
                row_tile(D),
                row_tile(D),
                whole(part),
                whole(part),
            ],
            scratch_shapes=[
                pltpu.VMEM((ROWS, D), bf16),
                pltpu.VMEM((4, WIN, D), bf16),
                pltpu.VMEM((D, D), f32),
                pltpu.VMEM((4, WIN, D), f32),
                pltpu.VMEM((4, WIN, D), f32),
                pltpu.VMEM((128, D), f32),
                pltpu.VMEM((D, 128), f32),
                pltpu.VMEM((D, GRAD_COLS), bf16),
            ],
        ),
        out_shape=[struct(*o) for o in outs],
        compiler_params=PARAMS,
        cost_estimate=pl.CostEstimate(
            flops=100_000_000, bytes_accessed=1_000_000, transcendentals=0
        ),
    )(len_arr, cot, ctx0, ctx1, n1, n2, inv, slope, act, full, wu, vecs)


def column_of(row_ref):
    count = row_ref.shape[1]
    row = lax.broadcasted_iota(jnp.int32, (count, count), 0)
    col = lax.broadcasted_iota(jnp.int32, (count, count), 1)
    values = jnp.broadcast_to(row_ref[...].astype(f32), (count, count))
    return jnp.sum(jnp.where(row == col, values, 0.0), axis=1, keepdims=True)


def pack_kernel(odd_ref, *refs):
    bias_refs, (up_bias_ref, o_ref, down_ref, q_ref, k_ref, v_ref, up_ref) = refs[:8], refs[8:15]
    out_ref, low_s, high_s = refs[15:]
    rows = o_ref.shape[0]
    odd = odd_ref[0]
    shift = lax.broadcasted_iota(jnp.int32, (192, WIN), 1) - lax.broadcasted_iota(
        jnp.int32, (192, WIN), 0
    )
    move = jnp.where(shift == 64 * odd, 1.0, 0.0).astype(bf16)

    def padded(weight, column):
        lane = lax.broadcasted_iota(jnp.int32, (weight.shape[0], WIN), 1)
        moved = mm(weight, move, NN)
        return jnp.where(lane == 192 * (1 - odd), column, moved)

    columns = [column_of(ref) for ref in bias_refs]
    out_ref[:, :D] = o_ref[...]
    out_ref[:, D : 2 * D] = down_ref[...]
    sources = ((q_ref, columns[6]), (k_ref, jnp.zeros((rows, 1), f32)), (v_ref, columns[7]))
    for which, (ref, column) in enumerate(sources):
        start = 2 * D + WIN * which
        out_ref[:, start : start + WIN] = padded(ref[...], column).astype(bf16)
    up = padded(up_ref[...], column_of(up_bias_ref))
    low_s[...] = up[:, :128]
    high_s[...] = up[:, 128:]
    for j in range(4):
        for half, source in enumerate((low_s, high_s)):
            start = 3 * D + WIN * j + 128 * half
            out_ref[:, start : start + 128] = source[pl.ds(j, rows, stride=4), :].astype(bf16)
    lane = lax.broadcasted_iota(jnp.int32, (rows, 128), 1)
    small = jnp.zeros((rows, 128), f32)
    for index, column in enumerate(columns[:6]):
        small = jnp.where(lane == index, column, small)
    out_ref[:, 3 * D + 4 * WIN :] = small.astype(bf16)


def pack(odd, biases, up_bias, o_weight, down_weight, in_weights, up_weight):
    rows = o_weight.shape[0]
    arrays = [bias[None, :] for bias in (*biases, up_bias)]
    arrays += [o_weight, down_weight, *in_weights, up_weight]
    return pl.pallas_call(
        pack_kernel,
        name="pack",
        grid_spec=pltpu.PrefetchScalarGridSpec(
            num_scalar_prefetch=1,
            grid=(1,),
            in_specs=[whole(array.shape) for array in arrays],
            out_specs=[kept((rows, ALL_COLS))],
            scratch_shapes=[pltpu.VMEM((4 * rows, 128), f32)] * 2,
        ),
        out_shape=[struct((rows, ALL_COLS), bf16)],
        compiler_params=PARAMS,
        cost_estimate=pl.CostEstimate(flops=0, bytes_accessed=400_000, transcendentals=0),
    )(odd.astype(jnp.int32).reshape(1), *arrays)[0]


def minor_of(count):
    return max(2, count // 4)


def spread_kernel(sizes, orders, lanes, *refs):
    held_ref, full_ref, own_sem, send_sems, recv_sems = refs
    minor = sizes[3]
    dp, fsdp = lax.axis_index("dp"), lax.axis_index("fsdp")
    spot = (dp // 2, dp % 2, fsdp // minor, fsdp % minor)
    done = (2,) if 2 not in orders[0] else ()
    lead = 4 if done else 1

    def device(place):
        return (place[0] * 2 + place[1], place[2] * minor + place[3])

    def moved(dim, shift):
        place = list(spot)
        place[dim] = lax.rem(place[dim] + shift, sizes[dim])
        return tuple(place)

    def region(place, gathered):
        index = tuple(slice(None) if d in gathered else place[d] for d in range(4))
        return index if lead == 4 else (index[2],)

    barrier = pltpu.get_barrier_semaphore()
    peers = [(dim, shift) for dim in orders[0] for shift in range(1, sizes[dim])]
    for dim, shift in peers:
        pl.semaphore_signal(
            barrier,
            inc=1,
            device_id=device(moved(dim, shift)),
            device_id_type=pl.DeviceIdType.MESH,
        )
    own = pltpu.make_async_copy(held_ref, full_ref.at[region(spot, done)], own_sem)
    own.start()
    pl.semaphore_wait(barrier, len(peers))
    slot_of = {}

    def copy(route, stage, shift, place, target):
        gathered = done + orders[route][:stage]
        slot = slot_of.setdefault((route, stage, shift), len(slot_of))
        window = full_ref.at[region(place, gathered)]
        window = window.at[(slice(None),) * (len(window.shape) - 1) + (lanes[route],)]
        source = window
        if stage == 0:
            source = held_ref.at[(slice(None),) * (len(held_ref.shape) - 1) + (lanes[route],)]
        return pltpu.make_async_remote_copy(
            src_ref=source,
            dst_ref=window,
            send_sem=send_sems.at[slot],
            recv_sem=recv_sems.at[slot],
            device_id=device(target),
            device_id_type=pl.DeviceIdType.MESH,
        )

    def shifts(route, stage):
        return range(1, sizes[orders[route][stage]])

    def arrived(route, stage):
        dim = orders[route][stage]
        for shift in shifts(route, stage):
            came = moved(dim, sizes[dim] - shift)
            copy(route, stage, shift, came, came).wait_recv()

    sent = []
    for stage in range(len(orders[0])):
        for route, order in enumerate(orders):
            if stage > 0:
                arrived(route, stage - 1)
            if stage == 1 and route == 0:
                own.wait()
            for shift in shifts(route, stage):
                one = copy(route, stage, shift, spot, moved(order[stage], shift))
                one.start()
                sent.append(one)
    if len(orders[0]) == 1:
        own.wait()
    for route in range(len(orders)):
        arrived(route, len(orders[0]) - 1)
    for one in sent:
        one.wait_send()


def spread_call(held, sizes, orders, lanes, shape, space, identity):
    copies = len(orders) * sum(sizes[dim] - 1 for dim in orders[0])
    return pl.pallas_call(
        functools.partial(spread_kernel, sizes, orders, lanes),
        name="spread",
        in_specs=[pl.BlockSpec(memory_space=pltpu.VMEM)],
        out_specs=pl.BlockSpec(memory_space=space),
        out_shape=struct(shape, bf16),
        scratch_shapes=[
            pltpu.SemaphoreType.DMA(()),
            pltpu.SemaphoreType.DMA((copies,)),
            pltpu.SemaphoreType.DMA((copies,)),
        ],
        compiler_params=pltpu.CompilerParams(
            collective_id=identity, has_side_effects=True, vmem_limit_bytes=63_000_000
        ),
        cost_estimate=pl.CostEstimate(flops=0, bytes_accessed=100_000_000, transcendentals=0),
    )(held)


def sizes_of(dp, fsdp):
    minor = minor_of(fsdp)
    return (dp // 2, 2, fsdp // minor, minor)


def spread_far(packed, sizes):
    whole_lanes = (pl.ds(0, packed.shape[1]),)
    shape = (sizes[2], *packed.shape)
    return spread_call(packed, sizes, ((2,),), whole_lanes, shape, pltpu.VMEM, 0)


def spread_near(held, sizes):
    _, rows, cols = held.shape
    lanes = (pl.ds(0, SPLIT), pl.ds(SPLIT, cols - SPLIT))
    orders = ((3, 0, 1), (0, 3, 1))
    full = spread_call(held, sizes, orders, lanes, (*sizes, rows, cols), pltpu.HBM, 1)
    return full.reshape(-1, cols)


def source_of(len_ref, perm_ref, place):
    first = perm_ref[place - place % 2]
    second = perm_ref[place - place % 2 + 1]
    swapped = (len_ref[first] < len_ref[second]).astype(jnp.int32)
    return jnp.where(swapped == place % 2, first, second)


def moved_rows(source_at, rows_refs, out_ref, buffer_ref, in_sems, out_sems, lane0=0):
    count = out_ref.shape[0] // STEPS

    lanes = pl.ds(lane0, buffer_ref.shape[2])

    def group(step):
        return pl.ds(step * count, count)

    for step in range(STEPS):

        def one(index, carry):
            place = step * count + index
            source = source_at(place)
            lane = 0
            for which, rows_ref in enumerate(rows_refs):
                width = rows_ref.shape[2]
                pltpu.make_async_copy(
                    rows_ref.at[source],
                    buffer_ref.at[place, :, pl.ds(lane, width)],
                    in_sems.at[step, which],
                ).start()
                lane += width
            return carry

        lax.fori_loop(0, count, one, 0)
    for step in range(STEPS):
        lane = 0
        for which, rows_ref in enumerate(rows_refs):
            width = rows_ref.shape[2]
            pltpu.make_async_copy(
                rows_ref.at[group(step)],
                buffer_ref.at[group(step), :, pl.ds(lane, width)],
                in_sems.at[step, which],
            ).wait()
            lane += width
        pltpu.make_async_copy(
            buffer_ref.at[group(step)], out_ref.at[group(step), :, lanes], out_sems.at[step]
        ).start()
    for step in range(STEPS):
        pltpu.make_async_copy(
            buffer_ref.at[group(step)], out_ref.at[group(step), :, lanes], out_sems.at[step]
        ).wait()


def moved_call(kernel, name, parts, lengths, permutation):
    total, size, _ = parts[0].shape
    shape = (total, size, sum(part.shape[2] for part in parts))
    return pl.pallas_call(
        kernel,
        name=name,
        grid_spec=pltpu.PrefetchScalarGridSpec(
            num_scalar_prefetch=2,
            grid=(1,),
            in_specs=[pl.BlockSpec(memory_space=pltpu.HBM)] * len(parts),
            out_specs=[pl.BlockSpec(memory_space=pltpu.HBM)],
            scratch_shapes=[
                pltpu.VMEM(shape, bf16),
                pltpu.SemaphoreType.DMA((STEPS, len(parts))),
                pltpu.SemaphoreType.DMA((STEPS,)),
            ],
        ),
        out_shape=[struct(shape, bf16)],
        compiler_params=PARAMS,
        cost_estimate=pl.CostEstimate(flops=0, bytes_accessed=100_000, transcendentals=0),
    )(lengths, permutation, *parts)[0]


def deal_kernel(len_ref, perm_ref, rows_ref, out_ref, buffer_ref, in_sems, out_sems):
    source_at = lambda place: source_of(len_ref, perm_ref, place)
    moved_rows(source_at, [rows_ref], out_ref, buffer_ref, in_sems, out_sems)


def deal(rows, lengths, permutation):
    return moved_call(deal_kernel, "deal", [rows], lengths, permutation)


def places_kernel(len_ref, perm_ref, place_ref):
    def note(index, carry):
        place_ref[source_of(len_ref, perm_ref, index)] = index
        return carry

    lax.fori_loop(0, place_ref.shape[0], note, 0)


def places_of(lengths, permutation):
    smem = pl.BlockSpec(memory_space=pltpu.SMEM)
    return pl.pallas_call(
        places_kernel,
        name="places",
        in_specs=[smem, smem],
        out_specs=smem,
        out_shape=struct(lengths.shape, jnp.int32),
        cost_estimate=pl.CostEstimate(flops=0, bytes_accessed=1_000, transcendentals=0),
    )(lengths, permutation)


def restore_kernel(lane0, place_ref, *refs):
    rows_ref, (out_ref, buffer_ref, in_sems, out_sems) = refs[0], refs[-4:]
    source_at = lambda place: place_ref[place]
    moved_rows(source_at, [rows_ref], out_ref, buffer_ref, in_sems, out_sems, lane0)


def restore(rows, places, base=None):
    total, size, width = rows.shape
    operands = [rows] if base is None else [rows, base]
    lane0 = 0 if base is None else base.shape[2] - width
    return pl.pallas_call(
        functools.partial(restore_kernel, lane0),
        name="restore",
        grid_spec=pltpu.PrefetchScalarGridSpec(
            num_scalar_prefetch=1,
            grid=(1,),
            in_specs=[pl.BlockSpec(memory_space=pltpu.HBM)] * len(operands),
            out_specs=[pl.BlockSpec(memory_space=pltpu.HBM)],
            scratch_shapes=[
                pltpu.VMEM(rows.shape, bf16),
                pltpu.SemaphoreType.DMA((STEPS, 1)),
                pltpu.SemaphoreType.DMA((STEPS,)),
            ],
        ),
        out_shape=[struct((total, size, D), bf16)],
        input_output_aliases={} if base is None else {2: 0},
        compiler_params=PARAMS,
        cost_estimate=pl.CostEstimate(flops=0, bytes_accessed=100_000, transcendentals=0),
    )(places, *operands)[0]


def pick(values, index):
    return values.at[index].get(mode="promise_in_bounds")


def tie(*values):
    return lax.optimization_barrier(values)


def on_device(
    tokens, cotangent, lengths, permutation, q_weight, q_bias, k_weight, v_weight, v_bias, o_weight,
    o_bias, norm1_gain, norm1_bias, up_weight, up_bias, down_weight, down_bias, norm2_gain,
    norm2_bias,
):
    devices = lax.axis_size(AXES)
    my_index = lax.axis_index(AXES)
    seq_total, piece_len, _ = tokens.shape
    seq_dev = seq_total // devices
    rows_dev = q_weight.shape[0]
    up_dev = up_weight.shape[0]
    odd = (my_index // (devices // 4)) % 2 == 1

    def padded(weight, bias):
        column = bias[:, None]
        gap = jnp.zeros((weight.shape[0], 63), bf16)
        return jnp.where(
            odd,
            jnp.concatenate([column, gap, weight], axis=1),
            jnp.concatenate([weight, column, gap], axis=1),
        )

    if rows_dev % 8 == 0:
        packed = pack(
            odd,
            [o_bias, norm1_gain, norm1_bias, down_bias, norm2_gain, norm2_bias, q_bias, v_bias],
            up_bias, o_weight, down_weight, [q_weight, k_weight, v_weight], up_weight,
        )
    else:
        small = [o_bias, norm1_gain, norm1_bias, down_bias, norm2_gain, norm2_bias]
        packed = jnp.concatenate(
            [
                o_weight,
                down_weight,
                padded(q_weight, q_bias),
                padded(k_weight, jnp.zeros_like(q_bias)),
                padded(v_weight, v_bias),
                padded(up_weight, up_bias).reshape(rows_dev, 4 * WIN),
                jnp.pad(jnp.stack(small, axis=1), ((0, 0), (0, 122))),
            ],
            axis=1,
        )

    dealt_lengths = pick(lengths, permutation).reshape(devices, seq_dev)
    chunks = lax.axis_size("dp")
    parity = lax.axis_index("dp") % 2
    pairing = [(i, i ^ 1) for i in range(chunks)]
    len_arr = jnp.stack(
        [jnp.max(lax.dynamic_slice_in_dim(dealt_lengths, my_index, 1, 0)), parity]
    ).astype(jnp.int32)

    def swap_blocks(rows):
        return lax.all_to_all(rows, AXES, split_axis=0, concat_axis=0, tiled=True)

    def arrive(rows):
        width = rows.shape[-1]
        moved = swap_blocks(rows.reshape(devices, seq_dev, piece_len, width))
        if piece_len == BLOCK:
            return moved
        moved = moved.transpose(1, 0, 2, 3).reshape(seq_dev, SEQ // BLOCK, BLOCK, width)
        return moved.transpose(1, 0, 2, 3)

    def leave(rows):
        width = rows.shape[-1]
        if piece_len != BLOCK:
            rows = rows.transpose(1, 0, 2, 3).reshape(seq_dev, devices, piece_len, width)
            rows = rows.transpose(1, 0, 2, 3)
        return swap_blocks(rows).reshape(seq_total, piece_len, width)

    fsdp = lax.axis_size("fsdp")
    minor = minor_of(fsdp)
    major = fsdp // minor
    place = (lax.axis_index("dp") // 2, lax.axis_index("fsdp") // minor, my_index % minor)

    def target_of(device, far, high, low):
        dp_index, rest = device // fsdp, device % fsdp
        dp_index = (dp_index + 2 * far) % chunks
        rest = (rest // minor + high) % major * minor + (rest % minor + low) % minor
        return dp_index * fsdp + rest

    def send_blocks(partial, shifts, block_of):
        parts = [block_of(0, 0, 0)]
        for shift in shifts:
            route = [(i, target_of(i, *shift)) for i in range(devices)]
            parts.append(lax.ppermute(block_of(*shift), AXES, route))
        return parts

    def send_near(partial):
        shape = (chunks // 2, major, minor, rows_dev, partial.shape[-1])
        blocks = partial.reshape(shape)

        def block_of(far, high, low):
            start = ((place[0] + far) % shape[0], 0, (place[2] + low) % minor, 0, 0)
            return lax.dynamic_slice(blocks, start, (1, major, 1, *shape[3:]))

        shifts = [(far, 0, low) for far in range(shape[0]) for low in range(minor)][1:]
        return send_blocks(blocks, shifts, block_of)

    def send_far(partial):
        blocks = partial.reshape(major, rows_dev, partial.shape[-1])

        def block_of(far, high, low):
            return lax.dynamic_index_in_dim(blocks, (place[1] + high) % major, 0, False)

        return send_blocks(blocks, [(0, high, 0) for high in range(1, major)], block_of)

    def total(parts):
        result = sum(part.astype(f32) for part in parts)
        return result.reshape(-1, result.shape[-1])

    def total_low(parts):
        return total(parts).astype(bf16)

    dealt_tok = deal(tokens, lengths, permutation)
    dealt_cot = deal(cotangent, lengths, permutation)
    if rows_dev % 8 == 0:
        sizes = sizes_of(chunks, lax.axis_size("fsdp"))
        packed, dealt_tok = tie(packed, dealt_tok)
        held = spread_far(packed, sizes)
        dealt_tok, held = tie(dealt_tok, held)
        tok = arrive(dealt_tok)
        held, dealt_cot = tie(held, dealt_cot)
        full = spread_near(held, sizes)
    else:
        tok = arrive(dealt_tok)
        full = lax.all_gather(packed, AXES, axis=0, tiled=True)
    wu = full[:, 3 * D : 3 * D + 4 * WIN].reshape(FF, WIN)
    vecs = jnp.pad(full[:, 3 * D + 4 * WIN : 3 * D + 4 * WIN + 6].astype(f32).T, ((0, 2), (0, 0)))
    dealt_cot, tok, full, wu, vecs, len_arr = tie(dealt_cot, tok, full, wu, vecs, len_arr)
    cot = arrive(dealt_cot)

    x0, qa0, ka0, va0, ctx0 = attn_fwd(len_arr, tok, full, 0)
    x1, qa1, ka1, va1, ctx1 = attn_fwd(len_arr, tok, full, 1)
    out, n1, n2, inv, slope, act, stat = mid_fwd(len_arr, x0, x1, ctx0, ctx1, full, wu, vecs)
    cot, out = tie(cot, out)
    back_out = leave(out)
    gctx, base, mine, given = mid_bwd(
        len_arr, cot, ctx0, ctx1, n1, n2, inv, slope, act, full, wu, vecs, chunks
    )
    mine = total_low([mine, lax.ppermute(given, "dp", pairing)])
    gctx, mine = tie(gctx, mine)
    parts = send_near(mine)
    ig0, dw0, given0 = attn_bwd(
        len_arr, qa0, ka0, va0, ctx0, gctx, x0, base, full, 0, chunks
    )
    ig0, dw0, given0, gctx, back_out, *parts = tie(ig0, dw0, given0, gctx, back_out, *parts)
    back0 = leave(ig0)
    given0 = lax.ppermute(given0, "dp", pairing)
    parts = send_far(total_low(parts))
    ig1, dw1, given1 = attn_bwd(
        len_arr, qa1, ka1, va1, ctx1, gctx, x1, base, full, 1, chunks
    )
    ig1, dw0, dw1, given0, given1, back0, *parts = tie(
        ig1, dw0, dw1, given0, given1, back0, *parts
    )
    back1 = leave(ig1)
    given1 = lax.ppermute(given1, "dp", pairing)
    mine_in = jnp.concatenate([total_low([dw0, given0]), total_low([dw1, given1])], axis=0)
    parts_in = send_near(mine_in)
    stat, dealt_lengths, lengths, *parts = tie(stat, dealt_lengths, lengths, *parts)
    places = places_of(lengths, permutation)
    output = restore(back_out, places)
    input_grad = restore(back0, places)
    output, input_grad, *parts_in = tie(output, input_grad, *parts_in)
    mine = total(parts)
    mine_in = total(send_far(total_low(parts_in)))

    swap = dealt_lengths[:, 0] < dealt_lengths[:, 1]
    my_swap = lax.dynamic_index_in_dim(swap, my_index, 0, False)
    input_grad = restore(back1, places, input_grad)
    lens = jnp.stack([len_arr[0], ROWS - len_arr[0]]).astype(f32)
    sums = jnp.stack([stat[4:8, 0], stat[0:4, 0] - stat[4:8, 0]], axis=1)
    rms = jnp.sqrt(sums / (lens[None, :] * D) + rms_eps)
    stream_rms = jnp.where(my_swap, rms[:, ::-1], rms)
    vec = lambda i: mine[:, 2 * D + 4 * WIN + i]

    def unpadded(block):
        return (
            jnp.where(odd, block[:, 64:], block[:, :192]),
            jnp.where(odd, block[:, 0], block[:, 192]),
        )

    dq, dqb = unpadded(mine_in[:, :WIN])
    dk, _ = unpadded(mine_in[:, WIN : 2 * WIN])
    dv, dvb = unpadded(mine_in[:, 2 * WIN :])
    dup, dub = unpadded(mine[:, 2 * D : 2 * D + 4 * WIN].reshape(up_dev, WIN))
    return (
        output, input_grad, dq, dqb, dk, dv, dvb, mine[:, :D], vec(0), vec(1), vec(2), dup, dub,
        mine[:, D : 2 * D], vec(3), vec(4), vec(5), stream_rms,
    )


def solution(mesh):
    rows = P(None, AXES, None)
    mat = P(AXES, None)
    vec = P(AXES)
    in_specs = (
        rows, rows, P(), P(), mat, vec, mat, mat, vec, mat, vec, vec, vec, mat, vec, mat, vec, vec,
        vec,
    )
    out_specs = (
        rows, rows, mat, vec, mat, mat, vec, mat, vec, vec, vec, mat, vec, mat, vec, vec, vec,
        P(None, AXES),
    )
    return jax.shard_map(
        on_device, mesh=mesh, in_specs=in_specs, out_specs=out_specs, check_vma=False
    )
```
